32 devices in a mesh: section: 2 (over core), chan: 4 (over z), tok: 4 (over y, x).
Axes of the slice: x: 2, y: 2, z: 4, core: 2. Of those that a mesh axis runs over, the one named last changes fastest.
Arguments:
- gate_streams: bfloat16 [2, 2, 8192, 2048], P('section', None, 'chan', 'tok'), may hold values from -6 to 6
- inputs: bfloat16 [8192, 2048], P('chan', 'tok'), may hold values from -6 to 6
- medium_taps: bfloat16 [8192, 128], P('chan'), may hold values from -0.5 to 0.5
- residues: float32 [8192, 16], P('chan'), may hold values from -3 to 3
- decay_rates: float32 [8192, 16], P('chan'), may hold values from 9.2773438e-05 to 0.034, as said below
Outputs:
- mixer_out: bfloat16 [2, 8192, 2048], P('section', 'chan', 'tok')
The draws below stay inside these ranges and needn't reach their ends.
Inputs may be any that keep to these rules, and one draw needn't show every extreme that they name: `decay_rates`: every rate is positive.
All inputs are finite; a program needn't handle non-finite values.
Results may differ from the reference program's by a relative error of at most 0.0057.
Values may be sent and summed in bfloat16 or wider, within the bound.
No kernel may reach another device: no remote copies, remote signals or barrier semaphores. Data moves between devices by JAX's collectives and lax.ppermute only.
A program may use at most 128 MiB of HBM per device.

```python
import math
import jax
import jax.numpy as jnp
from jax import lax

D = 8192
MR_LEN = 128
ORDER = 16
SEQ = 2048


def draw_decay_rates(key, part):
    choose_key, slow_key, fast_key = jax.random.split(jax.random.fold_in(key, 7), 3)
    rate_shape = (D, ORDER)
    slow_rates = jnp.exp(jax.random.uniform(slow_key, rate_shape, jnp.float32, jnp.log(0.2 / SEQ), jnp.log(2.0 / SEQ)))
    fast_rates = jnp.exp(jax.random.uniform(fast_key, rate_shape, jnp.float32, jnp.log(1.0 / 50.0), jnp.log(1.0 / 30.0)))
    slow_share = 0.5
    chosen = jax.random.uniform(choose_key, rate_shape, jnp.float32) < slow_share
    return jnp.where(chosen, slow_rates, fast_rates).astype(jnp.float32)


def level_of(own_key, shape, cuts, smallest, top_value):
    gain, own = 1.0, jax.random.fold_in(own_key, 6)
    for dim, shards_of in cuts:
        heights = jnp.exp(jax.random.uniform(jax.random.fold_in(own, dim), (shards_of,), jnp.float32, smallest / len(cuts), top_value / len(cuts)))
        gain = gain * jnp.repeat(heights, shape[dim] // shards_of).reshape([-1 if axis == dim else 1 for axis in range(len(shape))])
    return gain


def noise(stream_key, shape, spread, bound, cuts=(), kind=jnp.bfloat16):
    drawn = spread * jax.random.normal(stream_key, shape, jnp.float32)
    if cuts:
        drawn = drawn * level_of(stream_key, shape, cuts, -0.22, 0.18)
    return jnp.clip(drawn, -bound, bound).astype(kind)


def setup_inputs(seed: int = 0) -> dict:
    arg_keys = jax.random.split(jax.random.key(seed), 6)
    return {
        "gate_streams": noise(arg_keys[0], (2, 2, D, SEQ), 1.0, 6.0, ((0, 2), (2, 4), (3, 4))),
        "inputs": noise(arg_keys[1], (D, SEQ), 1.0, 6.0, ((0, 4), (1, 4))),
        "medium_taps": noise(arg_keys[2], (D, MR_LEN), MR_LEN ** -0.5, 0.5, ((0, 4),)),
        "residues": noise(arg_keys[3], (D, ORDER), 0.5, 3.0, ((0, 4),), jnp.float32),
        "decay_rates": draw_decay_rates(jax.random.fold_in(arg_keys[5], 71), 0),
    }


def medium_filter(product, medium_taps):
    padded = jnp.pad(product.astype(jnp.float32), ((0, 0), (MR_LEN - 1, 0)))
    taps_wide = medium_taps.astype(jnp.float32)
    summed = jnp.zeros(product.shape, jnp.float32)
    for offset in range(MR_LEN):
        begin = MR_LEN - 1 - offset
        summed = summed + taps_wide[:, offset:offset + 1] * padded[:, begin:begin + SEQ]
    return summed

def long_convolve(gated_signal, residues, decay_rates):
    scaled = residues * jnp.sqrt(1.0 - jnp.exp(-2.0 * decay_rates))
    positions = jnp.arange(SEQ).astype(jnp.float32)
    long_taps = lax.optimization_barrier(jnp.sum(scaled[:, :, None] * jnp.exp(-decay_rates[:, :, None] * positions[None, None, :]), axis=1))
    length = 2 * SEQ
    spectrum = jnp.fft.rfft(gated_signal.astype(jnp.float32), n=length, axis=1) * jnp.fft.rfft(long_taps, n=length, axis=1)
    return jnp.fft.irfft(spectrum, n=length, axis=1)[:, :SEQ]

def reference(gate_streams, inputs, medium_taps, residues, decay_rates):
    channel_group = math.gcd(D, 64)
    groups_count = D // channel_group

    def grouped(array):
        return array.reshape(groups_count, channel_group, array.shape[-1])
    product = (gate_streams[0, 1].astype(jnp.float32) * inputs.astype(jnp.float32)).astype(jnp.bfloat16)
    medium = lax.map(lambda members: medium_filter(members[0], members[1]), (grouped(product), grouped(medium_taps))).reshape(D, SEQ)
    gated_medium = (gate_streams[0, 0].astype(jnp.float32) * medium).astype(jnp.bfloat16)
    stream = inputs.astype(jnp.float32) + gated_medium.astype(jnp.float32)
    gated_signal = (gate_streams[1, 1].astype(jnp.float32) * stream).astype(jnp.bfloat16)
    long_out = lax.map(lambda members: long_convolve(members[0], members[1], members[2]), (grouped(gated_signal), grouped(residues), grouped(decay_rates))).reshape(D, SEQ)
    mixed_long = (stream + gate_streams[1, 0].astype(jnp.float32) * long_out).astype(jnp.bfloat16)
    return jnp.stack([gated_medium, mixed_long])
```

```python
import functools

import jax
import jax.numpy as jnp
import numpy as np
from jax import lax
from jax.experimental import pallas as pl
from jax.experimental.pallas import tpu as pltpu
from jax.sharding import PartitionSpec as P

SEGS = 8


def split_pair(matrix):
    high = jnp.asarray(matrix, jnp.float32).astype(jnp.bfloat16)
    low = (jnp.asarray(matrix, jnp.float32) - high.astype(jnp.float32)).astype(jnp.bfloat16)
    return high, low


def fourier_tables(window):
    size = 2 * window
    time = np.arange(size)[:, None]
    freq = np.arange(window)[None, :]
    angle = 2.0 * np.pi * ((time * freq) % size) / size
    nyquist = np.where(time % 2 == 0, 1.0, -1.0)
    real = np.cos(angle)
    imag = -np.sin(angle)
    imag_packed = imag.copy()
    imag_packed[:, :1] = nyquist
    forward = np.concatenate([real, imag_packed], axis=1)
    real_packed = real.copy()
    real_packed[:, :1] = nyquist
    taps_forward = np.concatenate([real, real_packed, imag], axis=1)[:window]
    weight = np.where(freq == 0, 1.0, 2.0) / size
    inverse_real = (np.cos(angle) * weight)[window:].T
    inverse_imag = -np.sin(angle) * weight
    inverse_imag[:, :1] = nyquist / size
    inverse = np.concatenate([inverse_real, inverse_imag[window:].T], axis=0)
    return forward, taps_forward, inverse


def dot_f32(left, right):
    return jnp.dot(left, right, preferred_element_type=jnp.float32)


def medium_kernel(
    place, gate_in, inputs, halo, gate_out, taps, fwd_h, fwd_l, tap_h, tap_l, inv_h, inv_l, out
):
    @pl.when(place[0] == 0)
    def _():
        channels, tokens = inputs.shape
        window = taps.shape[1]
        blocks = tokens // window
        product = (gate_in[0, 0].astype(jnp.float32) * inputs[...].astype(jnp.float32)).astype(
            jnp.bfloat16
        )
        started = jnp.where(place[1] > 0, 1.0, 0.0).astype(jnp.bfloat16)
        previous = halo[...] * started
        tap_rows = taps[...]
        tap_spec = dot_f32(tap_rows, tap_h[...]) + dot_f32(tap_rows, tap_l[...])
        real_a = tap_spec[:, :window]
        real_b = tap_spec[:, window : 2 * window]
        imag = tap_spec[:, 2 * window :]
        for block in range(blocks):
            current = product[:, block * window : (block + 1) * window]
            both = jnp.concatenate([previous, current], axis=1)
            spec = dot_f32(both, fwd_h[...]) + dot_f32(both, fwd_l[...])
            spec_a = spec[:, :window]
            spec_b = spec[:, window:]
            filtered = jnp.concatenate(
                [spec_a * real_a - spec_b * imag, spec_a * imag + spec_b * real_b], axis=1
            )
            high = filtered.astype(jnp.bfloat16)
            low = (filtered - high.astype(jnp.float32)).astype(jnp.bfloat16)
            medium = dot_f32(high, inv_h[...]) + (
                dot_f32(low, inv_h[...]) + dot_f32(high, inv_l[...])
            )
            gate = gate_out[0, 0, :, block * window : (block + 1) * window].astype(jnp.float32)
            out[:, block * window : (block + 1) * window] = (gate * medium).astype(jnp.bfloat16)
            previous = current


def medium_call(place, gate_streams, inputs, halo, taps, first, count):
    channels, tokens = count, inputs.shape[1]
    window = taps.shape[1]
    step = min(256, channels)
    base = first // step
    forward, taps_forward, inverse = fourier_tables(window)
    tables = split_pair(forward) + split_pair(taps_forward) + split_pair(inverse)

    def mine(i, place):
        return jnp.where(place[0] == 0, base + i, base)

    def whole(array):
        return pl.BlockSpec(array.shape, lambda i, place: (0, 0))

    return pl.pallas_call(
        medium_kernel,
        out_shape=jax.ShapeDtypeStruct((channels, tokens), jnp.bfloat16),
        grid_spec=pltpu.PrefetchScalarGridSpec(
            num_scalar_prefetch=1,
            grid=(channels // step,),
            in_specs=[
                pl.BlockSpec((1, 1, step, tokens), lambda i, place: (0, 1, mine(i, place), 0)),
                pl.BlockSpec((step, tokens), lambda i, place: (mine(i, place), 0)),
                pl.BlockSpec((step, window), lambda i, place: (mine(i, place), 0)),
                pl.BlockSpec((1, 1, step, tokens), lambda i, place: (0, 0, mine(i, place), 0)),
                pl.BlockSpec((step, window), lambda i, place: (mine(i, place), 0)),
            ]
            + [whole(t) for t in tables],
            out_specs=pl.BlockSpec(
                (step, tokens), lambda i, place: (jnp.where(place[0] == 0, i, 0), 0)
            ),
        ),
        name="medium",
    )(place, gate_streams, inputs, halo, gate_streams, taps, *tables)


def transposed_signal(signal, target):
    size = signal.shape[0]
    for block in range(signal.shape[1] // size):
        target[block * size : (block + 1) * size, :] = signal[
            :, block * size : (block + 1) * size
        ].T


def gated(gate_in, inputs, gated_medium):
    stream = inputs[...].astype(jnp.float32) + gated_medium[...].astype(jnp.float32)
    signal = (gate_in[0, 0].astype(jnp.float32) * stream).astype(jnp.bfloat16)
    return stream, signal.astype(jnp.float32)


def final_kernel(place, gate_in, inputs, gated_medium, rates, ends, total, turned):
    @pl.when(place[0] == 1)
    def _():
        _, signal = gated(gate_in, inputs, gated_medium)
        transposed_signal(signal, turned)
        width, tokens = signal.shape
        length = tokens // SEGS
        slow = rates[...].T
        modes = slow.shape[0]
        decay = jnp.exp(-slow)
        factors = [jnp.broadcast_to(decay[n : n + 1], (SEGS, width)) for n in range(modes)]

        def advance(i, states):
            fresh = turned[pl.ds(i, SEGS, stride=length), :]
            return tuple(s * f + fresh for s, f in zip(states, factors))

        states = lax.fori_loop(
            0,
            length,
            advance,
            tuple(jnp.zeros((SEGS, width), jnp.float32) for _ in range(modes)),
            unroll=4,
        )
        behind = (
            (SEGS - 1 - lax.broadcasted_iota(jnp.int32, (SEGS, width), 0)) * length
        ).astype(jnp.float32)
        rows = []
        for n in range(modes):
            ends[n] = states[n]
            weight = jnp.exp(-jnp.broadcast_to(slow[n : n + 1], (SEGS, width)) * behind)
            rows.append(jnp.sum(states[n] * weight, axis=0, keepdims=True))
        total[...] = jnp.concatenate(rows, axis=0)


def final_call(place, gate_streams, inputs, gated_medium, rates, first, count):
    tokens = inputs.shape[1]
    modes = rates.shape[1]
    step = 128
    base = first // step

    def here(i, place):
        return jnp.where(place[0] == 1, i, 0)

    def mine(i, place):
        return base + here(i, place)

    return pl.pallas_call(
        final_kernel,
        out_shape=(
            jax.ShapeDtypeStruct((modes, SEGS, count), jnp.float32),
            jax.ShapeDtypeStruct((modes, count), jnp.float32),
        ),
        grid_spec=pltpu.PrefetchScalarGridSpec(
            num_scalar_prefetch=1,
            grid=(count // step,),
            in_specs=[
                pl.BlockSpec((1, 1, step, tokens), lambda i, place: (0, 1, mine(i, place), 0)),
                pl.BlockSpec((step, tokens), lambda i, place: (mine(i, place), 0)),
                pl.BlockSpec((step, tokens), lambda i, place: (here(i, place), 0)),
                pl.BlockSpec((step, modes), lambda i, place: (mine(i, place), 0)),
            ],
            out_specs=(
                pl.BlockSpec((modes, SEGS, step), lambda i, place: (0, 0, here(i, place))),
                pl.BlockSpec((modes, step), lambda i, place: (0, here(i, place))),
            ),
            scratch_shapes=[pltpu.VMEM((tokens, step), jnp.float32)],
        ),
        name="final_states",
    )(place, gate_streams, inputs, gated_medium, rates)


def long_kernel(
    hops,
    place,
    gate_in,
    inputs,
    other_medium,
    own_medium,
    gate_out,
    rates,
    residues,
    ends,
    *rest,
):
    arrived = rest[:hops]
    out, turned, answer = rest[hops:]

    @pl.when(place[0] == 0)
    def _():
        out[0] = own_medium[...]

    @pl.when(place[0] == 1)
    def _():
        stream, signal = gated(gate_in, inputs, other_medium)
        transposed_signal(signal, turned)
        width, tokens = signal.shape
        length = tokens // SEGS
        slow = rates[...].T
        modes = slow.shape[0]
        scaled = residues[...].T * jnp.sqrt(1.0 - jnp.exp(-2.0 * slow))
        decay = jnp.exp(-slow)
        leap = jnp.exp(-slow * length)
        entering = jnp.zeros((modes, width), jnp.float32)
        for k in range(hops):
            keep = jnp.where(place[1] > k, 1.0, 0.0)
            entering = entering + arrived[k][...] * (jnp.exp(-slow * (tokens * k)) * keep)
        starts = []
        for n in range(modes):
            state = entering[n : n + 1]
            rows = [state]
            for seg in range(SEGS - 1):
                state = state * leap[n : n + 1] + ends[n, seg : seg + 1, :]
                rows.append(state)
            starts.append(jnp.concatenate(rows, axis=0))
        factors = [jnp.broadcast_to(decay[n : n + 1], (SEGS, width)) for n in range(modes)]
        weights = [jnp.broadcast_to(scaled[n : n + 1], (SEGS, width)) for n in range(modes)]

        def advance(i, states):
            fresh = turned[pl.ds(i, SEGS, stride=length), :]
            states = tuple(s * f + fresh for s, f in zip(states, factors))
            terms = [s * w for s, w in zip(states, weights)]
            while len(terms) > 1:
                terms = [a + b for a, b in zip(terms[::2], terms[1::2])]
            answer[pl.ds(i, SEGS, stride=length), :] = terms[0]
            return states

        lax.fori_loop(0, length, advance, tuple(starts), unroll=4)
        for block in range(tokens // width):
            part = slice(block * width, (block + 1) * width)
            gate = gate_out[0, 0, :, part].astype(jnp.float32)
            out[0, :, part] = (stream[:, part] + gate * answer[part, :].T).astype(jnp.bfloat16)


def long_call(place, gate_streams, inputs, other, own, rates, residues, ends, arrived, first):
    count, tokens = own.shape
    modes = rates.shape[1]
    step = 128
    base = first // step

    def here(i, place):
        return jnp.where(place[0] == 1, i, 0)

    def mine(i, place):
        return base + here(i, place)

    wide = (step, tokens)
    return pl.pallas_call(
        functools.partial(long_kernel, len(arrived)),
        out_shape=jax.ShapeDtypeStruct((1, count, tokens), jnp.bfloat16),
        grid_spec=pltpu.PrefetchScalarGridSpec(
            num_scalar_prefetch=1,
            grid=(count // step,),
            in_specs=[
                pl.BlockSpec((1, 1) + wide, lambda i, place: (0, 1, mine(i, place), 0)),
                pl.BlockSpec(wide, lambda i, place: (mine(i, place), 0)),
                pl.BlockSpec(wide, lambda i, place: (here(i, place), 0)),
                pl.BlockSpec(wide, lambda i, place: (jnp.where(place[0] == 0, i, 0), 0)),
                pl.BlockSpec((1, 1) + wide, lambda i, place: (0, 0, mine(i, place), 0)),
                pl.BlockSpec((step, modes), lambda i, place: (mine(i, place), 0)),
                pl.BlockSpec((step, modes), lambda i, place: (mine(i, place), 0)),
                pl.BlockSpec((modes, SEGS, step), lambda i, place: (0, 0, here(i, place))),
            ]
            + [pl.BlockSpec((modes, step), lambda i, place: (0, here(i, place)))] * len(arrived),
            out_specs=pl.BlockSpec((1,) + wide, lambda i, place: (0, i, 0)),
            scratch_shapes=[pltpu.VMEM((tokens, step), jnp.float32)] * 2,
        ),
        name="long",
    )(place, gate_streams, inputs, other, own, gate_streams, rates, residues, ends, *arrived)


def ring(value, axis, by):
    peers = lax.axis_size(axis)
    return lax.ppermute(value, axis, [(i, (i + by) % peers) for i in range(peers)])


def on_device(gate_streams, inputs, medium_taps, residues, decay_rates):
    channels, tokens = inputs.shape
    window = medium_taps.shape[1]
    place = jnp.stack([lax.axis_index("section"), lax.axis_index("tok")]).astype(jnp.int32)
    tail = slice(tokens - window, tokens)
    edge = (
        gate_streams[0, 1, :, tail].astype(jnp.float32) * inputs[:, tail].astype(jnp.float32)
    ).astype(jnp.bfloat16)
    halo = ring(edge, "tok", 1)
    medium = medium_call(place, gate_streams, inputs, halo, medium_taps, 0, channels)
    other = ring(medium, "section", 1)
    ends, total = final_call(place, gate_streams, inputs, other, decay_rates, 0, channels)
    arrived = [ring(total, "tok", by) for by in range(1, lax.axis_size("tok"))]
    return long_call(
        place, gate_streams, inputs, other, medium, decay_rates, residues, ends, arrived, 0
    )


def solution(mesh):
    placed = (
        P("section", None, "chan", "tok"),
        P("chan", "tok"),
        P("chan", None),
        P("chan", None),
        P("chan", None),
    )
    return jax.shard_map(
        on_device,
        mesh=mesh,
        in_specs=placed,
        out_specs=P("section", "chan", "tok"),
        check_vma=False,
    )
```

```python
import functools

import jax
import jax.numpy as jnp
import numpy as np
from jax import lax
from jax.experimental import pallas as pl
from jax.experimental.pallas import tpu as pltpu
from jax.sharding import PartitionSpec as P

ROWS = 8


def split_pair(matrix):
    high = jnp.asarray(matrix, jnp.float32).astype(jnp.bfloat16)
    low = (jnp.asarray(matrix, jnp.float32) - high.astype(jnp.float32)).astype(jnp.bfloat16)
    return high, low


def stacked(matrix, axis):
    return jnp.concatenate(split_pair(matrix), axis=axis)


def fourier_tables(window):
    size = 2 * window
    time = np.arange(window)[:, None]
    freq = np.arange(window)[None, :]
    angle = 2.0 * np.pi * ((time * freq) % size) / size
    sign = np.where(freq % 2 == 0, 1.0, -1.0)
    nyquist = np.where(time % 2 == 0, 1.0, -1.0)
    weight = np.where(freq == 0, 1.0, 2.0) / size
    forward, inverse = [], []
    for odd in range(2):
        flip = sign if odd else np.ones_like(sign)
        real = np.cos(angle) * flip
        imag = -np.sin(angle) * flip
        imag[:, :1] = nyquist
        forward.append(stacked(np.concatenate([real, imag], axis=1), 0))
        back_real = np.cos(angle) * weight * flip
        back_imag = -np.sin(angle) * weight * flip
        back_imag[:, :1] = nyquist / size
        inverse.append(stacked(np.concatenate([back_real.T, back_imag.T], axis=0), 1))
    return forward, inverse


def turned_tables(window):
    half = window // 2
    time = np.arange(window)[:, None]
    freq = 2 * np.arange(half)[None, :] + 1
    angle = np.pi * ((time * freq) % (2 * window)) / window
    real, imag = np.cos(angle), -np.sin(angle)
    zero = np.zeros_like(real)
    forward = np.concatenate(
        [
            np.concatenate([real, zero, imag, zero], axis=1),
            np.concatenate([zero, real, zero, imag], axis=1),
        ],
        axis=0,
    )
    inverse = forward.T * (2.0 / window)
    doubled = np.concatenate([real, real, imag, imag], axis=1)
    return forward, inverse, doubled


def dot_f32(left, right):
    return jnp.dot(left, right, preferred_element_type=jnp.float32)


def dot_turned(left, right):
    return lax.dot_general(
        left, right, (((1,), (1,)), ((), ())), preferred_element_type=jnp.float32
    )


def medium_kernel(
    place, gate_in, inputs, halo, gate_out, taps, fwd_even, fwd_odd, inv_even, inv_odd, out
):
    @pl.when(place[0] == 0)
    def _():
        channels, tokens = inputs.shape
        window = taps.shape[1]
        blocks = tokens // window
        forward = (fwd_even, fwd_odd)
        inverse = (inv_even, inv_odd)
        tap_rows = taps[...]
        spec = dot_f32(jnp.concatenate([tap_rows, tap_rows], axis=1), fwd_even[...])
        lane = lax.broadcasted_iota(jnp.int32, (channels, window), 1)
        real, packed = spec[:, :window], spec[:, window:]
        real_b = jnp.where(lane == 0, packed, real)
        imag = jnp.where(lane == 0, 0.0, packed)
        started = jnp.where(place[1] > 0, 1.0, 0.0).astype(jnp.bfloat16)

        def spectrum(block, rows):
            return dot_f32(jnp.concatenate([rows, rows], axis=1), forward[block % 2][...])

        before = spectrum(-1, halo[...] * started)
        for block in range(blocks):
            part = slice(block * window, (block + 1) * window)
            product = gate_in[0, 0, :, part].astype(jnp.float32) * inputs[:, part].astype(
                jnp.float32
            )
            current = spectrum(block, product.astype(jnp.bfloat16))
            total = before + current
            before = current
            a, b = total[:, :window], total[:, window:]
            filtered = jnp.concatenate([a * real - b * imag, a * imag + b * real_b], axis=1)
            pair = dot_f32(filtered.astype(jnp.bfloat16), inverse[block % 2][...])
            medium = pair[:, :window] + pair[:, window:]
            gate = gate_out[0, 0, :, part].astype(jnp.float32)
            out[:, part] = (gate * medium).astype(jnp.bfloat16)


def whole(array):
    return pl.BlockSpec(array.shape, lambda i, place: (0,) * array.ndim)


def only(section, base=0):
    return lambda i, place: jnp.where(place[0] == section, base + i, base)


def medium_call(place, gate_streams, inputs, halo, taps, first, count):
    tokens = inputs.shape[1]
    window = taps.shape[1]
    step = min(256, count)
    forward, inverse = fourier_tables(window)
    tables = forward + inverse
    row = only(0, first // step)
    own = only(0)
    return pl.pallas_call(
        medium_kernel,
        out_shape=jax.ShapeDtypeStruct((count, tokens), jnp.bfloat16),
        grid_spec=pltpu.PrefetchScalarGridSpec(
            num_scalar_prefetch=1,
            grid=(count // step,),
            in_specs=[
                pl.BlockSpec((1, 1, step, tokens), lambda i, p: (0, 1, row(i, p), 0)),
                pl.BlockSpec((step, tokens), lambda i, p: (row(i, p), 0)),
                pl.BlockSpec((step, window), lambda i, p: (own(i, p), 0)),
                pl.BlockSpec((1, 1, step, tokens), lambda i, p: (0, 0, row(i, p), 0)),
                pl.BlockSpec((step, window), lambda i, p: (row(i, p), 0)),
            ]
            + [whole(t) for t in tables],
            out_specs=pl.BlockSpec((step, tokens), lambda i, p: (own(i, p), 0)),
        ),
        name="medium",
    )(place, gate_streams, inputs, halo, gate_streams, taps, *tables)


def lane_mask(modes):
    shape = (ROWS, ROWS * modes)
    lane = lax.broadcasted_iota(jnp.int32, shape, 1)
    return lane // modes == lax.broadcasted_iota(jnp.int32, shape, 0)


def wide_row(ref, group, modes):
    return jnp.broadcast_to(ref[group : group + 1, :], (ROWS, ROWS * modes))


def powers(slow, window, first, falling):
    row = lax.broadcasted_iota(jnp.int32, slow.shape, 0).astype(jnp.float32)
    hop = jnp.exp(-slow * ROWS)
    tile = jnp.exp(-slow * (first + (ROWS - 1 - row if falling else row)))
    tiles = [tile]
    for _ in range(window // ROWS - 1):
        tile = tile * hop
        tiles.append(tile)
    if falling:
        tiles = tiles[::-1]
    return jnp.concatenate(tiles, axis=0).astype(jnp.bfloat16)


def scale_of(residues, slow):
    return residues * jnp.sqrt(1.0 - jnp.exp(-2.0 * slow))


def response_kernel(modes, place, rates, residues, table_h, table_l, out):
    @pl.when(place[0] == 1)
    def _():
        window = table_h.shape[0]
        mask = lane_mask(modes)
        parts = []
        for group in range(rates.shape[0]):
            slow = wide_row(rates, group, modes)
            scale = scale_of(wide_row(residues, group, modes), slow)
            scale = jnp.where(mask, scale / (1.0 + jnp.exp(-slow * window)), 0.0)
            high = scale.astype(jnp.bfloat16).astype(jnp.float32)
            both = jnp.concatenate([high, scale - high], axis=0).astype(jnp.bfloat16)
            pair = dot_turned(both, powers(slow, window, 0.0, False))
            parts.append(pair[:ROWS] + pair[ROWS:])
        taps = jnp.concatenate(parts, axis=0)
        high = taps.astype(jnp.bfloat16)
        low = (taps - high.astype(jnp.float32)).astype(jnp.bfloat16)
        out[...] = dot_f32(high, table_h[...]) + (
            dot_f32(low, table_h[...]) + dot_f32(high, table_l[...])
        )


def response_call(place, rates, residues, modes, window, first, count):
    step = 128
    tables = split_pair(turned_tables(window)[2])
    rows = step // ROWS
    row = only(1, first // step)
    own = only(1)
    return pl.pallas_call(
        functools.partial(response_kernel, modes),
        out_shape=jax.ShapeDtypeStruct((count, 2 * window), jnp.float32),
        grid_spec=pltpu.PrefetchScalarGridSpec(
            num_scalar_prefetch=1,
            grid=(count // step,),
            in_specs=[
                pl.BlockSpec((rows, ROWS * modes), lambda i, p: (row(i, p), 0)),
                pl.BlockSpec((rows, ROWS * modes), lambda i, p: (row(i, p), 0)),
            ]
            + [whole(t) for t in tables],
            out_specs=pl.BlockSpec((step, 2 * window), lambda i, p: (own(i, p), 0)),
        ),
        name="response",
    )(place, rates, residues, *tables)


def stream_part(inputs, gated_medium, part):
    return inputs[:, part].astype(jnp.float32) + gated_medium[:, part].astype(jnp.float32)


def states_kernel(modes, window, place, gate_in, inputs, gated_medium, rates, ends, total):
    @pl.when(place[0] == 1)
    def _():
        blocks = inputs.shape[1] // window
        mask = lane_mask(modes)
        signal = (
            gate_in[0, 0].astype(jnp.float32) * stream_part(inputs, gated_medium, slice(None))
        ).astype(jnp.bfloat16)
        sums = []
        for group in range(rates.shape[0]):
            rows = slice(group * ROWS, (group + 1) * ROWS)
            slow = wide_row(rates, group, modes)
            left = jnp.concatenate(
                [signal[rows, b * window : (b + 1) * window] for b in range(blocks)], axis=0
            )
            found = dot_f32(left, powers(slow, window, 0.0, True))
            leap = jnp.exp(-slow * window)
            state = None
            for b in range(blocks):
                end = jnp.where(mask, found[b * ROWS : (b + 1) * ROWS], 0.0)
                ends[b, rows, :] = end
                state = end if state is None else state * leap + end
            sums.append(jnp.sum(state, axis=0, keepdims=True))
        total[...] = jnp.concatenate(sums, axis=0)


def states_call(place, gate_streams, inputs, gated_medium, rates, modes, window, first, count):
    tokens = inputs.shape[1]
    step = 128
    row = only(1, first // step)
    own = only(1)
    lanes = ROWS * modes
    return pl.pallas_call(
        functools.partial(states_kernel, modes, window),
        out_shape=(
            jax.ShapeDtypeStruct((tokens // window, count, lanes), jnp.float32),
            jax.ShapeDtypeStruct((count // ROWS, lanes), jnp.float32),
        ),
        grid_spec=pltpu.PrefetchScalarGridSpec(
            num_scalar_prefetch=1,
            grid=(count // step,),
            in_specs=[
                pl.BlockSpec((1, 1, step, tokens), lambda i, p: (0, 1, row(i, p), 0)),
                pl.BlockSpec((step, tokens), lambda i, p: (row(i, p), 0)),
                pl.BlockSpec((step, tokens), lambda i, p: (own(i, p), 0)),
                pl.BlockSpec((step // ROWS, lanes), lambda i, p: (row(i, p), 0)),
            ],
            out_specs=(
                pl.BlockSpec((tokens // window, step, lanes), lambda i, p: (0, own(i, p), 0)),
                pl.BlockSpec((step // ROWS, lanes), lambda i, p: (own(i, p), 0)),
            ),
        ),
        name="states",
    )(place, gate_streams, inputs, gated_medium, rates)


def within_kernel(place, gate_in, inputs, gated_medium, response, fwd_h, fwd_l, inverse, out):
    @pl.when(place[0] == 1)
    def _():
        size = fwd_h.shape[0]
        half = size // 2
        real, imag = response[:, :half], response[:, half:]
        for pair in range(inputs.shape[1] // size):
            part = slice(pair * size, (pair + 1) * size)
            signal = (
                gate_in[0, 0, :, part].astype(jnp.float32)
                * stream_part(inputs, gated_medium, part)
            ).astype(jnp.bfloat16)
            spec = dot_f32(signal, fwd_h[...]) + dot_f32(signal, fwd_l[...])
            a, b = spec[:, :half], spec[:, half:]
            filtered = jnp.concatenate([a * real - b * imag, a * imag + b * real], axis=1)
            out[:, part] = dot_f32(filtered.astype(jnp.bfloat16), inverse[...])


def within_call(place, gate_streams, inputs, gated_medium, response, first, count):
    tokens = inputs.shape[1]
    window = response.shape[1] // 2
    step = min(256, count)
    forward, inverse, _ = turned_tables(window)
    tables = split_pair(forward) + split_pair(inverse)[:1]
    row = only(1, first // step)
    own = only(1)
    return pl.pallas_call(
        within_kernel,
        out_shape=jax.ShapeDtypeStruct((count, tokens), jnp.float32),
        grid_spec=pltpu.PrefetchScalarGridSpec(
            num_scalar_prefetch=1,
            grid=(count // step,),
            in_specs=[
                pl.BlockSpec((1, 1, step, tokens), lambda i, p: (0, 1, row(i, p), 0)),
                pl.BlockSpec((step, tokens), lambda i, p: (row(i, p), 0)),
                pl.BlockSpec((step, tokens), lambda i, p: (own(i, p), 0)),
                pl.BlockSpec((step, 2 * window), lambda i, p: (own(i, p), 0)),
            ]
            + [whole(t) for t in tables],
            out_specs=pl.BlockSpec((step, tokens), lambda i, p: (own(i, p), 0)),
        ),
        name="within",
    )(place, gate_streams, inputs, gated_medium, response, *tables)


def output_kernel(
    hops,
    modes,
    window,
    place,
    within,
    inputs,
    other_medium,
    own_medium,
    gate_out,
    rates,
    residues,
    ends,
    *rest,
):
    arrived, out = rest[:hops], rest[hops]

    @pl.when(place[0] == 0)
    def _():
        out[0] = own_medium[...]

    @pl.when(place[0] == 1)
    def _():
        tokens = inputs.shape[1]
        blocks = tokens // window
        mask = lane_mask(modes)
        rows_all = rates[...]
        entering = jnp.zeros_like(rows_all)
        for k in range(hops):
            keep = jnp.where(place[1] > k, 1.0, 0.0)
            entering = entering + arrived[k][...] * (jnp.exp(-rows_all * (tokens * k)) * keep)
        for group in range(rates.shape[0]):
            rows = slice(group * ROWS, (group + 1) * ROWS)
            slow = wide_row(rates, group, modes)
            scale = scale_of(wide_row(residues, group, modes), slow)
            leap = jnp.exp(-slow * window)
            share = scale / (1.0 + leap)
            start = jnp.broadcast_to(entering[group : group + 1], slow.shape)
            state = jnp.where(mask, start, 0.0)
            lefts = []
            for b in range(blocks):
                end = ends[b, rows, :]
                lefts.append(state * scale + end * share)
                state = state * leap + end
            left = jnp.concatenate(lefts, axis=0).astype(jnp.bfloat16)
            across = dot_turned(left, powers(slow, window, 1.0, False))
            for b in range(blocks):
                part = slice(b * window, (b + 1) * window)
                stream = inputs[rows, part].astype(jnp.float32) + other_medium[
                    rows, part
                ].astype(jnp.float32)
                long_out = within[rows, part] + across[b * ROWS : (b + 1) * ROWS]
                gate = gate_out[0, 0, rows, part].astype(jnp.float32)
                out[0, rows, part] = (stream + gate * long_out).astype(jnp.bfloat16)


def output_call(
    place, gate_streams, within, inputs, other, own, rates, residues, ends, arrived, window, first
):
    count, tokens = own.shape
    lanes = rates.shape[1]
    step = 128
    row = only(1, first // step)
    here = only(1)
    there = only(0)
    wide = (step, tokens)
    small = (step // ROWS, lanes)
    return pl.pallas_call(
        functools.partial(output_kernel, len(arrived), lanes // ROWS, window),
        out_shape=jax.ShapeDtypeStruct((1, count, tokens), jnp.bfloat16),
        grid_spec=pltpu.PrefetchScalarGridSpec(
            num_scalar_prefetch=1,
            grid=(count // step,),
            in_specs=[
                pl.BlockSpec(wide, lambda i, p: (here(i, p), 0)),
                pl.BlockSpec(wide, lambda i, p: (row(i, p), 0)),
                pl.BlockSpec(wide, lambda i, p: (here(i, p), 0)),
                pl.BlockSpec(wide, lambda i, p: (there(i, p), 0)),
                pl.BlockSpec((1, 1) + wide, lambda i, p: (0, 0, row(i, p), 0)),
                pl.BlockSpec(small, lambda i, p: (row(i, p), 0)),
                pl.BlockSpec(small, lambda i, p: (row(i, p), 0)),
                pl.BlockSpec(
                    (tokens // window, step, lanes), lambda i, p: (0, here(i, p), 0)
                ),
            ]
            + [pl.BlockSpec(small, lambda i, p: (here(i, p), 0))] * len(arrived),
            out_specs=pl.BlockSpec((1,) + wide, lambda i, p: (0, i, 0)),
        ),
        name="output",
    )(place, within, inputs, other, own, gate_streams, rates, residues, ends, *arrived)


def ring(value, axis, by):
    peers = lax.axis_size(axis)
    return lax.ppermute(value, axis, [(i, (i + by) % peers) for i in range(peers)])


def on_device(gate_streams, inputs, medium_taps, residues, decay_rates):
    channels, tokens = inputs.shape
    window = medium_taps.shape[1]
    modes = decay_rates.shape[1]
    place = jnp.stack([lax.axis_index("section"), lax.axis_index("tok")]).astype(jnp.int32)
    tail = slice(tokens - window, tokens)
    edge = (
        gate_streams[0, 1, :, tail].astype(jnp.float32) * inputs[:, tail].astype(jnp.float32)
    ).astype(jnp.bfloat16)
    halo = ring(edge, "tok", 1)
    rates = decay_rates.reshape(channels // ROWS, ROWS * modes)
    weights = residues.reshape(channels // ROWS, ROWS * modes)
    response = response_call(place, rates, weights, modes, window, 0, channels)
    medium = medium_call(place, gate_streams, inputs, halo, medium_taps, 0, channels)
    other = ring(medium, "section", 1)
    ends, total = states_call(
        place, gate_streams, inputs, other, rates, modes, window, 0, channels
    )
    arrived = [ring(total, "tok", by) for by in range(1, lax.axis_size("tok"))]
    within = within_call(place, gate_streams, inputs, other, response, 0, channels)
    return output_call(
        place, gate_streams, within, inputs, other, medium, rates, weights, ends, arrived, window, 0
    )


def solution(mesh):
    placed = (
        P("section", None, "chan", "tok"),
        P("chan", "tok"),
        P("chan", None),
        P("chan", None),
        P("chan", None),
    )
    return jax.shard_map(
        on_device,
        mesh=mesh,
        in_specs=placed,
        out_specs=P("section", "chan", "tok"),
        check_vma=False,
    )
```

```python
import functools

import jax
import jax.numpy as jnp
import numpy as np
from jax import lax
from jax.experimental import pallas as pl
from jax.experimental.pallas import tpu as pltpu
from jax.sharding import PartitionSpec as P

ROWS = 8


def split_pair(matrix):
    high = jnp.asarray(matrix, jnp.float32).astype(jnp.bfloat16)
    low = (jnp.asarray(matrix, jnp.float32) - high.astype(jnp.float32)).astype(jnp.bfloat16)
    return high, low


def stacked(matrix, axis):
    return jnp.concatenate(split_pair(matrix), axis=axis)


def fourier_tables(window):
    size = 2 * window
    time = np.arange(window)[:, None]
    freq = np.arange(window)[None, :]
    angle = 2.0 * np.pi * ((time * freq) % size) / size
    sign = np.where(freq % 2 == 0, 1.0, -1.0)
    nyquist = np.where(time % 2 == 0, 1.0, -1.0)
    weight = np.where(freq == 0, 1.0, 2.0) / size
    forward, inverse = [], []
    for odd in range(2):
        flip = sign if odd else np.ones_like(sign)
        real = np.cos(angle) * flip
        imag = -np.sin(angle) * flip
        imag[:, :1] = nyquist
        forward.append(stacked(np.concatenate([real, imag], axis=1), 0))
        back_real = np.cos(angle) * weight * flip
        back_imag = -np.sin(angle) * weight * flip
        back_imag[:, :1] = nyquist / size
        inverse.append(stacked(np.concatenate([back_real.T, back_imag.T], axis=0), 1))
    return forward, inverse


def turned_tables(window):
    half = window // 2
    time = np.arange(window)[:, None]
    freq = 2 * np.arange(half)[None, :] + 1
    angle = np.pi * ((time * freq) % (2 * window)) / window
    real, imag = np.cos(angle), -np.sin(angle)
    zero = np.zeros_like(real)
    forward = np.concatenate(
        [
            np.concatenate([real, zero, imag, zero], axis=1),
            np.concatenate([zero, real, zero, imag], axis=1),
        ],
        axis=0,
    )
    inverse = forward.T * (2.0 / window)
    doubled = np.concatenate([real, real, imag, imag], axis=1)
    return forward, inverse, doubled


PAIR = 16


def dot_f32(left, right):
    return jnp.dot(left, right, preferred_element_type=jnp.float32)


def dot_turned(left, right):
    return lax.dot_general(
        left, right, (((1,), (1,)), ((), ())), preferred_element_type=jnp.float32
    )


def whole(array):
    return pl.BlockSpec(array.shape, lambda i, place: (0,) * array.ndim)


def mine(share, step):
    return lambda i, place: place[0] * (share // step) + i


def by_section(place, body):
    for section in range(2):
        pl.when(place[0] == section)(functools.partial(body, section))


def lane_mask(modes):
    shape = (ROWS, ROWS * modes)
    lane = lax.broadcasted_iota(jnp.int32, shape, 1)
    return lane // modes == lax.broadcasted_iota(jnp.int32, shape, 0)


def spread(ref, group):
    return jnp.broadcast_to(ref[group : group + 1, :], (ROWS, ref.shape[1]))


def powers(slow, hop, window, first, falling):
    row = lax.broadcasted_iota(jnp.int32, slow.shape, 0).astype(jnp.float32)
    tiles = [jnp.exp(-slow * (first + (ROWS - 1 - row if falling else row)))]
    while len(tiles) < window // ROWS:
        tiles = tiles + [tile * hop for tile in tiles]
        hop = hop * hop
    if falling:
        tiles = tiles[::-1]
    return jnp.concatenate(tiles, axis=0).astype(jnp.bfloat16)


def both_powers(rates, hops, pair, window, first, falling):
    sides = [
        powers(spread(rates, g), spread(hops, g), window, first, falling)
        for g in (2 * pair, 2 * pair + 1)
    ]
    return jnp.concatenate(sides, axis=1)


def two_sided(upper, lower):
    zero = jnp.zeros_like(upper)
    return jnp.concatenate(
        [
            jnp.concatenate([upper, zero], axis=1),
            jnp.concatenate([zero, lower], axis=1),
        ],
        axis=0,
    )


def scale_of(residues, slow):
    return residues * jnp.sqrt(1.0 - jnp.exp(-2.0 * slow))


def response_kernel(modes, place, rates, residues, table_h, table_l, out, hops, scales):
    window = table_h.shape[0]
    mask = lane_mask(modes)
    slow = rates[...]
    hops[...] = jnp.exp(-slow * ROWS)
    scales[...] = scale_of(residues[...], slow) / (1.0 + jnp.exp(-slow * window))
    parts = []
    for pair in range(rates.shape[0] // 2):
        scale = two_sided(
            jnp.where(mask, spread(scales, 2 * pair), 0.0),
            jnp.where(mask, spread(scales, 2 * pair + 1), 0.0),
        )
        high = scale.astype(jnp.bfloat16).astype(jnp.float32)
        both = jnp.concatenate([high, scale - high], axis=0).astype(jnp.bfloat16)
        found = dot_turned(both, both_powers(rates, hops, pair, window, 0.0, False))
        parts.append(found[:PAIR] + found[PAIR:])
    taps = jnp.concatenate(parts, axis=0)
    high = taps.astype(jnp.bfloat16)
    low = (taps - high.astype(jnp.float32)).astype(jnp.bfloat16)
    out[...] = dot_f32(high, table_h[...]) + (
        dot_f32(low, table_h[...]) + dot_f32(high, table_l[...])
    )


def response_call(place, rates, residues, modes, window, share):
    step = min(256, share)
    tables = split_pair(turned_tables(window)[2])
    small = (step // ROWS, ROWS * modes)
    row = mine(share, step)
    return pl.pallas_call(
        functools.partial(response_kernel, modes),
        out_shape=jax.ShapeDtypeStruct((share, 2 * window), jnp.float32),
        grid_spec=pltpu.PrefetchScalarGridSpec(
            num_scalar_prefetch=1,
            grid=(share // step,),
            in_specs=[pl.BlockSpec(small, lambda i, p: (row(i, p), 0))] * 2
            + [whole(t) for t in tables],
            out_specs=pl.BlockSpec((step, 2 * window), lambda i, p: (i, 0)),
            scratch_shapes=[pltpu.VMEM(small, jnp.float32)] * 2,
        ),
        name="response",
    )(place, rates, residues, *tables)


def front_kernel(
    modes,
    place,
    local,
    remote,
    inputs,
    halo_low,
    halo_high,
    taps,
    rates,
    fwd_even,
    fwd_odd,
    inv_even,
    inv_odd,
    medium_out,
    ends,
    total,
    hops,
    leaps,
):
    channels, tokens = inputs.shape
    window = taps.shape[1]
    blocks = tokens // window
    forward = (fwd_even, fwd_odd)
    inverse = (inv_even, inv_odd)
    slow = rates[...]
    hops[...] = jnp.exp(-slow * ROWS)
    leaps[...] = jnp.exp(-slow * window)

    def body(section):
        first = local.at[0] if section == 0 else remote
        second = remote if section == 0 else local.at[0]
        halo = halo_low if section == 0 else halo_high
        tap_rows = taps[...]
        started = jnp.where(place[1] > 0, 1.0, 0.0).astype(jnp.bfloat16)
        parts = [slice(b * window, (b + 1) * window) for b in range(blocks)]
        sources = [
            (first[1, :, part].astype(jnp.float32) * inputs[:, part].astype(jnp.float32)).astype(
                jnp.bfloat16
            )
            for part in parts
        ]
        sources = [halo[...] * started] + sources
        even = [tap_rows] + sources[1::2]
        odd = sources[0::2]
        spectra = []
        for table, members in zip(forward, (even, odd)):
            rows = jnp.concatenate(members, axis=0)
            found = dot_f32(jnp.concatenate([rows, rows], axis=1), table[...])
            spectra.append(
                [found[k * channels : (k + 1) * channels] for k in range(len(members))]
            )
        lane = lax.broadcasted_iota(jnp.int32, (channels, window), 1)
        real, packed = spectra[0][0][:, :window], spectra[0][0][:, window:]
        real_b = jnp.where(lane == 0, packed, real)
        imag = jnp.where(lane == 0, 0.0, packed)
        in_order = [None] * (blocks + 1)
        in_order[1::2] = spectra[0][1:]
        in_order[0::2] = spectra[1]
        products = []
        for block in range(blocks):
            mixed = in_order[block] + in_order[block + 1]
            a, b = mixed[:, :window], mixed[:, window:]
            products.append(
                jnp.concatenate([a * real - b * imag, a * imag + b * real_b], axis=1).astype(
                    jnp.bfloat16
                )
            )
        signals = [None] * blocks
        for parity in range(2):
            members = products[parity::2]
            found = dot_f32(jnp.concatenate(members, axis=0), inverse[parity][...])
            for k in range(len(members)):
                block = 2 * k + parity
                rows = slice(k * channels, (k + 1) * channels)
                medium = found[rows, :window] + found[rows, window:]
                gate = first[0, :, parts[block]].astype(jnp.float32)
                gated = (gate * medium).astype(jnp.bfloat16)
                medium_out[:, parts[block]] = gated
                stream = inputs[:, parts[block]].astype(jnp.float32) + gated.astype(jnp.float32)
                signals[block] = (
                    second[1, :, parts[block]].astype(jnp.float32) * stream
                ).astype(jnp.bfloat16)
        mask = lane_mask(modes)
        lanes = ROWS * modes
        sums = []
        for pair in range(channels // PAIR):
            rows = slice(pair * PAIR, (pair + 1) * PAIR)
            left = jnp.concatenate([signal[rows] for signal in signals], axis=0)
            found = dot_f32(left, both_powers(rates, hops, pair, window, 0.0, True))
            for side in range(2):
                leap = spread(leaps, 2 * pair + side)
                state = None
                for b in range(blocks):
                    top = b * PAIR + side * ROWS
                    end = jnp.where(
                        mask, found[top : top + ROWS, side * lanes : (side + 1) * lanes], 0.0
                    )
                    at = pair * PAIR + side * ROWS
                    ends[b, at : at + ROWS, :] = end
                    state = end if state is None else state * leap + end
                sums.append(jnp.sum(state, axis=0, keepdims=True))
        total[...] = jnp.concatenate(sums, axis=0)

    by_section(place, body)


def front_call(place, gate_streams, swapped, inputs, halos, taps, rates, modes, share):
    tokens = inputs.shape[1]
    window = taps.shape[1]
    step = min(256, share)
    forward, inverse = fourier_tables(window)
    tables = forward + inverse
    row = mine(share, step)
    lanes = ROWS * modes
    small = (step // ROWS, lanes)
    blocks = tokens // window
    return pl.pallas_call(
        functools.partial(front_kernel, modes),
        out_shape=(
            jax.ShapeDtypeStruct((share, tokens), jnp.bfloat16),
            jax.ShapeDtypeStruct((blocks, share, lanes), jnp.float32),
            jax.ShapeDtypeStruct((share // ROWS, lanes), jnp.float32),
        ),
        grid_spec=pltpu.PrefetchScalarGridSpec(
            num_scalar_prefetch=1,
            grid=(share // step,),
            in_specs=[
                pl.BlockSpec((1, 2, step, tokens), lambda i, p: (0, 0, row(i, p), 0)),
                pl.BlockSpec((2, step, tokens), lambda i, p: (0, i, 0)),
                pl.BlockSpec((step, tokens), lambda i, p: (row(i, p), 0)),
                pl.BlockSpec((step, window), lambda i, p: (i, 0)),
                pl.BlockSpec((step, window), lambda i, p: (i, 0)),
                pl.BlockSpec((step, window), lambda i, p: (row(i, p), 0)),
                pl.BlockSpec(small, lambda i, p: (row(i, p), 0)),
            ]
            + [whole(t) for t in tables],
            out_specs=(
                pl.BlockSpec((step, tokens), lambda i, p: (i, 0)),
                pl.BlockSpec((blocks, step, lanes), lambda i, p: (0, i, 0)),
                pl.BlockSpec(small, lambda i, p: (i, 0)),
            ),
            scratch_shapes=[pltpu.VMEM(small, jnp.float32)] * 2,
        ),
        name="front",
    )(place, gate_streams, swapped, inputs, *halos, taps, rates, *tables)


def within_kernel(place, local, remote, inputs, gated_medium, response, fwd_h, fwd_l, inverse, out):
    size = fwd_h.shape[0]
    half = size // 2

    def body(section):
        gate_in = remote.at[0] if section == 0 else local.at[0, 0]
        real, imag = response[:, :half], response[:, half:]
        for pair in range(inputs.shape[1] // size):
            part = slice(pair * size, (pair + 1) * size)
            stream = inputs[:, part].astype(jnp.float32) + gated_medium[:, part].astype(
                jnp.float32
            )
            signal = (gate_in[:, part].astype(jnp.float32) * stream).astype(jnp.bfloat16)
            spec = dot_f32(signal, fwd_h[...]) + dot_f32(signal, fwd_l[...])
            a, b = spec[:, :half], spec[:, half:]
            filtered = jnp.concatenate([a * real - b * imag, a * imag + b * real], axis=1)
            out[:, part] = dot_f32(filtered.astype(jnp.bfloat16), inverse[...])

    by_section(place, body)


def within_call(place, gate_streams, swapped, inputs, gated_medium, response, share):
    tokens = inputs.shape[1]
    window = response.shape[1] // 2
    step = min(256, share)
    forward, inverse, _ = turned_tables(window)
    tables = split_pair(forward) + split_pair(inverse)[:1]
    row = mine(share, step)
    return pl.pallas_call(
        within_kernel,
        out_shape=jax.ShapeDtypeStruct((share, tokens), jnp.float32),
        grid_spec=pltpu.PrefetchScalarGridSpec(
            num_scalar_prefetch=1,
            grid=(share // step,),
            in_specs=[
                pl.BlockSpec((1, 1, step, tokens), lambda i, p: (0, 1, row(i, p), 0)),
                pl.BlockSpec((1, step, tokens), lambda i, p: (1, i, 0)),
                pl.BlockSpec((step, tokens), lambda i, p: (row(i, p), 0)),
                pl.BlockSpec((step, tokens), lambda i, p: (i, 0)),
                pl.BlockSpec((step, 2 * window), lambda i, p: (i, 0)),
            ]
            + [whole(t) for t in tables],
            out_specs=pl.BlockSpec((step, tokens), lambda i, p: (i, 0)),
        ),
        name="within",
    )(place, gate_streams, swapped, inputs, gated_medium, response, *tables)


def output_kernel(
    count,
    modes,
    window,
    place,
    local,
    remote,
    within,
    inputs,
    gated_medium,
    rates,
    residues,
    ends,
    *rest,
):
    arrived, (out, hops, leaps, scales, shares, starts) = rest[:count], rest[count:]
    channels, tokens = inputs.shape
    blocks = tokens // window
    mask = lane_mask(modes)
    slow = rates[...]
    leap_all = jnp.exp(-slow * window)
    scale_all = scale_of(residues[...], slow)
    hops[...] = jnp.exp(-slow * ROWS)
    leaps[...] = leap_all
    scales[...] = scale_all
    shares[...] = scale_all / (1.0 + leap_all)
    entering = jnp.zeros_like(slow)
    for k in range(count):
        keep = jnp.where(place[1] > k, 1.0, 0.0)
        entering = entering + arrived[k][...] * (jnp.exp(-slow * (tokens * k)) * keep)
    starts[...] = entering

    def body(section):
        gate_out = remote.at[0] if section == 0 else local.at[0, 0]
        for pair in range(channels // PAIR):
            rows = slice(pair * PAIR, (pair + 1) * PAIR)
            sides = []
            for side in range(2):
                group = 2 * pair + side
                leap, scale = spread(leaps, group), spread(scales, group)
                share = spread(shares, group)
                state = jnp.where(mask, spread(starts, group), 0.0)
                at = pair * PAIR + side * ROWS
                lefts = []
                for b in range(blocks):
                    end = ends[b, at : at + ROWS, :]
                    lefts.append(state * scale + end * share)
                    state = state * leap + end
                sides.append(lefts)
            left = jnp.concatenate(
                [two_sided(upper, lower) for upper, lower in zip(*sides)], axis=0
            ).astype(jnp.bfloat16)
            across = dot_turned(left, both_powers(rates, hops, pair, window, 1.0, False))
            for b in range(blocks):
                part = slice(b * window, (b + 1) * window)
                stream = inputs[rows, part].astype(jnp.float32) + gated_medium[
                    rows, part
                ].astype(jnp.float32)
                long_out = within[rows, part] + across[b * PAIR : (b + 1) * PAIR]
                gate = gate_out[rows, part].astype(jnp.float32)
                out[rows, part] = (stream + gate * long_out).astype(jnp.bfloat16)

    by_section(place, body)


def output_call(
    place, gate_streams, swapped, within, inputs, medium, rates, residues, ends, arrived, window
):
    share, tokens = medium.shape
    lanes = rates.shape[1]
    step = min(256, share)
    row = mine(share, step)
    wide = (step, tokens)
    small = (step // ROWS, lanes)
    return pl.pallas_call(
        functools.partial(output_kernel, len(arrived), lanes // ROWS, window),
        out_shape=jax.ShapeDtypeStruct((share, tokens), jnp.bfloat16),
        grid_spec=pltpu.PrefetchScalarGridSpec(
            num_scalar_prefetch=1,
            grid=(share // step,),
            in_specs=[
                pl.BlockSpec((1, 1) + wide, lambda i, p: (0, 0, row(i, p), 0)),
                pl.BlockSpec((1,) + wide, lambda i, p: (0, i, 0)),
                pl.BlockSpec(wide, lambda i, p: (i, 0)),
                pl.BlockSpec(wide, lambda i, p: (row(i, p), 0)),
                pl.BlockSpec(wide, lambda i, p: (i, 0)),
                pl.BlockSpec(small, lambda i, p: (row(i, p), 0)),
                pl.BlockSpec(small, lambda i, p: (row(i, p), 0)),
                pl.BlockSpec((tokens // window, step, lanes), lambda i, p: (0, i, 0)),
            ]
            + [pl.BlockSpec(small, lambda i, p: (i, 0))] * len(arrived),
            out_specs=pl.BlockSpec(wide, lambda i, p: (i, 0)),
            scratch_shapes=[pltpu.VMEM(small, jnp.float32)] * 5,
        ),
        name="output",
    )(
        place, gate_streams, swapped, within, inputs, medium, rates, residues, ends, *arrived
    )


def ring(value, axis, by):
    peers = lax.axis_size(axis)
    return lax.ppermute(value, axis, [(i, (i + by) % peers) for i in range(peers)])


def edge_to(value, section):
    peers = lax.axis_size("tok")
    pairs = [(i, section * peers + (i + 1) % peers) for i in range(peers)]
    pairs += [(peers + i, (1 - section) * peers + i) for i in range(peers)]
    return lax.ppermute(value, ("section", "tok"), pairs)


def on_device(gate_streams, inputs, medium_taps, residues, decay_rates):
    channels, tokens = inputs.shape
    share = channels // 2
    window = medium_taps.shape[1]
    modes = decay_rates.shape[1]
    section = lax.axis_index("section")
    place = jnp.stack([section, lax.axis_index("tok")]).astype(jnp.int32)
    tail = slice(tokens - window, tokens)
    edge = (
        gate_streams[0, 1, :, tail].astype(jnp.float32) * inputs[:, tail].astype(jnp.float32)
    ).astype(jnp.bfloat16)
    halos = [edge_to(edge[s * share : (s + 1) * share], s) for s in range(2)]
    lent = lax.dynamic_slice_in_dim(gate_streams[0], (1 - section) * share, share, 1)
    swapped = ring(lent, "section", 1)
    rates = decay_rates.reshape(channels // ROWS, ROWS * modes)
    weights = residues.reshape(channels // ROWS, ROWS * modes)
    response = response_call(place, rates, weights, modes, window, share)
    medium, ends, total = front_call(
        place, gate_streams, swapped, inputs, halos, medium_taps, rates, modes, share
    )
    arrived = [ring(total, "tok", by) for by in range(1, lax.axis_size("tok"))]
    medium_other = ring(medium, "section", 1)
    within = within_call(place, gate_streams, swapped, inputs, medium, response, share)
    mixed = output_call(
        place, gate_streams, swapped, within, inputs, medium, rates, weights, ends, arrived, window
    )
    mixed_other = ring(mixed, "section", 1)
    leading = section == 0
    upper = jnp.where(leading, medium, mixed_other)
    lower = jnp.where(leading, medium_other, mixed)
    return jnp.concatenate([upper, lower], axis=0)[None]


def solution(mesh):
    placed = (
        P("section", None, "chan", "tok"),
        P("chan", "tok"),
        P("chan", None),
        P("chan", None),
        P("chan", None),
    )
    return jax.shard_map(
        on_device,
        mesh=mesh,
        in_specs=placed,
        out_specs=P("section", "chan", "tok"),
        check_vma=False,
    )
```

```python
import functools

import jax
import jax.numpy as jnp
import numpy as np
from jax import lax
from jax.experimental import pallas as pl
from jax.experimental.pallas import tpu as pltpu
from jax.sharding import PartitionSpec as P

ROWS = 8


def split_pair(matrix):
    high = jnp.asarray(matrix, jnp.float32).astype(jnp.bfloat16)
    low = (jnp.asarray(matrix, jnp.float32) - high.astype(jnp.float32)).astype(jnp.bfloat16)
    return high, low


def stacked(matrix, axis):
    return jnp.concatenate(split_pair(matrix), axis=axis)


def fourier_tables(window):
    size = 2 * window
    time = np.arange(window)[:, None]
    freq = np.arange(window)[None, :]
    angle = 2.0 * np.pi * ((time * freq) % size) / size
    sign = np.where(freq % 2 == 0, 1.0, -1.0)
    nyquist = np.where(time % 2 == 0, 1.0, -1.0)
    weight = np.where(freq == 0, 1.0, 2.0) / size
    forward, inverse = [], []
    for odd in range(2):
        flip = sign if odd else np.ones_like(sign)
        real = np.cos(angle) * flip
        imag = -np.sin(angle) * flip
        imag[:, :1] = nyquist
        forward.append(stacked(np.concatenate([real, imag], axis=1), 0))
        back_real = np.cos(angle) * weight * flip
        back_imag = -np.sin(angle) * weight * flip
        back_imag[:, :1] = nyquist / size
        inverse.append(stacked(np.concatenate([back_real.T, back_imag.T], axis=0), 1))
    return forward, inverse


def turned_tables(window):
    half = window // 2
    time = np.arange(window)[:, None]
    freq = 2 * np.arange(half)[None, :] + 1
    angle = np.pi * ((time * freq) % (2 * window)) / window
    real, imag = np.cos(angle), -np.sin(angle)
    zero = np.zeros_like(real)
    forward = np.concatenate(
        [
            np.concatenate([real, zero, imag, zero], axis=1),
            np.concatenate([zero, real, zero, imag], axis=1),
        ],
        axis=0,
    )
    inverse = forward.T * (2.0 / window)
    doubled = np.concatenate([real, real, imag, imag], axis=1)
    return forward, inverse, doubled


PAIR = 16
COMPILER = pltpu.CompilerParams(vmem_limit_bytes=16 << 20)


def parked(*arrays):
    return [pltpu.with_memory_space_constraint(a, pltpu.HBM) for a in arrays]


def cost(share, tokens, work):
    size = share * tokens
    return pl.CostEstimate(
        flops=size * work, bytes_accessed=size * 12, transcendentals=size // 64
    )


def dot_f32(left, right):
    return jnp.dot(left, right, preferred_element_type=jnp.float32)


def dot_turned(left, right):
    return lax.dot_general(
        left, right, (((1,), (1,)), ((), ())), preferred_element_type=jnp.float32
    )


def whole(array):
    return pl.BlockSpec(array.shape, lambda i, p, t: (0,) * array.ndim)


def mine(share, step):
    return lambda i, p, t: p[0] * (share // step) + i


def by_section(sec, body):
    for section in range(2):
        pl.when(sec[0] == section)(functools.partial(body, section))


def lane_mask(modes):
    shape = (ROWS, ROWS * modes)
    lane = lax.broadcasted_iota(jnp.int32, shape, 1)
    return lane // modes == lax.broadcasted_iota(jnp.int32, shape, 0)


def spread(ref, group):
    return jnp.broadcast_to(ref[group : group + 1, :], (ROWS, ref.shape[1]))


def powers(slow, hop, window, first, falling):
    row = lax.broadcasted_iota(jnp.int32, slow.shape, 0).astype(jnp.float32)
    tiles = [jnp.exp(-slow * (first + (ROWS - 1 - row if falling else row)))]
    while len(tiles) < window // ROWS:
        tiles = tiles + [tile * hop for tile in tiles]
        hop = hop * hop
    if falling:
        tiles = tiles[::-1]
    return jnp.concatenate(tiles, axis=0).astype(jnp.bfloat16)


def both_powers(rates, hops, pair, window, first, falling):
    sides = [
        powers(spread(rates, g), spread(hops, g), window, first, falling)
        for g in (2 * pair, 2 * pair + 1)
    ]
    return jnp.concatenate(sides, axis=1)


def two_sided(upper, lower):
    zero = jnp.zeros_like(upper)
    return jnp.concatenate(
        [
            jnp.concatenate([upper, zero], axis=1),
            jnp.concatenate([zero, lower], axis=1),
        ],
        axis=0,
    )


def scale_of(residues, slow):
    return residues * jnp.sqrt(1.0 - jnp.exp(-2.0 * slow))


def response_kernel(modes, sec, tok, rates, residues, table_h, table_l, out, hops, scales):
    window = table_h.shape[0]
    mask = lane_mask(modes)
    slow = rates[...]
    hops[...] = jnp.exp(-slow * ROWS)
    scales[...] = scale_of(residues[...], slow) / (1.0 + jnp.exp(-slow * window))
    parts = []
    for pair in range(rates.shape[0] // 2):
        scale = two_sided(
            jnp.where(mask, spread(scales, 2 * pair), 0.0),
            jnp.where(mask, spread(scales, 2 * pair + 1), 0.0),
        )
        high = scale.astype(jnp.bfloat16).astype(jnp.float32)
        both = jnp.concatenate([high, scale - high], axis=0).astype(jnp.bfloat16)
        found = dot_turned(both, both_powers(rates, hops, pair, window, 0.0, False))
        parts.append(found[:PAIR] + found[PAIR:])
    taps = jnp.concatenate(parts, axis=0)
    high = taps.astype(jnp.bfloat16)
    low = (taps - high.astype(jnp.float32)).astype(jnp.bfloat16)
    out[...] = dot_f32(high, table_h[...]) + (
        dot_f32(low, table_h[...]) + dot_f32(high, table_l[...])
    )


def response_call(place, rates, residues, modes, window, share):
    step = min(256, share)
    tables = split_pair(turned_tables(window)[2])
    small = (step // ROWS, ROWS * modes)
    row = mine(share, step)
    return pl.pallas_call(
        functools.partial(response_kernel, modes),
        out_shape=jax.ShapeDtypeStruct((share, 2 * window), jnp.float32),
        grid_spec=pltpu.PrefetchScalarGridSpec(
            num_scalar_prefetch=2,
            grid=(share // step,),
            in_specs=[pl.BlockSpec(small, lambda i, p, t: (row(i, p, t), 0))] * 2
            + [whole(t) for t in tables],
            out_specs=pl.BlockSpec((step, 2 * window), lambda i, p, t: (i, 0)),
            scratch_shapes=[pltpu.VMEM(small, jnp.float32)] * 2,
        ),
        name="response",
        cost_estimate=cost(share, 4 * window, 600),
        compiler_params=COMPILER,
    )(*place, rates, residues, *parked(*tables))


def front_kernel(
    modes,
    sec,
    tok,
    local,
    remote,
    inputs,
    halo_low,
    halo_high,
    taps,
    rates,
    after,
    fwd_even,
    fwd_odd,
    inv_even,
    inv_odd,
    medium_out,
    ends,
    total,
    hops,
    leaps,
):
    channels, tokens = inputs.shape
    window = taps.shape[1]
    blocks = tokens // window
    forward = (fwd_even, fwd_odd)
    inverse = (inv_even, inv_odd)
    slow = rates[...]
    hops[...] = jnp.exp(-slow * ROWS)
    leaps[...] = jnp.exp(-slow * window)

    def body(section):
        first = local.at[0] if section == 0 else remote
        second = remote if section == 0 else local.at[0]
        halo = halo_low if section == 0 else halo_high
        tap_rows = taps[...]
        started = jnp.where(tok[0] > 0, 1.0, 0.0).astype(jnp.bfloat16)
        parts = [slice(b * window, (b + 1) * window) for b in range(blocks)]
        sources = [
            (first[1, :, part].astype(jnp.float32) * inputs[:, part].astype(jnp.float32)).astype(
                jnp.bfloat16
            )
            for part in parts
        ]
        sources = [halo[...] * started] + sources
        even = [tap_rows] + sources[1::2]
        odd = sources[0::2]
        spectra = []
        for table, members in zip(forward, (even, odd)):
            rows = jnp.concatenate(members, axis=0)
            found = dot_f32(jnp.concatenate([rows, rows], axis=1), table[...])
            spectra.append(
                [found[k * channels : (k + 1) * channels] for k in range(len(members))]
            )
        lane = lax.broadcasted_iota(jnp.int32, (channels, window), 1)
        real, packed = spectra[0][0][:, :window], spectra[0][0][:, window:]
        real_b = jnp.where(lane == 0, packed, real)
        imag = jnp.where(lane == 0, 0.0, packed)
        in_order = [None] * (blocks + 1)
        in_order[1::2] = spectra[0][1:]
        in_order[0::2] = spectra[1]
        products = []
        for block in range(blocks):
            mixed = in_order[block] + in_order[block + 1]
            a, b = mixed[:, :window], mixed[:, window:]
            products.append(
                jnp.concatenate([a * real - b * imag, a * imag + b * real_b], axis=1).astype(
                    jnp.bfloat16
                )
            )
        signals = [None] * blocks
        for parity in range(2):
            members = products[parity::2]
            found = dot_f32(jnp.concatenate(members, axis=0), inverse[parity][...])
            for k in range(len(members)):
                block = 2 * k + parity
                rows = slice(k * channels, (k + 1) * channels)
                medium = found[rows, :window] + found[rows, window:]
                gate = first[0, :, parts[block]].astype(jnp.float32)
                gated = (gate * medium).astype(jnp.bfloat16)
                medium_out[:, parts[block]] = gated
                stream = inputs[:, parts[block]].astype(jnp.float32) + gated.astype(jnp.float32)
                signals[block] = (
                    second[1, :, parts[block]].astype(jnp.float32) * stream
                ).astype(jnp.bfloat16)
        mask = lane_mask(modes)
        lanes = ROWS * modes
        sums = []
        for pair in range(channels // PAIR):
            rows = slice(pair * PAIR, (pair + 1) * PAIR)
            left = jnp.concatenate([signal[rows] for signal in signals], axis=0)
            found = dot_f32(left, both_powers(rates, hops, pair, window, 0.0, True))
            for side in range(2):
                leap = spread(leaps, 2 * pair + side)
                state = None
                for b in range(blocks):
                    top = b * PAIR + side * ROWS
                    end = jnp.where(
                        mask, found[top : top + ROWS, side * lanes : (side + 1) * lanes], 0.0
                    )
                    at = pair * PAIR + side * ROWS
                    ends[b, at : at + ROWS, :] = end
                    state = end if state is None else state * leap + end
                sums.append(jnp.sum(state, axis=0, keepdims=True))
        total[...] = jnp.concatenate(sums, axis=0)

    by_section(sec, body)


def front_call(
    place, gate_streams, swapped, inputs, halos, taps, rates, after, modes, share
):
    tokens = inputs.shape[1]
    window = taps.shape[1]
    step = min(256, share)
    forward, inverse = fourier_tables(window)
    tables = forward + inverse
    row = mine(share, step)
    lanes = ROWS * modes
    small = (step // ROWS, lanes)
    blocks = tokens // window
    return pl.pallas_call(
        functools.partial(front_kernel, modes),
        out_shape=(
            jax.ShapeDtypeStruct((share, tokens), jnp.bfloat16),
            jax.ShapeDtypeStruct((blocks, share, lanes), jnp.float32),
            jax.ShapeDtypeStruct((share // ROWS, lanes), jnp.float32),
        ),
        grid_spec=pltpu.PrefetchScalarGridSpec(
            num_scalar_prefetch=2,
            grid=(share // step,),
            in_specs=[
                pl.BlockSpec((1, 2, step, tokens), lambda i, p, t: (0, 0, row(i, p, t), 0)),
                pl.BlockSpec((2, step, tokens), lambda i, p, t: (0, i, 0)),
                pl.BlockSpec((step, tokens), lambda i, p, t: (row(i, p, t), 0)),
                pl.BlockSpec((step, window), lambda i, p, t: (i, 0)),
                pl.BlockSpec((step, window), lambda i, p, t: (i, 0)),
                pl.BlockSpec((step, window), lambda i, p, t: (row(i, p, t), 0)),
                pl.BlockSpec(small, lambda i, p, t: (row(i, p, t), 0)),
                pl.BlockSpec(memory_space=pl.ANY),
            ]
            + [whole(t) for t in tables],
            out_specs=(
                pl.BlockSpec((step, tokens), lambda i, p, t: (i, 0)),
                pl.BlockSpec((blocks, step, lanes), lambda i, p, t: (0, i, 0)),
                pl.BlockSpec(small, lambda i, p, t: (i, 0)),
            ),
            scratch_shapes=[pltpu.VMEM(small, jnp.float32)] * 2,
        ),
        name="front",
        cost_estimate=cost(share, tokens, 2000),
        compiler_params=COMPILER,
    )(*place, gate_streams, swapped, inputs, *halos, taps, rates, after, *parked(*tables))


def within_kernel(sec, tok, local, remote, inputs, gated_medium, response, fwd_h, fwd_l, inverse, out):
    size = fwd_h.shape[0]
    half = size // 2

    def body(section):
        gate_in = remote.at[0] if section == 0 else local.at[0, 0]
        real, imag = response[:, :half], response[:, half:]
        for pair in range(inputs.shape[1] // size):
            part = slice(pair * size, (pair + 1) * size)
            stream = inputs[:, part].astype(jnp.float32) + gated_medium[:, part].astype(
                jnp.float32
            )
            signal = (gate_in[:, part].astype(jnp.float32) * stream).astype(jnp.bfloat16)
            spec = dot_f32(signal, fwd_h[...]) + dot_f32(signal, fwd_l[...])
            a, b = spec[:, :half], spec[:, half:]
            filtered = jnp.concatenate([a * real - b * imag, a * imag + b * real], axis=1)
            out[:, part] = dot_f32(filtered.astype(jnp.bfloat16), inverse[...])

    by_section(sec, body)


def within_call(place, gate_streams, swapped, inputs, gated_medium, response, share):
    tokens = inputs.shape[1]
    window = response.shape[1] // 2
    step = min(256, share)
    forward, inverse, _ = turned_tables(window)
    tables = split_pair(forward) + split_pair(inverse)[:1]
    row = mine(share, step)
    return pl.pallas_call(
        within_kernel,
        out_shape=jax.ShapeDtypeStruct((share, tokens), jnp.float32),
        grid_spec=pltpu.PrefetchScalarGridSpec(
            num_scalar_prefetch=2,
            grid=(share // step,),
            in_specs=[
                pl.BlockSpec((1, 1, step, tokens), lambda i, p, t: (0, 1, row(i, p, t), 0)),
                pl.BlockSpec((1, step, tokens), lambda i, p, t: (1, i, 0)),
                pl.BlockSpec((step, tokens), lambda i, p, t: (row(i, p, t), 0)),
                pl.BlockSpec((step, tokens), lambda i, p, t: (i, 0)),
                pl.BlockSpec((step, 2 * window), lambda i, p, t: (i, 0)),
            ]
            + [whole(t) for t in tables],
            out_specs=pl.BlockSpec((step, tokens), lambda i, p, t: (i, 0)),
        ),
        name="within",
        cost_estimate=cost(share, tokens, 1500),
        compiler_params=COMPILER,
    )(*place, gate_streams, swapped, inputs, gated_medium, response, *parked(*tables))


def output_kernel(
    count,
    modes,
    window,
    sec,
    tok,
    local,
    remote,
    within,
    inputs,
    gated_medium,
    rates,
    residues,
    ends,
    *rest,
):
    arrived, (out, hops, leaps, scales, shares, starts) = rest[:count], rest[count:]
    channels, tokens = inputs.shape
    blocks = tokens // window
    mask = lane_mask(modes)
    slow = rates[...]
    leap_all = jnp.exp(-slow * window)
    scale_all = scale_of(residues[...], slow)
    hops[...] = jnp.exp(-slow * ROWS)
    leaps[...] = leap_all
    scales[...] = scale_all
    shares[...] = scale_all / (1.0 + leap_all)
    entering = jnp.zeros_like(slow)
    for k in range(count):
        keep = jnp.where(tok[0] > k, 1.0, 0.0)
        entering = entering + arrived[k][...] * (jnp.exp(-slow * (tokens * k)) * keep)
    starts[...] = entering

    def body(section):
        gate_out = remote.at[0] if section == 0 else local.at[0, 0]
        for pair in range(channels // PAIR):
            rows = slice(pair * PAIR, (pair + 1) * PAIR)
            sides = []
            for side in range(2):
                group = 2 * pair + side
                leap, scale = spread(leaps, group), spread(scales, group)
                share = spread(shares, group)
                state = jnp.where(mask, spread(starts, group), 0.0)
                at = pair * PAIR + side * ROWS
                lefts = []
                for b in range(blocks):
                    end = ends[b, at : at + ROWS, :]
                    lefts.append(state * scale + end * share)
                    state = state * leap + end
                sides.append(lefts)
            left = jnp.concatenate(
                [two_sided(upper, lower) for upper, lower in zip(*sides)], axis=0
            ).astype(jnp.bfloat16)
            across = dot_turned(left, both_powers(rates, hops, pair, window, 1.0, False))
            for b in range(blocks):
                part = slice(b * window, (b + 1) * window)
                stream = inputs[rows, part].astype(jnp.float32) + gated_medium[
                    rows, part
                ].astype(jnp.float32)
                long_out = within[rows, part] + across[b * PAIR : (b + 1) * PAIR]
                gate = gate_out[rows, part].astype(jnp.float32)
                out[rows, part] = (stream + gate * long_out).astype(jnp.bfloat16)

    by_section(sec, body)


def output_call(
    place, gate_streams, swapped, within, inputs, medium, rates, residues, ends, arrived, window
):
    share, tokens = medium.shape
    lanes = rates.shape[1]
    step = min(256, share)
    row = mine(share, step)
    wide = (step, tokens)
    small = (step // ROWS, lanes)
    return pl.pallas_call(
        functools.partial(output_kernel, len(arrived), lanes // ROWS, window),
        out_shape=jax.ShapeDtypeStruct((share, tokens), jnp.bfloat16),
        grid_spec=pltpu.PrefetchScalarGridSpec(
            num_scalar_prefetch=2,
            grid=(share // step,),
            in_specs=[
                pl.BlockSpec((1, 1) + wide, lambda i, p, t: (0, 0, row(i, p, t), 0)),
                pl.BlockSpec((1,) + wide, lambda i, p, t: (0, i, 0)),
                pl.BlockSpec(wide, lambda i, p, t: (i, 0)),
                pl.BlockSpec(wide, lambda i, p, t: (row(i, p, t), 0)),
                pl.BlockSpec(wide, lambda i, p, t: (i, 0)),
                pl.BlockSpec(small, lambda i, p, t: (row(i, p, t), 0)),
                pl.BlockSpec(small, lambda i, p, t: (row(i, p, t), 0)),
                pl.BlockSpec((tokens // window, step, lanes), lambda i, p, t: (0, i, 0)),
            ]
            + [pl.BlockSpec(small, lambda i, p, t: (i, 0))] * len(arrived),
            out_specs=pl.BlockSpec(wide, lambda i, p, t: (i, 0)),
            scratch_shapes=[pltpu.VMEM(small, jnp.float32)] * 5,
        ),
        name="output",
        cost_estimate=cost(share, tokens, 1500),
        compiler_params=COMPILER,
    )(
        *place, gate_streams, swapped, within, inputs, medium, rates, residues, ends, *arrived
    )


def lend_kernel(sec, tok, gates, gate_tail, input_tail, out, low, high):
    out[...] = gates[0]
    share = low.shape[0]

    @pl.when(pl.program_id(0) == 0)
    def _():
        for half, target in enumerate((low, high)):
            rows = slice(half * share, (half + 1) * share)
            target[...] = (
                gate_tail[0, 0, rows, :].astype(jnp.float32)
                * input_tail[rows, :].astype(jnp.float32)
            ).astype(jnp.bfloat16)


def lend_call(place, gate_streams, inputs, window, share):
    channels, tokens = inputs.shape
    step = min(512, share)
    count = share // step
    last = tokens // window - 1
    edge = jax.ShapeDtypeStruct((share, window), jnp.bfloat16)
    return pl.pallas_call(
        lend_kernel,
        out_shape=(jax.ShapeDtypeStruct((2, share, tokens), jnp.bfloat16), edge, edge),
        grid_spec=pltpu.PrefetchScalarGridSpec(
            num_scalar_prefetch=2,
            grid=(count,),
            in_specs=[
                pl.BlockSpec(
                    (1, 2, step, tokens), lambda i, p, t: (0, 0, (1 - p[0]) * count + i, 0)
                ),
                pl.BlockSpec((1, 1, channels, window), lambda i, p, t: (0, 1, 0, last)),
                pl.BlockSpec((channels, window), lambda i, p, t: (0, last)),
            ],
            out_specs=(
                pl.BlockSpec((2, step, tokens), lambda i, p, t: (0, i, 0)),
                pl.BlockSpec((share, window), lambda i, p, t: (0, 0)),
                pl.BlockSpec((share, window), lambda i, p, t: (0, 0)),
            ),
        ),
        name="lend",
        cost_estimate=cost(share, tokens, 2),
        compiler_params=COMPILER,
    )(*place, gate_streams, gate_streams, inputs)


def ring(value, axis, by):
    peers = lax.axis_size(axis)
    return lax.ppermute(value, axis, [(i, (i + by) % peers) for i in range(peers)])


def edge_to(value, section):
    peers = lax.axis_size("tok")
    pairs = [(i, section * peers + (i + 1) % peers) for i in range(peers)]
    pairs += [(peers + i, (1 - section) * peers + i) for i in range(peers)]
    return lax.ppermute(value, ("section", "tok"), pairs)


def on_device(gate_streams, inputs, medium_taps, residues, decay_rates):
    channels, tokens = inputs.shape
    share = channels // 2
    gate_streams, inputs, medium_taps = parked(gate_streams, inputs, medium_taps)
    window = medium_taps.shape[1]
    modes = decay_rates.shape[1]
    section = lax.axis_index("section")
    place = tuple(
        lax.axis_index(axis).astype(jnp.int32).reshape(1) for axis in ("section", "tok")
    )
    lent, *edges = lend_call(place, gate_streams, inputs, window, share)
    halos = parked(*(edge_to(edges[s], s) for s in range(2)))
    swapped = ring(lent, "section", 1)
    rates = decay_rates.reshape(channels // ROWS, ROWS * modes)
    weights = residues.reshape(channels // ROWS, ROWS * modes)
    response = response_call(place, rates, weights, modes, window, share)
    medium, ends, total = front_call(
        place, gate_streams, swapped, inputs, halos, medium_taps, rates, response, modes, share
    )
    arrived = [ring(total, "tok", by) for by in range(1, lax.axis_size("tok"))]
    medium_other = ring(medium, "section", 1)
    within = within_call(place, gate_streams, swapped, inputs, medium, response, share)
    mixed = output_call(
        place, gate_streams, swapped, within, inputs, medium, rates, weights, ends, arrived, window
    )
    mixed_other = ring(mixed, "section", 1)
    leading = section == 0
    upper = jnp.where(leading, medium, mixed_other)
    lower = jnp.where(leading, medium_other, mixed)
    return jnp.concatenate([upper, lower], axis=0)[None]


def solution(mesh):
    placed = (
        P("section", None, "chan", "tok"),
        P("chan", "tok"),
        P("chan", None),
        P("chan", None),
        P("chan", None),
    )
    return jax.shard_map(
        on_device,
        mesh=mesh,
        in_specs=placed,
        out_specs=P("section", "chan", "tok"),
        check_vma=False,
    )
```

```python
import functools

import jax
import jax.numpy as jnp
import numpy as np
from jax import lax
from jax.experimental import pallas as pl
from jax.experimental.pallas import tpu as pltpu
from jax.sharding import PartitionSpec as P

ROWS = 8


def split_pair(matrix):
    high = jnp.asarray(matrix, jnp.float32).astype(jnp.bfloat16)
    low = (jnp.asarray(matrix, jnp.float32) - high.astype(jnp.float32)).astype(jnp.bfloat16)
    return high, low


def stacked(matrix, axis):
    return jnp.concatenate(split_pair(matrix), axis=axis)


def fourier_tables(window):
    size = 2 * window
    time = np.arange(window)[:, None]
    freq = np.arange(window)[None, :]
    angle = 2.0 * np.pi * ((time * freq) % size) / size
    sign = np.where(freq % 2 == 0, 1.0, -1.0)
    nyquist = np.where(time % 2 == 0, 1.0, -1.0)
    weight = np.where(freq == 0, 1.0, 2.0) / size
    forward, inverse = [], []
    for odd in range(2):
        flip = sign if odd else np.ones_like(sign)
        real = np.cos(angle) * flip
        imag = -np.sin(angle) * flip
        imag[:, :1] = nyquist
        forward.append(stacked(np.concatenate([real, imag], axis=1), 0))
        back_real = np.cos(angle) * weight * flip
        back_imag = -np.sin(angle) * weight * flip
        back_imag[:, :1] = nyquist / size
        inverse.append(stacked(np.concatenate([back_real.T, back_imag.T], axis=0), 1))
    return forward, inverse


def turned_tables(window):
    half = window // 2
    time = np.arange(window)[:, None]
    freq = 2 * np.arange(half)[None, :] + 1
    angle = np.pi * ((time * freq) % (2 * window)) / window
    real, imag = np.cos(angle), -np.sin(angle)
    zero = np.zeros_like(real)
    forward = np.concatenate(
        [
            np.concatenate([real, zero, imag, zero], axis=1),
            np.concatenate([zero, real, zero, imag], axis=1),
        ],
        axis=0,
    )
    inverse = forward.T * (2.0 / window)
    doubled = np.concatenate([real, real, imag, imag], axis=1)
    return forward, inverse, doubled


PAIR = 16
WITHIN_STEP = 512
COMPILER = pltpu.CompilerParams(vmem_limit_bytes=16 << 20)


def parked(*arrays):
    return [pltpu.with_memory_space_constraint(a, pltpu.HBM) for a in arrays]


def cost(share, tokens, work):
    size = share * tokens
    return pl.CostEstimate(
        flops=size * work, bytes_accessed=size * 12, transcendentals=size // 64
    )


def dot_f32(left, right):
    return jnp.dot(left, right, preferred_element_type=jnp.float32)


def dot_turned(left, right):
    return lax.dot_general(
        left, right, (((1,), (1,)), ((), ())), preferred_element_type=jnp.float32
    )


def whole(array):
    return pl.BlockSpec(array.shape, lambda i, p, t: (0,) * array.ndim)


def mine(share, step):
    return lambda i, p, t: p[0] * (share // step) + i


def by_section(sec, body):
    for section in range(2):
        pl.when(sec[0] == section)(functools.partial(body, section))


def lane_mask(modes):
    shape = (ROWS, ROWS * modes)
    lane = lax.broadcasted_iota(jnp.int32, shape, 1)
    return lane // modes == lax.broadcasted_iota(jnp.int32, shape, 0)


def spread(ref, group):
    return jnp.broadcast_to(ref[group : group + 1, :], (ROWS, ref.shape[1]))


def powers(slow, hop, window, first, falling):
    row = lax.broadcasted_iota(jnp.int32, slow.shape, 0).astype(jnp.float32)
    tiles = [jnp.exp(-slow * (first + (ROWS - 1 - row if falling else row)))]
    while len(tiles) < window // ROWS:
        tiles = tiles + [tile * hop for tile in tiles]
        hop = hop * hop
    if falling:
        tiles = tiles[::-1]
    return jnp.concatenate(tiles, axis=0).astype(jnp.bfloat16)


def both_powers(rates, hops, pair, window, falling):
    sides = [
        powers(spread(rates, g), spread(hops, g), window, 0.0, falling)
        for g in (2 * pair, 2 * pair + 1)
    ]
    return jnp.concatenate(sides, axis=1)


def two_sided(upper, lower):
    zero = jnp.zeros_like(upper)
    return jnp.concatenate(
        [
            jnp.concatenate([upper, zero], axis=1),
            jnp.concatenate([zero, lower], axis=1),
        ],
        axis=0,
    )


def scale_of(residues, slow):
    return residues * jnp.sqrt(1.0 - jnp.exp(-2.0 * slow))


def in_rows(ref, tall):
    modes, channels = ref.shape
    tall[...] = ref[...].T
    count = channels // ROWS
    return jnp.concatenate(
        [tall[pl.ds(c, count, stride=ROWS), :] for c in range(ROWS)], axis=1
    )


def response_kernel(
    sec,
    tok,
    rates,
    residues,
    table_h,
    table_l,
    out,
    rate_rows,
    scale_rows,
    rising,
    falling,
    tall,
    hops,
    scales,
):
    window = table_h.shape[0]
    modes = rates.shape[0]
    mask = lane_mask(modes)
    slow = in_rows(rates, tall)
    rate_rows[...] = slow
    scale = scale_of(in_rows(residues, tall), slow)
    scale_rows[...] = scale
    hops[...] = jnp.exp(-slow * ROWS)
    scales[...] = scale / (1.0 + jnp.exp(-slow * window))
    parts = []
    for pair in range(rate_rows.shape[0] // 2):
        both = two_sided(
            jnp.where(mask, spread(scales, 2 * pair), 0.0),
            jnp.where(mask, spread(scales, 2 * pair + 1), 0.0),
        )
        high = both.astype(jnp.bfloat16).astype(jnp.float32)
        both = jnp.concatenate([high, both - high], axis=0).astype(jnp.bfloat16)
        table = both_powers(rate_rows, hops, pair, window, False)
        rising[pair] = table
        falling[pair] = both_powers(rate_rows, hops, pair, window, True)
        found = dot_turned(both, table)
        parts.append(found[:PAIR] + found[PAIR:])
    taps = jnp.concatenate(parts, axis=0)
    high = taps.astype(jnp.bfloat16)
    low = (taps - high.astype(jnp.float32)).astype(jnp.bfloat16)
    out[...] = dot_f32(high, table_h[...]) + (
        dot_f32(low, table_h[...]) + dot_f32(high, table_l[...])
    )


def response_call(place, rates, residues, window, share):
    step = min(256, share)
    modes = rates.shape[0]
    lanes = ROWS * modes
    tables = split_pair(turned_tables(window)[2])
    small = (step // ROWS, lanes)
    large = (step // PAIR, window, 2 * lanes)
    row = mine(share, step)
    rows_shape = jax.ShapeDtypeStruct((share // ROWS, lanes), jnp.float32)
    table_shape = jax.ShapeDtypeStruct((share // PAIR, window, 2 * lanes), jnp.bfloat16)
    return pl.pallas_call(
        response_kernel,
        out_shape=(
            jax.ShapeDtypeStruct((share, 2 * window), jnp.float32),
            rows_shape,
            rows_shape,
            table_shape,
            table_shape,
        ),
        grid_spec=pltpu.PrefetchScalarGridSpec(
            num_scalar_prefetch=2,
            grid=(share // step,),
            in_specs=[pl.BlockSpec((modes, step), lambda i, p, t: (0, row(i, p, t)))] * 2
            + [whole(t) for t in tables],
            out_specs=(
                pl.BlockSpec((step, 2 * window), lambda i, p, t: (i, 0)),
                pl.BlockSpec(small, lambda i, p, t: (i, 0)),
                pl.BlockSpec(small, lambda i, p, t: (i, 0)),
                pl.BlockSpec(large, lambda i, p, t: (i, 0, 0)),
                pl.BlockSpec(large, lambda i, p, t: (i, 0, 0)),
            ),
            scratch_shapes=[
                pltpu.VMEM((step, modes), jnp.float32),
                pltpu.VMEM(small, jnp.float32),
                pltpu.VMEM(small, jnp.float32),
            ],
        ),
        name="response",
        cost_estimate=cost(share, 4 * window, 600),
        compiler_params=COMPILER,
    )(*place, rates, residues, *parked(*tables))


def front_kernel(
    modes,
    sec,
    tok,
    local,
    remote,
    inputs,
    halo_low,
    halo_high,
    taps,
    rates,
    falling,
    fwd_even,
    fwd_odd,
    inv_even,
    inv_odd,
    medium_out,
    ends,
    total,
    leaps,
):
    channels, tokens = inputs.shape
    window = taps.shape[1]
    blocks = tokens // window
    forward = (fwd_even, fwd_odd)
    inverse = (inv_even, inv_odd)
    leaps[...] = jnp.exp(-rates[...] * window)

    def body(section):
        first = local.at[0] if section == 0 else remote
        second = remote if section == 0 else local.at[0]
        halo = halo_low if section == 0 else halo_high
        tap_rows = taps[...]
        started = jnp.where(tok[0] > 0, 1.0, 0.0).astype(jnp.bfloat16)
        parts = [slice(b * window, (b + 1) * window) for b in range(blocks)]
        sources = [first[1, :, part] * inputs[:, part] for part in parts]
        sources = [halo[...] * started] + sources
        even = [tap_rows] + sources[1::2]
        odd = sources[0::2]
        spectra = []
        for table, members in zip(forward, (even, odd)):
            rows = jnp.concatenate(members, axis=0)
            found = dot_f32(jnp.concatenate([rows, rows], axis=1), table[...])
            spectra.append(
                [found[k * channels : (k + 1) * channels] for k in range(len(members))]
            )
        lane = lax.broadcasted_iota(jnp.int32, (channels, window), 1)
        real, packed = spectra[0][0][:, :window], spectra[0][0][:, window:]
        real_b = jnp.where(lane == 0, packed, real)
        imag = jnp.where(lane == 0, 0.0, packed)
        in_order = [None] * (blocks + 1)
        in_order[1::2] = spectra[0][1:]
        in_order[0::2] = spectra[1]
        products = []
        for block in range(blocks):
            mixed = in_order[block] + in_order[block + 1]
            a, b = mixed[:, :window], mixed[:, window:]
            products.append(
                jnp.concatenate([a * real - b * imag, a * imag + b * real_b], axis=1).astype(
                    jnp.bfloat16
                )
            )
        signals = [None] * blocks
        for parity in range(2):
            members = products[parity::2]
            found = dot_f32(jnp.concatenate(members, axis=0), inverse[parity][...])
            for k in range(len(members)):
                block = 2 * k + parity
                rows = slice(k * channels, (k + 1) * channels)
                medium = found[rows, :window] + found[rows, window:]
                gate = first[0, :, parts[block]].astype(jnp.float32)
                gated = (gate * medium).astype(jnp.bfloat16)
                medium_out[:, parts[block]] = gated
                stream = inputs[:, parts[block]].astype(jnp.float32) + gated.astype(jnp.float32)
                signals[block] = (
                    second[1, :, parts[block]].astype(jnp.float32) * stream
                ).astype(jnp.bfloat16)
        mask = lane_mask(modes)
        lanes = ROWS * modes
        sums = []
        for pair in range(channels // PAIR):
            rows = slice(pair * PAIR, (pair + 1) * PAIR)
            left = jnp.concatenate([signal[rows] for signal in signals], axis=0)
            found = dot_f32(left, falling[pair])
            for side in range(2):
                leap = spread(leaps, 2 * pair + side)
                state = None
                for b in range(blocks):
                    top = b * PAIR + side * ROWS
                    end = jnp.where(
                        mask, found[top : top + ROWS, side * lanes : (side + 1) * lanes], 0.0
                    )
                    at = pair * PAIR + side * ROWS
                    ends[b, at : at + ROWS, :] = end
                    state = end if state is None else state * leap + end
                sums.append(jnp.sum(state, axis=0, keepdims=True))
        total[...] = jnp.concatenate(sums, axis=0)

    by_section(sec, body)


def front_call(
    place, gate_streams, swapped, inputs, halos, taps, rates, falling, modes, share
):
    tokens = inputs.shape[1]
    window = taps.shape[1]
    step = min(256, share)
    forward, inverse = fourier_tables(window)
    tables = forward + inverse
    row = mine(share, step)
    lanes = ROWS * modes
    small = (step // ROWS, lanes)
    blocks = tokens // window
    return pl.pallas_call(
        functools.partial(front_kernel, modes),
        out_shape=(
            jax.ShapeDtypeStruct((share, tokens), jnp.bfloat16),
            jax.ShapeDtypeStruct((blocks, share, lanes), jnp.float32),
            jax.ShapeDtypeStruct((share // ROWS, lanes), jnp.float32),
        ),
        grid_spec=pltpu.PrefetchScalarGridSpec(
            num_scalar_prefetch=2,
            grid=(share // step,),
            in_specs=[
                pl.BlockSpec((1, 2, step, tokens), lambda i, p, t: (0, 0, row(i, p, t), 0)),
                pl.BlockSpec((2, step, tokens), lambda i, p, t: (0, i, 0)),
                pl.BlockSpec((step, tokens), lambda i, p, t: (row(i, p, t), 0)),
                pl.BlockSpec((step, window), lambda i, p, t: (i, 0)),
                pl.BlockSpec((step, window), lambda i, p, t: (i, 0)),
                pl.BlockSpec((step, window), lambda i, p, t: (row(i, p, t), 0)),
                pl.BlockSpec(small, lambda i, p, t: (i, 0)),
                pl.BlockSpec((step // PAIR, window, 2 * lanes), lambda i, p, t: (i, 0, 0)),
            ]
            + [whole(t) for t in tables],
            out_specs=(
                pl.BlockSpec((step, tokens), lambda i, p, t: (i, 0)),
                pl.BlockSpec((blocks, step, lanes), lambda i, p, t: (0, i, 0)),
                pl.BlockSpec(small, lambda i, p, t: (i, 0)),
            ),
            scratch_shapes=[pltpu.VMEM(small, jnp.float32)],
        ),
        name="front",
        cost_estimate=cost(share, tokens, 2000),
        compiler_params=COMPILER,
    )(*place, gate_streams, swapped, inputs, *halos, taps, rates, falling, *parked(*tables))


def within_kernel(sec, tok, local, remote, inputs, gated_medium, response, fwd_h, fwd_l, inverse, out):
    size = fwd_h.shape[0]
    half = size // 2

    def body(section):
        gate_in = remote.at[0] if section == 0 else local.at[0, 0]
        channels, tokens = inputs.shape
        real, imag = response[:, :half], response[:, half:]
        parts = [slice(k * size, (k + 1) * size) for k in range(tokens // size)]
        signals = []
        for part in parts:
            stream = inputs[:, part].astype(jnp.float32) + gated_medium[:, part].astype(
                jnp.float32
            )
            signals.append((gate_in[:, part].astype(jnp.float32) * stream).astype(jnp.bfloat16))
        signal = jnp.concatenate(signals, axis=0)
        spec = dot_f32(signal, fwd_h[...]) + dot_f32(signal, fwd_l[...])
        filtered = []
        for k in range(len(parts)):
            rows = slice(k * channels, (k + 1) * channels)
            a, b = spec[rows, :half], spec[rows, half:]
            filtered.append(
                jnp.concatenate([a * real - b * imag, a * imag + b * real], axis=1).astype(
                    jnp.bfloat16
                )
            )
        found = dot_f32(jnp.concatenate(filtered, axis=0), inverse[...])
        for k, part in enumerate(parts):
            out[:, part] = found[k * channels : (k + 1) * channels]

    by_section(sec, body)


def within_call(place, gate_streams, swapped, inputs, gated_medium, response, share):
    tokens = inputs.shape[1]
    window = response.shape[1] // 2
    step = min(WITHIN_STEP, share)
    forward, inverse, _ = turned_tables(window)
    tables = split_pair(forward) + split_pair(inverse)[:1]
    row = mine(share, step)
    return pl.pallas_call(
        within_kernel,
        out_shape=jax.ShapeDtypeStruct((share, tokens), jnp.float32),
        grid_spec=pltpu.PrefetchScalarGridSpec(
            num_scalar_prefetch=2,
            grid=(share // step,),
            in_specs=[
                pl.BlockSpec((1, 1, step, tokens), lambda i, p, t: (0, 1, row(i, p, t), 0)),
                pl.BlockSpec((1, step, tokens), lambda i, p, t: (1, i, 0)),
                pl.BlockSpec((step, tokens), lambda i, p, t: (row(i, p, t), 0)),
                pl.BlockSpec((step, tokens), lambda i, p, t: (i, 0)),
                pl.BlockSpec((step, 2 * window), lambda i, p, t: (i, 0)),
            ]
            + [whole(t) for t in tables],
            out_specs=pl.BlockSpec((step, tokens), lambda i, p, t: (i, 0)),
        ),
        name="within",
        cost_estimate=cost(share, tokens, 1500),
        compiler_params=COMPILER,
    )(*place, gate_streams, swapped, inputs, gated_medium, response, *parked(*tables))


def output_kernel(
    count,
    modes,
    window,
    sec,
    tok,
    local,
    remote,
    within,
    inputs,
    gated_medium,
    rates,
    scale_rows,
    rising,
    ends,
    *rest,
):
    arrived, (keep, send, leaps, scales, shares, starts) = rest[:count], rest[count:]
    channels, tokens = inputs.shape
    blocks = tokens // window
    mask = lane_mask(modes)
    slow = rates[...]
    leap_all = jnp.exp(-slow * window)
    scale_all = scale_rows[...] * jnp.exp(-slow)
    leaps[...] = leap_all
    scales[...] = scale_all
    shares[...] = scale_all / (1.0 + leap_all)
    entering = jnp.zeros_like(slow)
    for k in range(count):
        known = jnp.where(tok[0] > k, 1.0, 0.0)
        entering = entering + arrived[k][...] * (jnp.exp(-slow * (tokens * k)) * known)
    starts[...] = entering

    def body(section):
        gate_out = remote.at[0] if section == 0 else local.at[0, 0]
        out = send if section == 0 else keep.at[0]
        (keep.at[0] if section == 0 else send)[...] = gated_medium[...]
        for pair in range(channels // PAIR):
            rows = slice(pair * PAIR, (pair + 1) * PAIR)
            sides = []
            for side in range(2):
                group = 2 * pair + side
                leap, scale = spread(leaps, group), spread(scales, group)
                share = spread(shares, group)
                state = jnp.where(mask, spread(starts, group), 0.0)
                at = pair * PAIR + side * ROWS
                lefts = []
                for b in range(blocks):
                    end = ends[b, at : at + ROWS, :]
                    lefts.append(state * scale + end * share)
                    state = state * leap + end
                sides.append(lefts)
            left = jnp.concatenate(
                [two_sided(upper, lower) for upper, lower in zip(*sides)], axis=0
            ).astype(jnp.bfloat16)
            across = dot_turned(left, rising[pair])
            for b in range(blocks):
                part = slice(b * window, (b + 1) * window)
                stream = inputs[rows, part].astype(jnp.float32) + gated_medium[
                    rows, part
                ].astype(jnp.float32)
                long_out = within[rows, part] + across[b * PAIR : (b + 1) * PAIR]
                gate = gate_out[rows, part].astype(jnp.float32)
                out[rows, part] = (stream + gate * long_out).astype(jnp.bfloat16)

    by_section(sec, body)


def output_call(
    place, gate_streams, swapped, within, inputs, medium, rates, scales, rising, ends, arrived, window
):
    share, tokens = medium.shape
    lanes = rates.shape[1]
    step = min(256, share)
    row = mine(share, step)
    wide = (step, tokens)
    small = (step // ROWS, lanes)
    return pl.pallas_call(
        functools.partial(output_kernel, len(arrived), lanes // ROWS, window),
        out_shape=(
            jax.ShapeDtypeStruct((1,) + inputs.shape, jnp.bfloat16),
            jax.ShapeDtypeStruct((share, tokens), jnp.bfloat16),
        ),
        grid_spec=pltpu.PrefetchScalarGridSpec(
            num_scalar_prefetch=2,
            grid=(share // step,),
            in_specs=[
                pl.BlockSpec((1, 1) + wide, lambda i, p, t: (0, 0, row(i, p, t), 0)),
                pl.BlockSpec((1,) + wide, lambda i, p, t: (0, i, 0)),
                pl.BlockSpec(wide, lambda i, p, t: (i, 0)),
                pl.BlockSpec(wide, lambda i, p, t: (row(i, p, t), 0)),
                pl.BlockSpec(wide, lambda i, p, t: (i, 0)),
                pl.BlockSpec(small, lambda i, p, t: (i, 0)),
                pl.BlockSpec(small, lambda i, p, t: (i, 0)),
                pl.BlockSpec((step // PAIR, window, 2 * lanes), lambda i, p, t: (i, 0, 0)),
                pl.BlockSpec((tokens // window, step, lanes), lambda i, p, t: (0, i, 0)),
            ]
            + [pl.BlockSpec(small, lambda i, p, t: (i, 0))] * len(arrived),
            out_specs=(
                pl.BlockSpec((1,) + wide, lambda i, p, t: (0, row(i, p, t), 0)),
                pl.BlockSpec(wide, lambda i, p, t: (i, 0)),
            ),
            scratch_shapes=[pltpu.VMEM(small, jnp.float32)] * 4,
        ),
        name="output",
        cost_estimate=cost(share, tokens, 1500),
        compiler_params=COMPILER,
    )(
        *place, gate_streams, swapped, within, inputs, medium, rates, scales, rising, ends, *arrived
    )


def place_kernel(sec, tok, own, received, out):
    out[0] = received[...]


def place_call(place, own, received):
    share, tokens = received.shape
    step = min(512, share)
    count = share // step
    return pl.pallas_call(
        place_kernel,
        out_shape=jax.ShapeDtypeStruct(own.shape, own.dtype),
        grid_spec=pltpu.PrefetchScalarGridSpec(
            num_scalar_prefetch=2,
            grid=(count,),
            in_specs=[
                pl.BlockSpec(memory_space=pl.ANY),
                pl.BlockSpec((step, tokens), lambda i, p, t: (i, 0)),
            ],
            out_specs=pl.BlockSpec(
                (1, step, tokens), lambda i, p, t: (0, (1 - p[0]) * count + i, 0)
            ),
        ),
        input_output_aliases={2: 0},
        name="placing",
        cost_estimate=cost(share, tokens, 2),
        compiler_params=COMPILER,
    )(*place, own, received)


def lend_kernel(sec, tok, gates, gate_tail, input_tail, out, low, high):
    out[...] = gates[0]
    share = low.shape[0]

    @pl.when(pl.program_id(0) == 0)
    def _():
        for half, target in enumerate((low, high)):
            rows = slice(half * share, (half + 1) * share)
            target[...] = (
                gate_tail[0, 0, rows, :].astype(jnp.float32)
                * input_tail[rows, :].astype(jnp.float32)
            ).astype(jnp.bfloat16)


def lend_call(place, gate_streams, inputs, window, share):
    channels, tokens = inputs.shape
    step = min(512, share)
    count = share // step
    last = tokens // window - 1
    edge = jax.ShapeDtypeStruct((share, window), jnp.bfloat16)
    return pl.pallas_call(
        lend_kernel,
        out_shape=(jax.ShapeDtypeStruct((2, share, tokens), jnp.bfloat16), edge, edge),
        grid_spec=pltpu.PrefetchScalarGridSpec(
            num_scalar_prefetch=2,
            grid=(count,),
            in_specs=[
                pl.BlockSpec(
                    (1, 2, step, tokens), lambda i, p, t: (0, 0, (1 - p[0]) * count + i, 0)
                ),
                pl.BlockSpec((1, 1, channels, window), lambda i, p, t: (0, 1, 0, last)),
                pl.BlockSpec((channels, window), lambda i, p, t: (0, last)),
            ],
            out_specs=(
                pl.BlockSpec((2, step, tokens), lambda i, p, t: (0, i, 0)),
                pl.BlockSpec((share, window), lambda i, p, t: (0, 0)),
                pl.BlockSpec((share, window), lambda i, p, t: (0, 0)),
            ),
        ),
        name="lend",
        cost_estimate=cost(share, tokens, 2),
        compiler_params=COMPILER,
    )(*place, gate_streams, gate_streams, inputs)


def ring(value, axis, by):
    peers = lax.axis_size(axis)
    return lax.ppermute(value, axis, [(i, (i + by) % peers) for i in range(peers)])


def edge_to(value, section):
    peers = lax.axis_size("tok")
    pairs = [(i, section * peers + (i + 1) % peers) for i in range(peers)]
    pairs += [(peers + i, (1 - section) * peers + i) for i in range(peers)]
    return lax.ppermute(value, ("section", "tok"), pairs)


def on_device(gate_streams, inputs, medium_taps, residues, decay_rates):
    channels, tokens = inputs.shape
    share = channels // 2
    gate_streams, inputs, medium_taps = parked(gate_streams, inputs, medium_taps)
    window = medium_taps.shape[1]
    modes = decay_rates.shape[1]
    section = lax.axis_index("section")
    place = tuple(
        lax.axis_index(axis).astype(jnp.int32).reshape(1) for axis in ("section", "tok")
    )
    lent, *edges = lend_call(place, gate_streams, inputs, window, share)
    halos = [edge_to(edges[s], s) for s in range(2)]
    swapped = ring(lent, "section", 1)
    response, rates, scales, rising, falling = response_call(
        place, decay_rates.T, residues.T, window, share
    )
    medium, ends, total = front_call(
        place, gate_streams, swapped, inputs, halos, medium_taps, rates, falling, modes, share
    )
    arrived = [ring(total, "tok", by) for by in range(1, lax.axis_size("tok"))]
    within = within_call(place, gate_streams, swapped, inputs, medium, response, share)
    keep, send = output_call(
        place, gate_streams, swapped, within, inputs, medium, rates, scales, rising, ends, arrived, window
    )
    return place_call(place, keep, ring(send, "section", 1))


def solution(mesh):
    placed = (
        P("section", None, "chan", "tok"),
        P("chan", "tok"),
        P("chan", None),
        P("chan", None),
        P("chan", None),
    )
    return jax.shard_map(
        on_device,
        mesh=mesh,
        in_specs=placed,
        out_specs=P("section", "chan", "tok"),
        check_vma=False,
    )
```

```python
import functools

import jax
import jax.numpy as jnp
import numpy as np
from jax import lax
from jax.experimental import pallas as pl
from jax.experimental.pallas import tpu as pltpu
from jax.sharding import PartitionSpec as P

ROWS = 8


def split_pair(matrix):
    high = jnp.asarray(matrix, jnp.float32).astype(jnp.bfloat16)
    low = (jnp.asarray(matrix, jnp.float32) - high.astype(jnp.float32)).astype(jnp.bfloat16)
    return high, low


def stacked(matrix, axis):
    return jnp.concatenate(split_pair(matrix), axis=axis)


def fourier_tables(window):
    size = 2 * window
    time = np.arange(window)[:, None]
    freq = np.arange(window)[None, :]
    angle = 2.0 * np.pi * ((time * freq) % size) / size
    sign = np.where(freq % 2 == 0, 1.0, -1.0)
    nyquist = np.where(time % 2 == 0, 1.0, -1.0)
    weight = np.where(freq == 0, 1.0, 2.0) / size
    forward, inverse = [], []
    for odd in range(2):
        flip = sign if odd else np.ones_like(sign)
        real = np.cos(angle) * flip
        imag = -np.sin(angle) * flip
        imag[:, :1] = nyquist
        forward.append(stacked(np.concatenate([real, imag], axis=1), 0))
        back_real = np.cos(angle) * weight * flip
        back_imag = -np.sin(angle) * weight * flip
        back_imag[:, :1] = nyquist / size
        inverse.append(stacked(np.concatenate([back_real.T, back_imag.T], axis=0), 1))
    return forward, inverse


def turned_tables(window):
    half = window // 2
    time = np.arange(window)[:, None]
    freq = 2 * np.arange(half)[None, :] + 1
    angle = np.pi * ((time * freq) % (2 * window)) / window
    real, imag = np.cos(angle), -np.sin(angle)
    zero = np.zeros_like(real)
    forward = np.concatenate(
        [
            np.concatenate([real, zero, imag, zero], axis=1),
            np.concatenate([zero, real, zero, imag], axis=1),
        ],
        axis=0,
    )
    inverse = forward.T * (2.0 / window)
    doubled = np.concatenate([real, real, imag, imag], axis=1)
    return forward, inverse, doubled


PAIR = 16
WITHIN_STEP = 512
COMPILER = pltpu.CompilerParams(vmem_limit_bytes=16 << 20)


def parked(*arrays):
    return [pltpu.with_memory_space_constraint(a, pltpu.HBM) for a in arrays]


def cost(share, tokens, work):
    size = share * tokens
    return pl.CostEstimate(
        flops=size * work, bytes_accessed=size * 12, transcendentals=size // 64
    )


def dot_f32(left, right):
    return jnp.dot(left, right, preferred_element_type=jnp.float32)


def dot_turned(left, right):
    return lax.dot_general(
        left, right, (((1,), (1,)), ((), ())), preferred_element_type=jnp.float32
    )


VMEM_SPEC = pl.BlockSpec(memory_space=pltpu.VMEM)
SMEM_SPEC = pl.BlockSpec(memory_space=pltpu.SMEM)
ANY_SPEC = pl.BlockSpec(memory_space=pl.ANY)


def rows_at(ref, step, i, axis=0):
    start = i * step
    if not isinstance(i, int):
        start = pl.multiple_of(start, step)
    return ref.at[(slice(None),) * axis + (pl.ds(start, step),)]


def by_section(sec, body):
    for section in range(2):
        pl.when(sec[0] == section)(functools.partial(body, section))


def lane_mask(modes):
    shape = (ROWS, ROWS * modes)
    lane = lax.broadcasted_iota(jnp.int32, shape, 1)
    return lane // modes == lax.broadcasted_iota(jnp.int32, shape, 0)


def spread(ref, group):
    return jnp.broadcast_to(ref[group : group + 1, :], (ROWS, ref.shape[1]))


def powers(slow, hop, window, first, falling):
    row = lax.broadcasted_iota(jnp.int32, slow.shape, 0).astype(jnp.float32)
    tiles = [jnp.exp(-slow * (first + (ROWS - 1 - row if falling else row)))]
    while len(tiles) < window // ROWS:
        tiles = tiles + [tile * hop for tile in tiles]
        hop = hop * hop
    if falling:
        tiles = tiles[::-1]
    return jnp.concatenate(tiles, axis=0).astype(jnp.bfloat16)


def both_powers(rates, hops, pair, window, falling):
    sides = [
        powers(spread(rates, g), spread(hops, g), window, 0.0, falling)
        for g in (2 * pair, 2 * pair + 1)
    ]
    return jnp.concatenate(sides, axis=1)


def two_sided(upper, lower):
    zero = jnp.zeros_like(upper)
    return jnp.concatenate(
        [
            jnp.concatenate([upper, zero], axis=1),
            jnp.concatenate([zero, lower], axis=1),
        ],
        axis=0,
    )


def scale_of(residues, slow):
    return residues * jnp.sqrt(1.0 - jnp.exp(-2.0 * slow))


def in_rows(ref, tall):
    modes, channels = ref.shape
    tall[...] = ref[...].T
    count = channels // ROWS
    return jnp.concatenate(
        [tall[pl.ds(c, count, stride=ROWS), :] for c in range(ROWS)], axis=1
    )


def response_kernel(count, sec, tok, rates, residues, table_h, table_l, *rest):
    gates, inputs, taps = rest[:3]
    tables = rest[3 : 3 + count]
    out, rate_rows, scale_rows, rising, falling = rest[3 + count : 8 + count]
    own_gates, own_inputs, own_taps = rest[8 + count : 11 + count]
    own_tables = rest[11 + count : 11 + 2 * count]
    tall, hops, scales, arrival = rest[11 + 2 * count :]
    share = out.shape[0]
    modes = rates.shape[0]
    window = table_h.shape[0]
    step = tall.shape[0]
    first = pl.multiple_of(sec[0] * share, share)
    mine = pl.ds(first, share)
    pairs = [(gates.at[0, :, mine, :], own_gates)]
    pairs += [(inputs.at[mine, :], own_inputs), (taps.at[mine, :], own_taps)]
    pairs += list(zip(tables, own_tables))
    copies = [
        pltpu.make_async_copy(source, target, arrival.at[k])
        for k, (source, target) in enumerate(pairs)
    ]
    for copy in copies:
        copy.start()
    mask = lane_mask(modes)

    @pl.loop(0, share // step)
    def _(i):
        lanes = pl.ds(pl.multiple_of(first + i * step, step), step)
        slow = in_rows(rates.at[:, lanes], tall)
        scale = scale_of(in_rows(residues.at[:, lanes], tall), slow)
        small = step // ROWS
        own_rates = rows_at(rate_rows, small, i)
        own_rates[...] = slow
        rows_at(scale_rows, small, i)[...] = scale
        hops[...] = jnp.exp(-slow * ROWS)
        scales[...] = scale / (1.0 + jnp.exp(-slow * window))
        up, down = rows_at(rising, step // PAIR, i), rows_at(falling, step // PAIR, i)
        parts = []
        for pair in range(step // PAIR):
            both = two_sided(
                jnp.where(mask, spread(scales, 2 * pair), 0.0),
                jnp.where(mask, spread(scales, 2 * pair + 1), 0.0),
            )
            high = both.astype(jnp.bfloat16).astype(jnp.float32)
            both = jnp.concatenate([high, both - high], axis=0).astype(jnp.bfloat16)
            table = both_powers(own_rates, hops, pair, window, False)
            up[pair] = table
            down[pair] = both_powers(own_rates, hops, pair, window, True)
            found = dot_turned(both, table)
            parts.append(found[:PAIR] + found[PAIR:])
        response = jnp.concatenate(parts, axis=0)
        high = response.astype(jnp.bfloat16)
        low = (response - high.astype(jnp.float32)).astype(jnp.bfloat16)
        rows_at(out, step, i)[...] = dot_f32(high, table_h[...]) + (
            dot_f32(low, table_h[...]) + dot_f32(high, table_l[...])
        )

    for copy in copies:
        copy.wait()


def response_call(place, rates, residues, gates, inputs, taps, tables, window, share):
    tokens = inputs.shape[1]
    step = min(256, share)
    modes = rates.shape[0]
    lanes = ROWS * modes
    spectra = split_pair(turned_tables(window)[2])
    small = (step // ROWS, lanes)
    shape = lambda dims, kind=jnp.float32: jax.ShapeDtypeStruct(dims, kind)
    power_shape = shape((share // PAIR, window, 2 * lanes), jnp.bfloat16)
    outs = [shape((share, 2 * window))] + [shape((share // ROWS, lanes))] * 2
    outs += [power_shape] * 2
    outs += [
        shape((2, share, tokens), gates.dtype),
        shape((share, tokens), inputs.dtype),
        shape((share, window), taps.dtype),
    ]
    outs += [shape(t.shape, t.dtype) for t in tables]
    staged = 3 + len(tables)
    found = pl.pallas_call(
        functools.partial(response_kernel, len(tables)),
        out_shape=tuple(outs),
        in_specs=[SMEM_SPEC] * 2 + [VMEM_SPEC] * 4 + [ANY_SPEC] * staged,
        out_specs=(VMEM_SPEC,) * len(outs),
        scratch_shapes=[
            pltpu.VMEM((step, modes), jnp.float32),
            pltpu.VMEM(small, jnp.float32),
            pltpu.VMEM(small, jnp.float32),
            pltpu.SemaphoreType.DMA((staged,)),
        ],
        name="response",
        cost_estimate=cost(share, 4 * window, 600),
        compiler_params=COMPILER,
    )(*place, rates, residues, *spectra, *parked(gates, inputs, taps, *tables))
    return found[:5], found[5:8], found[8:]


def front_kernel(
    modes,
    step,
    sec,
    tok,
    local_all,
    remote_all,
    inputs_all,
    halo_low,
    halo_high,
    taps_all,
    rates,
    falling_all,
    fwd_even,
    fwd_odd,
    inv_even,
    inv_odd,
    medium_all,
    ends_all,
    total_all,
    leaps_all,
):
    share, tokens = inputs_all.shape
    window = taps_all.shape[1]
    blocks = tokens // window
    forward = (fwd_even, fwd_odd)
    inverse = (inv_even, inv_odd)
    leaps_all[...] = jnp.exp(-rates[...] * window)

    def chunk(section, i):
        first, second = (local_all, remote_all) if section == 0 else (remote_all, local_all)
        first, second = rows_at(first, step, i, 1), rows_at(second, step, i, 1)
        halo = rows_at(halo_low if section == 0 else halo_high, step, i)
        inputs, taps = rows_at(inputs_all, step, i), rows_at(taps_all, step, i)
        medium_out, ends = rows_at(medium_all, step, i), rows_at(ends_all, step, i, 1)
        leaps = rows_at(leaps_all, step // ROWS, i)
        falling = rows_at(falling_all, step // PAIR, i)
        total = rows_at(total_all, step // ROWS, i)
        channels = step
        tap_rows = taps[...]
        started = jnp.where(tok[0] > 0, 1.0, 0.0).astype(jnp.bfloat16)
        parts = [slice(b * window, (b + 1) * window) for b in range(blocks)]
        sources = [first[1, :, part] * inputs[:, part] for part in parts]
        sources = [halo[...] * started] + sources
        even = [tap_rows] + sources[1::2]
        odd = sources[0::2]
        spectra = []
        for table, members in zip(forward, (even, odd)):
            rows = jnp.concatenate(members, axis=0)
            found = dot_f32(jnp.concatenate([rows, rows], axis=1), table[...])
            spectra.append(
                [found[k * channels : (k + 1) * channels] for k in range(len(members))]
            )
        lane = lax.broadcasted_iota(jnp.int32, (channels, window), 1)
        real, packed = spectra[0][0][:, :window], spectra[0][0][:, window:]
        real_b = jnp.where(lane == 0, packed, real)
        imag = jnp.where(lane == 0, 0.0, packed)
        in_order = [None] * (blocks + 1)
        in_order[1::2] = spectra[0][1:]
        in_order[0::2] = spectra[1]
        products = []
        for block in range(blocks):
            mixed = in_order[block] + in_order[block + 1]
            a, b = mixed[:, :window], mixed[:, window:]
            products.append(
                jnp.concatenate([a * real - b * imag, a * imag + b * real_b], axis=1).astype(
                    jnp.bfloat16
                )
            )
        signals = [None] * blocks
        for parity in range(2):
            members = products[parity::2]
            found = dot_f32(jnp.concatenate(members, axis=0), inverse[parity][...])
            for k in range(len(members)):
                block = 2 * k + parity
                rows = slice(k * channels, (k + 1) * channels)
                medium = found[rows, :window] + found[rows, window:]
                gate = first[0, :, parts[block]].astype(jnp.float32)
                gated = (gate * medium).astype(jnp.bfloat16)
                medium_out[:, parts[block]] = gated
                stream = inputs[:, parts[block]].astype(jnp.float32) + gated.astype(jnp.float32)
                signals[block] = (
                    second[1, :, parts[block]].astype(jnp.float32) * stream
                ).astype(jnp.bfloat16)
        mask = lane_mask(modes)
        lanes = ROWS * modes
        sums = []
        for pair in range(channels // PAIR):
            rows = slice(pair * PAIR, (pair + 1) * PAIR)
            left = jnp.concatenate([signal[rows] for signal in signals], axis=0)
            found = dot_f32(left, falling[pair])
            for side in range(2):
                leap = spread(leaps, 2 * pair + side)
                state = None
                for b in range(blocks):
                    top = b * PAIR + side * ROWS
                    end = jnp.where(
                        mask, found[top : top + ROWS, side * lanes : (side + 1) * lanes], 0.0
                    )
                    at = pair * PAIR + side * ROWS
                    ends[b, at : at + ROWS, :] = end
                    state = end if state is None else state * leap + end
                sums.append(jnp.sum(state, axis=0, keepdims=True))
        total[...] = jnp.concatenate(sums, axis=0)

    def body(section):
        pl.loop(0, share // step)(functools.partial(chunk, section))

    by_section(sec, body)


def front_call(place, gates, swapped, inputs, halos, taps, rates, falling, tables, modes):
    share, tokens = inputs.shape
    window = taps.shape[1]
    lanes = ROWS * modes
    small = (share // ROWS, lanes)
    operands = [gates, swapped, inputs, *halos, taps, rates, falling, *tables]
    return pl.pallas_call(
        functools.partial(front_kernel, modes, min(256, share)),
        out_shape=(
            jax.ShapeDtypeStruct((share, tokens), jnp.bfloat16),
            jax.ShapeDtypeStruct((tokens // window, share, lanes), jnp.float32),
            jax.ShapeDtypeStruct(small, jnp.float32),
        ),
        in_specs=[SMEM_SPEC] * 2 + [VMEM_SPEC] * len(operands),
        out_specs=(VMEM_SPEC,) * 3,
        scratch_shapes=[pltpu.VMEM(small, jnp.float32)],
        name="front",
        cost_estimate=cost(share, tokens, 2000),
        compiler_params=COMPILER,
    )(*place, *operands)


def within_kernel(
    step,
    sec,
    tok,
    local_all,
    remote_all,
    inputs_all,
    medium_all,
    response_all,
    fwd_h,
    fwd_l,
    inverse,
    out_all,
):
    share, tokens = inputs_all.shape
    size = fwd_h.shape[0]
    half = size // 2

    def chunk(section, i):
        gate_in = rows_at((remote_all if section == 0 else local_all).at[1], step, i)
        inputs, gated_medium = rows_at(inputs_all, step, i), rows_at(medium_all, step, i)
        response, out = rows_at(response_all, step, i), rows_at(out_all, step, i)
        channels = step
        real, imag = response[:, :half], response[:, half:]
        parts = [slice(k * size, (k + 1) * size) for k in range(tokens // size)]
        signals = []
        for part in parts:
            stream = inputs[:, part].astype(jnp.float32) + gated_medium[:, part].astype(
                jnp.float32
            )
            signals.append((gate_in[:, part].astype(jnp.float32) * stream).astype(jnp.bfloat16))
        signal = jnp.concatenate(signals, axis=0)
        spec = dot_f32(signal, fwd_h[...]) + dot_f32(signal, fwd_l[...])
        filtered = []
        for k in range(len(parts)):
            rows = slice(k * channels, (k + 1) * channels)
            a, b = spec[rows, :half], spec[rows, half:]
            filtered.append(
                jnp.concatenate([a * real - b * imag, a * imag + b * real], axis=1).astype(
                    jnp.bfloat16
                )
            )
        found = dot_f32(jnp.concatenate(filtered, axis=0), inverse[...])
        for k, part in enumerate(parts):
            out[:, part] = found[k * channels : (k + 1) * channels]

    def body(section):
        pl.loop(0, share // step)(functools.partial(chunk, section))

    by_section(sec, body)


def within_call(place, gates, swapped, inputs, medium, response, tables):
    share, tokens = inputs.shape
    operands = [gates, swapped, inputs, medium, response, *tables]
    return pl.pallas_call(
        functools.partial(within_kernel, min(WITHIN_STEP, share)),
        out_shape=jax.ShapeDtypeStruct((share, tokens), jnp.float32),
        in_specs=[SMEM_SPEC] * 2 + [VMEM_SPEC] * len(operands),
        out_specs=VMEM_SPEC,
        name="within",
        cost_estimate=cost(share, tokens, 1500),
        compiler_params=COMPILER,
    )(*place, *operands)


def output_kernel(
    count,
    modes,
    window,
    step,
    sec,
    tok,
    local_all,
    remote_all,
    within_all,
    inputs_all,
    medium_all,
    rates,
    scale_rows,
    rising_all,
    ends_all,
    *rest,
):
    arrived = rest[:count]
    result, send, leaps_all, scales_all, shares_all, starts_all, mixed, done = rest[count:]
    share, tokens = inputs_all.shape
    blocks = tokens // window
    mask = lane_mask(modes)
    slow = rates[...]
    leap_all = jnp.exp(-slow * window)
    scale_all = scale_rows[...] * jnp.exp(-slow)
    leaps_all[...] = leap_all
    scales_all[...] = scale_all
    shares_all[...] = scale_all / (1.0 + leap_all)
    entering = jnp.zeros_like(slow)
    for k in range(count):
        known = jnp.where(tok[0] > k, 1.0, 0.0)
        entering = entering + arrived[k][...] * (jnp.exp(-slow * (tokens * k)) * known)
    starts_all[...] = entering

    def chunk(section, out_all, i):
        gate_out = rows_at((remote_all if section == 0 else local_all).at[0], step, i)
        inputs, gated_medium = rows_at(inputs_all, step, i), rows_at(medium_all, step, i)
        within, out = rows_at(within_all, step, i), rows_at(out_all, step, i)
        ends = rows_at(ends_all, step, i, 1)
        rising = rows_at(rising_all, step // PAIR, i)
        small = step // ROWS
        leaps, scales = rows_at(leaps_all, small, i), rows_at(scales_all, small, i)
        shares, starts = rows_at(shares_all, small, i), rows_at(starts_all, small, i)
        channels = step
        for pair in range(channels // PAIR):
            rows = slice(pair * PAIR, (pair + 1) * PAIR)
            sides = []
            for side in range(2):
                group = 2 * pair + side
                leap, scale = spread(leaps, group), spread(scales, group)
                share = spread(shares, group)
                state = jnp.where(mask, spread(starts, group), 0.0)
                at = pair * PAIR + side * ROWS
                lefts = []
                for b in range(blocks):
                    end = ends[b, at : at + ROWS, :]
                    lefts.append(state * scale + end * share)
                    state = state * leap + end
                sides.append(lefts)
            left = jnp.concatenate(
                [two_sided(upper, lower) for upper, lower in zip(*sides)], axis=0
            ).astype(jnp.bfloat16)
            across = dot_turned(left, rising[pair])
            for b in range(blocks):
                part = slice(b * window, (b + 1) * window)
                stream = inputs[rows, part].astype(jnp.float32) + gated_medium[
                    rows, part
                ].astype(jnp.float32)
                long_out = within[rows, part] + across[b * PAIR : (b + 1) * PAIR]
                gate = gate_out[rows, part].astype(jnp.float32)
                out[rows, part] = (stream + gate * long_out).astype(jnp.bfloat16)

    def body(section):
        target = result.at[0, pl.ds(section * share, share), :]
        early = pltpu.make_async_copy(medium_all, target if section == 0 else send, done.at[0])
        early.start()
        pl.loop(0, share // step)(functools.partial(chunk, section, mixed if section else send))
        if section == 1:
            late = pltpu.make_async_copy(mixed, target, done.at[1])
            late.start()
            late.wait()
        early.wait()

    by_section(sec, body)


def output_call(
    place, gates, swapped, within, inputs, medium, rates, scales, rising, ends, arrived, window
):
    share, tokens = medium.shape
    lanes = rates.shape[1]
    step = min(256, share)
    small = (share // ROWS, lanes)
    operands = [gates, swapped, within, inputs, medium, rates, scales, rising, ends, *arrived]
    return pl.pallas_call(
        functools.partial(output_kernel, len(arrived), lanes // ROWS, window, step),
        out_shape=(
            jax.ShapeDtypeStruct((1, 2 * share, tokens), jnp.bfloat16),
            jax.ShapeDtypeStruct((share, tokens), jnp.bfloat16),
        ),
        in_specs=[SMEM_SPEC] * 2 + [VMEM_SPEC] * len(operands),
        out_specs=(ANY_SPEC, VMEM_SPEC),
        scratch_shapes=[pltpu.VMEM(small, jnp.float32)] * 4
        + [pltpu.VMEM((share, tokens), jnp.bfloat16), pltpu.SemaphoreType.DMA((2,))],
        name="output",
        cost_estimate=cost(share, tokens, 1500),
        compiler_params=COMPILER,
    )(*place, *operands)


def place_kernel(sec, tok, own, received, out, done):
    share = received.shape[0]
    other = pl.ds(pl.multiple_of((1 - sec[0]) * share, share), share)
    copy = pltpu.make_async_copy(received, out.at[0, other, :], done)
    copy.start()
    copy.wait()


def place_call(place, own, received):
    share, tokens = received.shape
    return pl.pallas_call(
        place_kernel,
        out_shape=jax.ShapeDtypeStruct(own.shape, own.dtype),
        in_specs=[SMEM_SPEC] * 2 + [ANY_SPEC, VMEM_SPEC],
        out_specs=ANY_SPEC,
        scratch_shapes=[pltpu.SemaphoreType.DMA],
        input_output_aliases={2: 0},
        name="placing",
        cost_estimate=cost(share, tokens, 2),
        compiler_params=COMPILER,
    )(*place, own, received)


def lend_kernel(sec, tok, gates, gate_tail, input_tail, out, low, high):
    out[...] = gates[0]
    share = low.shape[0]

    @pl.when(pl.program_id(0) == 0)
    def _():
        for half, target in enumerate((low, high)):
            rows = slice(half * share, (half + 1) * share)
            target[...] = (
                gate_tail[0, 0, rows, :].astype(jnp.float32)
                * input_tail[rows, :].astype(jnp.float32)
            ).astype(jnp.bfloat16)


def lend_call(place, gate_streams, inputs, window, share):
    channels, tokens = inputs.shape
    step = min(512, share)
    count = share // step
    last = tokens // window - 1
    edge = jax.ShapeDtypeStruct((share, window), jnp.bfloat16)
    return pl.pallas_call(
        lend_kernel,
        out_shape=(jax.ShapeDtypeStruct((2, share, tokens), jnp.bfloat16), edge, edge),
        grid_spec=pltpu.PrefetchScalarGridSpec(
            num_scalar_prefetch=2,
            grid=(count,),
            in_specs=[
                pl.BlockSpec(
                    (1, 2, step, tokens), lambda i, p, t: (0, 0, (1 - p[0]) * count + i, 0)
                ),
                pl.BlockSpec((1, 1, channels, window), lambda i, p, t: (0, 1, 0, last)),
                pl.BlockSpec((channels, window), lambda i, p, t: (0, last)),
            ],
            out_specs=(
                pl.BlockSpec((2, step, tokens), lambda i, p, t: (0, i, 0)),
                pl.BlockSpec((share, window), lambda i, p, t: (0, 0)),
                pl.BlockSpec((share, window), lambda i, p, t: (0, 0)),
            ),
        ),
        name="lend",
        cost_estimate=cost(share, tokens, 2),
        compiler_params=COMPILER,
    )(*place, *parked(gate_streams, gate_streams, inputs))


def ring(value, axis, by):
    peers = lax.axis_size(axis)
    return lax.ppermute(value, axis, [(i, (i + by) % peers) for i in range(peers)])


def edge_to(value, section):
    peers = lax.axis_size("tok")
    pairs = [(i, section * peers + (i + 1) % peers) for i in range(peers)]
    pairs += [(peers + i, (1 - section) * peers + i) for i in range(peers)]
    return lax.ppermute(value, ("section", "tok"), pairs)


def on_device(gate_streams, inputs, medium_taps, residues, decay_rates):
    channels, tokens = inputs.shape
    share = channels // 2
    window = medium_taps.shape[1]
    modes = decay_rates.shape[1]
    section = lax.axis_index("section")
    place = tuple(
        lax.axis_index(axis).astype(jnp.int32).reshape(1) for axis in ("section", "tok")
    )
    lent, *edges = lend_call(place, gate_streams, inputs, window, share)
    halos = [edge_to(edges[s], s) for s in range(2)]
    swapped = ring(lent, "section", 1)
    forward, inverse = fourier_tables(window)
    turned, back, _ = turned_tables(window)
    tables = [*forward, *inverse, *split_pair(turned), split_pair(back)[0]]
    built, own, tables = response_call(
        place,
        decay_rates.T,
        residues.T,
        gate_streams,
        inputs,
        medium_taps,
        tables,
        window,
        share,
    )
    response, rates, scales, rising, falling = built
    gates, inputs, taps = own
    medium, ends, total = front_call(
        place, gates, swapped, inputs, halos, taps, rates, falling, tables[:4], modes
    )
    arrived = [ring(total, "tok", by) for by in range(1, lax.axis_size("tok"))]
    within = within_call(place, gates, swapped, inputs, medium, response, tables[4:])
    keep, send = output_call(
        place, gates, swapped, within, inputs, medium, rates, scales, rising, ends, arrived, window
    )
    return place_call(place, keep, ring(send, "section", 1))


def solution(mesh):
    placed = (
        P("section", None, "chan", "tok"),
        P("chan", "tok"),
        P("chan", None),
        P("chan", None),
        P("chan", None),
    )
    return jax.shard_map(
        on_device,
        mesh=mesh,
        in_specs=placed,
        out_specs=P("section", "chan", "tok"),
        check_vma=False,
    )
```

```python
import functools

import jax
import jax.numpy as jnp
import numpy as np
from jax import lax
from jax.experimental import pallas as pl
from jax.experimental.pallas import tpu as pltpu
from jax.sharding import PartitionSpec as P

ROWS = 8


def split_pair(matrix):
    high = jnp.asarray(matrix, jnp.float32).astype(jnp.bfloat16)
    low = (jnp.asarray(matrix, jnp.float32) - high.astype(jnp.float32)).astype(jnp.bfloat16)
    return high, low


def stacked(matrix, axis):
    return jnp.concatenate(split_pair(matrix), axis=axis)


def fourier_tables(window):
    size = 2 * window
    time = np.arange(window)[:, None]
    freq = np.arange(window)[None, :]
    angle = 2.0 * np.pi * ((time * freq) % size) / size
    sign = np.where(freq % 2 == 0, 1.0, -1.0)
    nyquist = np.where(time % 2 == 0, 1.0, -1.0)
    weight = np.where(freq == 0, 1.0, 2.0) / size
    forward, inverse = [], []
    for odd in range(2):
        flip = sign if odd else np.ones_like(sign)
        real = np.cos(angle) * flip
        imag = -np.sin(angle) * flip
        imag[:, :1] = nyquist
        forward.append(stacked(np.concatenate([real, imag], axis=1), 0))
        back_real = np.cos(angle) * weight * flip
        back_imag = -np.sin(angle) * weight * flip
        back_imag[:, :1] = nyquist / size
        inverse.append(stacked(np.concatenate([back_real.T, back_imag.T], axis=0), 1))
    return forward, inverse


def turned_tables(window):
    half = window // 2
    time = np.arange(window)[:, None]
    freq = 2 * np.arange(half)[None, :] + 1
    angle = np.pi * ((time * freq) % (2 * window)) / window
    real, imag = np.cos(angle), -np.sin(angle)
    zero = np.zeros_like(real)
    forward = np.concatenate(
        [
            np.concatenate([real, zero, imag, zero], axis=1),
            np.concatenate([zero, real, zero, imag], axis=1),
        ],
        axis=0,
    )
    inverse = forward.T * (2.0 / window)
    doubled = np.concatenate([real, real, imag, imag], axis=1)
    return forward, inverse, doubled


PAIR = 16
WITHIN_STEP = 512
HALVES = 2
COMPILER = pltpu.CompilerParams(vmem_limit_bytes=16 << 20)


def parked(*arrays):
    return [pltpu.with_memory_space_constraint(a, pltpu.HBM) for a in arrays]


def cost(share, tokens, work):
    size = share * tokens
    return pl.CostEstimate(
        flops=size * work, bytes_accessed=size * 12, transcendentals=size // 64
    )


def dot_f32(left, right):
    return jnp.dot(left, right, preferred_element_type=jnp.float32)


def dot_turned(left, right):
    return lax.dot_general(
        left, right, (((1,), (1,)), ((), ())), preferred_element_type=jnp.float32
    )


VMEM_SPEC = pl.BlockSpec(memory_space=pltpu.VMEM)
SMEM_SPEC = pl.BlockSpec(memory_space=pltpu.SMEM)
ANY_SPEC = pl.BlockSpec(memory_space=pl.ANY)


def rows_at(ref, step, i, axis=0):
    start = i * step
    if not isinstance(i, int):
        start = pl.multiple_of(start, step)
    return ref.at[(slice(None),) * axis + (pl.ds(start, step),)]


def by_section(sec, body):
    for section in range(2):
        pl.when(sec[0] == section)(functools.partial(body, section))


def lane_mask(modes):
    shape = (ROWS, ROWS * modes)
    lane = lax.broadcasted_iota(jnp.int32, shape, 1)
    return lane // modes == lax.broadcasted_iota(jnp.int32, shape, 0)


def spread(ref, group):
    return jnp.broadcast_to(ref[group : group + 1, :], (ROWS, ref.shape[1]))


def powers(slow, hop, window, first, falling):
    row = lax.broadcasted_iota(jnp.int32, slow.shape, 0).astype(jnp.float32)
    tiles = [jnp.exp(-slow * (first + (ROWS - 1 - row if falling else row)))]
    while len(tiles) < window // ROWS:
        tiles = tiles + [tile * hop for tile in tiles]
        hop = hop * hop
    if falling:
        tiles = tiles[::-1]
    return jnp.concatenate(tiles, axis=0).astype(jnp.bfloat16)


def both_powers(rates, hops, pair, window, falling):
    sides = [
        powers(spread(rates, g), spread(hops, g), window, 0.0, falling)
        for g in (2 * pair, 2 * pair + 1)
    ]
    return jnp.concatenate(sides, axis=1)


def two_sided(upper, lower):
    zero = jnp.zeros_like(upper)
    return jnp.concatenate(
        [
            jnp.concatenate([upper, zero], axis=1),
            jnp.concatenate([zero, lower], axis=1),
        ],
        axis=0,
    )


def scale_of(residues, slow):
    return residues * jnp.sqrt(1.0 - jnp.exp(-2.0 * slow))


def in_rows(ref, tall):
    modes, channels = ref.shape
    tall[...] = ref[...].T
    count = channels // ROWS
    return jnp.concatenate(
        [tall[pl.ds(c, count, stride=ROWS), :] for c in range(ROWS)], axis=1
    )


def response_kernel(count, sec, tok, rates, residues, table_h, table_l, *rest):
    gates, inputs, taps = rest[:3]
    tables = rest[3 : 3 + count]
    out, rate_rows, scale_rows, rising, falling = rest[3 + count : 8 + count]
    own_gates, own_inputs, own_taps = rest[8 + count : 11 + count]
    own_tables = rest[11 + count : 11 + 2 * count]
    tall, hops, scales, arrival = rest[11 + 2 * count :]
    share = out.shape[0]
    modes = rates.shape[0]
    window = table_h.shape[0]
    step = tall.shape[0]
    first = pl.multiple_of(sec[0] * share, share)
    mine = pl.ds(first, share)
    pairs = [(gates.at[0, :, mine, :], own_gates)]
    pairs += [(inputs.at[mine, :], own_inputs), (taps.at[mine, :], own_taps)]
    pairs += list(zip(tables, own_tables))
    copies = [
        pltpu.make_async_copy(source, target, arrival.at[k])
        for k, (source, target) in enumerate(pairs)
    ]
    for copy in copies:
        copy.start()
    mask = lane_mask(modes)

    @pl.loop(0, share // step)
    def _(i):
        lanes = pl.ds(pl.multiple_of(first + i * step, step), step)
        slow = in_rows(rates.at[:, lanes], tall)
        scale = scale_of(in_rows(residues.at[:, lanes], tall), slow)
        small = step // ROWS
        own_rates = rows_at(rate_rows, small, i)
        own_rates[...] = slow
        rows_at(scale_rows, small, i)[...] = scale
        hops[...] = jnp.exp(-slow * ROWS)
        scales[...] = scale / (1.0 + jnp.exp(-slow * window))
        up, down = rows_at(rising, step // PAIR, i), rows_at(falling, step // PAIR, i)
        parts = []
        for pair in range(step // PAIR):
            both = two_sided(
                jnp.where(mask, spread(scales, 2 * pair), 0.0),
                jnp.where(mask, spread(scales, 2 * pair + 1), 0.0),
            )
            high = both.astype(jnp.bfloat16).astype(jnp.float32)
            both = jnp.concatenate([high, both - high], axis=0).astype(jnp.bfloat16)
            table = both_powers(own_rates, hops, pair, window, False)
            up[pair] = table
            down[pair] = both_powers(own_rates, hops, pair, window, True)
            found = dot_turned(both, table)
            parts.append(found[:PAIR] + found[PAIR:])
        response = jnp.concatenate(parts, axis=0)
        high = response.astype(jnp.bfloat16)
        low = (response - high.astype(jnp.float32)).astype(jnp.bfloat16)
        rows_at(out, step, i)[...] = dot_f32(high, table_h[...]) + (
            dot_f32(low, table_h[...]) + dot_f32(high, table_l[...])
        )

    for copy in copies:
        copy.wait()


def response_call(place, rates, residues, gates, inputs, taps, tables, window, share):
    tokens = inputs.shape[1]
    step = min(256, share)
    modes = rates.shape[0]
    lanes = ROWS * modes
    spectra = split_pair(turned_tables(window)[2])
    small = (step // ROWS, lanes)
    shape = lambda dims, kind=jnp.float32: jax.ShapeDtypeStruct(dims, kind)
    power_shape = shape((share // PAIR, window, 2 * lanes), jnp.bfloat16)
    outs = [shape((share, 2 * window))] + [shape((share // ROWS, lanes))] * 2
    outs += [power_shape] * 2
    outs += [
        shape((2, share, tokens), gates.dtype),
        shape((share, tokens), inputs.dtype),
        shape((share, window), taps.dtype),
    ]
    outs += [shape(t.shape, t.dtype) for t in tables]
    staged = 3 + len(tables)
    found = pl.pallas_call(
        functools.partial(response_kernel, len(tables)),
        out_shape=tuple(outs),
        in_specs=[SMEM_SPEC] * 2 + [VMEM_SPEC] * 4 + [ANY_SPEC] * staged,
        out_specs=(VMEM_SPEC,) * len(outs),
        scratch_shapes=[
            pltpu.VMEM((step, modes), jnp.float32),
            pltpu.VMEM(small, jnp.float32),
            pltpu.VMEM(small, jnp.float32),
            pltpu.SemaphoreType.DMA((staged,)),
        ],
        name="response",
        cost_estimate=cost(share, 4 * window, 600),
        compiler_params=COMPILER,
    )(*place, rates, residues, *spectra, *parked(gates, inputs, taps, *tables))
    return found[:5], found[5:8], found[8:]


def products(members, tap_spec):
    window = tap_spec.shape[1] // 2
    real, packed = tap_spec[:, :window], tap_spec[:, window:]
    lane = lax.broadcasted_iota(jnp.int32, real.shape, 1)
    real_b = jnp.where(lane == 0, packed, real)
    imag = jnp.where(lane == 0, 0.0, packed)
    found = []
    for mixed in members:
        a, b = mixed[:, :window], mixed[:, window:]
        found.append(
            jnp.concatenate([a * real - b * imag, a * imag + b * real_b], axis=1).astype(
                jnp.bfloat16
            )
        )
    return found


def doubled_spectrum(members, table):
    rows = jnp.concatenate(members, axis=0)
    found = dot_f32(jnp.concatenate([rows, rows], axis=1), table[...])
    size = members[0].shape[0]
    return [found[k * size : (k + 1) * size] for k in range(len(members))]


def finish_medium(members, table, gates_out, gates_in, streams, targets):
    found = dot_f32(jnp.concatenate(members, axis=0), table[...])
    size, window = streams[0].shape
    signals = []
    for k in range(len(members)):
        rows = slice(k * size, (k + 1) * size)
        medium = found[rows, :window] + found[rows, window:]
        gated = (gates_out[k].astype(jnp.float32) * medium).astype(jnp.bfloat16)
        targets[k][...] = gated
        stream = streams[k].astype(jnp.float32) + gated.astype(jnp.float32)
        signals.append((gates_in[k].astype(jnp.float32) * stream).astype(jnp.bfloat16))
    return signals


def end_states(signals, powers_of_pair, pair, modes, mask):
    rows = slice(pair * PAIR, (pair + 1) * PAIR)
    lanes = ROWS * modes
    left = jnp.concatenate([signal[rows] for signal in signals], axis=0)
    found = dot_f32(left, powers_of_pair)
    sides = []
    for side in range(2):
        tops = [k * PAIR + side * ROWS for k in range(len(signals))]
        sides.append(
            [
                jnp.where(mask, found[top : top + ROWS, side * lanes : (side + 1) * lanes], 0.0)
                for top in tops
            ]
        )
    return sides


def later_kernel(
    modes,
    step,
    sec,
    tok,
    local_all,
    remote_all,
    inputs_all,
    taps_all,
    falling_all,
    fwd_even,
    fwd_odd,
    inv_even,
    inv_odd,
    medium_all,
    ends_all,
    tap_spec_all,
    edge_spec_all,
):
    share, tokens = inputs_all.shape
    window = taps_all.shape[1]
    blocks = tokens // window
    parts = [slice(b * window, (b + 1) * window) for b in range(blocks)]
    mask = lane_mask(modes)

    def chunk(section, i):
        first, second = (local_all, remote_all) if section == 0 else (remote_all, local_all)
        first, second = rows_at(first, step, i, 1), rows_at(second, step, i, 1)
        inputs = rows_at(inputs_all, step, i)
        medium_out, ends = rows_at(medium_all, step, i), rows_at(ends_all, step, i, 1)
        falling = rows_at(falling_all, step // PAIR, i)
        sources = [first[1, :, part] * inputs[:, part] for part in parts]
        tap_rows = rows_at(taps_all, step, i)[...]
        tap_spec, *even = doubled_spectrum([tap_rows] + sources[0::2], fwd_even)
        odd = doubled_spectrum(sources[1::2], fwd_odd)
        in_order = [None] * blocks
        in_order[0::2] = even
        in_order[1::2] = odd
        rows_at(tap_spec_all, step, i)[...] = tap_spec
        rows_at(edge_spec_all, step, i)[...] = in_order[0]
        mixed = products([in_order[b - 1] + in_order[b] for b in range(1, blocks)], tap_spec)
        signals = [None] * blocks
        for parity, table in enumerate((inv_even, inv_odd)):
            chosen = [b for b in range(1, blocks) if b % 2 == parity]
            if not chosen:
                continue
            found = finish_medium(
                [mixed[b - 1] for b in chosen],
                table,
                [first[0, :, parts[b]] for b in chosen],
                [second[1, :, parts[b]] for b in chosen],
                [inputs[:, parts[b]] for b in chosen],
                [medium_out.at[:, parts[b]] for b in chosen],
            )
            for b, signal in zip(chosen, found):
                signals[b] = signal
        for pair in range(step // PAIR):
            sides = end_states(signals[1:], falling[pair], pair, modes, mask)
            for side, found in enumerate(sides):
                at = pair * PAIR + side * ROWS
                for k, end in enumerate(found):
                    ends[k + 1, at : at + ROWS, :] = end

    def body(section):
        pl.loop(0, share // step)(functools.partial(chunk, section))

    by_section(sec, body)


def later_call(place, gates, swapped, inputs, taps, falling, tables, modes):
    share, tokens = inputs.shape
    window = taps.shape[1]
    lanes = ROWS * modes
    operands = [gates, swapped, inputs, taps, falling, *tables]
    spec = jax.ShapeDtypeStruct((share, 2 * window), jnp.float32)
    return pl.pallas_call(
        functools.partial(later_kernel, modes, min(256, share)),
        out_shape=(
            jax.ShapeDtypeStruct((share, tokens), jnp.bfloat16),
            jax.ShapeDtypeStruct((tokens // window, share, lanes), jnp.float32),
            spec,
            spec,
        ),
        in_specs=[SMEM_SPEC] * 2 + [VMEM_SPEC] * len(operands),
        out_specs=(VMEM_SPEC,) * 4,
        name="later",
        cost_estimate=cost(share, tokens, 1500),
        compiler_params=COMPILER,
    )(*place, *operands)


def first_kernel(
    modes,
    step,
    sec,
    tok,
    local_all,
    remote_all,
    inputs_all,
    halo_low,
    halo_high,
    rates,
    falling_all,
    tap_spec_all,
    edge_spec_all,
    fwd_odd,
    inv_even,
    medium_before,
    ends_before,
    medium_all,
    ends_all,
    total_all,
    leaps_all,
):
    share = inputs_all.shape[0]
    window = tap_spec_all.shape[1] // 2
    part = slice(0, window)
    mask = lane_mask(modes)
    leaps_all[...] = jnp.exp(-rates[...] * window)

    def chunk(section, i):
        first, second = (local_all, remote_all) if section == 0 else (remote_all, local_all)
        first, second = rows_at(first, step, i, 1), rows_at(second, step, i, 1)
        halo = rows_at(halo_low if section == 0 else halo_high, step, i)
        leaps = rows_at(leaps_all, step // ROWS, i)
        falling = rows_at(falling_all, step // PAIR, i)
        ends = rows_at(ends_all, step, i, 1)
        started = jnp.where(tok[0] > 0, 1.0, 0.0).astype(jnp.bfloat16)
        (before,) = doubled_spectrum([halo[...] * started], fwd_odd)
        mixed = products(
            [before + rows_at(edge_spec_all, step, i)[...]],
            rows_at(tap_spec_all, step, i)[...],
        )
        signals = finish_medium(
            mixed,
            inv_even,
            [first[0, :, part]],
            [second[1, :, part]],
            [rows_at(inputs_all, step, i)[:, part]],
            [rows_at(medium_all, step, i).at[:, part]],
        )
        sums = []
        for pair in range(step // PAIR):
            sides = end_states(signals, falling[pair], pair, modes, mask)
            for side, (end,) in enumerate(sides):
                at = pair * PAIR + side * ROWS
                leap = spread(leaps, 2 * pair + side)
                ends[0, at : at + ROWS, :] = end
                state = end
                for k in range(1, ends.shape[0]):
                    state = state * leap + ends[k, at : at + ROWS, :]
                sums.append(jnp.sum(state, axis=0, keepdims=True))
        total = rows_at(total_all, step // ROWS, i)
        total[...] = jnp.concatenate(sums, axis=0).astype(total.dtype)

    def body(section):
        pl.loop(0, share // step)(functools.partial(chunk, section))

    by_section(sec, body)


def first_call(
    place, gates, swapped, inputs, halos, rates, falling, specs, tables, medium, ends, modes
):
    share, tokens = inputs.shape
    lanes = ROWS * modes
    small = (share // ROWS, lanes)
    operands = [gates, swapped, inputs, *halos, rates, falling, *specs, *tables, medium, ends]
    return pl.pallas_call(
        functools.partial(first_kernel, modes, min(256, share)),
        out_shape=(
            jax.ShapeDtypeStruct(medium.shape, medium.dtype),
            jax.ShapeDtypeStruct(ends.shape, ends.dtype),
            jax.ShapeDtypeStruct(small, jnp.bfloat16),
        ),
        in_specs=[SMEM_SPEC] * 2 + [VMEM_SPEC] * len(operands),
        out_specs=(VMEM_SPEC,) * 3,
        scratch_shapes=[pltpu.VMEM(small, jnp.float32)],
        input_output_aliases={len(operands): 0, len(operands) + 1: 1},
        name="first",
        cost_estimate=cost(share, tokens, 500),
        compiler_params=COMPILER,
    )(*place, *operands)


def within_kernel(
    step,
    sec,
    tok,
    local_all,
    remote_all,
    inputs_all,
    medium_all,
    response_all,
    fwd_h,
    fwd_l,
    inverse,
    out_all,
):
    share, tokens = inputs_all.shape
    size = fwd_h.shape[0]
    half = size // 2

    def chunk(section, i):
        gate_in = rows_at((remote_all if section == 0 else local_all).at[1], step, i)
        inputs, gated_medium = rows_at(inputs_all, step, i), rows_at(medium_all, step, i)
        response, out = rows_at(response_all, step, i), rows_at(out_all, step, i)
        channels = step
        real, imag = response[:, :half], response[:, half:]
        parts = [slice(k * size, (k + 1) * size) for k in range(tokens // size)]
        signals = []
        for part in parts:
            stream = inputs[:, part].astype(jnp.float32) + gated_medium[:, part].astype(
                jnp.float32
            )
            signals.append((gate_in[:, part].astype(jnp.float32) * stream).astype(jnp.bfloat16))
        signal = jnp.concatenate(signals, axis=0)
        spec = dot_f32(signal, fwd_h[...]) + dot_f32(signal, fwd_l[...])
        filtered = []
        for k in range(len(parts)):
            rows = slice(k * channels, (k + 1) * channels)
            a, b = spec[rows, :half], spec[rows, half:]
            filtered.append(
                jnp.concatenate([a * real - b * imag, a * imag + b * real], axis=1).astype(
                    jnp.bfloat16
                )
            )
        found = dot_f32(jnp.concatenate(filtered, axis=0), inverse[...])
        for k, part in enumerate(parts):
            out[:, part] = found[k * channels : (k + 1) * channels]

    def body(section):
        pl.loop(0, share // step)(functools.partial(chunk, section))

    by_section(sec, body)


def within_call(place, gates, swapped, inputs, medium, response, tables):
    share, tokens = inputs.shape
    operands = [gates, swapped, inputs, medium, response, *tables]
    return pl.pallas_call(
        functools.partial(within_kernel, min(WITHIN_STEP, share)),
        out_shape=jax.ShapeDtypeStruct((share, tokens), jnp.float32),
        in_specs=[SMEM_SPEC] * 2 + [VMEM_SPEC] * len(operands),
        out_specs=VMEM_SPEC,
        name="within",
        cost_estimate=cost(share, tokens, 1500),
        compiler_params=COMPILER,
    )(*place, *operands)


def output_kernel(
    count,
    modes,
    window,
    step,
    first,
    share,
    sec,
    tok,
    local_all,
    remote_all,
    within_all,
    inputs_all,
    medium_all,
    rates,
    scale_rows,
    rising_all,
    ends_all,
    *rest,
):
    arrived = rest[:count]
    (result, send, leaps_all, scales_all, shares_all, starts_all, mixed, done) = rest[-8:]
    part_rows, tokens = send.shape
    base = first // step
    groups = pl.ds(first // ROWS, part_rows // ROWS)
    blocks = tokens // window
    mask = lane_mask(modes)
    slow = rates[groups, :]
    leap_all = jnp.exp(-slow * window)
    scale_all = scale_rows[groups, :] * jnp.exp(-slow)
    leaps_all[...] = leap_all
    scales_all[...] = scale_all
    shares_all[...] = scale_all / (1.0 + leap_all)
    entering = jnp.zeros_like(slow)
    for k in range(count):
        known = jnp.where(tok[0] > k, 1.0, 0.0)
        entering = entering + arrived[k][groups, :].astype(jnp.float32) * (jnp.exp(-slow * (tokens * k)) * known)
    starts_all[...] = entering

    def chunk(section, out_all, i):
        out = rows_at(out_all, step, i)
        at_all = base + i
        gate_out = rows_at((remote_all if section == 0 else local_all).at[0], step, at_all)
        inputs = rows_at(inputs_all, step, at_all)
        gated_medium = rows_at(medium_all, step, at_all)
        within = rows_at(within_all, step, at_all)
        ends = rows_at(ends_all, step, at_all, 1)
        rising = rows_at(rising_all, step // PAIR, at_all)
        small = step // ROWS
        leaps, scales = rows_at(leaps_all, small, i), rows_at(scales_all, small, i)
        shares, starts = rows_at(shares_all, small, i), rows_at(starts_all, small, i)
        channels = step
        for pair in range(channels // PAIR):
            rows = slice(pair * PAIR, (pair + 1) * PAIR)
            sides = []
            for side in range(2):
                group = 2 * pair + side
                leap, scale = spread(leaps, group), spread(scales, group)
                share = spread(shares, group)
                state = jnp.where(mask, spread(starts, group), 0.0)
                at = pair * PAIR + side * ROWS
                lefts = []
                for b in range(blocks):
                    end = ends[b, at : at + ROWS, :]
                    lefts.append(state * scale + end * share)
                    state = state * leap + end
                sides.append(lefts)
            left = jnp.concatenate(
                [two_sided(upper, lower) for upper, lower in zip(*sides)], axis=0
            ).astype(jnp.bfloat16)
            across = dot_turned(left, rising[pair])
            for b in range(blocks):
                part = slice(b * window, (b + 1) * window)
                stream = inputs[rows, part].astype(jnp.float32) + gated_medium[
                    rows, part
                ].astype(jnp.float32)
                long_out = within[rows, part] + across[b * PAIR : (b + 1) * PAIR]
                gate = gate_out[rows, part].astype(jnp.float32)
                out[rows, part] = (stream + gate * long_out).astype(jnp.bfloat16)

    def body(section):
        target = result.at[0, pl.ds(section * share + first, part_rows), :]
        source = medium_all.at[pl.ds(first, part_rows), :]
        early = pltpu.make_async_copy(source, target if section == 0 else send, done.at[0])
        early.start()
        pl.loop(0, part_rows // step)(
            functools.partial(chunk, section, mixed if section else send)
        )
        if section == 1:
            late = pltpu.make_async_copy(mixed, target, done.at[1])
            late.start()
            late.wait()
        early.wait()

    by_section(sec, body)


def output_call(
    place, half, gates, swapped, within, inputs, medium, rates, scales, rising, ends, arrived, before
):
    share, tokens = medium.shape
    lanes = rates.shape[1]
    window = rising.shape[1]
    part_rows = share // HALVES
    step = min(256, part_rows)
    small = (part_rows // ROWS, lanes)
    operands = [gates, swapped, within, inputs, medium, rates, scales, rising, ends, *arrived]
    result = jax.ShapeDtypeStruct((1, 2 * share, tokens), jnp.bfloat16)
    chained = [] if before is None else [before]
    return pl.pallas_call(
        functools.partial(
            output_kernel,
            len(arrived),
            lanes // ROWS,
            window,
            step,
            half * part_rows,
            share,
        ),
        out_shape=(result, jax.ShapeDtypeStruct((part_rows, tokens), jnp.bfloat16)),
        in_specs=[SMEM_SPEC] * 2 + [VMEM_SPEC] * len(operands) + [ANY_SPEC] * len(chained),
        out_specs=(ANY_SPEC, VMEM_SPEC),
        scratch_shapes=[pltpu.VMEM(small, jnp.float32)] * 4
        + [pltpu.VMEM((part_rows, tokens), jnp.bfloat16), pltpu.SemaphoreType.DMA((2,))],
        input_output_aliases={2 + len(operands): 0} if chained else {},
        name="output",
        cost_estimate=cost(part_rows, tokens, 1500),
        compiler_params=COMPILER,
    )(*place, *operands, *chained)


def place_kernel(first, share, sec, tok, own, received, out, done):
    rows = received.shape[0]
    other = pl.ds(pl.multiple_of((1 - sec[0]) * share + first, rows), rows)
    copy = pltpu.make_async_copy(received, out.at[0, other, :], done)
    copy.start()
    copy.wait()


def place_call(place, half, own, received):
    rows, tokens = received.shape
    return pl.pallas_call(
        functools.partial(place_kernel, half * rows, own.shape[1] // 2),
        out_shape=jax.ShapeDtypeStruct(own.shape, own.dtype),
        in_specs=[SMEM_SPEC] * 2 + [ANY_SPEC, VMEM_SPEC],
        out_specs=ANY_SPEC,
        scratch_shapes=[pltpu.SemaphoreType.DMA],
        input_output_aliases={2: 0},
        name="placing",
        cost_estimate=cost(rows, tokens, 2),
        compiler_params=COMPILER,
    )(*place, own, received)


def lend_kernel(sec, tok, gates, inputs, lent, low, high, gate_tail, input_tail, arrival):
    share, window = low.shape
    tokens = inputs.shape[1]
    tail = pl.ds(tokens - window, window)
    other = pl.ds(pl.multiple_of((1 - sec[0]) * share, share), share)
    copies = [
        pltpu.make_async_copy(source, target, arrival.at[k])
        for k, (source, target) in enumerate(
            [
                (gates.at[0, 1, :, tail], gate_tail),
                (inputs.at[:, tail], input_tail),
                (gates.at[0, :, other, :], lent),
            ]
        )
    ]
    for copy in copies:
        copy.start()
    copies[0].wait()
    copies[1].wait()
    low[...] = gate_tail[:share, :] * input_tail[:share, :]
    high[...] = gate_tail[share:, :] * input_tail[share:, :]
    copies[2].wait()


def lend_call(place, gate_streams, inputs, window, share):
    channels, tokens = inputs.shape
    edge = jax.ShapeDtypeStruct((share, window), jnp.bfloat16)
    return pl.pallas_call(
        lend_kernel,
        out_shape=(jax.ShapeDtypeStruct((2, share, tokens), jnp.bfloat16), edge, edge),
        in_specs=[SMEM_SPEC] * 2 + [ANY_SPEC] * 2,
        out_specs=(VMEM_SPEC,) * 3,
        scratch_shapes=[pltpu.VMEM((channels, window), jnp.bfloat16)] * 2
        + [pltpu.SemaphoreType.DMA((3,))],
        name="lend",
        cost_estimate=cost(share, tokens, 2),
        compiler_params=COMPILER,
    )(*place, *parked(gate_streams, inputs))


def ring(value, axis, by):
    peers = lax.axis_size(axis)
    return lax.ppermute(value, axis, [(i, (i + by) % peers) for i in range(peers)])


def onward(value, by):
    peers = lax.axis_size("tok")
    sources, targets = range(peers - by, peers), range(by)
    alone = [i for i in sources if i in targets]
    spare = zip([i for i in sources if i not in alone], [i for i in targets if i not in alone])
    pairs = [(i, i + by) for i in range(peers - by)] + [(i, i) for i in alone] + list(spare)
    return lax.ppermute(value, "tok", pairs)


def edge_to(value, section):
    peers = lax.axis_size("tok")
    pairs = [(i, section * peers + (i + 1) % peers) for i in range(peers)]
    pairs += [(peers + i, (1 - section) * peers + i) for i in range(peers)]
    return lax.ppermute(value, ("section", "tok"), pairs)


def on_device(gate_streams, inputs, medium_taps, residues, decay_rates):
    channels, tokens = inputs.shape
    share = channels // 2
    window = medium_taps.shape[1]
    modes = decay_rates.shape[1]
    section = lax.axis_index("section")
    place = tuple(
        lax.axis_index(axis).astype(jnp.int32).reshape(1) for axis in ("section", "tok")
    )
    lent, *edges = lend_call(place, gate_streams, inputs, window, share)
    halos = [edge_to(edges[s], s) for s in range(2)]
    swapped = ring(lent, "section", 1)
    forward, inverse = fourier_tables(window)
    turned, back, _ = turned_tables(window)
    tables = [*forward, *inverse, *split_pair(turned), split_pair(back)[0]]
    built, own, tables = response_call(
        place,
        decay_rates.T,
        residues.T,
        gate_streams,
        inputs,
        medium_taps,
        tables,
        window,
        share,
    )
    response, rates, scales, rising, falling = built
    gates, inputs, taps = own
    medium, ends, *specs = later_call(
        place, gates, swapped, inputs, taps, falling, tables[:4], modes
    )
    medium, ends, total = first_call(
        place,
        gates,
        swapped,
        inputs,
        halos,
        rates,
        falling,
        specs,
        tables[1:3],
        medium,
        ends,
        modes,
    )
    arrived = [onward(total, by) for by in range(1, lax.axis_size("tok"))]
    within = within_call(place, gates, swapped, inputs, medium, response, tables[4:])
    result, received = None, []
    for half in range(HALVES):
        result, send = output_call(
            place,
            half,
            gates,
            swapped,
            within,
            inputs,
            medium,
            rates,
            scales,
            rising,
            ends,
            arrived,
            result,
        )
        received.append(ring(send, "section", 1))
    for half in range(HALVES):
        result = place_call(place, half, result, received[half])
    return result


def solution(mesh):
    placed = (
        P("section", None, "chan", "tok"),
        P("chan", "tok"),
        P("chan", None),
        P("chan", None),
        P("chan", None),
    )
    return jax.shard_map(
        on_device,
        mesh=mesh,
        in_specs=placed,
        out_specs=P("section", "chan", "tok"),
        check_vma=False,
    )
```

```python
import functools

import jax
import jax.numpy as jnp
import numpy as np
from jax import lax
from jax.experimental import pallas as pl
from jax.experimental.pallas import tpu as pltpu
from jax.sharding import PartitionSpec as P

ROWS = 8


def split_pair(matrix):
    high = jnp.asarray(matrix, jnp.float32).astype(jnp.bfloat16)
    low = (jnp.asarray(matrix, jnp.float32) - high.astype(jnp.float32)).astype(jnp.bfloat16)
    return high, low


def stacked(matrix, axis):
    return jnp.concatenate(split_pair(matrix), axis=axis)


def fourier_tables(window):
    size = 2 * window
    time = np.arange(window)[:, None]
    freq = np.arange(window)[None, :]
    angle = 2.0 * np.pi * ((time * freq) % size) / size
    sign = np.where(freq % 2 == 0, 1.0, -1.0)
    nyquist = np.where(time % 2 == 0, 1.0, -1.0)
    weight = np.where(freq == 0, 1.0, 2.0) / size
    forward, inverse = [], []
    for odd in range(2):
        flip = sign if odd else np.ones_like(sign)
        real = np.cos(angle) * flip
        imag = -np.sin(angle) * flip
        imag[:, :1] = nyquist
        forward.append(stacked(np.concatenate([real, imag], axis=1), 0))
        back_real = np.cos(angle) * weight * flip
        back_imag = -np.sin(angle) * weight * flip
        back_imag[:, :1] = nyquist / size
        inverse.append(stacked(np.concatenate([back_real.T, back_imag.T], axis=0), 1))
    return forward, inverse


def turned_tables(window):
    half = window // 2
    time = np.arange(window)[:, None]
    freq = 2 * np.arange(half)[None, :] + 1
    angle = np.pi * ((time * freq) % (2 * window)) / window
    real, imag = np.cos(angle), -np.sin(angle)
    zero = np.zeros_like(real)
    forward = np.concatenate(
        [
            np.concatenate([real, zero, imag, zero], axis=1),
            np.concatenate([zero, real, zero, imag], axis=1),
        ],
        axis=0,
    )
    inverse = forward.T * (2.0 / window)
    doubled = np.concatenate([real, real, imag, imag], axis=1)
    return forward, inverse, doubled


PAIR = 16
WITHIN_STEP = 512
HALVES = 2
COMPILER = pltpu.CompilerParams(vmem_limit_bytes=16 << 20)


def parked(*arrays):
    return [pltpu.with_memory_space_constraint(a, pltpu.HBM) for a in arrays]


def cost(share, tokens, work):
    size = share * tokens
    return pl.CostEstimate(
        flops=size * work, bytes_accessed=size * 12, transcendentals=size // 64
    )


def dot_f32(left, right):
    return jnp.dot(left, right, preferred_element_type=jnp.float32)


def dot_turned(left, right):
    return lax.dot_general(
        left, right, (((1,), (1,)), ((), ())), preferred_element_type=jnp.float32
    )


VMEM_SPEC = pl.BlockSpec(memory_space=pltpu.VMEM)
SMEM_SPEC = pl.BlockSpec(memory_space=pltpu.SMEM)
ANY_SPEC = pl.BlockSpec(memory_space=pl.ANY)


def rows_at(ref, step, i, axis=0):
    start = i * step
    if not isinstance(i, int):
        start = pl.multiple_of(start, step)
    return ref.at[(slice(None),) * axis + (pl.ds(start, step),)]


def by_section(sec, body):
    for section in range(2):
        pl.when(sec[0] == section)(functools.partial(body, section))


def lane_mask(modes):
    shape = (ROWS, ROWS * modes)
    lane = lax.broadcasted_iota(jnp.int32, shape, 1)
    return lane // modes == lax.broadcasted_iota(jnp.int32, shape, 0)


def spread(ref, group):
    return jnp.broadcast_to(ref[group : group + 1, :], (ROWS, ref.shape[1]))


def powers(slow, hop, window, first, falling):
    row = lax.broadcasted_iota(jnp.int32, slow.shape, 0).astype(jnp.float32)
    tiles = [jnp.exp(-slow * (first + (ROWS - 1 - row if falling else row)))]
    while len(tiles) < window // ROWS:
        tiles = tiles + [tile * hop for tile in tiles]
        hop = hop * hop
    if falling:
        tiles = tiles[::-1]
    return jnp.concatenate(tiles, axis=0).astype(jnp.bfloat16)


def both_powers(rates, hops, pair, window, falling):
    sides = [
        powers(spread(rates, g), spread(hops, g), window, 0.0, falling)
        for g in (2 * pair, 2 * pair + 1)
    ]
    return jnp.concatenate(sides, axis=1)


def two_sided(upper, lower):
    zero = jnp.zeros_like(upper)
    return jnp.concatenate(
        [
            jnp.concatenate([upper, zero], axis=1),
            jnp.concatenate([zero, lower], axis=1),
        ],
        axis=0,
    )


def scale_of(residues, slow):
    return residues * jnp.sqrt(1.0 - jnp.exp(-2.0 * slow))


def in_rows(ref, tall):
    modes, channels = ref.shape
    tall[...] = ref[...].T
    count = channels // ROWS
    return jnp.concatenate(
        [tall[pl.ds(c, count, stride=ROWS), :] for c in range(ROWS)], axis=1
    )


def response_kernel(count, sec, tok, rates, residues, table_h, table_l, *rest):
    gates, inputs, taps = rest[:3]
    tables = rest[3 : 3 + count]
    out, rate_rows, scale_rows, rising, falling = rest[3 + count : 8 + count]
    own_gates, own_inputs, own_taps = rest[8 + count : 11 + count]
    own_tables = rest[11 + count : 11 + 2 * count]
    tall, hops, scales, arrival = rest[11 + 2 * count :]
    share = out.shape[0]
    modes = rates.shape[0]
    window = table_h.shape[0]
    step = tall.shape[0]
    first = pl.multiple_of(sec[0] * share, share)
    mine = pl.ds(first, share)
    pairs = [(gates.at[0, :, mine, :], own_gates)]
    pairs += [(inputs.at[mine, :], own_inputs), (taps.at[mine, :], own_taps)]
    pairs += list(zip(tables, own_tables))
    copies = [
        pltpu.make_async_copy(source, target, arrival.at[k])
        for k, (source, target) in enumerate(pairs)
    ]
    for copy in copies:
        copy.start()
    mask = lane_mask(modes)

    @pl.loop(0, share // step)
    def _(i):
        lanes = pl.ds(pl.multiple_of(first + i * step, step), step)
        slow = in_rows(rates.at[:, lanes], tall)
        scale = scale_of(in_rows(residues.at[:, lanes], tall), slow)
        small = step // ROWS
        own_rates = rows_at(rate_rows, small, i)
        own_rates[...] = slow
        rows_at(scale_rows, small, i)[...] = scale
        hops[...] = jnp.exp(-slow * ROWS)
        scales[...] = scale / (1.0 + jnp.exp(-slow * window))
        up, down = rows_at(rising, step // PAIR, i), rows_at(falling, step // PAIR, i)
        parts = []
        for pair in range(step // PAIR):
            both = two_sided(
                jnp.where(mask, spread(scales, 2 * pair), 0.0),
                jnp.where(mask, spread(scales, 2 * pair + 1), 0.0),
            )
            high = both.astype(jnp.bfloat16).astype(jnp.float32)
            both = jnp.concatenate([high, both - high], axis=0).astype(jnp.bfloat16)
            table = both_powers(own_rates, hops, pair, window, False)
            up[pair] = table
            down[pair] = both_powers(own_rates, hops, pair, window, True)
            found = dot_turned(both, table)
            parts.append(found[:PAIR] + found[PAIR:])
        response = jnp.concatenate(parts, axis=0)
        high = response.astype(jnp.bfloat16)
        low = (response - high.astype(jnp.float32)).astype(jnp.bfloat16)
        rows_at(out, step, i)[...] = dot_f32(high, table_h[...]) + (
            dot_f32(low, table_h[...]) + dot_f32(high, table_l[...])
        )

    for copy in copies:
        copy.wait()


def response_call(place, rates, residues, gates, inputs, taps, tables, window, share):
    tokens = inputs.shape[1]
    step = min(256, share)
    modes = rates.shape[0]
    lanes = ROWS * modes
    spectra = split_pair(turned_tables(window)[2])
    small = (step // ROWS, lanes)
    shape = lambda dims, kind=jnp.float32: jax.ShapeDtypeStruct(dims, kind)
    power_shape = shape((share // PAIR, window, 2 * lanes), jnp.bfloat16)
    outs = [shape((share, 2 * window))] + [shape((share // ROWS, lanes))] * 2
    outs += [power_shape] * 2
    outs += [
        shape((2, share, tokens), gates.dtype),
        shape((share, tokens), inputs.dtype),
        shape((share, window), taps.dtype),
    ]
    outs += [shape(t.shape, t.dtype) for t in tables]
    staged = 3 + len(tables)
    found = pl.pallas_call(
        functools.partial(response_kernel, len(tables)),
        out_shape=tuple(outs),
        in_specs=[SMEM_SPEC] * 2 + [VMEM_SPEC] * 4 + [ANY_SPEC] * staged,
        out_specs=(VMEM_SPEC,) * len(outs),
        scratch_shapes=[
            pltpu.VMEM((step, modes), jnp.float32),
            pltpu.VMEM(small, jnp.float32),
            pltpu.VMEM(small, jnp.float32),
            pltpu.SemaphoreType.DMA((staged,)),
        ],
        name="response",
        cost_estimate=cost(share, 4 * window, 600),
        compiler_params=COMPILER,
    )(*place, rates, residues, *spectra, *parked(gates, inputs, taps, *tables))
    return found[:5], found[5:8], found[8:]


def products(members, tap_spec):
    window = tap_spec.shape[1] // 2
    real, packed = tap_spec[:, :window], tap_spec[:, window:]
    lane = lax.broadcasted_iota(jnp.int32, real.shape, 1)
    real_b = jnp.where(lane == 0, packed, real)
    imag = jnp.where(lane == 0, 0.0, packed)
    found = []
    for mixed in members:
        a, b = mixed[:, :window], mixed[:, window:]
        found.append(
            jnp.concatenate([a * real - b * imag, a * imag + b * real_b], axis=1).astype(
                jnp.bfloat16
            )
        )
    return found


def doubled_spectrum(members, table):
    rows = jnp.concatenate(members, axis=0)
    found = dot_f32(jnp.concatenate([rows, rows], axis=1), table[...])
    size = members[0].shape[0]
    return [found[k * size : (k + 1) * size] for k in range(len(members))]


def finish_medium(members, table, gates_out, gates_in, streams, targets):
    found = dot_f32(jnp.concatenate(members, axis=0), table[...])
    size, window = streams[0].shape
    signals = []
    for k in range(len(members)):
        rows = slice(k * size, (k + 1) * size)
        medium = found[rows, :window] + found[rows, window:]
        gated = (gates_out[k].astype(jnp.float32) * medium).astype(jnp.bfloat16)
        targets[k][...] = gated
        stream = streams[k].astype(jnp.float32) + gated.astype(jnp.float32)
        signals.append((gates_in[k].astype(jnp.float32) * stream).astype(jnp.bfloat16))
    return signals


def end_states(signals, powers_of_pair, pair, modes, mask):
    rows = slice(pair * PAIR, (pair + 1) * PAIR)
    lanes = ROWS * modes
    left = jnp.concatenate([signal[rows] for signal in signals], axis=0)
    found = dot_f32(left, powers_of_pair)
    sides = []
    for side in range(2):
        tops = [k * PAIR + side * ROWS for k in range(len(signals))]
        sides.append(
            [
                jnp.where(mask, found[top : top + ROWS, side * lanes : (side + 1) * lanes], 0.0)
                for top in tops
            ]
        )
    return sides


def later_kernel(
    step,
    sec,
    tok,
    local_all,
    remote_all,
    inputs_all,
    taps_all,
    fwd_even,
    fwd_odd,
    inv_even,
    inv_odd,
    medium_all,
    signals_all,
    tap_spec_all,
    edge_spec_all,
):
    share, tokens = inputs_all.shape
    window = taps_all.shape[1]
    blocks = tokens // window
    parts = [slice(b * window, (b + 1) * window) for b in range(blocks)]

    def chunk(section, i):
        first, second = (local_all, remote_all) if section == 0 else (remote_all, local_all)
        first, second = rows_at(first, step, i, 1), rows_at(second, step, i, 1)
        inputs = rows_at(inputs_all, step, i)
        medium_out, signals = rows_at(medium_all, step, i), rows_at(signals_all, step, i)
        sources = [first[1, :, part] * inputs[:, part] for part in parts]
        tap_rows = rows_at(taps_all, step, i)[...]
        tap_spec, *even = doubled_spectrum([tap_rows] + sources[0::2], fwd_even)
        odd = doubled_spectrum(sources[1::2], fwd_odd)
        in_order = [None] * blocks
        in_order[0::2] = even
        in_order[1::2] = odd
        rows_at(tap_spec_all, step, i)[...] = tap_spec
        rows_at(edge_spec_all, step, i)[...] = in_order[0]
        mixed = products([in_order[b - 1] + in_order[b] for b in range(1, blocks)], tap_spec)
        for parity, table in enumerate((inv_even, inv_odd)):
            chosen = [b for b in range(1, blocks) if b % 2 == parity]
            if not chosen:
                continue
            found = finish_medium(
                [mixed[b - 1] for b in chosen],
                table,
                [first[0, :, parts[b]] for b in chosen],
                [second[1, :, parts[b]] for b in chosen],
                [inputs[:, parts[b]] for b in chosen],
                [medium_out.at[:, parts[b]] for b in chosen],
            )
            for b, signal in zip(chosen, found):
                signals[:, parts[b]] = signal

    def body(section):
        pl.loop(0, share // step)(functools.partial(chunk, section))

    by_section(sec, body)


def later_call(place, gates, swapped, inputs, taps, tables):
    share, tokens = inputs.shape
    window = taps.shape[1]
    operands = [gates, swapped, inputs, taps, *tables]
    spec = jax.ShapeDtypeStruct((share, 2 * window), jnp.float32)
    wide = jax.ShapeDtypeStruct((share, tokens), jnp.bfloat16)
    return pl.pallas_call(
        functools.partial(later_kernel, min(256, share)),
        out_shape=(wide, wide, spec, spec),
        in_specs=[SMEM_SPEC] * 2 + [VMEM_SPEC] * len(operands),
        out_specs=(VMEM_SPEC,) * 4,
        name="later",
        cost_estimate=cost(share, tokens, 1500),
        compiler_params=COMPILER,
    )(*place, *operands)


def first_kernel(
    modes,
    step,
    sec,
    tok,
    local_all,
    remote_all,
    inputs_all,
    halo_low,
    halo_high,
    rates,
    falling_all,
    tap_spec_all,
    edge_spec_all,
    fwd_odd,
    inv_even,
    medium_before,
    signals_before,
    medium_all,
    signals_all,
    ends_all,
    total_all,
    leaps_all,
):
    share = inputs_all.shape[0]
    window = tap_spec_all.shape[1] // 2
    part = slice(0, window)
    mask = lane_mask(modes)
    leaps_all[...] = jnp.exp(-rates[...] * window)

    def chunk(section, i):
        first, second = (local_all, remote_all) if section == 0 else (remote_all, local_all)
        first, second = rows_at(first, step, i, 1), rows_at(second, step, i, 1)
        halo = rows_at(halo_low if section == 0 else halo_high, step, i)
        leaps = rows_at(leaps_all, step // ROWS, i)
        falling = rows_at(falling_all, step // PAIR, i)
        ends = rows_at(ends_all, step, i, 1)
        started = jnp.where(tok[0] > 0, 1.0, 0.0).astype(jnp.bfloat16)
        (before,) = doubled_spectrum([halo[...] * started], fwd_odd)
        mixed = products(
            [before + rows_at(edge_spec_all, step, i)[...]],
            rows_at(tap_spec_all, step, i)[...],
        )
        (signal,) = finish_medium(
            mixed,
            inv_even,
            [first[0, :, part]],
            [second[1, :, part]],
            [rows_at(inputs_all, step, i)[:, part]],
            [rows_at(medium_all, step, i).at[:, part]],
        )
        signals = rows_at(signals_all, step, i)
        signals[:, part] = signal
        members = [signal] + [
            signals[:, b * window : (b + 1) * window] for b in range(1, ends.shape[0])
        ]
        sums = []
        for pair in range(step // PAIR):
            sides = end_states(members, falling[pair], pair, modes, mask)
            for side, found in enumerate(sides):
                at = pair * PAIR + side * ROWS
                leap = spread(leaps, 2 * pair + side)
                state = None
                for b, end in enumerate(found):
                    ends[b, at : at + ROWS, :] = end
                    state = end if state is None else state * leap + end
                sums.append(jnp.sum(state, axis=0, keepdims=True))
        total = rows_at(total_all, step // ROWS, i)
        total[...] = jnp.concatenate(sums, axis=0).astype(total.dtype)

    def body(section):
        pl.loop(0, share // step)(functools.partial(chunk, section))

    by_section(sec, body)


def first_call(
    place, gates, swapped, inputs, halos, rates, falling, specs, tables, medium, signals, modes
):
    share, tokens = inputs.shape
    window = halos[0].shape[1]
    lanes = ROWS * modes
    small = (share // ROWS, lanes)
    operands = [gates, swapped, inputs, *halos, rates, falling, *specs, *tables, medium, signals]
    return pl.pallas_call(
        functools.partial(first_kernel, modes, min(256, share)),
        out_shape=(
            jax.ShapeDtypeStruct(medium.shape, medium.dtype),
            jax.ShapeDtypeStruct(signals.shape, signals.dtype),
            jax.ShapeDtypeStruct((tokens // window, share, lanes), jnp.float32),
            jax.ShapeDtypeStruct(small, jnp.bfloat16),
        ),
        in_specs=[SMEM_SPEC] * 2 + [VMEM_SPEC] * len(operands),
        out_specs=(VMEM_SPEC,) * 4,
        scratch_shapes=[pltpu.VMEM(small, jnp.float32)],
        input_output_aliases={len(operands): 0, len(operands) + 1: 1},
        name="first",
        cost_estimate=cost(share, tokens, 500),
        compiler_params=COMPILER,
    )(*place, *operands)


def within_kernel(
    step,
    signals_all,
    response_all,
    fwd_h,
    fwd_l,
    inverse,
    out_all,
):
    share, tokens = signals_all.shape
    size = fwd_h.shape[0]
    half = size // 2

    def chunk(i):
        signals = rows_at(signals_all, step, i)
        response, out = rows_at(response_all, step, i), rows_at(out_all, step, i)
        channels = step
        real, imag = response[:, :half], response[:, half:]
        parts = [slice(k * size, (k + 1) * size) for k in range(tokens // size)]
        signal = jnp.concatenate([signals[:, part] for part in parts], axis=0)
        spec = dot_f32(signal, fwd_h[...]) + dot_f32(signal, fwd_l[...])
        filtered = []
        for k in range(len(parts)):
            rows = slice(k * channels, (k + 1) * channels)
            a, b = spec[rows, :half], spec[rows, half:]
            filtered.append(
                jnp.concatenate([a * real - b * imag, a * imag + b * real], axis=1).astype(
                    jnp.bfloat16
                )
            )
        found = dot_f32(jnp.concatenate(filtered, axis=0), inverse[...])
        for k, part in enumerate(parts):
            out[:, part] = found[k * channels : (k + 1) * channels]

    pl.loop(0, share // step)(chunk)


def within_call(signals, response, tables):
    share, tokens = signals.shape
    operands = [signals, response, *tables]
    return pl.pallas_call(
        functools.partial(within_kernel, min(WITHIN_STEP, share)),
        out_shape=jax.ShapeDtypeStruct((share, tokens), jnp.float32),
        in_specs=[VMEM_SPEC] * len(operands),
        out_specs=VMEM_SPEC,
        name="within",
        cost_estimate=cost(share, tokens, 1500),
        compiler_params=COMPILER,
    )(*operands)


def output_kernel(
    count,
    modes,
    window,
    step,
    first,
    share,
    sec,
    tok,
    local_all,
    remote_all,
    within_all,
    inputs_all,
    medium_all,
    rates,
    scale_rows,
    rising_all,
    ends_all,
    *rest,
):
    arrived = rest[:count]
    (result, send, keep, leaps_all, scales_all, shares_all, starts_all, done) = rest[-8:]
    part_rows, tokens = send.shape
    base = first // step
    groups = pl.ds(first // ROWS, part_rows // ROWS)
    blocks = tokens // window
    mask = lane_mask(modes)
    slow = rates[groups, :]
    leap_all = jnp.exp(-slow * window)
    scale_all = scale_rows[groups, :] * jnp.exp(-slow)
    leaps_all[...] = leap_all
    scales_all[...] = scale_all
    shares_all[...] = scale_all / (1.0 + leap_all)
    entering = jnp.zeros_like(slow)
    for k in range(count):
        known = jnp.where(tok[0] > k, 1.0, 0.0)
        entering = entering + arrived[k][groups, :].astype(jnp.float32) * (jnp.exp(-slow * (tokens * k)) * known)
    starts_all[...] = entering

    def chunk(section, out_all, i):
        out = rows_at(out_all, step, i)
        at_all = base + i
        gate_out = rows_at((remote_all if section == 0 else local_all).at[0], step, at_all)
        inputs = rows_at(inputs_all, step, at_all)
        gated_medium = rows_at(medium_all, step, at_all)
        within = rows_at(within_all, step, at_all)
        ends = rows_at(ends_all, step, at_all, 1)
        rising = rows_at(rising_all, step // PAIR, at_all)
        small = step // ROWS
        leaps, scales = rows_at(leaps_all, small, i), rows_at(scales_all, small, i)
        shares, starts = rows_at(shares_all, small, i), rows_at(starts_all, small, i)
        channels = step
        for pair in range(channels // PAIR):
            rows = slice(pair * PAIR, (pair + 1) * PAIR)
            sides = []
            for side in range(2):
                group = 2 * pair + side
                leap, scale = spread(leaps, group), spread(scales, group)
                share = spread(shares, group)
                state = jnp.where(mask, spread(starts, group), 0.0)
                at = pair * PAIR + side * ROWS
                lefts = []
                for b in range(blocks):
                    end = ends[b, at : at + ROWS, :]
                    lefts.append(state * scale + end * share)
                    state = state * leap + end
                sides.append(lefts)
            left = jnp.concatenate(
                [two_sided(upper, lower) for upper, lower in zip(*sides)], axis=0
            ).astype(jnp.bfloat16)
            across = dot_turned(left, rising[pair])
            for b in range(blocks):
                part = slice(b * window, (b + 1) * window)
                stream = inputs[rows, part].astype(jnp.float32) + gated_medium[
                    rows, part
                ].astype(jnp.float32)
                long_out = within[rows, part] + across[b * PAIR : (b + 1) * PAIR]
                gate = gate_out[rows, part].astype(jnp.float32)
                out[rows, part] = (stream + gate * long_out).astype(jnp.bfloat16)

    def body(section):
        target = result.at[0, pl.ds(section * share + first, part_rows), :]
        source = medium_all.at[pl.ds(first, part_rows), :]
        copy = pltpu.make_async_copy(source, send if section else target, done)
        copy.start()
        pl.loop(0, part_rows // step)(
            functools.partial(chunk, section, keep if section else send)
        )
        copy.wait()

    by_section(sec, body)


def output_call(
    place, half, gates, swapped, within, inputs, medium, rates, scales, rising, ends, arrived, before
):
    share, tokens = medium.shape
    lanes = rates.shape[1]
    window = rising.shape[1]
    part_rows = share // HALVES
    step = min(256, part_rows)
    small = (part_rows // ROWS, lanes)
    operands = [gates, swapped, within, inputs, medium, rates, scales, rising, ends, *arrived]
    result = jax.ShapeDtypeStruct((1, 2 * share, tokens), jnp.bfloat16)
    chained = [] if before is None else [before]
    return pl.pallas_call(
        functools.partial(
            output_kernel,
            len(arrived),
            lanes // ROWS,
            window,
            step,
            half * part_rows,
            share,
        ),
        out_shape=(result,) + (jax.ShapeDtypeStruct((part_rows, tokens), jnp.bfloat16),) * 2,
        in_specs=[SMEM_SPEC] * 2 + [VMEM_SPEC] * len(operands) + [ANY_SPEC] * len(chained),
        out_specs=(ANY_SPEC, VMEM_SPEC, VMEM_SPEC),
        scratch_shapes=[pltpu.VMEM(small, jnp.float32)] * 4
        + [pltpu.SemaphoreType.DMA],
        input_output_aliases={2 + len(operands): 0} if chained else {},
        name="output",
        cost_estimate=cost(part_rows, tokens, 1500),
        compiler_params=COMPILER,
    )(*place, *operands, *chained)


def place_kernel(first, share, sec, tok, before, received, keep, out, done):
    rows = received.shape[0]

    def target(section):
        return out.at[0, pl.ds(pl.multiple_of(section * share + first, rows), rows), :]

    foreign = pltpu.make_async_copy(received, target(1 - sec[0]), done.at[0])
    foreign.start()

    @pl.when(sec[0] == 1)
    def _():
        own = pltpu.make_async_copy(keep, target(1), done.at[1])
        own.start()
        own.wait()

    foreign.wait()


def place_call(place, half, before, received, keep):
    rows, tokens = received.shape
    return pl.pallas_call(
        functools.partial(place_kernel, half * rows, before.shape[1] // 2),
        out_shape=jax.ShapeDtypeStruct(before.shape, before.dtype),
        in_specs=[SMEM_SPEC] * 2 + [ANY_SPEC, VMEM_SPEC, VMEM_SPEC],
        out_specs=ANY_SPEC,
        scratch_shapes=[pltpu.SemaphoreType.DMA((2,))],
        input_output_aliases={2: 0},
        name="placing",
        cost_estimate=cost(rows, tokens, 2),
        compiler_params=COMPILER,
    )(*place, before, received, keep)


def lend_kernel(sec, tok, gates, inputs, lent, low, high, gate_tail, input_tail, arrival):
    share, window = low.shape
    tokens = inputs.shape[1]
    tail = pl.ds(tokens - window, window)
    other = pl.ds(pl.multiple_of((1 - sec[0]) * share, share), share)
    copies = [
        pltpu.make_async_copy(source, target, arrival.at[k])
        for k, (source, target) in enumerate(
            [
                (gates.at[0, 1, :, tail], gate_tail),
                (inputs.at[:, tail], input_tail),
                (gates.at[0, :, other, :], lent),
            ]
        )
    ]
    for copy in copies:
        copy.start()
    copies[0].wait()
    copies[1].wait()
    low[...] = gate_tail[:share, :] * input_tail[:share, :]
    high[...] = gate_tail[share:, :] * input_tail[share:, :]
    copies[2].wait()


def lend_call(place, gate_streams, inputs, window, share):
    channels, tokens = inputs.shape
    edge = jax.ShapeDtypeStruct((share, window), jnp.bfloat16)
    return pl.pallas_call(
        lend_kernel,
        out_shape=(jax.ShapeDtypeStruct((2, share, tokens), jnp.bfloat16), edge, edge),
        in_specs=[SMEM_SPEC] * 2 + [ANY_SPEC] * 2,
        out_specs=(VMEM_SPEC,) * 3,
        scratch_shapes=[pltpu.VMEM((channels, window), jnp.bfloat16)] * 2
        + [pltpu.SemaphoreType.DMA((3,))],
        name="lend",
        cost_estimate=cost(share, tokens, 2),
        compiler_params=COMPILER,
    )(*place, *parked(gate_streams, inputs))


def ring(value, axis, by):
    peers = lax.axis_size(axis)
    return lax.ppermute(value, axis, [(i, (i + by) % peers) for i in range(peers)])


def onward(value, by):
    peers = lax.axis_size("tok")
    sources, targets = range(peers - by, peers), range(by)
    alone = [i for i in sources if i in targets]
    spare = zip([i for i in sources if i not in alone], [i for i in targets if i not in alone])
    pairs = [(i, i + by) for i in range(peers - by)] + [(i, i) for i in alone] + list(spare)
    return lax.ppermute(value, "tok", pairs)


def edge_to(value, section):
    peers = lax.axis_size("tok")
    pairs = [(i, section * peers + (i + 1) % peers) for i in range(peers)]
    pairs += [(peers + i, (1 - section) * peers + i) for i in range(peers)]
    return lax.ppermute(value, ("section", "tok"), pairs)


def on_device(gate_streams, inputs, medium_taps, residues, decay_rates):
    channels, tokens = inputs.shape
    share = channels // 2
    window = medium_taps.shape[1]
    modes = decay_rates.shape[1]
    section = lax.axis_index("section")
    place = tuple(
        lax.axis_index(axis).astype(jnp.int32).reshape(1) for axis in ("section", "tok")
    )
    lent, *edges = lend_call(place, gate_streams, inputs, window, share)
    halos = [edge_to(edges[s], s) for s in range(2)]
    swapped = ring(lent, "section", 1)
    forward, inverse = fourier_tables(window)
    turned, back, _ = turned_tables(window)
    tables = [*forward, *inverse, *split_pair(turned), split_pair(back)[0]]
    built, own, tables = response_call(
        place,
        decay_rates.T,
        residues.T,
        gate_streams,
        inputs,
        medium_taps,
        tables,
        window,
        share,
    )
    response, rates, scales, rising, falling = built
    gates, inputs, taps = own
    medium, signals, *specs = later_call(place, gates, swapped, inputs, taps, tables[:4])
    medium, signals, ends, total = first_call(
        place,
        gates,
        swapped,
        inputs,
        halos,
        rates,
        falling,
        specs,
        tables[1:3],
        medium,
        signals,
        modes,
    )
    arrived = [onward(total, by) for by in range(1, lax.axis_size("tok"))]
    within = within_call(signals, response, tables[4:])
    result, waiting = None, []
    for half in range(HALVES):
        result, send, keep = output_call(
            place,
            half,
            gates,
            swapped,
            within,
            inputs,
            medium,
            rates,
            scales,
            rising,
            ends,
            arrived,
            result,
        )
        waiting.append((ring(send, "section", 1), keep))
    for half, (received, keep) in enumerate(waiting):
        result = place_call(place, half, result, received, keep)
    return result


def solution(mesh):
    placed = (
        P("section", None, "chan", "tok"),
        P("chan", "tok"),
        P("chan", None),
        P("chan", None),
        P("chan", None),
    )
    return jax.shard_map(
        on_device,
        mesh=mesh,
        in_specs=placed,
        out_specs=P("section", "chan", "tok"),
        check_vma=False,
    )
```

```python
import functools

import jax
import jax.numpy as jnp
import numpy as np
from jax import lax
from jax.experimental import pallas as pl
from jax.experimental.pallas import tpu as pltpu
from jax.sharding import PartitionSpec as P

ROWS = 8


def split_pair(matrix):
    high = jnp.asarray(matrix, jnp.float32).astype(jnp.bfloat16)
    low = (jnp.asarray(matrix, jnp.float32) - high.astype(jnp.float32)).astype(jnp.bfloat16)
    return high, low


def stacked(matrix, axis):
    return jnp.concatenate(split_pair(matrix), axis=axis)


def fourier_tables(window):
    size = 2 * window
    time = np.arange(window)[:, None]
    freq = np.arange(window)[None, :]
    angle = 2.0 * np.pi * ((time * freq) % size) / size
    sign = np.where(freq % 2 == 0, 1.0, -1.0)
    nyquist = np.where(time % 2 == 0, 1.0, -1.0)
    weight = np.where(freq == 0, 1.0, 2.0) / size
    forward, inverse = [], []
    for odd in range(2):
        flip = sign if odd else np.ones_like(sign)
        real = np.cos(angle) * flip
        imag = -np.sin(angle) * flip
        imag[:, :1] = nyquist
        forward.append(stacked(np.concatenate([real, imag], axis=1), 0))
        back_real = np.cos(angle) * weight * flip
        back_imag = -np.sin(angle) * weight * flip
        back_imag[:, :1] = nyquist / size
        inverse.append(stacked(np.concatenate([back_real.T, back_imag.T], axis=0), 1))
    return forward, inverse


def turned_tables(window):
    half = window // 2
    time = np.arange(window)[:, None]
    freq = 2 * np.arange(half)[None, :] + 1
    angle = np.pi * ((time * freq) % (2 * window)) / window
    real, imag = np.cos(angle), -np.sin(angle)
    zero = np.zeros_like(real)
    forward = np.concatenate(
        [
            np.concatenate([real, zero, imag, zero], axis=1),
            np.concatenate([zero, real, zero, imag], axis=1),
        ],
        axis=0,
    )
    inverse = forward.T * (2.0 / window)
    doubled = np.concatenate([real, real, imag, imag], axis=1)
    return forward, inverse, doubled


PAIR = 16
WITHIN_STEP = 512
STEP = 512
HALVES = 2
COMPILER = pltpu.CompilerParams(vmem_limit_bytes=16 << 20)


def parked(*arrays):
    return [pltpu.with_memory_space_constraint(a, pltpu.HBM) for a in arrays]


def cost(share, tokens, work):
    size = share * tokens
    return pl.CostEstimate(
        flops=size * work, bytes_accessed=size * 12, transcendentals=size // 64
    )


def dot_f32(left, right):
    return jnp.dot(left, right, preferred_element_type=jnp.float32)


def dot_turned(left, right):
    return lax.dot_general(
        left, right, (((1,), (1,)), ((), ())), preferred_element_type=jnp.float32
    )


VMEM_SPEC = pl.BlockSpec(memory_space=pltpu.VMEM)
SMEM_SPEC = pl.BlockSpec(memory_space=pltpu.SMEM)
ANY_SPEC = pl.BlockSpec(memory_space=pl.ANY)


def rows_at(ref, step, i, axis=0):
    start = i * step
    if not isinstance(i, int):
        start = pl.multiple_of(start, step)
    return ref.at[(slice(None),) * axis + (pl.ds(start, step),)]


def by_section(sec, body):
    for section in range(2):
        pl.when(sec[0] == section)(functools.partial(body, section))


def lane_mask(modes):
    shape = (ROWS, ROWS * modes)
    lane = lax.broadcasted_iota(jnp.int32, shape, 1)
    return lane // modes == lax.broadcasted_iota(jnp.int32, shape, 0)


def spread(ref, group):
    return jnp.broadcast_to(ref[group : group + 1, :], (ROWS, ref.shape[1]))


def powers(slow, hop, window, first, falling):
    row = lax.broadcasted_iota(jnp.int32, slow.shape, 0).astype(jnp.float32)
    tiles = [jnp.exp(-slow * (first + (ROWS - 1 - row if falling else row)))]
    while len(tiles) < window // ROWS:
        tiles = tiles + [tile * hop for tile in tiles]
        hop = hop * hop
    if falling:
        tiles = tiles[::-1]
    return jnp.concatenate(tiles, axis=0).astype(jnp.bfloat16)


def both_powers(rates, hops, pair, window, falling):
    sides = [
        powers(spread(rates, g), spread(hops, g), window, 0.0, falling)
        for g in (2 * pair, 2 * pair + 1)
    ]
    return jnp.concatenate(sides, axis=1)


def two_sided(upper, lower):
    zero = jnp.zeros_like(upper)
    return jnp.concatenate(
        [
            jnp.concatenate([upper, zero], axis=1),
            jnp.concatenate([zero, lower], axis=1),
        ],
        axis=0,
    )


def scale_of(residues, slow):
    return residues * jnp.sqrt(1.0 - jnp.exp(-2.0 * slow))


def in_rows(ref, tall):
    modes, channels = ref.shape
    tall[...] = ref[...].T
    count = channels // ROWS
    return jnp.concatenate(
        [tall[pl.ds(c, count, stride=ROWS), :] for c in range(ROWS)], axis=1
    )


def response_kernel(count, sec, tok, rates, residues, table_h, table_l, *rest):
    gates, inputs, taps = rest[:3]
    tables = rest[3 : 3 + count]
    out, rate_rows, scale_rows, rising, falling = rest[3 + count : 8 + count]
    own_gates, own_inputs, own_taps = rest[8 + count : 11 + count]
    own_tables = rest[11 + count : 11 + 2 * count]
    tall, hops, scales, arrival = rest[11 + 2 * count :]
    share = out.shape[0]
    modes = rates.shape[0]
    window = table_h.shape[0]
    step = tall.shape[0]
    first = pl.multiple_of(sec[0] * share, share)
    mine = pl.ds(first, share)
    pairs = [(gates.at[0, :, mine, :], own_gates)]
    pairs += [(inputs.at[mine, :], own_inputs), (taps.at[mine, :], own_taps)]
    pairs += list(zip(tables, own_tables))
    copies = [
        pltpu.make_async_copy(source, target, arrival.at[k])
        for k, (source, target) in enumerate(pairs)
    ]
    for copy in copies:
        copy.start()
    mask = lane_mask(modes)

    @pl.loop(0, share // step)
    def _(i):
        lanes = pl.ds(pl.multiple_of(first + i * step, step), step)
        slow = in_rows(rates.at[:, lanes], tall)
        scale = scale_of(in_rows(residues.at[:, lanes], tall), slow)
        small = step // ROWS
        own_rates = rows_at(rate_rows, small, i)
        own_rates[...] = slow
        rows_at(scale_rows, small, i)[...] = scale
        hops[...] = jnp.exp(-slow * ROWS)
        scales[...] = scale / (1.0 + jnp.exp(-slow * window))
        up, down = rows_at(rising, step // PAIR, i), rows_at(falling, step // PAIR, i)
        parts = []
        for pair in range(step // PAIR):
            both = two_sided(
                jnp.where(mask, spread(scales, 2 * pair), 0.0),
                jnp.where(mask, spread(scales, 2 * pair + 1), 0.0),
            )
            high = both.astype(jnp.bfloat16).astype(jnp.float32)
            both = jnp.concatenate([high, both - high], axis=0).astype(jnp.bfloat16)
            table = both_powers(own_rates, hops, pair, window, False)
            up[pair] = table
            down[pair] = both_powers(own_rates, hops, pair, window, True)
            found = dot_turned(both, table)
            parts.append(found[:PAIR] + found[PAIR:])
        response = jnp.concatenate(parts, axis=0)
        high = response.astype(jnp.bfloat16)
        low = (response - high.astype(jnp.float32)).astype(jnp.bfloat16)
        rows_at(out, step, i)[...] = dot_f32(high, table_h[...]) + (
            dot_f32(low, table_h[...]) + dot_f32(high, table_l[...])
        )

    for copy in copies:
        copy.wait()


def response_call(place, rates, residues, gates, inputs, taps, tables, window, share):
    tokens = inputs.shape[1]
    step = min(256, share)
    modes = rates.shape[0]
    lanes = ROWS * modes
    spectra = split_pair(turned_tables(window)[2])
    small = (step // ROWS, lanes)
    shape = lambda dims, kind=jnp.float32: jax.ShapeDtypeStruct(dims, kind)
    power_shape = shape((share // PAIR, window, 2 * lanes), jnp.bfloat16)
    outs = [shape((share, 2 * window))] + [shape((share // ROWS, lanes))] * 2
    outs += [power_shape] * 2
    outs += [
        shape((2, share, tokens), gates.dtype),
        shape((share, tokens), inputs.dtype),
        shape((share, window), taps.dtype),
    ]
    outs += [shape(t.shape, t.dtype) for t in tables]
    staged = 3 + len(tables)
    found = pl.pallas_call(
        functools.partial(response_kernel, len(tables)),
        out_shape=tuple(outs),
        in_specs=[SMEM_SPEC] * 2 + [VMEM_SPEC] * 4 + [ANY_SPEC] * staged,
        out_specs=(VMEM_SPEC,) * len(outs),
        scratch_shapes=[
            pltpu.VMEM((step, modes), jnp.float32),
            pltpu.VMEM(small, jnp.float32),
            pltpu.VMEM(small, jnp.float32),
            pltpu.SemaphoreType.DMA((staged,)),
        ],
        name="response",
        cost_estimate=cost(share, 4 * window, 600),
        compiler_params=COMPILER,
    )(*place, rates, residues, *spectra, *parked(gates, inputs, taps, *tables))
    return found[:5], found[5:8], found[8:]


def products(members, tap_spec):
    window = tap_spec.shape[1] // 2
    real, packed = tap_spec[:, :window], tap_spec[:, window:]
    lane = lax.broadcasted_iota(jnp.int32, real.shape, 1)
    real_b = jnp.where(lane == 0, packed, real)
    imag = jnp.where(lane == 0, 0.0, packed)
    found = []
    for mixed in members:
        a, b = mixed[:, :window], mixed[:, window:]
        found.append(
            jnp.concatenate([a * real - b * imag, a * imag + b * real_b], axis=1).astype(
                jnp.bfloat16
            )
        )
    return found


def doubled_spectrum(members, table):
    rows = jnp.concatenate(members, axis=0)
    found = dot_f32(jnp.concatenate([rows, rows], axis=1), table[...])
    size = members[0].shape[0]
    return [found[k * size : (k + 1) * size] for k in range(len(members))]


def finish_medium(members, table, gates_out, gates_in, streams, targets):
    found = dot_f32(jnp.concatenate(members, axis=0), table[...])
    size, window = streams[0].shape
    signals = []
    for k in range(len(members)):
        rows = slice(k * size, (k + 1) * size)
        medium = found[rows, :window] + found[rows, window:]
        gated = (gates_out[k].astype(jnp.float32) * medium).astype(jnp.bfloat16)
        targets[k][...] = gated
        stream = streams[k].astype(jnp.float32) + gated.astype(jnp.float32)
        signals.append((gates_in[k].astype(jnp.float32) * stream).astype(jnp.bfloat16))
    return signals


def end_states(signals, powers_of_pair, pair, modes, mask):
    rows = slice(pair * PAIR, (pair + 1) * PAIR)
    lanes = ROWS * modes
    left = jnp.concatenate([signal[rows] for signal in signals], axis=0)
    found = dot_f32(left, powers_of_pair)
    sides = []
    for side in range(2):
        tops = [k * PAIR + side * ROWS for k in range(len(signals))]
        sides.append(
            [
                jnp.where(mask, found[top : top + ROWS, side * lanes : (side + 1) * lanes], 0.0)
                for top in tops
            ]
        )
    return sides


def later_kernel(
    step,
    sec,
    tok,
    local_all,
    remote_all,
    inputs_all,
    taps_all,
    fwd_even,
    fwd_odd,
    inv_even,
    inv_odd,
    medium_all,
    signals_all,
    tap_spec_all,
    edge_spec_all,
):
    share, tokens = inputs_all.shape
    window = taps_all.shape[1]
    blocks = tokens // window
    parts = [slice(b * window, (b + 1) * window) for b in range(blocks)]

    def chunk(section, i):
        first, second = (local_all, remote_all) if section == 0 else (remote_all, local_all)
        first, second = rows_at(first, step, i, 1), rows_at(second, step, i, 1)
        inputs = rows_at(inputs_all, step, i)
        medium_out, signals = rows_at(medium_all, step, i), rows_at(signals_all, step, i)
        sources = [first[1, :, part] * inputs[:, part] for part in parts]
        tap_rows = rows_at(taps_all, step, i)[...]
        tap_spec, *even = doubled_spectrum([tap_rows] + sources[0::2], fwd_even)
        odd = doubled_spectrum(sources[1::2], fwd_odd)
        in_order = [None] * blocks
        in_order[0::2] = even
        in_order[1::2] = odd
        rows_at(tap_spec_all, step, i)[...] = tap_spec
        rows_at(edge_spec_all, step, i)[...] = in_order[0]
        mixed = products([in_order[b - 1] + in_order[b] for b in range(1, blocks)], tap_spec)
        for parity, table in enumerate((inv_even, inv_odd)):
            chosen = [b for b in range(1, blocks) if b % 2 == parity]
            if not chosen:
                continue
            found = finish_medium(
                [mixed[b - 1] for b in chosen],
                table,
                [first[0, :, parts[b]] for b in chosen],
                [second[1, :, parts[b]] for b in chosen],
                [inputs[:, parts[b]] for b in chosen],
                [medium_out.at[:, parts[b]] for b in chosen],
            )
            for b, signal in zip(chosen, found):
                signals[:, parts[b]] = signal

    def body(section):
        pl.loop(0, share // step)(functools.partial(chunk, section))

    by_section(sec, body)


def later_call(place, gates, swapped, inputs, taps, tables):
    share, tokens = inputs.shape
    window = taps.shape[1]
    operands = [gates, swapped, inputs, taps, *tables]
    spec = jax.ShapeDtypeStruct((share, 2 * window), jnp.float32)
    wide = jax.ShapeDtypeStruct((share, tokens), jnp.bfloat16)
    return pl.pallas_call(
        functools.partial(later_kernel, min(STEP, share)),
        out_shape=(wide, wide, spec, spec),
        in_specs=[SMEM_SPEC] * 2 + [VMEM_SPEC] * len(operands),
        out_specs=(VMEM_SPEC,) * 4,
        name="later",
        cost_estimate=cost(share, tokens, 1500),
        compiler_params=COMPILER,
    )(*place, *operands)


def first_kernel(
    modes,
    step,
    sec,
    tok,
    local_all,
    remote_all,
    inputs_all,
    halo_low,
    halo_high,
    rates,
    falling_all,
    tap_spec_all,
    edge_spec_all,
    fwd_odd,
    inv_even,
    medium_before,
    signals_before,
    medium_all,
    signals_all,
    ends_all,
    total_all,
    leaps_all,
):
    share = inputs_all.shape[0]
    window = tap_spec_all.shape[1] // 2
    part = slice(0, window)
    mask = lane_mask(modes)
    leaps_all[...] = jnp.exp(-rates[...] * window)

    def chunk(section, i):
        first, second = (local_all, remote_all) if section == 0 else (remote_all, local_all)
        first, second = rows_at(first, step, i, 1), rows_at(second, step, i, 1)
        halo = rows_at(halo_low if section == 0 else halo_high, step, i)
        leaps = rows_at(leaps_all, step // ROWS, i)
        falling = rows_at(falling_all, step // PAIR, i)
        ends = rows_at(ends_all, step, i, 1)
        started = jnp.where(tok[0] > 0, 1.0, 0.0).astype(jnp.bfloat16)
        (before,) = doubled_spectrum([halo[...] * started], fwd_odd)
        mixed = products(
            [before + rows_at(edge_spec_all, step, i)[...]],
            rows_at(tap_spec_all, step, i)[...],
        )
        (signal,) = finish_medium(
            mixed,
            inv_even,
            [first[0, :, part]],
            [second[1, :, part]],
            [rows_at(inputs_all, step, i)[:, part]],
            [rows_at(medium_all, step, i).at[:, part]],
        )
        signals = rows_at(signals_all, step, i)
        signals[:, part] = signal
        members = [signal] + [
            signals[:, b * window : (b + 1) * window] for b in range(1, ends.shape[0])
        ]
        sums = []
        for pair in range(step // PAIR):
            sides = end_states(members, falling[pair], pair, modes, mask)
            for side, found in enumerate(sides):
                at = pair * PAIR + side * ROWS
                leap = spread(leaps, 2 * pair + side)
                state = None
                for b, end in enumerate(found):
                    ends[b, at : at + ROWS, :] = end
                    state = end if state is None else state * leap + end
                sums.append(jnp.sum(state, axis=0, keepdims=True))
        total = rows_at(total_all, step // ROWS, i)
        total[...] = jnp.concatenate(sums, axis=0).astype(total.dtype)

    def body(section):
        pl.loop(0, share // step)(functools.partial(chunk, section))

    by_section(sec, body)


def first_call(
    place, gates, swapped, inputs, halos, rates, falling, specs, tables, medium, signals, modes
):
    share, tokens = inputs.shape
    window = halos[0].shape[1]
    lanes = ROWS * modes
    small = (share // ROWS, lanes)
    operands = [gates, swapped, inputs, *halos, rates, falling, *specs, *tables, medium, signals]
    return pl.pallas_call(
        functools.partial(first_kernel, modes, min(STEP, share)),
        out_shape=(
            jax.ShapeDtypeStruct(medium.shape, medium.dtype),
            jax.ShapeDtypeStruct(signals.shape, signals.dtype),
            jax.ShapeDtypeStruct((tokens // window, share, lanes), jnp.float32),
            jax.ShapeDtypeStruct(small, jnp.bfloat16),
        ),
        in_specs=[SMEM_SPEC] * 2 + [VMEM_SPEC] * len(operands),
        out_specs=(VMEM_SPEC,) * 4,
        scratch_shapes=[pltpu.VMEM(small, jnp.float32)],
        input_output_aliases={len(operands): 0, len(operands) + 1: 1},
        name="first",
        cost_estimate=cost(share, tokens, 500),
        compiler_params=COMPILER,
    )(*place, *operands)


def within_kernel(
    step,
    signals_all,
    response_all,
    fwd_h,
    fwd_l,
    inverse,
    out_all,
):
    share, tokens = signals_all.shape
    size = fwd_h.shape[0]
    half = size // 2

    def chunk(i):
        signals = rows_at(signals_all, step, i)
        response, out = rows_at(response_all, step, i), rows_at(out_all, step, i)
        channels = step
        real, imag = response[:, :half], response[:, half:]
        parts = [slice(k * size, (k + 1) * size) for k in range(tokens // size)]
        signal = jnp.concatenate([signals[:, part] for part in parts], axis=0)
        spec = dot_f32(signal, fwd_h[...]) + dot_f32(signal, fwd_l[...])
        filtered = []
        for k in range(len(parts)):
            rows = slice(k * channels, (k + 1) * channels)
            a, b = spec[rows, :half], spec[rows, half:]
            filtered.append(
                jnp.concatenate([a * real - b * imag, a * imag + b * real], axis=1).astype(
                    jnp.bfloat16
                )
            )
        found = dot_f32(jnp.concatenate(filtered, axis=0), inverse[...])
        for k, part in enumerate(parts):
            out[:, part] = found[k * channels : (k + 1) * channels]

    pl.loop(0, share // step)(chunk)


def within_call(signals, response, tables):
    share, tokens = signals.shape
    operands = [signals, response, *tables]
    return pl.pallas_call(
        functools.partial(within_kernel, min(WITHIN_STEP, share)),
        out_shape=jax.ShapeDtypeStruct((share, tokens), jnp.float32),
        in_specs=[VMEM_SPEC] * len(operands),
        out_specs=VMEM_SPEC,
        name="within",
        cost_estimate=cost(share, tokens, 1500),
        compiler_params=COMPILER,
    )(*operands)


def output_kernel(
    count,
    modes,
    window,
    step,
    first,
    share,
    sec,
    tok,
    local_all,
    remote_all,
    within_all,
    inputs_all,
    medium_all,
    rates,
    scale_rows,
    rising_all,
    ends_all,
    *rest,
):
    arrived = rest[:count]
    (result, send, keep, leaps_all, scales_all, shares_all, starts_all, done) = rest[-8:]
    part_rows, tokens = send.shape
    base = first // step
    groups = pl.ds(first // ROWS, part_rows // ROWS)
    blocks = tokens // window
    mask = lane_mask(modes)
    slow = rates[groups, :]
    leap_all = jnp.exp(-slow * window)
    scale_all = scale_rows[groups, :] * jnp.exp(-slow)
    leaps_all[...] = leap_all
    scales_all[...] = scale_all
    shares_all[...] = scale_all / (1.0 + leap_all)
    entering = jnp.zeros_like(slow)
    for k in range(count):
        gap = tok[0] - (tok[0] ^ (k + 1))
        known = jnp.where(gap > 0, 1.0, 0.0)
        distance = (tokens * jnp.maximum(gap - 1, 0)).astype(jnp.float32)
        entering = entering + arrived[k][groups, :].astype(jnp.float32) * (
            jnp.exp(-slow * distance) * known
        )
    starts_all[...] = entering

    def chunk(section, out_all, i):
        out = rows_at(out_all, step, i)
        at_all = base + i
        gate_out = rows_at((remote_all if section == 0 else local_all).at[0], step, at_all)
        inputs = rows_at(inputs_all, step, at_all)
        gated_medium = rows_at(medium_all, step, at_all)
        within = rows_at(within_all, step, at_all)
        ends = rows_at(ends_all, step, at_all, 1)
        rising = rows_at(rising_all, step // PAIR, at_all)
        small = step // ROWS
        leaps, scales = rows_at(leaps_all, small, i), rows_at(scales_all, small, i)
        shares, starts = rows_at(shares_all, small, i), rows_at(starts_all, small, i)
        channels = step
        for pair in range(channels // PAIR):
            rows = slice(pair * PAIR, (pair + 1) * PAIR)
            sides = []
            for side in range(2):
                group = 2 * pair + side
                leap, scale = spread(leaps, group), spread(scales, group)
                share = spread(shares, group)
                state = jnp.where(mask, spread(starts, group), 0.0)
                at = pair * PAIR + side * ROWS
                lefts = []
                for b in range(blocks):
                    end = ends[b, at : at + ROWS, :]
                    lefts.append(state * scale + end * share)
                    state = state * leap + end
                sides.append(lefts)
            left = jnp.concatenate(
                [two_sided(upper, lower) for upper, lower in zip(*sides)], axis=0
            ).astype(jnp.bfloat16)
            across = dot_turned(left, rising[pair])
            for b in range(blocks):
                part = slice(b * window, (b + 1) * window)
                stream = inputs[rows, part].astype(jnp.float32) + gated_medium[
                    rows, part
                ].astype(jnp.float32)
                long_out = within[rows, part] + across[b * PAIR : (b + 1) * PAIR]
                gate = gate_out[rows, part].astype(jnp.float32)
                out[rows, part] = (stream + gate * long_out).astype(jnp.bfloat16)

    def body(section):
        target = result.at[0, pl.ds(section * share + first, part_rows), :]
        source = medium_all.at[pl.ds(first, part_rows), :]
        copy = pltpu.make_async_copy(source, send if section else target, done)
        copy.start()
        pl.loop(0, part_rows // step)(
            functools.partial(chunk, section, keep if section else send)
        )
        copy.wait()

    by_section(sec, body)


def output_call(
    place, half, gates, swapped, within, inputs, medium, rates, scales, rising, ends, arrived, before
):
    share, tokens = medium.shape
    lanes = rates.shape[1]
    window = rising.shape[1]
    part_rows = share // HALVES
    step = min(STEP, part_rows)
    small = (part_rows // ROWS, lanes)
    operands = [gates, swapped, within, inputs, medium, rates, scales, rising, ends, *arrived]
    result = jax.ShapeDtypeStruct((1, 2 * share, tokens), jnp.bfloat16)
    chained = [] if before is None else [before]
    return pl.pallas_call(
        functools.partial(
            output_kernel,
            len(arrived),
            lanes // ROWS,
            window,
            step,
            half * part_rows,
            share,
        ),
        out_shape=(result,) + (jax.ShapeDtypeStruct((part_rows, tokens), jnp.bfloat16),) * 2,
        in_specs=[SMEM_SPEC] * 2 + [VMEM_SPEC] * len(operands) + [ANY_SPEC] * len(chained),
        out_specs=(ANY_SPEC, VMEM_SPEC, VMEM_SPEC),
        scratch_shapes=[pltpu.VMEM(small, jnp.float32)] * 4
        + [pltpu.SemaphoreType.DMA],
        input_output_aliases={2 + len(operands): 0} if chained else {},
        name="output",
        cost_estimate=cost(part_rows, tokens, 1500),
        compiler_params=COMPILER,
    )(*place, *operands, *chained)


def place_kernel(first, share, sec, tok, before, received, keep, out, done):
    rows = received.shape[0]

    def target(section):
        return out.at[0, pl.ds(pl.multiple_of(section * share + first, rows), rows), :]

    foreign = pltpu.make_async_copy(received, target(1 - sec[0]), done.at[0])
    foreign.start()

    @pl.when(sec[0] == 1)
    def _():
        own = pltpu.make_async_copy(keep, target(1), done.at[1])
        own.start()
        own.wait()

    foreign.wait()


def place_call(place, half, before, received, keep):
    rows, tokens = received.shape
    return pl.pallas_call(
        functools.partial(place_kernel, half * rows, before.shape[1] // 2),
        out_shape=jax.ShapeDtypeStruct(before.shape, before.dtype),
        in_specs=[SMEM_SPEC] * 2 + [ANY_SPEC, VMEM_SPEC, VMEM_SPEC],
        out_specs=ANY_SPEC,
        scratch_shapes=[pltpu.SemaphoreType.DMA((2,))],
        input_output_aliases={2: 0},
        name="placing",
        cost_estimate=cost(rows, tokens, 2),
        compiler_params=COMPILER,
    )(*place, before, received, keep)


def lend_kernel(sec, tok, gates, inputs, lent, low, high, gate_tail, input_tail, arrival):
    share, window = low.shape
    tokens = inputs.shape[1]
    tail = pl.ds(tokens - window, window)
    other = pl.ds(pl.multiple_of((1 - sec[0]) * share, share), share)
    copies = [
        pltpu.make_async_copy(source, target, arrival.at[k])
        for k, (source, target) in enumerate(
            [
                (gates.at[0, 1, :, tail], gate_tail),
                (inputs.at[:, tail], input_tail),
                (gates.at[0, :, other, :], lent),
            ]
        )
    ]
    for copy in copies:
        copy.start()
    copies[0].wait()
    copies[1].wait()
    low[...] = gate_tail[:share, :] * input_tail[:share, :]
    high[...] = gate_tail[share:, :] * input_tail[share:, :]
    copies[2].wait()


def lend_call(place, gate_streams, inputs, window, share):
    channels, tokens = inputs.shape
    edge = jax.ShapeDtypeStruct((share, window), jnp.bfloat16)
    return pl.pallas_call(
        lend_kernel,
        out_shape=(jax.ShapeDtypeStruct((2, share, tokens), jnp.bfloat16), edge, edge),
        in_specs=[SMEM_SPEC] * 2 + [ANY_SPEC] * 2,
        out_specs=(VMEM_SPEC,) * 3,
        scratch_shapes=[pltpu.VMEM((channels, window), jnp.bfloat16)] * 2
        + [pltpu.SemaphoreType.DMA((3,))],
        name="lend",
        cost_estimate=cost(share, tokens, 2),
        compiler_params=COMPILER,
    )(*place, *parked(gate_streams, inputs))


def ring(value, axis, by):
    peers = lax.axis_size(axis)
    return lax.ppermute(value, axis, [(i, (i + by) % peers) for i in range(peers)])


def met(value, by):
    peers = lax.axis_size("tok")
    return lax.ppermute(value, "tok", [(i, i ^ by) for i in range(peers)])


def edge_to(value, section):
    peers = lax.axis_size("tok")
    pairs = [(i, section * peers + (i + 1) % peers) for i in range(peers)]
    pairs += [(peers + i, (1 - section) * peers + i) for i in range(peers)]
    return lax.ppermute(value, ("section", "tok"), pairs)


def on_device(gate_streams, inputs, medium_taps, residues, decay_rates):
    channels, tokens = inputs.shape
    share = channels // 2
    window = medium_taps.shape[1]
    modes = decay_rates.shape[1]
    section = lax.axis_index("section")
    place = tuple(
        lax.axis_index(axis).astype(jnp.int32).reshape(1) for axis in ("section", "tok")
    )
    lent, *edges = lend_call(place, gate_streams, inputs, window, share)
    halos = [edge_to(edges[s], s) for s in range(2)]
    swapped = ring(lent, "section", 1)
    forward, inverse = fourier_tables(window)
    turned, back, _ = turned_tables(window)
    tables = [*forward, *inverse, *split_pair(turned), split_pair(back)[0]]
    built, own, tables = response_call(
        place,
        decay_rates.T,
        residues.T,
        gate_streams,
        inputs,
        medium_taps,
        tables,
        window,
        share,
    )
    response, rates, scales, rising, falling = built
    gates, inputs, taps = own
    medium, signals, *specs = later_call(place, gates, swapped, inputs, taps, tables[:4])
    medium, signals, ends, total = first_call(
        place,
        gates,
        swapped,
        inputs,
        halos,
        rates,
        falling,
        specs,
        tables[1:3],
        medium,
        signals,
        modes,
    )
    arrived = [met(total, by) for by in range(1, lax.axis_size("tok"))]
    within = within_call(signals, response, tables[4:])
    result, waiting = None, []
    for half in range(HALVES):
        result, send, keep = output_call(
            place,
            half,
            gates,
            swapped,
            within,
            inputs,
            medium,
            rates,
            scales,
            rising,
            ends,
            arrived,
            result,
        )
        waiting.append((ring(send, "section", 1), keep))
    for half, (received, keep) in enumerate(waiting):
        result = place_call(place, half, result, received, keep)
    return result


def solution(mesh):
    placed = (
        P("section", None, "chan", "tok"),
        P("chan", "tok"),
        P("chan", None),
        P("chan", None),
        P("chan", None),
    )
    return jax.shard_map(
        on_device,
        mesh=mesh,
        in_specs=placed,
        out_specs=P("section", "chan", "tok"),
        check_vma=False,
    )
```

```python
import functools

import jax
import jax.numpy as jnp
import numpy as np
from jax import lax
from jax.experimental import pallas as pl
from jax.experimental.pallas import tpu as pltpu
from jax.sharding import PartitionSpec as P

ROWS = 8


def split_pair(matrix):
    high = jnp.asarray(matrix, jnp.float32).astype(jnp.bfloat16)
    low = (jnp.asarray(matrix, jnp.float32) - high.astype(jnp.float32)).astype(jnp.bfloat16)
    return high, low


def stacked(matrix, axis):
    return jnp.concatenate(split_pair(matrix), axis=axis)


def fourier_tables(window):
    size = 2 * window
    time = np.arange(window)[:, None]
    freq = np.arange(window)[None, :]
    angle = 2.0 * np.pi * ((time * freq) % size) / size
    sign = np.where(freq % 2 == 0, 1.0, -1.0)
    nyquist = np.where(time % 2 == 0, 1.0, -1.0)
    weight = np.where(freq == 0, 1.0, 2.0) / size
    forward, inverse = [], []
    for odd in range(2):
        flip = sign if odd else np.ones_like(sign)
        real = np.cos(angle) * flip
        imag = -np.sin(angle) * flip
        imag[:, :1] = nyquist
        forward.append(stacked(np.concatenate([real, imag], axis=1), 0))
        back_real = np.cos(angle) * weight * flip
        back_imag = -np.sin(angle) * weight * flip
        back_imag[:, :1] = nyquist / size
        inverse.append(stacked(np.concatenate([back_real.T, back_imag.T], axis=0), 1))
    return forward, inverse


def turned_tables(window):
    half = window // 2
    time = np.arange(window)[:, None]
    freq = 2 * np.arange(half)[None, :] + 1
    angle = np.pi * ((time * freq) % (2 * window)) / window
    real, imag = np.cos(angle), -np.sin(angle)
    zero = np.zeros_like(real)
    forward = np.concatenate(
        [
            np.concatenate([real, zero, imag, zero], axis=1),
            np.concatenate([zero, real, zero, imag], axis=1),
        ],
        axis=0,
    )
    inverse = forward.T * (2.0 / window)
    doubled = np.concatenate([real, real, imag, imag], axis=1)
    return forward, inverse, doubled


PAIR = 16
STEP = 512
HALVES = 2
COMPILER = pltpu.CompilerParams(vmem_limit_bytes=16 << 20)


def parked(*arrays):
    return [pltpu.with_memory_space_constraint(a, pltpu.HBM) for a in arrays]


def cost(share, tokens, work):
    size = share * tokens
    return pl.CostEstimate(
        flops=size * work, bytes_accessed=size * 12, transcendentals=size // 64
    )


def dot_f32(left, right):
    return jnp.dot(left, right, preferred_element_type=jnp.float32)


def dot_turned(left, right):
    return lax.dot_general(
        left, right, (((1,), (1,)), ((), ())), preferred_element_type=jnp.float32
    )


VMEM_SPEC = pl.BlockSpec(memory_space=pltpu.VMEM)
SMEM_SPEC = pl.BlockSpec(memory_space=pltpu.SMEM)
ANY_SPEC = pl.BlockSpec(memory_space=pl.ANY)


def rows_at(ref, step, i, axis=0):
    start = i * step
    if not isinstance(i, int):
        start = pl.multiple_of(start, step)
    return ref.at[(slice(None),) * axis + (pl.ds(start, step),)]


def both_gates(local, remote, section, step, i):
    mine, other = rows_at(local, step, i, 1), rows_at(remote, step, i, 1)
    return (mine, other) if section == 0 else (other, mine)


def by_section(sec, body):
    for section in range(2):
        pl.when(sec[0] == section)(functools.partial(body, section))


def lane_mask(modes):
    shape = (ROWS, ROWS * modes)
    lane = lax.broadcasted_iota(jnp.int32, shape, 1)
    return lane // modes == lax.broadcasted_iota(jnp.int32, shape, 0)


def spread(ref, group):
    return jnp.broadcast_to(ref[group : group + 1, :], (ROWS, ref.shape[1]))


def powers(slow, hop, window, first, falling):
    row = lax.broadcasted_iota(jnp.int32, slow.shape, 0).astype(jnp.float32)
    tiles = [jnp.exp(-slow * (first + (ROWS - 1 - row if falling else row)))]
    while len(tiles) < window // ROWS:
        tiles = tiles + [tile * hop for tile in tiles]
        hop = hop * hop
    if falling:
        tiles = tiles[::-1]
    return jnp.concatenate(tiles, axis=0).astype(jnp.bfloat16)


def both_powers(rates, hops, pair, window, falling):
    sides = [
        powers(spread(rates, g), spread(hops, g), window, 0.0, falling)
        for g in (2 * pair, 2 * pair + 1)
    ]
    return jnp.concatenate(sides, axis=1)


def two_sided(upper, lower):
    zero = jnp.zeros_like(upper)
    return jnp.concatenate(
        [
            jnp.concatenate([upper, zero], axis=1),
            jnp.concatenate([zero, lower], axis=1),
        ],
        axis=0,
    )


def scale_of(residues, slow):
    return residues * jnp.sqrt(1.0 - jnp.exp(-2.0 * slow))


def in_rows(ref, tall):
    modes, channels = ref.shape
    tall[...] = ref[...].T
    count = channels // ROWS
    return jnp.concatenate(
        [tall[pl.ds(c, count, stride=ROWS), :] for c in range(ROWS)], axis=1
    )


def response_kernel(count, window, sec, tok, rates, residues, *rest):
    gates, inputs, taps = rest[:3]
    tables = rest[3 : 3 + count]
    out, rate_rows, scale_rows, rising, falling = rest[3 + count : 8 + count]
    own_gates, own_inputs, own_taps = rest[8 + count : 11 + count]
    own_tables = rest[11 + count : 11 + 2 * count]
    tall, hops, scales, arrival = rest[11 + 2 * count :]
    share = out.shape[0]
    step = tall.shape[0]
    modes = rates.shape[0]
    first = pl.multiple_of(sec[0] * share, share)
    mine = pl.ds(first, share)
    pairs = [(gates.at[0, :, mine, :], own_gates)]
    pairs += [(inputs.at[mine, :], own_inputs), (taps.at[mine, :], own_taps)]
    pairs += list(zip(tables, own_tables))
    copies = [
        pltpu.make_async_copy(source, target, arrival.at[k])
        for k, (source, target) in enumerate(pairs)
    ]
    for copy in copies:
        copy.start()
    mask = lane_mask(modes)

    @pl.loop(0, share // step)
    def _(i):
        lanes = pl.ds(pl.multiple_of(first + i * step, step), step)
        slow = in_rows(rates.at[:, lanes], tall)
        scale = scale_of(in_rows(residues.at[:, lanes], tall), slow)
        small = step // ROWS
        own_rates = rows_at(rate_rows, small, i)
        own_rates[...] = slow
        rows_at(scale_rows, small, i)[...] = scale
        hops[...] = jnp.exp(-slow * ROWS)
        scales[...] = scale / (1.0 + jnp.exp(-slow * window))
        up, down = rows_at(rising, step // PAIR, i), rows_at(falling, step // PAIR, i)
        own_out = rows_at(out, step, i)
        for pair in range(step // PAIR):
            both = two_sided(
                jnp.where(mask, spread(scales, 2 * pair), 0.0),
                jnp.where(mask, spread(scales, 2 * pair + 1), 0.0),
            )
            high = both.astype(jnp.bfloat16).astype(jnp.float32)
            both = jnp.concatenate([high, both - high], axis=0).astype(jnp.bfloat16)
            table = both_powers(own_rates, hops, pair, window, False)
            up[pair] = table
            down[pair] = both_powers(own_rates, hops, pair, window, True)
            found = dot_turned(both, table)
            out_rows = pl.ds(pair * PAIR, PAIR)
            own_out[out_rows, :] = found[:PAIR] + found[PAIR:]

    for copy in copies:
        copy.wait()


def response_call(place, rates, residues, gates, inputs, taps, tables, window, share):
    tokens = inputs.shape[1]
    step = min(STEP, share)
    modes = rates.shape[0]
    lanes = ROWS * modes
    small = (step // ROWS, lanes)
    shape = lambda dims, kind=jnp.float32: jax.ShapeDtypeStruct(dims, kind)
    power_shape = shape((share // PAIR, window, 2 * lanes), jnp.bfloat16)
    outs = [shape((share, window))] + [shape((share // ROWS, lanes))] * 2
    outs += [power_shape] * 2
    outs += [
        shape((2, share, tokens), gates.dtype),
        shape((share, tokens), inputs.dtype),
        shape((share, window), taps.dtype),
    ]
    outs += [shape(t.shape, t.dtype) for t in tables]
    staged = 3 + len(tables)
    found = pl.pallas_call(
        functools.partial(response_kernel, len(tables), window),
        out_shape=tuple(outs),
        in_specs=[SMEM_SPEC] * 2 + [VMEM_SPEC] * 2 + [ANY_SPEC] * staged,
        out_specs=(VMEM_SPEC,) * len(outs),
        scratch_shapes=[
            pltpu.VMEM((step, modes), jnp.float32),
            pltpu.VMEM(small, jnp.float32),
            pltpu.VMEM(small, jnp.float32),
            pltpu.SemaphoreType.DMA((staged,)),
        ],
        name="response",
        cost_estimate=cost(share, 4 * window, 900),
        compiler_params=COMPILER,
    )(*place, rates, residues, *parked(gates, inputs, taps, *tables))
    return found[:5], found[5:8], found[8:]


def products(members, tap_spec):
    window = tap_spec.shape[1] // 2
    real, packed = tap_spec[:, :window], tap_spec[:, window:]
    lane = lax.broadcasted_iota(jnp.int32, real.shape, 1)
    real_b = jnp.where(lane == 0, packed, real)
    imag = jnp.where(lane == 0, 0.0, packed)
    found = []
    for mixed in members:
        a, b = mixed[:, :window], mixed[:, window:]
        found.append(
            jnp.concatenate([a * real - b * imag, a * imag + b * real_b], axis=1).astype(
                jnp.bfloat16
            )
        )
    return found


def doubled_spectrum(members, table):
    rows = jnp.concatenate(members, axis=0)
    found = dot_f32(jnp.concatenate([rows, rows], axis=1), table[...])
    size = members[0].shape[0]
    return [found[k * size : (k + 1) * size] for k in range(len(members))]


def finish_medium(members, table, gates_out, gates_in, streams, targets):
    found = dot_f32(jnp.concatenate(members, axis=0), table[...])
    size, window = streams[0].shape
    signals = []
    for k in range(len(members)):
        rows = slice(k * size, (k + 1) * size)
        medium = found[rows, :window] + found[rows, window:]
        gated = (gates_out[k].astype(jnp.float32) * medium).astype(jnp.bfloat16)
        targets[k][...] = gated
        stream = streams[k].astype(jnp.float32) + gated.astype(jnp.float32)
        signals.append((gates_in[k].astype(jnp.float32) * stream).astype(jnp.bfloat16))
    return signals


def end_states(signals, powers_of_pair, pair, modes, mask):
    rows = slice(pair * PAIR, (pair + 1) * PAIR)
    lanes = ROWS * modes
    left = jnp.concatenate([signal[rows] for signal in signals], axis=0)
    found = dot_f32(left, powers_of_pair)
    sides = []
    for side in range(2):
        tops = [k * PAIR + side * ROWS for k in range(len(signals))]
        sides.append(
            [
                jnp.where(mask, found[top : top + ROWS, side * lanes : (side + 1) * lanes], 0.0)
                for top in tops
            ]
        )
    return sides


def later_kernel(
    step,
    sec,
    tok,
    local_all,
    swapped,
    inputs_all,
    taps_all,
    fwd_even,
    fwd_odd,
    inv_even,
    inv_odd,
    medium_all,
    signals_all,
    tap_spec_all,
    edge_spec_all,
    remote_all,
    arrival,
):
    share, tokens = inputs_all.shape
    window = taps_all.shape[1]
    blocks = tokens // window
    parts = [slice(b * window, (b + 1) * window) for b in range(blocks)]

    def fetch(i):
        source = pl.ds(pl.multiple_of(sec[0] * share + i * step, step), step)
        return pltpu.make_async_copy(
            swapped.at[:, source, :], rows_at(remote_all, step, i, 1), arrival.at[i]
        )

    for i in range(share // step):
        fetch(i).start()

    def chunk(section, i):
        fetch(i).wait()
        first, second = both_gates(local_all, remote_all, section, step, i)
        inputs = rows_at(inputs_all, step, i)
        medium_out, signals = rows_at(medium_all, step, i), rows_at(signals_all, step, i)
        sources = [first[1, :, part] * inputs[:, part] for part in parts]
        tap_rows = rows_at(taps_all, step, i)[...]
        tap_spec, *even = doubled_spectrum([tap_rows] + sources[0::2], fwd_even)
        odd = doubled_spectrum(sources[1::2], fwd_odd)
        in_order = [None] * blocks
        in_order[0::2] = even
        in_order[1::2] = odd
        rows_at(tap_spec_all, step, i)[...] = tap_spec
        rows_at(edge_spec_all, step, i)[...] = in_order[0]
        mixed = products([in_order[b - 1] + in_order[b] for b in range(1, blocks)], tap_spec)
        for parity, table in enumerate((inv_even, inv_odd)):
            chosen = [b for b in range(1, blocks) if b % 2 == parity]
            if not chosen:
                continue
            found = finish_medium(
                [mixed[b - 1] for b in chosen],
                table,
                [first[0, :, parts[b]] for b in chosen],
                [second[1, :, parts[b]] for b in chosen],
                [inputs[:, parts[b]] for b in chosen],
                [medium_out.at[:, parts[b]] for b in chosen],
            )
            for b, signal in zip(chosen, found):
                signals[:, parts[b]] = signal

    def body(section):
        pl.loop(0, share // step)(functools.partial(chunk, section))

    by_section(sec, body)


def later_call(place, gates, swapped, inputs, taps, tables):
    share, tokens = inputs.shape
    window = taps.shape[1]
    operands = [gates, *parked(swapped), inputs, taps, *tables]
    spec = jax.ShapeDtypeStruct((share, 2 * window), jnp.float32)
    wide = jax.ShapeDtypeStruct((share, tokens), jnp.bfloat16)
    return pl.pallas_call(
        functools.partial(later_kernel, min(STEP, share)),
        out_shape=(wide, wide, spec, spec, jax.ShapeDtypeStruct(gates.shape, gates.dtype)),
        in_specs=[SMEM_SPEC] * 2 + [VMEM_SPEC, ANY_SPEC] + [VMEM_SPEC] * (len(operands) - 2),
        out_specs=(VMEM_SPEC,) * 5,
        scratch_shapes=[pltpu.SemaphoreType.DMA((share // min(STEP, share),))],
        name="later",
        cost_estimate=cost(share, tokens, 1500),
        compiler_params=COMPILER,
    )(*place, *operands)


def first_kernel(
    modes,
    step,
    sec,
    tok,
    local_all,
    remote_all,
    inputs_all,
    halo_low,
    halo_high,
    rates,
    falling_all,
    tap_spec_all,
    edge_spec_all,
    fwd_odd,
    inv_even,
    medium_before,
    signals_before,
    medium_all,
    signals_all,
    ends_all,
    total_all,
    leaps_all,
):
    share = inputs_all.shape[0]
    window = tap_spec_all.shape[1] // 2
    part = slice(0, window)
    mask = lane_mask(modes)
    leaps_all[...] = jnp.exp(-rates[...] * window)

    def chunk(section, i):
        first, second = both_gates(local_all, remote_all, section, step, i)
        halo = rows_at(halo_low if section == 0 else halo_high, step, i)
        leaps = rows_at(leaps_all, step // ROWS, i)
        falling = rows_at(falling_all, step // PAIR, i)
        ends = rows_at(ends_all, step, i, 1)
        started = jnp.where(tok[0] > 0, 1.0, 0.0).astype(jnp.bfloat16)
        (before,) = doubled_spectrum([halo[...] * started], fwd_odd)
        mixed = products(
            [before + rows_at(edge_spec_all, step, i)[...]],
            rows_at(tap_spec_all, step, i)[...],
        )
        (signal,) = finish_medium(
            mixed,
            inv_even,
            [first[0, :, part]],
            [second[1, :, part]],
            [rows_at(inputs_all, step, i)[:, part]],
            [rows_at(medium_all, step, i).at[:, part]],
        )
        signals = rows_at(signals_all, step, i)
        signals[:, part] = signal
        members = [signal] + [
            signals[:, b * window : (b + 1) * window] for b in range(1, ends.shape[0])
        ]
        sums = []
        for pair in range(step // PAIR):
            sides = end_states(members, falling[pair], pair, modes, mask)
            for side, found in enumerate(sides):
                at = pair * PAIR + side * ROWS
                leap = spread(leaps, 2 * pair + side)
                state = None
                for b, end in enumerate(found):
                    ends[b, at : at + ROWS, :] = end
                    state = end if state is None else state * leap + end
                sums.append(jnp.sum(state, axis=0, keepdims=True))
        total = rows_at(total_all, step // ROWS, i)
        total[...] = jnp.concatenate(sums, axis=0).astype(total.dtype)

    def body(section):
        pl.loop(0, share // step)(functools.partial(chunk, section))

    by_section(sec, body)


def first_call(
    place, gates, swapped, inputs, halos, rates, falling, specs, tables, medium, signals, modes
):
    share, tokens = inputs.shape
    window = halos[0].shape[1]
    lanes = ROWS * modes
    small = (share // ROWS, lanes)
    operands = [gates, swapped, inputs, *halos, rates, falling, *specs, *tables, medium, signals]
    return pl.pallas_call(
        functools.partial(first_kernel, modes, min(2 * STEP, share)),
        out_shape=(
            jax.ShapeDtypeStruct(medium.shape, medium.dtype),
            jax.ShapeDtypeStruct(signals.shape, signals.dtype),
            jax.ShapeDtypeStruct((tokens // window, share, lanes), jnp.float32),
            jax.ShapeDtypeStruct(small, jnp.bfloat16),
        ),
        in_specs=[SMEM_SPEC] * 2 + [VMEM_SPEC] * len(operands),
        out_specs=(VMEM_SPEC,) * 4,
        scratch_shapes=[pltpu.VMEM(small, jnp.float32)],
        input_output_aliases={len(operands): 0, len(operands) + 1: 1},
        name="first",
        cost_estimate=cost(share, tokens, 500),
        compiler_params=COMPILER,
    )(*place, *operands)


def within_kernel(
    step,
    signals_all,
    response_all,
    fwd_h,
    fwd_l,
    inverse,
    table_h,
    table_l,
    out_all,
):
    share, tokens = signals_all.shape
    size = fwd_h.shape[0]
    half = size // 2

    def chunk(i):
        signals = rows_at(signals_all, step, i)
        taps, out = rows_at(response_all, step, i)[...], rows_at(out_all, step, i)
        high = taps.astype(jnp.bfloat16)
        low = (taps - high.astype(jnp.float32)).astype(jnp.bfloat16)
        response = dot_f32(jnp.concatenate([high, low], axis=1), table_h[...]) + dot_f32(
            high, table_l[...]
        )
        channels = step
        real, imag = response[:, :half], response[:, half:]
        parts = [slice(k * size, (k + 1) * size) for k in range(tokens // size)]
        signal = jnp.concatenate([signals[:, part] for part in parts], axis=0)
        spec = dot_f32(signal, fwd_h[...]) + dot_f32(signal, fwd_l[...])
        filtered = []
        for k in range(len(parts)):
            rows = slice(k * channels, (k + 1) * channels)
            a, b = spec[rows, :half], spec[rows, half:]
            filtered.append(
                jnp.concatenate([a * real - b * imag, a * imag + b * real], axis=1).astype(
                    jnp.bfloat16
                )
            )
        found = dot_f32(jnp.concatenate(filtered, axis=0), inverse[...])
        for k, part in enumerate(parts):
            out[:, part] = found[k * channels : (k + 1) * channels]

    pl.loop(0, share // step)(chunk)


def within_call(signals, response, tables):
    share, tokens = signals.shape
    operands = [signals, response, *tables]
    return pl.pallas_call(
        functools.partial(within_kernel, min(2 * STEP, share)),
        out_shape=jax.ShapeDtypeStruct((share, tokens), jnp.float32),
        in_specs=[VMEM_SPEC] * len(operands),
        out_specs=VMEM_SPEC,
        name="within",
        cost_estimate=cost(share, tokens, 1500),
        compiler_params=COMPILER,
    )(*operands)


def output_kernel(
    count,
    modes,
    window,
    step,
    first,
    share,
    sec,
    tok,
    local_all,
    remote_all,
    within_all,
    inputs_all,
    medium_all,
    rates,
    scale_rows,
    rising_all,
    ends_all,
    *rest,
):
    arrived = rest[:count]
    (result, send, keep, leaps_all, scales_all, shares_all, starts_all, done) = rest[-8:]
    part_rows, tokens = send.shape
    base = first // step
    groups = pl.ds(first // ROWS, part_rows // ROWS)
    blocks = tokens // window
    mask = lane_mask(modes)
    slow = rates[groups, :]
    leap_all = jnp.exp(-slow * window)
    scale_all = scale_rows[groups, :] * jnp.exp(-slow)
    leaps_all[...] = leap_all
    scales_all[...] = scale_all
    shares_all[...] = scale_all / (1.0 + leap_all)
    entering = jnp.zeros_like(slow)
    for k in range(count):
        gap = tok[0] - (tok[0] ^ (k + 1))
        known = jnp.where(gap > 0, 1.0, 0.0)
        distance = (tokens * jnp.maximum(gap - 1, 0)).astype(jnp.float32)
        entering = entering + arrived[k][groups, :].astype(jnp.float32) * (
            jnp.exp(-slow * distance) * known
        )
    starts_all[...] = entering

    def chunk(section, out_all, i):
        out = rows_at(out_all, step, i)
        at_all = base + i
        gate_out = both_gates(local_all, remote_all, section, step, at_all)[1].at[0]
        inputs = rows_at(inputs_all, step, at_all)
        gated_medium = rows_at(medium_all, step, at_all)
        within = rows_at(within_all, step, at_all)
        ends = rows_at(ends_all, step, at_all, 1)
        rising = rows_at(rising_all, step // PAIR, at_all)
        small = step // ROWS
        leaps, scales = rows_at(leaps_all, small, i), rows_at(scales_all, small, i)
        shares, starts = rows_at(shares_all, small, i), rows_at(starts_all, small, i)
        channels = step
        for pair in range(channels // PAIR):
            rows = slice(pair * PAIR, (pair + 1) * PAIR)
            sides = []
            for side in range(2):
                group = 2 * pair + side
                leap, scale = spread(leaps, group), spread(scales, group)
                portion = spread(shares, group)
                state = jnp.where(mask, spread(starts, group), 0.0)
                at = pair * PAIR + side * ROWS
                lefts = []
                for b in range(blocks):
                    end = ends[b, at : at + ROWS, :]
                    lefts.append(state * scale + end * portion)
                    state = state * leap + end
                sides.append(lefts)
            left = jnp.concatenate(
                [two_sided(upper, lower) for upper, lower in zip(*sides)], axis=0
            ).astype(jnp.bfloat16)
            across = dot_turned(left, rising[pair])
            for b in range(blocks):
                part = slice(b * window, (b + 1) * window)
                stream = inputs[rows, part].astype(jnp.float32) + gated_medium[
                    rows, part
                ].astype(jnp.float32)
                long_out = within[rows, part] + across[b * PAIR : (b + 1) * PAIR]
                gate = gate_out[rows, part].astype(jnp.float32)
                out[rows, part] = (stream + gate * long_out).astype(jnp.bfloat16)

    def body(section):
        target = result.at[0, pl.ds(section * share + first, part_rows), :]
        source = medium_all.at[pl.ds(first, part_rows), :]
        copy = pltpu.make_async_copy(source, send if section else target, done)
        copy.start()
        pl.loop(0, part_rows // step)(
            functools.partial(chunk, section, keep if section else send)
        )
        copy.wait()

    by_section(sec, body)


def output_call(
    place, half, gates, swapped, within, inputs, medium, rates, scales, rising, ends, arrived, before
):
    share, tokens = medium.shape
    lanes = rates.shape[1]
    window = rising.shape[1]
    part_rows = share // HALVES
    step = min(STEP, part_rows)
    small = (part_rows // ROWS, lanes)
    operands = [gates, swapped, within, inputs, medium, rates, scales, rising, ends, *arrived]
    result = jax.ShapeDtypeStruct((1, 2 * share, tokens), jnp.bfloat16)
    chained = [] if before is None else [before]
    return pl.pallas_call(
        functools.partial(
            output_kernel,
            len(arrived),
            lanes // ROWS,
            window,
            step,
            half * part_rows,
            share,
        ),
        out_shape=(result,) + (jax.ShapeDtypeStruct((part_rows, tokens), jnp.bfloat16),) * 2,
        in_specs=[SMEM_SPEC] * 2 + [VMEM_SPEC] * len(operands) + [ANY_SPEC] * len(chained),
        out_specs=(ANY_SPEC, VMEM_SPEC, VMEM_SPEC),
        scratch_shapes=[pltpu.VMEM(small, jnp.float32)] * 4
        + [pltpu.SemaphoreType.DMA],
        input_output_aliases={2 + len(operands): 0} if chained else {},
        name="output",
        cost_estimate=cost(part_rows, tokens, 1500),
        compiler_params=COMPILER,
    )(*place, *operands, *chained)


def place_kernel(first, share, sec, tok, before, received, keep, out, done):
    rows = received.shape[0]

    def target(section):
        return out.at[0, pl.ds(pl.multiple_of(section * share + first, rows), rows), :]

    foreign = pltpu.make_async_copy(received, target(1 - sec[0]), done.at[0])
    foreign.start()

    @pl.when(sec[0] == 1)
    def _():
        own = pltpu.make_async_copy(keep, target(1), done.at[1])
        own.start()
        own.wait()

    foreign.wait()


def place_call(place, half, before, received, keep):
    rows, tokens = received.shape
    return pl.pallas_call(
        functools.partial(place_kernel, half * rows, before.shape[1] // 2),
        out_shape=jax.ShapeDtypeStruct(before.shape, before.dtype),
        in_specs=[SMEM_SPEC] * 2 + [ANY_SPEC, VMEM_SPEC, VMEM_SPEC],
        out_specs=ANY_SPEC,
        scratch_shapes=[pltpu.SemaphoreType.DMA((2,))],
        input_output_aliases={2: 0},
        name="placing",
        cost_estimate=cost(rows, tokens, 2),
        compiler_params=COMPILER,
    )(*place, before, received, keep)


def edge_kernel(gates, inputs, low, high, gate_tail, input_tail, arrival):
    share, window = low.shape
    tail = pl.ds(inputs.shape[1] - window, window)
    pairs = [(gates.at[0, 1, :, tail], gate_tail), (inputs.at[:, tail], input_tail)]
    copies = [
        pltpu.make_async_copy(source, target, arrival.at[k])
        for k, (source, target) in enumerate(pairs)
    ]
    for copy in copies:
        copy.start()
    for copy in copies:
        copy.wait()
    low[...] = gate_tail[:share, :] * input_tail[:share, :]
    high[...] = gate_tail[share:, :] * input_tail[share:, :]


def edge_call(gate_streams, inputs, window, share):
    channels, tokens = inputs.shape
    edge = jax.ShapeDtypeStruct((share, window), jnp.bfloat16)
    return pl.pallas_call(
        edge_kernel,
        out_shape=(edge, edge),
        in_specs=[ANY_SPEC] * 2,
        out_specs=(VMEM_SPEC,) * 2,
        scratch_shapes=[pltpu.VMEM((channels, window), jnp.bfloat16)] * 2
        + [pltpu.SemaphoreType.DMA((2,))],
        name="edge",
        cost_estimate=cost(share, tokens, 2),
        compiler_params=COMPILER,
    )(*parked(gate_streams, inputs))


def ring(value, axis, by):
    peers = lax.axis_size(axis)
    return lax.ppermute(value, axis, [(i, (i + by) % peers) for i in range(peers)])


def met(value, by):
    peers = lax.axis_size("tok")
    return lax.ppermute(value, "tok", [(i, i ^ by) for i in range(peers)])


def edge_to(value, section):
    peers = lax.axis_size("tok")
    pairs = [(i, section * peers + (i + 1) % peers) for i in range(peers)]
    pairs += [(peers + i, (1 - section) * peers + i) for i in range(peers)]
    return lax.ppermute(value, ("section", "tok"), pairs)


def on_device(gate_streams, inputs, medium_taps, residues, decay_rates):
    channels, tokens = inputs.shape
    share = channels // 2
    window = medium_taps.shape[1]
    modes = decay_rates.shape[1]
    section = lax.axis_index("section")
    place = tuple(
        lax.axis_index(axis).astype(jnp.int32).reshape(1) for axis in ("section", "tok")
    )
    edges = edge_call(gate_streams, inputs, window, share)
    halos = [edge_to(edges[s], s) for s in range(2)]
    swapped = ring(gate_streams[0], "section", 1)
    forward, inverse = fourier_tables(window)
    turned, back, doubled = turned_tables(window)
    tables = [*forward, *inverse, *split_pair(turned), split_pair(back)[0]]
    high, low = split_pair(doubled)
    tables += [jnp.concatenate([high, high], axis=0), low]
    built, own, tables = response_call(
        place,
        decay_rates.T,
        residues.T,
        gate_streams,
        inputs,
        medium_taps,
        tables,
        window,
        share,
    )
    response, rates, scales, rising, falling = built
    gates, inputs, taps = own
    medium, signals, *specs, remote = later_call(
        place, gates, swapped, inputs, taps, tables[:4]
    )
    medium, signals, ends, total = first_call(
        place,
        gates,
        remote,
        inputs,
        halos,
        rates,
        falling,
        specs,
        tables[1:3],
        medium,
        signals,
        modes,
    )
    arrived = [met(total, by) for by in range(1, lax.axis_size("tok"))]
    within = within_call(signals, response, tables[4:])
    result, waiting = None, []
    for half in range(HALVES):
        result, send, keep = output_call(
            place,
            half,
            gates,
            remote,
            within,
            inputs,
            medium,
            rates,
            scales,
            rising,
            ends,
            arrived,
            result,
        )
        waiting.append((ring(send, "section", 1), keep))
    for half, (received, keep) in enumerate(waiting):
        result = place_call(place, half, result, received, keep)
    return result


def solution(mesh):
    placed = (
        P("section", None, "chan", "tok"),
        P("chan", "tok"),
        P("chan", None),
        P("chan", None),
        P("chan", None),
    )
    return jax.shard_map(
        on_device,
        mesh=mesh,
        in_specs=placed,
        out_specs=P("section", "chan", "tok"),
        check_vma=False,
    )
```

```python
import functools

import jax
import jax.numpy as jnp
import numpy as np
from jax import lax
from jax.experimental import pallas as pl
from jax.experimental.pallas import tpu as pltpu
from jax.sharding import PartitionSpec as P


ROWS = 8


def split_pair(matrix):
    high = jnp.asarray(matrix, jnp.float32).astype(jnp.bfloat16)
    low = (jnp.asarray(matrix, jnp.float32) - high.astype(jnp.float32)).astype(jnp.bfloat16)
    return high, low


def stacked(matrix, axis):
    return jnp.concatenate(split_pair(matrix), axis=axis)


def fourier_tables(window):
    size = 2 * window
    time = np.arange(window)[:, None]
    freq = np.arange(window)[None, :]
    angle = 2.0 * np.pi * ((time * freq) % size) / size
    sign = np.where(freq % 2 == 0, 1.0, -1.0)
    nyquist = np.where(time % 2 == 0, 1.0, -1.0)
    weight = np.where(freq == 0, 1.0, 2.0) / size
    forward, inverse = [], []
    for odd in range(2):
        flip = sign if odd else np.ones_like(sign)
        real = np.cos(angle) * flip
        imag = -np.sin(angle) * flip
        imag[:, :1] = nyquist
        forward.append(stacked(np.concatenate([real, imag], axis=1), 0))
        back_real = np.cos(angle) * weight * flip
        back_imag = -np.sin(angle) * weight * flip
        back_imag[:, :1] = nyquist / size
        inverse.append(stacked(np.concatenate([back_real.T, back_imag.T], axis=0), 1))
    return forward, inverse


def turned_tables(window):
    half = window // 2
    time = np.arange(window)[:, None]
    freq = 2 * np.arange(half)[None, :] + 1
    angle = np.pi * ((time * freq) % (2 * window)) / window
    real, imag = np.cos(angle), -np.sin(angle)
    zero = np.zeros_like(real)
    forward = np.concatenate(
        [
            np.concatenate([real, zero, imag, zero], axis=1),
            np.concatenate([zero, real, zero, imag], axis=1),
        ],
        axis=0,
    )
    inverse = forward.T * (2.0 / window)
    doubled = np.concatenate([real, real, imag, imag], axis=1)
    return forward, inverse, doubled


PAIR = 16
STEP = 512
HALVES = 2
COMPILER = pltpu.CompilerParams(vmem_limit_bytes=16 << 20)


def parked(*arrays):
    return [pltpu.with_memory_space_constraint(a, pltpu.HBM) for a in arrays]


def cost(share, tokens, work):
    size = share * tokens
    return pl.CostEstimate(
        flops=size * work, bytes_accessed=size * 12, transcendentals=size // 64
    )


def dot_f32(left, right):
    return jnp.dot(left, right, preferred_element_type=jnp.float32)


def dot_turned(left, right):
    return lax.dot_general(
        left, right, (((1,), (1,)), ((), ())), preferred_element_type=jnp.float32
    )


VMEM_SPEC = pl.BlockSpec(memory_space=pltpu.VMEM)
SMEM_SPEC = pl.BlockSpec(memory_space=pltpu.SMEM)
ANY_SPEC = pl.BlockSpec(memory_space=pl.ANY)


def rows_at(ref, step, i, axis=0):
    start = i * step
    if not isinstance(i, int):
        start = pl.multiple_of(start, step)
    return ref.at[(slice(None),) * axis + (pl.ds(start, step),)]


def both_gates(local, remote, section, step, i):
    mine, other = rows_at(local, step, i, 1), rows_at(remote, step, i, 1)
    return (mine, other) if section == 0 else (other, mine)


def by_section(sec, body):
    for section in range(2):
        pl.when(sec[0] == section)(functools.partial(body, section))


def lane_mask(modes):
    shape = (ROWS, ROWS * modes)
    lane = lax.broadcasted_iota(jnp.int32, shape, 1)
    return lane // modes == lax.broadcasted_iota(jnp.int32, shape, 0)


def spread(ref, group):
    return jnp.broadcast_to(ref[group : group + 1, :], (ROWS, ref.shape[1]))


def powers(slow, hop, window, first, falling):
    row = lax.broadcasted_iota(jnp.int32, slow.shape, 0).astype(jnp.float32)
    tiles = [jnp.exp(-slow * (first + (ROWS - 1 - row if falling else row)))]
    while len(tiles) < window // ROWS:
        tiles = tiles + [tile * hop for tile in tiles]
        hop = hop * hop
    if falling:
        tiles = tiles[::-1]
    return jnp.concatenate(tiles, axis=0).astype(jnp.bfloat16)


def both_powers(rates, hops, pair, window, falling):
    sides = [
        powers(spread(rates, g), spread(hops, g), window, 0.0, falling)
        for g in (2 * pair, 2 * pair + 1)
    ]
    return jnp.concatenate(sides, axis=1)


def two_sided(upper, lower):
    zero = jnp.zeros_like(upper)
    return jnp.concatenate(
        [
            jnp.concatenate([upper, zero], axis=1),
            jnp.concatenate([zero, lower], axis=1),
        ],
        axis=0,
    )


def scale_of(residues, slow):
    return residues * jnp.sqrt(1.0 - jnp.exp(-2.0 * slow))


def in_rows(ref, tall):
    _, channels = ref.shape
    tall[...] = ref[...].T
    count = channels // ROWS
    return jnp.concatenate(
        [tall[pl.ds(c, count, stride=ROWS), :] for c in range(ROWS)], axis=1
    )


def response_kernel(count, window, sec, tok, rates, residues, *rest):
    gates, inputs, taps = rest[:3]
    tables = rest[3 : 3 + count]
    out, rate_rows, scale_rows, rising, falling = rest[3 + count : 8 + count]
    own_gates, own_inputs, own_taps = rest[8 + count : 11 + count]
    own_tables = rest[11 + count : 11 + 2 * count]
    tall, hops, scales, arrival = rest[11 + 2 * count :]
    share = out.shape[0]
    step = tall.shape[0]
    modes = rates.shape[0]
    first = pl.multiple_of(sec[0] * share, share)
    mine = pl.ds(first, share)
    pairs = [(gates.at[0, :, mine, :], own_gates)]
    pairs += [(inputs.at[mine, :], own_inputs), (taps.at[mine, :], own_taps)]
    pairs += list(zip(tables, own_tables))
    copies = [
        pltpu.make_async_copy(source, target, arrival.at[k])
        for k, (source, target) in enumerate(pairs)
    ]
    for copy in copies:
        copy.start()
    mask = lane_mask(modes)

    @pl.loop(0, share // step)
    def _(i):
        lanes = pl.ds(pl.multiple_of(first + i * step, step), step)
        slow = in_rows(rates.at[:, lanes], tall)
        scale = scale_of(in_rows(residues.at[:, lanes], tall), slow)
        small = step // ROWS
        own_rates = rows_at(rate_rows, small, i)
        own_rates[...] = slow
        rows_at(scale_rows, small, i)[...] = scale
        hops[...] = jnp.exp(-slow * ROWS)
        scales[...] = scale / (1.0 + jnp.exp(-slow * window))
        up, down = rows_at(rising, step // PAIR, i), rows_at(falling, step // PAIR, i)
        own_out = rows_at(out, step, i)
        for pair in range(step // PAIR):
            both = two_sided(
                jnp.where(mask, spread(scales, 2 * pair), 0.0),
                jnp.where(mask, spread(scales, 2 * pair + 1), 0.0),
            )
            high = both.astype(jnp.bfloat16).astype(jnp.float32)
            both = jnp.concatenate([high, both - high], axis=0).astype(jnp.bfloat16)
            table = both_powers(own_rates, hops, pair, window, False)
            up[pair] = table
            down[pair] = both_powers(own_rates, hops, pair, window, True)
            found = dot_turned(both, table)
            out_rows = pl.ds(pair * PAIR, PAIR)
            own_out[out_rows, :] = found[:PAIR] + found[PAIR:]

    for copy in copies:
        copy.wait()


def response_call(place, rates, residues, gates, inputs, taps, tables, window, share):
    tokens = inputs.shape[1]
    step = min(STEP, share)
    modes = rates.shape[0]
    lanes = ROWS * modes
    small = (step // ROWS, lanes)
    shape = lambda dims, kind=jnp.float32: jax.ShapeDtypeStruct(dims, kind)
    power_shape = shape((share // PAIR, window, 2 * lanes), jnp.bfloat16)
    outs = [shape((share, window))] + [shape((share // ROWS, lanes))] * 2
    outs += [power_shape] * 2
    outs += [
        shape((2, share, tokens), gates.dtype),
        shape((share, tokens), inputs.dtype),
        shape((share, window), taps.dtype),
    ]
    outs += [shape(t.shape, t.dtype) for t in tables]
    staged = 3 + len(tables)
    found = pl.pallas_call(
        functools.partial(response_kernel, len(tables), window),
        out_shape=tuple(outs),
        in_specs=[SMEM_SPEC] * 2 + [VMEM_SPEC] * 2 + [ANY_SPEC] * staged,
        out_specs=(VMEM_SPEC,) * len(outs),
        scratch_shapes=[
            pltpu.VMEM((step, modes), jnp.float32),
            pltpu.VMEM(small, jnp.float32),
            pltpu.VMEM(small, jnp.float32),
            pltpu.SemaphoreType.DMA((staged,)),
        ],
        name="response",
        cost_estimate=cost(share, 4 * window, 900),
        compiler_params=COMPILER,
    )(*place, rates, residues, *parked(gates, inputs, taps, *tables))
    return found[:5], found[5:8], found[8:]


def products(members, tap_spec):
    window = tap_spec.shape[1] // 2
    real, packed = tap_spec[:, :window], tap_spec[:, window:]
    lane = lax.broadcasted_iota(jnp.int32, real.shape, 1)
    real_b = jnp.where(lane == 0, packed, real)
    imag = jnp.where(lane == 0, 0.0, packed)
    found = []
    for mixed in members:
        a, b = mixed[:, :window], mixed[:, window:]
        found.append(
            jnp.concatenate([a * real - b * imag, a * imag + b * real_b], axis=1).astype(
                jnp.bfloat16
            )
        )
    return found


def doubled_spectrum(members, table):
    rows = jnp.concatenate(members, axis=0)
    found = dot_f32(jnp.concatenate([rows, rows], axis=1), table[...])
    size = members[0].shape[0]
    return [found[k * size : (k + 1) * size] for k in range(len(members))]


def finish_medium(members, table, gates_out, gates_in, streams, targets):
    found = dot_f32(jnp.concatenate(members, axis=0), table[...])
    size, window = streams[0].shape
    signals = []
    for k in range(len(members)):
        rows = slice(k * size, (k + 1) * size)
        medium = found[rows, :window] + found[rows, window:]
        gated = (gates_out[k].astype(jnp.float32) * medium).astype(jnp.bfloat16)
        targets[k][...] = gated
        stream = streams[k].astype(jnp.float32) + gated.astype(jnp.float32)
        signals.append((gates_in[k].astype(jnp.float32) * stream).astype(jnp.bfloat16))
    return signals


def end_states(signals, powers_of_pair, pair, modes, mask):
    rows = slice(pair * PAIR, (pair + 1) * PAIR)
    lanes = ROWS * modes
    left = jnp.concatenate([signal[rows] for signal in signals], axis=0)
    found = dot_f32(left, powers_of_pair)
    sides = []
    for side in range(2):
        tops = [k * PAIR + side * ROWS for k in range(len(signals))]
        sides.append(
            [
                jnp.where(mask, found[top : top + ROWS, side * lanes : (side + 1) * lanes], 0.0)
                for top in tops
            ]
        )
    return sides


def later_kernel(
    step,
    sec,
    tok,
    local_all,
    swapped,
    inputs_all,
    taps_all,
    fwd_even,
    fwd_odd,
    inv_even,
    inv_odd,
    medium_all,
    signals_all,
    tap_spec_all,
    edge_spec_all,
    remote_all,
    arrival,
):
    share, tokens = inputs_all.shape
    window = taps_all.shape[1]
    blocks = tokens // window
    parts = [slice(b * window, (b + 1) * window) for b in range(blocks)]

    def fetch(i):
        source = pl.ds(pl.multiple_of(sec[0] * share + i * step, step), step)
        return pltpu.make_async_copy(
            swapped.at[:, source, :], rows_at(remote_all, step, i, 1), arrival.at[i]
        )

    for i in range(share // step):
        fetch(i).start()

    def chunk(section, i):
        fetch(i).wait()
        first, second = both_gates(local_all, remote_all, section, step, i)
        inputs = rows_at(inputs_all, step, i)
        medium_out, signals = rows_at(medium_all, step, i), rows_at(signals_all, step, i)
        sources = [first[1, :, part] * inputs[:, part] for part in parts]
        tap_rows = rows_at(taps_all, step, i)[...]
        tap_spec, *even = doubled_spectrum([tap_rows] + sources[0::2], fwd_even)
        odd = doubled_spectrum(sources[1::2], fwd_odd)
        in_order = [None] * blocks
        in_order[0::2] = even
        in_order[1::2] = odd
        rows_at(tap_spec_all, step, i)[...] = tap_spec
        rows_at(edge_spec_all, step, i)[...] = in_order[0]
        mixed = products([in_order[b - 1] + in_order[b] for b in range(1, blocks)], tap_spec)
        for parity, table in enumerate((inv_even, inv_odd)):
            chosen = [b for b in range(1, blocks) if b % 2 == parity]
            if not chosen:
                continue
            found = finish_medium(
                [mixed[b - 1] for b in chosen],
                table,
                [first[0, :, parts[b]] for b in chosen],
                [second[1, :, parts[b]] for b in chosen],
                [inputs[:, parts[b]] for b in chosen],
                [medium_out.at[:, parts[b]] for b in chosen],
            )
            for b, signal in zip(chosen, found):
                signals[:, parts[b]] = signal

    def body(section):
        pl.loop(0, share // step)(functools.partial(chunk, section))

    by_section(sec, body)


def later_call(place, gates, swapped, inputs, taps, tables):
    share, tokens = inputs.shape
    window = taps.shape[1]
    operands = [gates, *parked(swapped), inputs, taps, *tables]
    spec = jax.ShapeDtypeStruct((share, 2 * window), jnp.float32)
    wide = jax.ShapeDtypeStruct((share, tokens), jnp.bfloat16)
    return pl.pallas_call(
        functools.partial(later_kernel, min(STEP, share)),
        out_shape=(wide, wide, spec, spec, jax.ShapeDtypeStruct(gates.shape, gates.dtype)),
        in_specs=[SMEM_SPEC] * 2 + [VMEM_SPEC, ANY_SPEC] + [VMEM_SPEC] * (len(operands) - 2),
        out_specs=(VMEM_SPEC,) * 5,
        scratch_shapes=[pltpu.SemaphoreType.DMA((share // min(STEP, share),))],
        name="later",
        cost_estimate=cost(share, tokens, 1500),
        compiler_params=COMPILER,
    )(*place, *operands)


def first_kernel(
    modes,
    step,
    sec,
    tok,
    local_all,
    remote_all,
    inputs_all,
    halo_low,
    halo_high,
    rates,
    falling_all,
    tap_spec_all,
    edge_spec_all,
    fwd_odd,
    inv_even,
    medium_before,
    signals_before,
    medium_all,
    signals_all,
    ends_all,
    total_all,
    leaps_all,
):
    share = inputs_all.shape[0]
    window = tap_spec_all.shape[1] // 2
    part = slice(0, window)
    mask = lane_mask(modes)
    leaps_all[...] = jnp.exp(-rates[...] * window)

    def chunk(section, i):
        first, second = both_gates(local_all, remote_all, section, step, i)
        halo = rows_at(halo_low if section == 0 else halo_high, step, i)
        leaps = rows_at(leaps_all, step // ROWS, i)
        falling = rows_at(falling_all, step // PAIR, i)
        ends = rows_at(ends_all, step, i, 1)
        started = jnp.where(tok[0] > 0, 1.0, 0.0).astype(jnp.bfloat16)
        (before,) = doubled_spectrum([halo[...] * started], fwd_odd)
        mixed = products(
            [before + rows_at(edge_spec_all, step, i)[...]],
            rows_at(tap_spec_all, step, i)[...],
        )
        (signal,) = finish_medium(
            mixed,
            inv_even,
            [first[0, :, part]],
            [second[1, :, part]],
            [rows_at(inputs_all, step, i)[:, part]],
            [rows_at(medium_all, step, i).at[:, part]],
        )
        signals = rows_at(signals_all, step, i)
        signals[:, part] = signal
        members = [signal] + [
            signals[:, b * window : (b + 1) * window] for b in range(1, ends.shape[0])
        ]
        sums = []
        for pair in range(step // PAIR):
            sides = end_states(members, falling[pair], pair, modes, mask)
            for side, found in enumerate(sides):
                at = pair * PAIR + side * ROWS
                leap = spread(leaps, 2 * pair + side)
                state = None
                for b, end in enumerate(found):
                    ends[b, at : at + ROWS, :] = end
                    state = end if state is None else state * leap + end
                sums.append(jnp.sum(state, axis=0, keepdims=True))
        total = rows_at(total_all, step // ROWS, i)
        total[...] = jnp.concatenate(sums, axis=0).astype(total.dtype)

    def body(section):
        pl.loop(0, share // step)(functools.partial(chunk, section))

    by_section(sec, body)


def first_call(
    place, gates, swapped, inputs, halos, rates, falling, specs, tables, medium, signals, modes
):
    share, tokens = inputs.shape
    window = halos[0].shape[1]
    lanes = ROWS * modes
    small = (share // ROWS, lanes)
    operands = [gates, swapped, inputs, *halos, rates, falling, *specs, *tables, medium, signals]
    return pl.pallas_call(
        functools.partial(first_kernel, modes, min(2 * STEP, share)),
        out_shape=(
            jax.ShapeDtypeStruct(medium.shape, medium.dtype),
            jax.ShapeDtypeStruct(signals.shape, signals.dtype),
            jax.ShapeDtypeStruct((tokens // window, share, lanes), jnp.float32),
            jax.ShapeDtypeStruct(small, jnp.bfloat16),
        ),
        in_specs=[SMEM_SPEC] * 2 + [VMEM_SPEC] * len(operands),
        out_specs=(VMEM_SPEC,) * 4,
        scratch_shapes=[pltpu.VMEM(small, jnp.float32)],
        input_output_aliases={len(operands): 0, len(operands) + 1: 1},
        name="first",
        cost_estimate=cost(share, tokens, 500),
        compiler_params=COMPILER,
    )(*place, *operands)


def within_kernel(
    step,
    signals_all,
    response_all,
    fwd_h,
    fwd_l,
    inverse,
    table_h,
    table_l,
    out_all,
):
    share, tokens = signals_all.shape
    size = fwd_h.shape[0]
    half = size // 2

    def chunk(i):
        signals = rows_at(signals_all, step, i)
        taps, out = rows_at(response_all, step, i)[...], rows_at(out_all, step, i)
        high = taps.astype(jnp.bfloat16)
        low = (taps - high.astype(jnp.float32)).astype(jnp.bfloat16)
        response = dot_f32(jnp.concatenate([high, low], axis=1), table_h[...]) + dot_f32(
            high, table_l[...]
        )
        channels = step
        real, imag = response[:, :half], response[:, half:]
        parts = [slice(k * size, (k + 1) * size) for k in range(tokens // size)]
        signal = jnp.concatenate([signals[:, part] for part in parts], axis=0)
        spec = dot_f32(signal, fwd_h[...]) + dot_f32(signal, fwd_l[...])
        filtered = []
        for k in range(len(parts)):
            rows = slice(k * channels, (k + 1) * channels)
            a, b = spec[rows, :half], spec[rows, half:]
            filtered.append(
                jnp.concatenate([a * real - b * imag, a * imag + b * real], axis=1).astype(
                    jnp.bfloat16
                )
            )
        found = dot_f32(jnp.concatenate(filtered, axis=0), inverse[...])
        for k, part in enumerate(parts):
            out[:, part] = found[k * channels : (k + 1) * channels]

    pl.loop(0, share // step)(chunk)


def within_call(signals, response, tables):
    share, tokens = signals.shape
    operands = [signals, response, *tables]
    return pl.pallas_call(
        functools.partial(within_kernel, min(2 * STEP, share)),
        out_shape=jax.ShapeDtypeStruct((share, tokens), jnp.float32),
        in_specs=[VMEM_SPEC] * len(operands),
        out_specs=VMEM_SPEC,
        name="within",
        cost_estimate=cost(share, tokens, 1500),
        compiler_params=COMPILER,
    )(*operands)


def output_kernel(
    count,
    modes,
    window,
    step,
    first,
    share,
    sec,
    tok,
    local_all,
    remote_all,
    within_all,
    inputs_all,
    medium_all,
    rates,
    scale_rows,
    rising_all,
    ends_all,
    *rest,
):
    arrived = rest[:count]
    (result, send, keep, leaps_all, scales_all, shares_all, starts_all, done) = rest[-8:]
    part_rows, tokens = send.shape
    base = first // step
    groups = pl.ds(first // ROWS, part_rows // ROWS)
    blocks = tokens // window
    mask = lane_mask(modes)
    slow = rates[groups, :]
    leap_all = jnp.exp(-slow * window)
    scale_all = scale_rows[groups, :] * jnp.exp(-slow)
    leaps_all[...] = leap_all
    scales_all[...] = scale_all
    shares_all[...] = scale_all / (1.0 + leap_all)
    entering = jnp.zeros_like(slow)
    for k in range(count):
        gap = tok[0] - (tok[0] ^ (k + 1))
        known = jnp.where(gap > 0, 1.0, 0.0)
        distance = (tokens * jnp.maximum(gap - 1, 0)).astype(jnp.float32)
        entering = entering + arrived[k][groups, :].astype(jnp.float32) * (
            jnp.exp(-slow * distance) * known
        )
    starts_all[...] = entering

    def chunk(section, out_all, i):
        out = rows_at(out_all, step, i)
        at_all = base + i
        gate_out = both_gates(local_all, remote_all, section, step, at_all)[1].at[0]
        inputs = rows_at(inputs_all, step, at_all)
        gated_medium = rows_at(medium_all, step, at_all)
        within = rows_at(within_all, step, at_all)
        ends = rows_at(ends_all, step, at_all, 1)
        rising = rows_at(rising_all, step // PAIR, at_all)
        small = step // ROWS
        leaps, scales = rows_at(leaps_all, small, i), rows_at(scales_all, small, i)
        shares, starts = rows_at(shares_all, small, i), rows_at(starts_all, small, i)
        channels = step
        for pair in range(channels // PAIR):
            rows = slice(pair * PAIR, (pair + 1) * PAIR)
            sides = []
            for side in range(2):
                group = 2 * pair + side
                leap, scale = spread(leaps, group), spread(scales, group)
                portion = spread(shares, group)
                state = jnp.where(mask, spread(starts, group), 0.0)
                at = pair * PAIR + side * ROWS
                lefts = []
                for b in range(blocks):
                    end = ends[b, at : at + ROWS, :]
                    lefts.append(state * scale + end * portion)
                    state = state * leap + end
                sides.append(lefts)
            left = jnp.concatenate(
                [two_sided(upper, lower) for upper, lower in zip(*sides)], axis=0
            ).astype(jnp.bfloat16)
            across = dot_turned(left, rising[pair])
            for b in range(blocks):
                part = slice(b * window, (b + 1) * window)
                stream = inputs[rows, part].astype(jnp.float32) + gated_medium[
                    rows, part
                ].astype(jnp.float32)
                long_out = within[rows, part] + across[b * PAIR : (b + 1) * PAIR]
                gate = gate_out[rows, part].astype(jnp.float32)
                out[rows, part] = (stream + gate * long_out).astype(jnp.bfloat16)

    def body(section):
        target = result.at[0, pl.ds(section * share + first, part_rows), :]
        source = medium_all.at[pl.ds(first, part_rows), :]
        copy = pltpu.make_async_copy(source, send if section else target, done)
        copy.start()
        pl.loop(0, part_rows // step)(
            functools.partial(chunk, section, keep if section else send)
        )
        copy.wait()

    by_section(sec, body)


def output_call(
    place, half, gates, swapped, within, inputs, medium, rates, scales, rising, ends, arrived, before
):
    share, tokens = medium.shape
    lanes = rates.shape[1]
    window = rising.shape[1]
    part_rows = share // HALVES
    step = min(STEP, part_rows)
    small = (part_rows // ROWS, lanes)
    operands = [gates, swapped, within, inputs, medium, rates, scales, rising, ends, *arrived]
    result = jax.ShapeDtypeStruct((1, 2 * share, tokens), jnp.bfloat16)
    chained = [] if before is None else [before]
    return pl.pallas_call(
        functools.partial(
            output_kernel,
            len(arrived),
            lanes // ROWS,
            window,
            step,
            half * part_rows,
            share,
        ),
        out_shape=(result,) + (jax.ShapeDtypeStruct((part_rows, tokens), jnp.bfloat16),) * 2,
        in_specs=[SMEM_SPEC] * 2 + [VMEM_SPEC] * len(operands) + [ANY_SPEC] * len(chained),
        out_specs=(ANY_SPEC, VMEM_SPEC, VMEM_SPEC),
        scratch_shapes=[pltpu.VMEM(small, jnp.float32)] * 4
        + [pltpu.SemaphoreType.DMA],
        input_output_aliases={2 + len(operands): 0} if chained else {},
        name="output",
        cost_estimate=cost(part_rows, tokens, 1500),
        compiler_params=COMPILER,
    )(*place, *operands, *chained)


def place_kernel(first, share, sec, tok, before, received, keep, out, done):
    rows = received.shape[0]

    def target(section):
        return out.at[0, pl.ds(pl.multiple_of(section * share + first, rows), rows), :]

    foreign = pltpu.make_async_copy(received, target(1 - sec[0]), done.at[0])
    foreign.start()

    @pl.when(sec[0] == 1)
    def _():
        own = pltpu.make_async_copy(keep, target(1), done.at[1])
        own.start()
        own.wait()

    foreign.wait()


def place_call(place, half, before, received, keep):
    rows, tokens = received.shape
    return pl.pallas_call(
        functools.partial(place_kernel, half * rows, before.shape[1] // 2),
        out_shape=jax.ShapeDtypeStruct(before.shape, before.dtype),
        in_specs=[SMEM_SPEC] * 2 + [ANY_SPEC, VMEM_SPEC, VMEM_SPEC],
        out_specs=ANY_SPEC,
        scratch_shapes=[pltpu.SemaphoreType.DMA((2,))],
        input_output_aliases={2: 0},
        name="placing",
        cost_estimate=cost(rows, tokens, 2),
        compiler_params=COMPILER,
    )(*place, before, received, keep)


def edge_kernel(gates, inputs, low, high, gate_tail, input_tail, arrival):
    share, window = low.shape
    tail = pl.ds(inputs.shape[1] - window, window)
    pairs = [(gates.at[0, 1, :, tail], gate_tail), (inputs.at[:, tail], input_tail)]
    copies = [
        pltpu.make_async_copy(source, target, arrival.at[k])
        for k, (source, target) in enumerate(pairs)
    ]
    for copy in copies:
        copy.start()
    for copy in copies:
        copy.wait()
    low[...] = gate_tail[:share, :] * input_tail[:share, :]
    high[...] = gate_tail[share:, :] * input_tail[share:, :]


def edge_call(gate_streams, inputs, window, share):
    channels, tokens = inputs.shape
    edge = jax.ShapeDtypeStruct((share, window), jnp.bfloat16)
    return pl.pallas_call(
        edge_kernel,
        out_shape=(edge, edge),
        in_specs=[ANY_SPEC] * 2,
        out_specs=(VMEM_SPEC,) * 2,
        scratch_shapes=[pltpu.VMEM((channels, window), jnp.bfloat16)] * 2
        + [pltpu.SemaphoreType.DMA((2,))],
        name="edge",
        cost_estimate=cost(share, tokens, 2),
        compiler_params=COMPILER,
    )(*parked(gate_streams, inputs))


def ring(value, axis, by):
    peers = lax.axis_size(axis)
    return lax.ppermute(value, axis, [(i, (i + by) % peers) for i in range(peers)])


def met(value, by):
    peers = lax.axis_size("tok")
    return lax.ppermute(value, "tok", [(i, i ^ by) for i in range(peers)])


def edge_to(value, section):
    peers = lax.axis_size("tok")
    pairs = [(i, section * peers + (i + 1) % peers) for i in range(peers)]
    pairs += [(peers + i, (1 - section) * peers + i) for i in range(peers)]
    return lax.ppermute(value, ("section", "tok"), pairs)


def on_device(gate_streams, inputs, medium_taps, residues, decay_rates):
    channels, _ = inputs.shape
    share = channels // 2
    window = medium_taps.shape[1]
    modes = decay_rates.shape[1]
    place = tuple(
        lax.axis_index(axis).astype(jnp.int32).reshape(1) for axis in ("section", "tok")
    )
    edges = edge_call(gate_streams, inputs, window, share)
    halos = [edge_to(edges[s], s) for s in range(2)]
    swapped = ring(gate_streams[0], "section", 1)
    forward, inverse = fourier_tables(window)
    turned, back, doubled = turned_tables(window)
    tables = [*forward, *inverse, *split_pair(turned), split_pair(back)[0]]
    high, low = split_pair(doubled)
    tables += [jnp.concatenate([high, high], axis=0), low]
    built, own, tables = response_call(
        place,
        decay_rates.T,
        residues.T,
        gate_streams,
        inputs,
        medium_taps,
        tables,
        window,
        share,
    )
    response, rates, scales, rising, falling = built
    gates, inputs, taps = own
    medium, signals, *specs, remote = later_call(
        place, gates, swapped, inputs, taps, tables[:4]
    )
    medium, signals, ends, total = first_call(
        place,
        gates,
        remote,
        inputs,
        halos,
        rates,
        falling,
        specs,
        tables[1:3],
        medium,
        signals,
        modes,
    )
    arrived = []
    for by in range(1, lax.axis_size("tok")):
        arrived.append(met(total, by))
    within = within_call(signals, response, tables[4:])
    result, waiting = None, []
    for half in range(HALVES):
        result, send, keep = output_call(
            place,
            half,
            gates,
            remote,
            within,
            inputs,
            medium,
            rates,
            scales,
            rising,
            ends,
            arrived,
            result,
        )
        waiting.append((ring(send, "section", 1), keep))
    for half, (received, keep) in enumerate(waiting):
        result = place_call(place, half, result, received, keep)
    return result


def solution(mesh):
    placed = (
        P("section", None, "chan", "tok"),
        P("chan", "tok"),
        P("chan", None),
        P("chan", None),
        P("chan", None),
    )
    return jax.shard_map(
        on_device,
        mesh=mesh,
        in_specs=placed,
        out_specs=P("section", "chan", "tok"),
        check_vma=False,
    )
```

```python
import functools

import jax
import jax.numpy as jnp
import numpy as np
from jax import lax
from jax.experimental import pallas as pl
from jax.experimental.pallas import tpu as pltpu
from jax.sharding import PartitionSpec as P


ROWS = 8


def split_pair(matrix):
    high = jnp.asarray(matrix, jnp.float32).astype(jnp.bfloat16)
    low = (jnp.asarray(matrix, jnp.float32) - high.astype(jnp.float32)).astype(jnp.bfloat16)
    return high, low


def stacked(matrix, axis):
    return jnp.concatenate(split_pair(matrix), axis=axis)


def fourier_tables(window):
    size = 2 * window
    time = np.arange(window)[:, None]
    freq = np.arange(window)[None, :]
    angle = 2.0 * np.pi * ((time * freq) % size) / size
    sign = np.where(freq % 2 == 0, 1.0, -1.0)
    nyquist = np.where(time % 2 == 0, 1.0, -1.0)
    weight = np.where(freq == 0, 1.0, 2.0) / size
    forward, inverse = [], []
    for odd in range(2):
        flip = sign if odd else np.ones_like(sign)
        real = np.cos(angle) * flip
        imag = -np.sin(angle) * flip
        imag[:, :1] = nyquist
        forward.append(stacked(np.concatenate([real, imag], axis=1), 0))
        back_real = np.cos(angle) * weight * flip
        back_imag = -np.sin(angle) * weight * flip
        back_imag[:, :1] = nyquist / size
        inverse.append(stacked(np.concatenate([back_real.T, back_imag.T], axis=0), 1))
    return forward, inverse


def turned_tables(window):
    half = window // 2
    time = np.arange(window)[:, None]
    freq = 2 * np.arange(half)[None, :] + 1
    angle = np.pi * ((time * freq) % (2 * window)) / window
    real, imag = np.cos(angle), -np.sin(angle)
    zero = np.zeros_like(real)
    forward = np.concatenate(
        [
            np.concatenate([real, zero, imag, zero], axis=1),
            np.concatenate([zero, real, zero, imag], axis=1),
        ],
        axis=0,
    )
    inverse = forward.T * (2.0 / window)
    doubled = np.concatenate([real, real, imag, imag], axis=1)
    return forward, inverse, doubled


PAIR = 16
STEP = 512
HALVES = 2
COMPILER = pltpu.CompilerParams(vmem_limit_bytes=16 << 20)


def parked(*arrays):
    return [pltpu.with_memory_space_constraint(a, pltpu.HBM) for a in arrays]


def cost(share, tokens, work):
    size = share * tokens
    return pl.CostEstimate(
        flops=size * work, bytes_accessed=size * 12, transcendentals=size // 64
    )


def dot_f32(left, right):
    return jnp.dot(left, right, preferred_element_type=jnp.float32)


def dot_turned(left, right):
    return lax.dot_general(
        left, right, (((1,), (1,)), ((), ())), preferred_element_type=jnp.float32
    )


VMEM_SPEC = pl.BlockSpec(memory_space=pltpu.VMEM)
SMEM_SPEC = pl.BlockSpec(memory_space=pltpu.SMEM)
ANY_SPEC = pl.BlockSpec(memory_space=pl.ANY)


def rows_at(ref, step, i, axis=0):
    start = i * step
    if not isinstance(i, int):
        start = pl.multiple_of(start, step)
    return ref.at[(slice(None),) * axis + (pl.ds(start, step),)]


def both_gates(local, remote, section, step, i):
    mine, other = rows_at(local, step, i, 1), rows_at(remote, step, i, 1)
    return (mine, other) if section == 0 else (other, mine)


def by_section(sec, body):
    for section in range(2):
        pl.when(sec[0] == section)(functools.partial(body, section))


def lane_mask(modes):
    shape = (ROWS, ROWS * modes)
    lane = lax.broadcasted_iota(jnp.int32, shape, 1)
    return lane // modes == lax.broadcasted_iota(jnp.int32, shape, 0)


def spread(ref, group):
    return jnp.broadcast_to(ref[group : group + 1, :], (ROWS, ref.shape[1]))


def powers(slow, hop, window, first, falling):
    row = lax.broadcasted_iota(jnp.int32, slow.shape, 0).astype(jnp.float32)
    tiles = [jnp.exp(-slow * (first + (ROWS - 1 - row if falling else row)))]
    while len(tiles) < window // ROWS:
        tiles = tiles + [tile * hop for tile in tiles]
        hop = hop * hop
    if falling:
        tiles = tiles[::-1]
    return jnp.concatenate(tiles, axis=0).astype(jnp.bfloat16)


def both_powers(rates, hops, pair, window, falling):
    sides = [
        powers(spread(rates, g), spread(hops, g), window, 0.0, falling)
        for g in (2 * pair, 2 * pair + 1)
    ]
    return jnp.concatenate(sides, axis=1)


def two_sided(upper, lower):
    zero = jnp.zeros_like(upper)
    return jnp.concatenate(
        [
            jnp.concatenate([upper, zero], axis=1),
            jnp.concatenate([zero, lower], axis=1),
        ],
        axis=0,
    )


def scale_of(residues, slow):
    return residues * jnp.sqrt(1.0 - jnp.exp(-2.0 * slow))


def in_rows(ref, tall):
    _, channels = ref.shape
    tall[...] = ref[...].T
    count = channels // ROWS
    return jnp.concatenate(
        [tall[pl.ds(c, count, stride=ROWS), :] for c in range(ROWS)], axis=1
    )


def response_kernel(count, window, sec, tok, rates, residues, *rest):
    gates, inputs, taps = rest[:3]
    tables = rest[3 : 3 + count]
    out, rate_rows, scale_rows, rising, falling = rest[3 + count : 8 + count]
    own_gates, own_inputs, own_taps = rest[8 + count : 11 + count]
    own_tables = rest[11 + count : 11 + 2 * count]
    tall, hops, scales, arrival = rest[11 + 2 * count :]
    share = out.shape[0]
    step = tall.shape[0]
    modes = rates.shape[0]
    first = pl.multiple_of(sec[0] * share, share)
    mine = pl.ds(first, share)
    pairs = [(gates.at[0, :, mine, :], own_gates)]
    pairs += [(inputs.at[mine, :], own_inputs), (taps.at[mine, :], own_taps)]
    pairs += list(zip(tables, own_tables))
    copies = [
        pltpu.make_async_copy(source, target, arrival.at[k])
        for k, (source, target) in enumerate(pairs)
    ]
    for copy in copies:
        copy.start()
    mask = lane_mask(modes)

    @pl.loop(0, share // step)
    def _(i):
        lanes = pl.ds(pl.multiple_of(first + i * step, step), step)
        slow = in_rows(rates.at[:, lanes], tall)
        scale = scale_of(in_rows(residues.at[:, lanes], tall), slow)
        small = step // ROWS
        own_rates = rows_at(rate_rows, small, i)
        own_rates[...] = slow
        rows_at(scale_rows, small, i)[...] = scale
        hops[...] = jnp.exp(-slow * ROWS)
        scales[...] = scale / (1.0 + jnp.exp(-slow * window))
        up, down = rows_at(rising, step // PAIR, i), rows_at(falling, step // PAIR, i)
        own_out = rows_at(out, step, i)
        for pair in range(step // PAIR):
            both = two_sided(
                jnp.where(mask, spread(scales, 2 * pair), 0.0),
                jnp.where(mask, spread(scales, 2 * pair + 1), 0.0),
            )
            high = both.astype(jnp.bfloat16).astype(jnp.float32)
            both = jnp.concatenate([high, both - high], axis=0).astype(jnp.bfloat16)
            table = both_powers(own_rates, hops, pair, window, False)
            up[pair] = table
            down[pair] = both_powers(own_rates, hops, pair, window, True)
            found = dot_turned(both, table)
            out_rows = pl.ds(pair * PAIR, PAIR)
            own_out[out_rows, :] = found[:PAIR] + found[PAIR:]

    for copy in copies:
        copy.wait()


def response_call(place, rates, residues, gates, inputs, taps, tables, window, share):
    tokens = inputs.shape[1]
    step = min(STEP, share)
    modes = rates.shape[0]
    lanes = ROWS * modes
    small = (step // ROWS, lanes)
    shape = lambda dims, kind=jnp.float32: jax.ShapeDtypeStruct(dims, kind)
    power_shape = shape((share // PAIR, window, 2 * lanes), jnp.bfloat16)
    outs = [shape((share, window))] + [shape((share // ROWS, lanes))] * 2
    outs += [power_shape] * 2
    outs += [
        shape((2, share, tokens), gates.dtype),
        shape((share, tokens), inputs.dtype),
        shape((share, window), taps.dtype),
    ]
    outs += [shape(t.shape, t.dtype) for t in tables]
    staged = 3 + len(tables)
    found = pl.pallas_call(
        functools.partial(response_kernel, len(tables), window),
        out_shape=tuple(outs),
        in_specs=[SMEM_SPEC] * 2 + [VMEM_SPEC] * 2 + [ANY_SPEC] * staged,
        out_specs=(VMEM_SPEC,) * len(outs),
        scratch_shapes=[
            pltpu.VMEM((step, modes), jnp.float32),
            pltpu.VMEM(small, jnp.float32),
            pltpu.VMEM(small, jnp.float32),
            pltpu.SemaphoreType.DMA((staged,)),
        ],
        name="response",
        cost_estimate=cost(share, 4 * window, 900),
        compiler_params=COMPILER,
    )(*place, rates, residues, *parked(gates, inputs, taps, *tables))
    return found[:5], found[5:8], found[8:]


def products(members, tap_spec):
    window = tap_spec.shape[1] // 2
    real, packed = tap_spec[:, :window], tap_spec[:, window:]
    lane = lax.broadcasted_iota(jnp.int32, real.shape, 1)
    real_b = jnp.where(lane == 0, packed, real)
    imag = jnp.where(lane == 0, 0.0, packed)
    found = []
    for mixed in members:
        a, b = mixed[:, :window], mixed[:, window:]
        found.append(
            jnp.concatenate([a * real - b * imag, a * imag + b * real_b], axis=1).astype(
                jnp.bfloat16
            )
        )
    return found


def doubled_spectrum(members, table):
    rows = jnp.concatenate(members, axis=0)
    found = dot_f32(jnp.concatenate([rows, rows], axis=1), table[...])
    size = members[0].shape[0]
    return [found[k * size : (k + 1) * size] for k in range(len(members))]


def finish_medium(members, table, gates_out, gates_in, streams, targets):
    found = dot_f32(jnp.concatenate(members, axis=0), table[...])
    size, window = streams[0].shape
    signals = []
    for k in range(len(members)):
        rows = slice(k * size, (k + 1) * size)
        medium = found[rows, :window] + found[rows, window:]
        gated = (gates_out[k].astype(jnp.float32) * medium).astype(jnp.bfloat16)
        targets[k][...] = gated
        stream = streams[k].astype(jnp.float32) + gated.astype(jnp.float32)
        signals.append((gates_in[k].astype(jnp.float32) * stream).astype(jnp.bfloat16))
    return signals


def end_states(signals, powers_of_pair, pair, modes, mask):
    rows = slice(pair * PAIR, (pair + 1) * PAIR)
    lanes = ROWS * modes
    left = jnp.concatenate([signal[rows] for signal in signals], axis=0)
    found = dot_f32(left, powers_of_pair)
    sides = []
    for side in range(2):
        tops = [k * PAIR + side * ROWS for k in range(len(signals))]
        sides.append(
            [
                jnp.where(mask, found[top : top + ROWS, side * lanes : (side + 1) * lanes], 0.0)
                for top in tops
            ]
        )
    return sides


def later_kernel(
    step,
    sec,
    tok,
    local_all,
    swapped,
    inputs_all,
    taps_all,
    fwd_even,
    fwd_odd,
    inv_even,
    inv_odd,
    medium_all,
    signals_all,
    tap_spec_all,
    edge_spec_all,
    remote_all,
    arrival,
):
    share, tokens = inputs_all.shape
    window = taps_all.shape[1]
    blocks = tokens // window
    parts = [slice(b * window, (b + 1) * window) for b in range(blocks)]

    def fetch(i):
        source = pl.ds(pl.multiple_of(sec[0] * share + i * step, step), step)
        return pltpu.make_async_copy(
            swapped.at[:, source, :], rows_at(remote_all, step, i, 1), arrival.at[i]
        )

    for i in range(share // step):
        fetch(i).start()

    def chunk(section, i):
        if section == 1:
            fetch(i).wait()
        first, second = both_gates(local_all, remote_all, section, step, i)
        inputs = rows_at(inputs_all, step, i)
        medium_out, signals = rows_at(medium_all, step, i), rows_at(signals_all, step, i)
        sources = [first[1, :, part] * inputs[:, part] for part in parts]
        tap_rows = rows_at(taps_all, step, i)[...]
        tap_spec, *even = doubled_spectrum([tap_rows] + sources[0::2], fwd_even)
        odd = doubled_spectrum(sources[1::2], fwd_odd)
        in_order = [None] * blocks
        in_order[0::2] = even
        in_order[1::2] = odd
        rows_at(tap_spec_all, step, i)[...] = tap_spec
        rows_at(edge_spec_all, step, i)[...] = in_order[0]
        mixed = products([in_order[b - 1] + in_order[b] for b in range(1, blocks)], tap_spec)
        if section == 0:
            fetch(i).wait()
        for parity, table in enumerate((inv_even, inv_odd)):
            chosen = [b for b in range(1, blocks) if b % 2 == parity]
            if not chosen:
                continue
            found = finish_medium(
                [mixed[b - 1] for b in chosen],
                table,
                [first[0, :, parts[b]] for b in chosen],
                [second[1, :, parts[b]] for b in chosen],
                [inputs[:, parts[b]] for b in chosen],
                [medium_out.at[:, parts[b]] for b in chosen],
            )
            for b, signal in zip(chosen, found):
                signals[:, parts[b]] = signal

    def body(section):
        pl.loop(0, share // step)(functools.partial(chunk, section))

    by_section(sec, body)


def later_call(place, gates, swapped, inputs, taps, tables):
    share, tokens = inputs.shape
    window = taps.shape[1]
    operands = [gates, *parked(swapped), inputs, taps, *tables]
    spec = jax.ShapeDtypeStruct((share, 2 * window), jnp.float32)
    wide = jax.ShapeDtypeStruct((share, tokens), jnp.bfloat16)
    return pl.pallas_call(
        functools.partial(later_kernel, min(STEP, share)),
        out_shape=(wide, wide, spec, spec, jax.ShapeDtypeStruct(gates.shape, gates.dtype)),
        in_specs=[SMEM_SPEC] * 2 + [VMEM_SPEC, ANY_SPEC] + [VMEM_SPEC] * (len(operands) - 2),
        out_specs=(VMEM_SPEC,) * 5,
        scratch_shapes=[pltpu.SemaphoreType.DMA((share // min(STEP, share),))],
        name="later",
        cost_estimate=cost(share, tokens, 1500),
        compiler_params=COMPILER,
    )(*place, *operands)


def first_kernel(
    modes,
    step,
    sec,
    tok,
    local_all,
    remote_all,
    inputs_all,
    halo_low,
    halo_high,
    rates,
    falling_all,
    tap_spec_all,
    edge_spec_all,
    fwd_odd,
    inv_even,
    medium_before,
    signals_before,
    medium_all,
    signals_all,
    ends_all,
    total_all,
    leaps_all,
):
    share = inputs_all.shape[0]
    window = tap_spec_all.shape[1] // 2
    part = slice(0, window)
    mask = lane_mask(modes)
    leaps_all[...] = jnp.exp(-rates[...] * window)

    def chunk(section, i):
        first, second = both_gates(local_all, remote_all, section, step, i)
        halo = rows_at(halo_low if section == 0 else halo_high, step, i)
        leaps = rows_at(leaps_all, step // ROWS, i)
        falling = rows_at(falling_all, step // PAIR, i)
        ends = rows_at(ends_all, step, i, 1)
        started = jnp.where(tok[0] > 0, 1.0, 0.0).astype(jnp.bfloat16)
        (before,) = doubled_spectrum([halo[...] * started], fwd_odd)
        mixed = products(
            [before + rows_at(edge_spec_all, step, i)[...]],
            rows_at(tap_spec_all, step, i)[...],
        )
        (signal,) = finish_medium(
            mixed,
            inv_even,
            [first[0, :, part]],
            [second[1, :, part]],
            [rows_at(inputs_all, step, i)[:, part]],
            [rows_at(medium_all, step, i).at[:, part]],
        )
        signals = rows_at(signals_all, step, i)
        signals[:, part] = signal
        members = [signal] + [
            signals[:, b * window : (b + 1) * window] for b in range(1, ends.shape[0])
        ]
        sums = []
        for pair in range(step // PAIR):
            sides = end_states(members, falling[pair], pair, modes, mask)
            for side, found in enumerate(sides):
                at = pair * PAIR + side * ROWS
                leap = spread(leaps, 2 * pair + side)
                state = None
                for b, end in enumerate(found):
                    ends[b, at : at + ROWS, :] = end
                    state = end if state is None else state * leap + end
                sums.append(jnp.sum(state, axis=0, keepdims=True))
        total = rows_at(total_all, step // ROWS, i)
        total[...] = jnp.concatenate(sums, axis=0).astype(total.dtype)

    def body(section):
        pl.loop(0, share // step)(functools.partial(chunk, section))

    by_section(sec, body)


def first_call(
    place, gates, swapped, inputs, halos, rates, falling, specs, tables, medium, signals, modes
):
    share, tokens = inputs.shape
    window = halos[0].shape[1]
    lanes = ROWS * modes
    small = (share // ROWS, lanes)
    operands = [gates, swapped, inputs, *halos, rates, falling, *specs, *tables, medium, signals]
    return pl.pallas_call(
        functools.partial(first_kernel, modes, min(2 * STEP, share)),
        out_shape=(
            jax.ShapeDtypeStruct(medium.shape, medium.dtype),
            jax.ShapeDtypeStruct(signals.shape, signals.dtype),
            jax.ShapeDtypeStruct((tokens // window, share, lanes), jnp.float32),
            jax.ShapeDtypeStruct(small, jnp.bfloat16),
        ),
        in_specs=[SMEM_SPEC] * 2 + [VMEM_SPEC] * len(operands),
        out_specs=(VMEM_SPEC,) * 4,
        scratch_shapes=[pltpu.VMEM(small, jnp.float32)],
        input_output_aliases={len(operands): 0, len(operands) + 1: 1},
        name="first",
        cost_estimate=cost(share, tokens, 500),
        compiler_params=COMPILER,
    )(*place, *operands)


def within_kernel(
    step,
    signals_all,
    response_all,
    fwd_h,
    fwd_l,
    inverse,
    table_h,
    table_l,
    out_all,
):
    share, tokens = signals_all.shape
    size = fwd_h.shape[0]
    half = size // 2

    def chunk(i):
        signals = rows_at(signals_all, step, i)
        taps, out = rows_at(response_all, step, i)[...], rows_at(out_all, step, i)
        high = taps.astype(jnp.bfloat16)
        low = (taps - high.astype(jnp.float32)).astype(jnp.bfloat16)
        response = dot_f32(jnp.concatenate([high, low], axis=1), table_h[...]) + dot_f32(
            high, table_l[...]
        )
        channels = step
        real, imag = response[:, :half], response[:, half:]
        parts = [slice(k * size, (k + 1) * size) for k in range(tokens // size)]
        signal = jnp.concatenate([signals[:, part] for part in parts], axis=0)
        spec = dot_f32(signal, fwd_h[...]) + dot_f32(signal, fwd_l[...])
        filtered = []
        for k in range(len(parts)):
            rows = slice(k * channels, (k + 1) * channels)
            a, b = spec[rows, :half], spec[rows, half:]
            filtered.append(
                jnp.concatenate([a * real - b * imag, a * imag + b * real], axis=1).astype(
                    jnp.bfloat16
                )
            )
        found = dot_f32(jnp.concatenate(filtered, axis=0), inverse[...])
        for k, part in enumerate(parts):
            out[:, part] = found[k * channels : (k + 1) * channels]

    pl.loop(0, share // step)(chunk)


def within_call(signals, response, tables):
    share, tokens = signals.shape
    operands = [signals, response, *tables]
    return pl.pallas_call(
        functools.partial(within_kernel, min(2 * STEP, share)),
        out_shape=jax.ShapeDtypeStruct((share, tokens), jnp.float32),
        in_specs=[VMEM_SPEC] * len(operands),
        out_specs=VMEM_SPEC,
        name="within",
        cost_estimate=cost(share, tokens, 1500),
        compiler_params=COMPILER,
    )(*operands)


def output_kernel(
    count,
    modes,
    window,
    step,
    first,
    share,
    sec,
    tok,
    local_all,
    remote_all,
    within_all,
    inputs_all,
    medium_all,
    rates,
    scale_rows,
    rising_all,
    ends_all,
    *rest,
):
    arrived = rest[:count]
    (result, send, keep, leaps_all, scales_all, shares_all, starts_all, done) = rest[-8:]
    part_rows, tokens = send.shape
    base = first // step
    groups = pl.ds(first // ROWS, part_rows // ROWS)
    blocks = tokens // window
    mask = lane_mask(modes)
    slow = rates[groups, :]
    leap_all = jnp.exp(-slow * window)
    scale_all = scale_rows[groups, :] * jnp.exp(-slow)
    leaps_all[...] = leap_all
    scales_all[...] = scale_all
    shares_all[...] = scale_all / (1.0 + leap_all)
    entering = jnp.zeros_like(slow)
    for k in range(count):
        gap = tok[0] - (tok[0] ^ (k + 1))
        known = jnp.where(gap > 0, 1.0, 0.0)
        distance = (tokens * jnp.maximum(gap - 1, 0)).astype(jnp.float32)
        entering = entering + arrived[k][groups, :].astype(jnp.float32) * (
            jnp.exp(-slow * distance) * known
        )
    starts_all[...] = entering

    def chunk(section, out_all, i):
        out = rows_at(out_all, step, i)
        at_all = base + i
        gate_out = both_gates(local_all, remote_all, section, step, at_all)[1].at[0]
        inputs = rows_at(inputs_all, step, at_all)
        gated_medium = rows_at(medium_all, step, at_all)
        within = rows_at(within_all, step, at_all)
        ends = rows_at(ends_all, step, at_all, 1)
        rising = rows_at(rising_all, step // PAIR, at_all)
        small = step // ROWS
        leaps, scales = rows_at(leaps_all, small, i), rows_at(scales_all, small, i)
        shares, starts = rows_at(shares_all, small, i), rows_at(starts_all, small, i)
        channels = step
        for pair in range(channels // PAIR):
            rows = slice(pair * PAIR, (pair + 1) * PAIR)
            sides = []
            for side in range(2):
                group = 2 * pair + side
                leap, scale = spread(leaps, group), spread(scales, group)
                portion = spread(shares, group)
                state = jnp.where(mask, spread(starts, group), 0.0)
                at = pair * PAIR + side * ROWS
                lefts = []
                for b in range(blocks):
                    end = ends[b, at : at + ROWS, :]
                    lefts.append(state * scale + end * portion)
                    state = state * leap + end
                sides.append(lefts)
            left = jnp.concatenate(
                [two_sided(upper, lower) for upper, lower in zip(*sides)], axis=0
            ).astype(jnp.bfloat16)
            across = dot_turned(left, rising[pair])
            for b in range(blocks):
                part = slice(b * window, (b + 1) * window)
                stream = inputs[rows, part].astype(jnp.float32) + gated_medium[
                    rows, part
                ].astype(jnp.float32)
                long_out = within[rows, part] + across[b * PAIR : (b + 1) * PAIR]
                gate = gate_out[rows, part].astype(jnp.float32)
                out[rows, part] = (stream + gate * long_out).astype(jnp.bfloat16)

    def body(section):
        target = result.at[0, pl.ds(section * share + first, part_rows), :]
        source = medium_all.at[pl.ds(first, part_rows), :]
        copy = pltpu.make_async_copy(source, send if section else target, done)
        copy.start()
        pl.loop(0, part_rows // step)(
            functools.partial(chunk, section, keep if section else send)
        )
        copy.wait()

    by_section(sec, body)


def output_call(
    place, half, gates, swapped, within, inputs, medium, rates, scales, rising, ends, arrived, before
):
    share, tokens = medium.shape
    lanes = rates.shape[1]
    window = rising.shape[1]
    part_rows = share // HALVES
    step = min(STEP, part_rows)
    small = (part_rows // ROWS, lanes)
    operands = [gates, swapped, within, inputs, medium, rates, scales, rising, ends, *arrived]
    result = jax.ShapeDtypeStruct((1, 2 * share, tokens), jnp.bfloat16)
    chained = [] if before is None else [before]
    return pl.pallas_call(
        functools.partial(
            output_kernel,
            len(arrived),
            lanes // ROWS,
            window,
            step,
            half * part_rows,
            share,
        ),
        out_shape=(result,) + (jax.ShapeDtypeStruct((part_rows, tokens), jnp.bfloat16),) * 2,
        in_specs=[SMEM_SPEC] * 2 + [VMEM_SPEC] * len(operands) + [ANY_SPEC] * len(chained),
        out_specs=(ANY_SPEC, VMEM_SPEC, VMEM_SPEC),
        scratch_shapes=[pltpu.VMEM(small, jnp.float32)] * 4
        + [pltpu.SemaphoreType.DMA],
        input_output_aliases={2 + len(operands): 0} if chained else {},
        name="output",
        cost_estimate=cost(part_rows, tokens, 1500),
        compiler_params=COMPILER,
    )(*place, *operands, *chained)


def place_kernel(first, share, sec, before, received, *rest):
    kept, (out, done) = rest[:-2], rest[-2:]
    rows = received.shape[0]

    def target(section, start):
        return out.at[0, pl.ds(pl.multiple_of(section * share + start, rows), rows), :]

    foreign = pltpu.make_async_copy(received, target(1 - sec[0], first), done.at[0])
    foreign.start()

    @pl.when(sec[0] == 1)
    def _():
        copies = [
            pltpu.make_async_copy(keep, target(1, k * rows), done.at[k + 1])
            for k, keep in enumerate(kept)
        ]
        for copy in copies:
            copy.start()
        for copy in copies:
            copy.wait()

    foreign.wait()


def place_call(place, half, before, received, kept):
    rows, tokens = received.shape
    return pl.pallas_call(
        functools.partial(place_kernel, half * rows, before.shape[1] // 2),
        out_shape=jax.ShapeDtypeStruct(before.shape, before.dtype),
        in_specs=[SMEM_SPEC, ANY_SPEC] + [VMEM_SPEC] * (1 + len(kept)),
        out_specs=ANY_SPEC,
        scratch_shapes=[pltpu.SemaphoreType.DMA((1 + len(kept),))],
        input_output_aliases={1: 0},
        name="placing",
        cost_estimate=cost(rows, tokens, 2),
        compiler_params=COMPILER,
    )(place[0], before, received, *kept)


def edge_kernel(first, gates, inputs, edge, gate_tail, input_tail, arrival):
    share, window = edge.shape
    rows = pl.ds(first, share)
    tail = pl.ds(inputs.shape[1] - window, window)
    pairs = [(gates.at[0, 1, rows, tail], gate_tail), (inputs.at[rows, tail], input_tail)]
    copies = [
        pltpu.make_async_copy(source, target, arrival.at[k])
        for k, (source, target) in enumerate(pairs)
    ]
    for copy in copies:
        copy.start()
    for copy in copies:
        copy.wait()
    edge[...] = gate_tail[...] * input_tail[...]


def edge_call(gate_streams, inputs, window, share, half):
    return pl.pallas_call(
        functools.partial(edge_kernel, half * share),
        out_shape=jax.ShapeDtypeStruct((share, window), jnp.bfloat16),
        in_specs=[ANY_SPEC] * 2,
        out_specs=VMEM_SPEC,
        scratch_shapes=[pltpu.VMEM((share, window), jnp.bfloat16)] * 2
        + [pltpu.SemaphoreType.DMA((2,))],
        name="edge",
        cost_estimate=cost(share, window, 2),
        compiler_params=COMPILER,
    )(*parked(gate_streams, inputs))


def ring(value, axis, by):
    peers = lax.axis_size(axis)
    return lax.ppermute(value, axis, [(i, (i + by) % peers) for i in range(peers)])


def met(value, by):
    peers = lax.axis_size("tok")
    return lax.ppermute(value, "tok", [(i, i ^ by) for i in range(peers)])


def edge_to(value, section):
    peers = lax.axis_size("tok")
    pairs = [(i, section * peers + (i + 1) % peers) for i in range(peers)]
    pairs += [(peers + i, (1 - section) * peers + i) for i in range(peers)]
    return lax.ppermute(value, ("section", "tok"), pairs)


def on_device(gate_streams, inputs, medium_taps, residues, decay_rates):
    channels, _ = inputs.shape
    share = channels // 2
    window = medium_taps.shape[1]
    modes = decay_rates.shape[1]
    place = tuple(
        lax.axis_index(axis).astype(jnp.int32).reshape(1) for axis in ("section", "tok")
    )
    halos = []
    for half in range(2):
        edge = edge_call(gate_streams, inputs, window, share, half)
        halos.append(edge_to(edge, half))
    swapped = ring(gate_streams[0], "section", 1)
    forward, inverse = fourier_tables(window)
    turned, back, doubled = turned_tables(window)
    tables = [*forward, *inverse, *split_pair(turned), split_pair(back)[0]]
    high, low = split_pair(doubled)
    tables += [jnp.concatenate([high, high], axis=0), low]
    built, own, tables = response_call(
        place,
        decay_rates.T,
        residues.T,
        gate_streams,
        inputs,
        medium_taps,
        tables,
        window,
        share,
    )
    response, rates, scales, rising, falling = built
    gates, inputs, taps = own
    medium, signals, *specs, remote = later_call(
        place, gates, swapped, inputs, taps, tables[:4]
    )
    medium, signals, ends, total = first_call(
        place,
        gates,
        remote,
        inputs,
        halos,
        rates,
        falling,
        specs,
        tables[1:3],
        medium,
        signals,
        modes,
    )
    arrived = []
    for by in range(1, lax.axis_size("tok")):
        arrived.append(met(total, by))
    within = within_call(signals, response, tables[4:])
    result, waiting = None, []
    for half in range(HALVES):
        result, send, keep = output_call(
            place,
            half,
            gates,
            remote,
            within,
            inputs,
            medium,
            rates,
            scales,
            rising,
            ends,
            arrived,
            result,
        )
        waiting.append((ring(send, "section", 1), keep))
    kept = [keep for _, keep in waiting]
    for half, (received, _) in enumerate(waiting):
        result = place_call(place, half, result, received, [] if half else kept)
    return result


def solution(mesh):
    placed = (
        P("section", None, "chan", "tok"),
        P("chan", "tok"),
        P("chan", None),
        P("chan", None),
        P("chan", None),
    )
    return jax.shard_map(
        on_device,
        mesh=mesh,
        in_specs=placed,
        out_specs=P("section", "chan", "tok"),
        check_vma=False,
    )
```

```python
import functools

import jax
import jax.numpy as jnp
import numpy as np
from jax import lax
from jax.experimental import pallas as pl
from jax.experimental.pallas import tpu as pltpu
from jax.sharding import PartitionSpec as P


ROWS = 8


def split_pair(matrix):
    high = jnp.asarray(matrix, jnp.float32).astype(jnp.bfloat16)
    low = (jnp.asarray(matrix, jnp.float32) - high.astype(jnp.float32)).astype(jnp.bfloat16)
    return high, low


def stacked(matrix, axis):
    return jnp.concatenate(split_pair(matrix), axis=axis)


def fourier_tables(window):
    size = 2 * window
    time = np.arange(window)[:, None]
    freq = np.arange(window)[None, :]
    angle = 2.0 * np.pi * ((time * freq) % size) / size
    sign = np.where(freq % 2 == 0, 1.0, -1.0)
    nyquist = np.where(time % 2 == 0, 1.0, -1.0)
    weight = np.where(freq == 0, 1.0, 2.0) / size
    forward, inverse = [], []
    for odd in range(2):
        flip = sign if odd else np.ones_like(sign)
        real = np.cos(angle) * flip
        imag = -np.sin(angle) * flip
        imag[:, :1] = nyquist
        forward.append(stacked(np.concatenate([real, imag], axis=1), 0))
        back_real = np.cos(angle) * weight * flip
        back_imag = -np.sin(angle) * weight * flip
        back_imag[:, :1] = nyquist / size
        inverse.append(stacked(np.concatenate([back_real.T, back_imag.T], axis=0), 1))
    return forward, inverse


def turned_tables(window):
    half = window // 2
    time = np.arange(window)[:, None]
    freq = 2 * np.arange(half)[None, :] + 1
    angle = np.pi * ((time * freq) % (2 * window)) / window
    real, imag = np.cos(angle), -np.sin(angle)
    zero = np.zeros_like(real)
    forward = np.concatenate(
        [
            np.concatenate([real, zero, imag, zero], axis=1),
            np.concatenate([zero, real, zero, imag], axis=1),
        ],
        axis=0,
    )
    inverse = forward.T * (2.0 / window)
    doubled = np.concatenate([real, real, imag, imag], axis=1)
    return forward, inverse, doubled


PAIR = 16
STEP = 512
HALVES = 2
COMPILER = pltpu.CompilerParams(vmem_limit_bytes=16 << 20)


def parked(*arrays):
    return [pltpu.with_memory_space_constraint(a, pltpu.HBM) for a in arrays]


def cost(share, tokens, work):
    size = share * tokens
    return pl.CostEstimate(
        flops=size * work, bytes_accessed=size * 12, transcendentals=size // 64
    )


def dot_f32(left, right):
    return jnp.dot(left, right, preferred_element_type=jnp.float32)


def dot_turned(left, right):
    return lax.dot_general(
        left, right, (((1,), (1,)), ((), ())), preferred_element_type=jnp.float32
    )


VMEM_SPEC = pl.BlockSpec(memory_space=pltpu.VMEM)
SMEM_SPEC = pl.BlockSpec(memory_space=pltpu.SMEM)
ANY_SPEC = pl.BlockSpec(memory_space=pl.ANY)


def rows_at(ref, step, i, axis=0):
    start = i * step
    if not isinstance(i, int):
        start = pl.multiple_of(start, step)
    return ref.at[(slice(None),) * axis + (pl.ds(start, step),)]


def both_gates(local, remote, section, step, i):
    mine, other = rows_at(local, step, i, 1), rows_at(remote, step, i, 1)
    return (mine, other) if section == 0 else (other, mine)


def by_section(sec, body):
    for section in range(2):
        pl.when(sec[0] == section)(functools.partial(body, section))


def lane_mask(modes):
    shape = (ROWS, ROWS * modes)
    lane = lax.broadcasted_iota(jnp.int32, shape, 1)
    return lane // modes == lax.broadcasted_iota(jnp.int32, shape, 0)


def spread(ref, group):
    return jnp.broadcast_to(ref[group : group + 1, :], (ROWS, ref.shape[1]))


def powers(slow, hop, window, first, falling):
    row = lax.broadcasted_iota(jnp.int32, slow.shape, 0).astype(jnp.float32)
    tiles = [jnp.exp(-slow * (first + (ROWS - 1 - row if falling else row)))]
    while len(tiles) < window // ROWS:
        tiles = tiles + [tile * hop for tile in tiles]
        hop = hop * hop
    if falling:
        tiles = tiles[::-1]
    return jnp.concatenate(tiles, axis=0).astype(jnp.bfloat16)


def both_powers(rates, hops, pair, window, falling):
    sides = [
        powers(spread(rates, g), spread(hops, g), window, 0.0, falling)
        for g in (2 * pair, 2 * pair + 1)
    ]
    return jnp.concatenate(sides, axis=1)


def two_sided(upper, lower):
    zero = jnp.zeros_like(upper)
    return jnp.concatenate(
        [
            jnp.concatenate([upper, zero], axis=1),
            jnp.concatenate([zero, lower], axis=1),
        ],
        axis=0,
    )


def scale_of(residues, slow):
    return residues * jnp.sqrt(1.0 - jnp.exp(-2.0 * slow))


def in_rows(ref, tall):
    _, channels = ref.shape
    tall[...] = ref[...].T
    count = channels // ROWS
    return jnp.concatenate(
        [tall[pl.ds(c, count, stride=ROWS), :] for c in range(ROWS)], axis=1
    )


def response_kernel(count, window, sec, tok, rates, residues, *rest):
    gates, inputs, taps = rest[:3]
    tables = rest[3 : 3 + count]
    out, rate_rows, scale_rows, rising, falling = rest[3 + count : 8 + count]
    own_gates, own_inputs, own_taps = rest[8 + count : 11 + count]
    own_tables = rest[11 + count : 11 + 2 * count]
    tall, hops, scales, arrival = rest[11 + 2 * count :]
    share = out.shape[0]
    step = tall.shape[0]
    modes = rates.shape[0]
    first = pl.multiple_of(sec[0] * share, share)
    mine = pl.ds(first, share)
    pairs = [(gates.at[0, :, mine, :], own_gates)]
    pairs += [(inputs.at[mine, :], own_inputs), (taps.at[mine, :], own_taps)]
    pairs += list(zip(tables, own_tables))
    copies = [
        pltpu.make_async_copy(source, target, arrival.at[k])
        for k, (source, target) in enumerate(pairs)
    ]
    for copy in copies:
        copy.start()
    mask = lane_mask(modes)

    @pl.loop(0, share // step)
    def _(i):
        lanes = pl.ds(pl.multiple_of(first + i * step, step), step)
        slow = in_rows(rates.at[:, lanes], tall)
        scale = scale_of(in_rows(residues.at[:, lanes], tall), slow)
        small = step // ROWS
        own_rates = rows_at(rate_rows, small, i)
        own_rates[...] = slow
        rows_at(scale_rows, small, i)[...] = scale
        hops[...] = jnp.exp(-slow * ROWS)
        scales[...] = scale / (1.0 + jnp.exp(-slow * window))
        up, down = rows_at(rising, step // PAIR, i), rows_at(falling, step // PAIR, i)
        own_out = rows_at(out, step, i)
        for pair in range(step // PAIR):
            both = two_sided(
                jnp.where(mask, spread(scales, 2 * pair), 0.0),
                jnp.where(mask, spread(scales, 2 * pair + 1), 0.0),
            )
            high = both.astype(jnp.bfloat16).astype(jnp.float32)
            both = jnp.concatenate([high, both - high], axis=0).astype(jnp.bfloat16)
            table = both_powers(own_rates, hops, pair, window, False)
            up[pair] = table
            down[pair] = both_powers(own_rates, hops, pair, window, True)
            found = dot_turned(both, table)
            out_rows = pl.ds(pair * PAIR, PAIR)
            own_out[out_rows, :] = found[:PAIR] + found[PAIR:]

    for copy in copies:
        copy.wait()


def response_call(place, rates, residues, gates, inputs, taps, tables, window, share):
    tokens = inputs.shape[1]
    step = min(STEP, share)
    modes = rates.shape[0]
    lanes = ROWS * modes
    small = (step // ROWS, lanes)
    shape = lambda dims, kind=jnp.float32: jax.ShapeDtypeStruct(dims, kind)
    power_shape = shape((share // PAIR, window, 2 * lanes), jnp.bfloat16)
    outs = [shape((share, window))] + [shape((share // ROWS, lanes))] * 2
    outs += [power_shape] * 2
    outs += [
        shape((2, share, tokens), gates.dtype),
        shape((share, tokens), inputs.dtype),
        shape((share, window), taps.dtype),
    ]
    outs += [shape(t.shape, t.dtype) for t in tables]
    staged = 3 + len(tables)
    found = pl.pallas_call(
        functools.partial(response_kernel, len(tables), window),
        out_shape=tuple(outs),
        in_specs=[SMEM_SPEC] * 2 + [VMEM_SPEC] * 2 + [ANY_SPEC] * staged,
        out_specs=(VMEM_SPEC,) * len(outs),
        scratch_shapes=[
            pltpu.VMEM((step, modes), jnp.float32),
            pltpu.VMEM(small, jnp.float32),
            pltpu.VMEM(small, jnp.float32),
            pltpu.SemaphoreType.DMA((staged,)),
        ],
        name="response",
        cost_estimate=cost(share, 4 * window, 900),
        compiler_params=COMPILER,
    )(*place, rates, residues, *parked(gates, inputs, taps, *tables))
    return found[:5], found[5:8], found[8:]


def products(members, tap_spec):
    window = tap_spec.shape[1] // 2
    real, packed = tap_spec[:, :window], tap_spec[:, window:]
    lane = lax.broadcasted_iota(jnp.int32, real.shape, 1)
    real_b = jnp.where(lane == 0, packed, real)
    imag = jnp.where(lane == 0, 0.0, packed)
    found = []
    for mixed in members:
        a, b = mixed[:, :window], mixed[:, window:]
        found.append(
            jnp.concatenate([a * real - b * imag, a * imag + b * real_b], axis=1).astype(
                jnp.bfloat16
            )
        )
    return found


def doubled_spectrum(members, table):
    rows = jnp.concatenate(members, axis=0)
    found = dot_f32(jnp.concatenate([rows, rows], axis=1), table[...])
    size = members[0].shape[0]
    return [found[k * size : (k + 1) * size] for k in range(len(members))]


def finish_medium(members, table, gates_out, gates_in, streams, targets):
    found = dot_f32(jnp.concatenate(members, axis=0), table[...])
    size, window = streams[0].shape
    signals = []
    for k in range(len(members)):
        rows = slice(k * size, (k + 1) * size)
        medium = found[rows, :window] + found[rows, window:]
        gated = (gates_out[k].astype(jnp.float32) * medium).astype(jnp.bfloat16)
        targets[k][...] = gated
        stream = streams[k].astype(jnp.float32) + gated.astype(jnp.float32)
        signals.append((gates_in[k].astype(jnp.float32) * stream).astype(jnp.bfloat16))
    return signals


def end_states(signals, powers_of_pair, pair, modes, mask):
    rows = slice(pair * PAIR, (pair + 1) * PAIR)
    lanes = ROWS * modes
    left = jnp.concatenate([signal[rows] for signal in signals], axis=0)
    found = dot_f32(left, powers_of_pair)
    sides = []
    for side in range(2):
        tops = [k * PAIR + side * ROWS for k in range(len(signals))]
        sides.append(
            [
                jnp.where(mask, found[top : top + ROWS, side * lanes : (side + 1) * lanes], 0.0)
                for top in tops
            ]
        )
    return sides


def later_kernel(
    step,
    sec,
    tok,
    local_all,
    remote_all,
    inputs_all,
    taps_all,
    fwd_even,
    fwd_odd,
    inv_even,
    inv_odd,
    medium_all,
    signals_all,
    tap_spec_all,
    edge_spec_all,
):
    share, tokens = inputs_all.shape
    window = taps_all.shape[1]
    blocks = tokens // window
    parts = [slice(b * window, (b + 1) * window) for b in range(blocks)]

    def chunk(section, i):
        first, second = both_gates(local_all, remote_all, section, step, i)
        inputs = rows_at(inputs_all, step, i)
        medium_out, signals = rows_at(medium_all, step, i), rows_at(signals_all, step, i)
        sources = [first[1, :, part] * inputs[:, part] for part in parts]
        tap_rows = rows_at(taps_all, step, i)[...]
        tap_spec, *even = doubled_spectrum([tap_rows] + sources[0::2], fwd_even)
        odd = doubled_spectrum(sources[1::2], fwd_odd)
        in_order = [None] * blocks
        in_order[0::2] = even
        in_order[1::2] = odd
        rows_at(tap_spec_all, step, i)[...] = tap_spec
        rows_at(edge_spec_all, step, i)[...] = in_order[0]
        mixed = products([in_order[b - 1] + in_order[b] for b in range(1, blocks)], tap_spec)
        for parity, table in enumerate((inv_even, inv_odd)):
            chosen = [b for b in range(1, blocks) if b % 2 == parity]
            if not chosen:
                continue
            found = finish_medium(
                [mixed[b - 1] for b in chosen],
                table,
                [first[0, :, parts[b]] for b in chosen],
                [second[1, :, parts[b]] for b in chosen],
                [inputs[:, parts[b]] for b in chosen],
                [medium_out.at[:, parts[b]] for b in chosen],
            )
            for b, signal in zip(chosen, found):
                signals[:, parts[b]] = signal

    def body(section):
        pl.loop(0, share // step)(functools.partial(chunk, section))

    by_section(sec, body)


def later_call(place, gates, remote, inputs, taps, tables):
    share, tokens = inputs.shape
    window = taps.shape[1]
    operands = [gates, remote, inputs, taps, *tables]
    spec = jax.ShapeDtypeStruct((share, 2 * window), jnp.float32)
    wide = jax.ShapeDtypeStruct((share, tokens), jnp.bfloat16)
    return pl.pallas_call(
        functools.partial(later_kernel, min(STEP, share)),
        out_shape=(wide, wide, spec, spec),
        in_specs=[SMEM_SPEC] * 2 + [VMEM_SPEC] * len(operands),
        out_specs=(VMEM_SPEC,) * 4,
        name="later",
        cost_estimate=cost(share, tokens, 1500),
        compiler_params=COMPILER,
    )(*place, *operands)


def first_kernel(
    modes,
    step,
    sec,
    tok,
    local_all,
    remote_all,
    inputs_all,
    halo_low,
    halo_high,
    rates,
    falling_all,
    tap_spec_all,
    edge_spec_all,
    fwd_odd,
    inv_even,
    medium_before,
    signals_before,
    medium_all,
    signals_all,
    ends_all,
    total_all,
    leaps_all,
):
    share = inputs_all.shape[0]
    window = tap_spec_all.shape[1] // 2
    part = slice(0, window)
    mask = lane_mask(modes)
    leaps_all[...] = jnp.exp(-rates[...] * window)

    def chunk(section, i):
        first, second = both_gates(local_all, remote_all, section, step, i)
        halo = rows_at(halo_low if section == 0 else halo_high, step, i)
        leaps = rows_at(leaps_all, step // ROWS, i)
        falling = rows_at(falling_all, step // PAIR, i)
        ends = rows_at(ends_all, step, i, 1)
        started = jnp.where(tok[0] > 0, 1.0, 0.0).astype(jnp.bfloat16)
        (before,) = doubled_spectrum([halo[...] * started], fwd_odd)
        mixed = products(
            [before + rows_at(edge_spec_all, step, i)[...]],
            rows_at(tap_spec_all, step, i)[...],
        )
        (signal,) = finish_medium(
            mixed,
            inv_even,
            [first[0, :, part]],
            [second[1, :, part]],
            [rows_at(inputs_all, step, i)[:, part]],
            [rows_at(medium_all, step, i).at[:, part]],
        )
        signals = rows_at(signals_all, step, i)
        signals[:, part] = signal
        members = [signal] + [
            signals[:, b * window : (b + 1) * window] for b in range(1, ends.shape[0])
        ]
        sums = []
        for pair in range(step // PAIR):
            sides = end_states(members, falling[pair], pair, modes, mask)
            for side, found in enumerate(sides):
                at = pair * PAIR + side * ROWS
                leap = spread(leaps, 2 * pair + side)
                state = None
                for b, end in enumerate(found):
                    ends[b, at : at + ROWS, :] = end
                    state = end if state is None else state * leap + end
                sums.append(jnp.sum(state, axis=0, keepdims=True))
        total = rows_at(total_all, step // ROWS, i)
        total[...] = jnp.concatenate(sums, axis=0).astype(total.dtype)

    def body(section):
        pl.loop(0, share // step)(functools.partial(chunk, section))

    by_section(sec, body)


def first_call(
    place, gates, swapped, inputs, halos, rates, falling, specs, tables, medium, signals, modes
):
    share, tokens = inputs.shape
    window = halos[0].shape[1]
    lanes = ROWS * modes
    small = (share // ROWS, lanes)
    operands = [gates, swapped, inputs, *halos, rates, falling, *specs, *tables, medium, signals]
    return pl.pallas_call(
        functools.partial(first_kernel, modes, min(2 * STEP, share)),
        out_shape=(
            jax.ShapeDtypeStruct(medium.shape, medium.dtype),
            jax.ShapeDtypeStruct(signals.shape, signals.dtype),
            jax.ShapeDtypeStruct((tokens // window, share, lanes), jnp.float32),
            jax.ShapeDtypeStruct(small, jnp.bfloat16),
        ),
        in_specs=[SMEM_SPEC] * 2 + [VMEM_SPEC] * len(operands),
        out_specs=(VMEM_SPEC,) * 4,
        scratch_shapes=[pltpu.VMEM(small, jnp.float32)],
        input_output_aliases={len(operands): 0, len(operands) + 1: 1},
        name="first",
        cost_estimate=cost(share, tokens, 500),
        compiler_params=COMPILER,
    )(*place, *operands)


def within_kernel(
    step,
    signals_all,
    response_all,
    fwd_h,
    fwd_l,
    inverse,
    table_h,
    table_l,
    out_all,
):
    share, tokens = signals_all.shape
    size = fwd_h.shape[0]
    half = size // 2

    def chunk(i):
        signals = rows_at(signals_all, step, i)
        taps, out = rows_at(response_all, step, i)[...], rows_at(out_all, step, i)
        high = taps.astype(jnp.bfloat16)
        low = (taps - high.astype(jnp.float32)).astype(jnp.bfloat16)
        response = dot_f32(jnp.concatenate([high, low], axis=1), table_h[...]) + dot_f32(
            high, table_l[...]
        )
        channels = step
        real, imag = response[:, :half], response[:, half:]
        parts = [slice(k * size, (k + 1) * size) for k in range(tokens // size)]
        signal = jnp.concatenate([signals[:, part] for part in parts], axis=0)
        spec = dot_f32(signal, fwd_h[...]) + dot_f32(signal, fwd_l[...])
        filtered = []
        for k in range(len(parts)):
            rows = slice(k * channels, (k + 1) * channels)
            a, b = spec[rows, :half], spec[rows, half:]
            filtered.append(
                jnp.concatenate([a * real - b * imag, a * imag + b * real], axis=1).astype(
                    jnp.bfloat16
                )
            )
        found = dot_f32(jnp.concatenate(filtered, axis=0), inverse[...])
        for k, part in enumerate(parts):
            out[:, part] = found[k * channels : (k + 1) * channels]

    pl.loop(0, share // step)(chunk)


def within_call(signals, response, tables):
    share, tokens = signals.shape
    operands = [signals, response, *tables]
    return pl.pallas_call(
        functools.partial(within_kernel, min(2 * STEP, share)),
        out_shape=jax.ShapeDtypeStruct((share, tokens), jnp.float32),
        in_specs=[VMEM_SPEC] * len(operands),
        out_specs=VMEM_SPEC,
        name="within",
        cost_estimate=cost(share, tokens, 1500),
        compiler_params=COMPILER,
    )(*operands)


def output_kernel(
    count,
    modes,
    window,
    step,
    first,
    share,
    sec,
    tok,
    local_all,
    remote_all,
    within_all,
    inputs_all,
    medium_all,
    rates,
    scale_rows,
    rising_all,
    ends_all,
    *rest,
):
    arrived = rest[:count]
    (result, send, keep, leaps_all, scales_all, shares_all, starts_all, done) = rest[-8:]
    part_rows, tokens = send.shape
    base = first // step
    groups = pl.ds(first // ROWS, part_rows // ROWS)
    blocks = tokens // window
    mask = lane_mask(modes)
    slow = rates[groups, :]
    leap_all = jnp.exp(-slow * window)
    scale_all = scale_rows[groups, :] * jnp.exp(-slow)
    leaps_all[...] = leap_all
    scales_all[...] = scale_all
    shares_all[...] = scale_all / (1.0 + leap_all)
    entering = jnp.zeros_like(slow)
    for k in range(count):
        gap = tok[0] - (tok[0] ^ (k + 1))
        known = jnp.where(gap > 0, 1.0, 0.0)
        distance = (tokens * jnp.maximum(gap - 1, 0)).astype(jnp.float32)
        entering = entering + arrived[k][groups, :].astype(jnp.float32) * (
            jnp.exp(-slow * distance) * known
        )
    starts_all[...] = entering

    def chunk(section, out_all, i):
        out = rows_at(out_all, step, i)
        at_all = base + i
        gate_out = both_gates(local_all, remote_all, section, step, at_all)[1].at[0]
        inputs = rows_at(inputs_all, step, at_all)
        gated_medium = rows_at(medium_all, step, at_all)
        within = rows_at(within_all, step, at_all)
        ends = rows_at(ends_all, step, at_all, 1)
        rising = rows_at(rising_all, step // PAIR, at_all)
        small = step // ROWS
        leaps, scales = rows_at(leaps_all, small, i), rows_at(scales_all, small, i)
        shares, starts = rows_at(shares_all, small, i), rows_at(starts_all, small, i)
        channels = step
        for pair in range(channels // PAIR):
            rows = slice(pair * PAIR, (pair + 1) * PAIR)
            sides = []
            for side in range(2):
                group = 2 * pair + side
                leap, scale = spread(leaps, group), spread(scales, group)
                portion = spread(shares, group)
                state = jnp.where(mask, spread(starts, group), 0.0)
                at = pair * PAIR + side * ROWS
                lefts = []
                for b in range(blocks):
                    end = ends[b, at : at + ROWS, :]
                    lefts.append(state * scale + end * portion)
                    state = state * leap + end
                sides.append(lefts)
            left = jnp.concatenate(
                [two_sided(upper, lower) for upper, lower in zip(*sides)], axis=0
            ).astype(jnp.bfloat16)
            across = dot_turned(left, rising[pair])
            for b in range(blocks):
                part = slice(b * window, (b + 1) * window)
                stream = inputs[rows, part].astype(jnp.float32) + gated_medium[
                    rows, part
                ].astype(jnp.float32)
                long_out = within[rows, part] + across[b * PAIR : (b + 1) * PAIR]
                gate = gate_out[rows, part].astype(jnp.float32)
                out[rows, part] = (stream + gate * long_out).astype(jnp.bfloat16)

    def body(section):
        target = result.at[0, pl.ds(section * share + first, part_rows), :]
        source = medium_all.at[pl.ds(first, part_rows), :]
        copy = pltpu.make_async_copy(source, send if section else target, done)
        copy.start()
        pl.loop(0, part_rows // step)(
            functools.partial(chunk, section, keep if section else send)
        )
        copy.wait()

    by_section(sec, body)


def output_call(
    place, half, gates, swapped, within, inputs, medium, rates, scales, rising, ends, arrived, before
):
    share, tokens = medium.shape
    lanes = rates.shape[1]
    window = rising.shape[1]
    part_rows = share // HALVES
    step = min(STEP, part_rows)
    small = (part_rows // ROWS, lanes)
    operands = [gates, swapped, within, inputs, medium, rates, scales, rising, ends, *arrived]
    result = jax.ShapeDtypeStruct((1, 2 * share, tokens), jnp.bfloat16)
    chained = [] if before is None else [before]
    return pl.pallas_call(
        functools.partial(
            output_kernel,
            len(arrived),
            lanes // ROWS,
            window,
            step,
            half * part_rows,
            share,
        ),
        out_shape=(result,) + (jax.ShapeDtypeStruct((part_rows, tokens), jnp.bfloat16),) * 2,
        in_specs=[SMEM_SPEC] * 2 + [VMEM_SPEC] * len(operands) + [ANY_SPEC] * len(chained),
        out_specs=(ANY_SPEC, VMEM_SPEC, VMEM_SPEC),
        scratch_shapes=[pltpu.VMEM(small, jnp.float32)] * 4
        + [pltpu.SemaphoreType.DMA],
        input_output_aliases={2 + len(operands): 0} if chained else {},
        name="output",
        cost_estimate=cost(part_rows, tokens, 1500),
        compiler_params=COMPILER,
    )(*place, *operands, *chained)


def place_kernel(first, share, sec, before, received, *rest):
    kept, (out, done) = rest[:-2], rest[-2:]
    rows = received.shape[0]

    def target(section, start):
        return out.at[0, pl.ds(pl.multiple_of(section * share + start, rows), rows), :]

    foreign = pltpu.make_async_copy(received, target(1 - sec[0], first), done.at[0])
    foreign.start()

    @pl.when(sec[0] == 1)
    def _():
        copies = [
            pltpu.make_async_copy(keep, target(1, k * rows), done.at[k + 1])
            for k, keep in enumerate(kept)
        ]
        for copy in copies:
            copy.start()
        for copy in copies:
            copy.wait()

    foreign.wait()


def place_call(place, half, before, received, kept):
    rows, tokens = received.shape
    return pl.pallas_call(
        functools.partial(place_kernel, half * rows, before.shape[1] // 2),
        out_shape=jax.ShapeDtypeStruct(before.shape, before.dtype),
        in_specs=[SMEM_SPEC, ANY_SPEC] + [VMEM_SPEC] * (1 + len(kept)),
        out_specs=ANY_SPEC,
        scratch_shapes=[pltpu.SemaphoreType.DMA((1 + len(kept),))],
        input_output_aliases={1: 0},
        name="placing",
        cost_estimate=cost(rows, tokens, 2),
        compiler_params=COMPILER,
    )(place[0], before, received, *kept)


def lend_kernel(sec, tok, gates, inputs, lent, low, high, gate_tail, input_tail, arrival):
    share, window = low.shape
    tokens = inputs.shape[1]
    tail = pl.ds(tokens - window, window)
    other = pl.ds(pl.multiple_of((1 - sec[0]) * share, share), share)
    copies = [
        pltpu.make_async_copy(source, target, arrival.at[k])
        for k, (source, target) in enumerate(
            [
                (gates.at[0, 1, :, tail], gate_tail),
                (inputs.at[:, tail], input_tail),
                (gates.at[0, :, other, :], lent),
            ]
        )
    ]
    for copy in copies:
        copy.start()
    copies[0].wait()
    copies[1].wait()
    low[...] = gate_tail[:share, :] * input_tail[:share, :]
    high[...] = gate_tail[share:, :] * input_tail[share:, :]
    copies[2].wait()


def lend_call(place, gate_streams, inputs, window, share):
    channels, tokens = inputs.shape
    edge = jax.ShapeDtypeStruct((share, window), jnp.bfloat16)
    return pl.pallas_call(
        lend_kernel,
        out_shape=(jax.ShapeDtypeStruct((2, share, tokens), jnp.bfloat16), edge, edge),
        in_specs=[SMEM_SPEC] * 2 + [ANY_SPEC] * 2,
        out_specs=(VMEM_SPEC,) * 3,
        scratch_shapes=[pltpu.VMEM((channels, window), jnp.bfloat16)] * 2
        + [pltpu.SemaphoreType.DMA((3,))],
        name="lend",
        cost_estimate=cost(share, tokens, 2),
        compiler_params=COMPILER,
    )(*place, *parked(gate_streams, inputs))


def ring(value, axis, by):
    peers = lax.axis_size(axis)
    return lax.ppermute(value, axis, [(i, (i + by) % peers) for i in range(peers)])


def met(value, by):
    peers = lax.axis_size("tok")
    return lax.ppermute(value, "tok", [(i, i ^ by) for i in range(peers)])


def edge_to(value, section):
    peers = lax.axis_size("tok")
    pairs = [(i, section * peers + (i + 1) % peers) for i in range(peers)]
    pairs += [(peers + i, (1 - section) * peers + i) for i in range(peers)]
    return lax.ppermute(value, ("section", "tok"), pairs)


def on_device(gate_streams, inputs, medium_taps, residues, decay_rates):
    channels, _ = inputs.shape
    share = channels // 2
    window = medium_taps.shape[1]
    modes = decay_rates.shape[1]
    place = tuple(
        lax.axis_index(axis).astype(jnp.int32).reshape(1) for axis in ("section", "tok")
    )
    lent, *edges = lend_call(place, gate_streams, inputs, window, share)
    halos = []
    for half in range(2):
        halos.append(edge_to(edges[half], half))
    remote = ring(lent, "section", 1)
    forward, inverse = fourier_tables(window)
    turned, back, doubled = turned_tables(window)
    tables = [*forward, *inverse, *split_pair(turned), split_pair(back)[0]]
    high, low = split_pair(doubled)
    tables += [jnp.concatenate([high, high], axis=0), low]
    built, own, tables = response_call(
        place,
        decay_rates.T,
        residues.T,
        gate_streams,
        inputs,
        medium_taps,
        tables,
        window,
        share,
    )
    response, rates, scales, rising, falling = built
    gates, inputs, taps = own
    medium, signals, *specs = later_call(place, gates, remote, inputs, taps, tables[:4])
    medium, signals, ends, total = first_call(
        place,
        gates,
        remote,
        inputs,
        halos,
        rates,
        falling,
        specs,
        tables[1:3],
        medium,
        signals,
        modes,
    )
    arrived = []
    for by in range(1, lax.axis_size("tok")):
        arrived.append(met(total, by))
    within = within_call(signals, response, tables[4:])
    result, waiting = None, []
    for half in range(HALVES):
        result, send, keep = output_call(
            place,
            half,
            gates,
            remote,
            within,
            inputs,
            medium,
            rates,
            scales,
            rising,
            ends,
            arrived,
            result,
        )
        waiting.append((ring(send, "section", 1), keep))
    kept = [keep for _, keep in waiting]
    for half, (received, _) in enumerate(waiting):
        result = place_call(place, half, result, received, [] if half else kept)
    return result


def solution(mesh):
    placed = (
        P("section", None, "chan", "tok"),
        P("chan", "tok"),
        P("chan", None),
        P("chan", None),
        P("chan", None),
    )
    return jax.shard_map(
        on_device,
        mesh=mesh,
        in_specs=placed,
        out_specs=P("section", "chan", "tok"),
        check_vma=False,
    )
```

```python
import functools

import jax
import jax.numpy as jnp
import numpy as np
from jax import lax
from jax.experimental import pallas as pl
from jax.experimental.pallas import tpu as pltpu
from jax.sharding import PartitionSpec as P


ROWS = 8


def split_pair(matrix):
    high = jnp.asarray(matrix, jnp.float32).astype(jnp.bfloat16)
    low = (jnp.asarray(matrix, jnp.float32) - high.astype(jnp.float32)).astype(jnp.bfloat16)
    return high, low


def stacked(matrix, axis):
    return jnp.concatenate(split_pair(matrix), axis=axis)


def fourier_tables(window):
    size = 2 * window
    time = np.arange(window)[:, None]
    freq = np.arange(window)[None, :]
    angle = 2.0 * np.pi * ((time * freq) % size) / size
    sign = np.where(freq % 2 == 0, 1.0, -1.0)
    nyquist = np.where(time % 2 == 0, 1.0, -1.0)
    weight = np.where(freq == 0, 1.0, 2.0) / size
    forward, inverse = [], []
    for odd in range(2):
        flip = sign if odd else np.ones_like(sign)
        real = np.cos(angle) * flip
        imag = -np.sin(angle) * flip
        imag[:, :1] = nyquist
        forward.append(stacked(np.concatenate([real, imag], axis=1), 0))
        back_real = np.cos(angle) * weight * flip
        back_imag = -np.sin(angle) * weight * flip
        back_imag[:, :1] = nyquist / size
        inverse.append(stacked(np.concatenate([back_real.T, back_imag.T], axis=0), 1))
    return forward, inverse


def turned_tables(window):
    half = window // 2
    time = np.arange(window)[:, None]
    freq = 2 * np.arange(half)[None, :] + 1
    angle = np.pi * ((time * freq) % (2 * window)) / window
    real, imag = np.cos(angle), -np.sin(angle)
    zero = np.zeros_like(real)
    forward = np.concatenate(
        [
            np.concatenate([real, zero, imag, zero], axis=1),
            np.concatenate([zero, real, zero, imag], axis=1),
        ],
        axis=0,
    )
    inverse = forward.T * (2.0 / window)
    doubled = np.concatenate([real, real, imag, imag], axis=1)
    return forward, inverse, doubled


PAIR = 16
STEP = 512
HALVES = 2
COMPILER = pltpu.CompilerParams(vmem_limit_bytes=16 << 20)


def parked(*arrays):
    return [pltpu.with_memory_space_constraint(a, pltpu.HBM) for a in arrays]


def cost(share, tokens, work):
    size = share * tokens
    return pl.CostEstimate(
        flops=size * work, bytes_accessed=size * 12, transcendentals=size // 64
    )


def dot_f32(left, right):
    return jnp.dot(left, right, preferred_element_type=jnp.float32)


def dot_turned(left, right):
    return lax.dot_general(
        left, right, (((1,), (1,)), ((), ())), preferred_element_type=jnp.float32
    )


VMEM_SPEC = pl.BlockSpec(memory_space=pltpu.VMEM)
SMEM_SPEC = pl.BlockSpec(memory_space=pltpu.SMEM)
ANY_SPEC = pl.BlockSpec(memory_space=pl.ANY)


def rows_at(ref, step, i, axis=0):
    start = i * step
    if not isinstance(i, int):
        start = pl.multiple_of(start, step)
    return ref.at[(slice(None),) * axis + (pl.ds(start, step),)]


def both_gates(local, remote, section, step, i):
    mine, other = rows_at(local, step, i, 1), rows_at(remote, step, i, 1)
    return (mine, other) if section == 0 else (other, mine)


def by_section(sec, body):
    for section in range(2):
        pl.when(sec[0] == section)(functools.partial(body, section))


def lane_mask(modes):
    shape = (ROWS, ROWS * modes)
    lane = lax.broadcasted_iota(jnp.int32, shape, 1)
    return lane // modes == lax.broadcasted_iota(jnp.int32, shape, 0)


def spread(ref, group):
    return jnp.broadcast_to(ref[group : group + 1, :], (ROWS, ref.shape[1]))


def powers(slow, hop, window, first, falling):
    row = lax.broadcasted_iota(jnp.int32, slow.shape, 0).astype(jnp.float32)
    tiles = [jnp.exp(-slow * (first + (ROWS - 1 - row if falling else row)))]
    while len(tiles) < window // ROWS:
        tiles = tiles + [tile * hop for tile in tiles]
        hop = hop * hop
    if falling:
        tiles = tiles[::-1]
    return jnp.concatenate(tiles, axis=0).astype(jnp.bfloat16)


def both_powers(rates, hops, pair, window, falling):
    sides = [
        powers(spread(rates, g), spread(hops, g), window, 0.0, falling)
        for g in (2 * pair, 2 * pair + 1)
    ]
    return jnp.concatenate(sides, axis=1)


def two_sided(upper, lower):
    zero = jnp.zeros_like(upper)
    return jnp.concatenate(
        [
            jnp.concatenate([upper, zero], axis=1),
            jnp.concatenate([zero, lower], axis=1),
        ],
        axis=0,
    )


def scale_of(residues, slow):
    return residues * jnp.sqrt(1.0 - jnp.exp(-2.0 * slow))


def in_rows(ref, tall):
    _, channels = ref.shape
    tall[...] = ref[...].T
    count = channels // ROWS
    return jnp.concatenate(
        [tall[pl.ds(c, count, stride=ROWS), :] for c in range(ROWS)], axis=1
    )


def response_kernel(count, window, sec, tok, rates, residues, *rest):
    gates, inputs, taps = rest[:3]
    tables = rest[3 : 3 + count]
    out, rate_rows, scale_rows, rising, falling = rest[3 + count : 8 + count]
    own_gates, own_inputs, own_taps = rest[8 + count : 11 + count]
    own_tables = rest[11 + count : 11 + 2 * count]
    tall, hops, scales, arrival = rest[11 + 2 * count :]
    share = out.shape[0]
    step = tall.shape[0]
    modes = rates.shape[0]
    first = pl.multiple_of(sec[0] * share, share)
    mine = pl.ds(first, share)
    pairs = [(gates.at[0, :, mine, :], own_gates)]
    pairs += [(inputs.at[mine, :], own_inputs), (taps.at[mine, :], own_taps)]
    pairs += list(zip(tables, own_tables))
    copies = [
        pltpu.make_async_copy(source, target, arrival.at[k])
        for k, (source, target) in enumerate(pairs)
    ]
    for copy in copies:
        copy.start()
    mask = lane_mask(modes)

    @pl.loop(0, share // step)
    def _(i):
        lanes = pl.ds(pl.multiple_of(first + i * step, step), step)
        slow = in_rows(rates.at[:, lanes], tall)
        scale = scale_of(in_rows(residues.at[:, lanes], tall), slow)
        small = step // ROWS
        own_rates = rows_at(rate_rows, small, i)
        own_rates[...] = slow
        rows_at(scale_rows, small, i)[...] = scale
        hops[...] = jnp.exp(-slow * ROWS)
        scales[...] = scale / (1.0 + jnp.exp(-slow * window))
        up, down = rows_at(rising, step // PAIR, i), rows_at(falling, step // PAIR, i)
        own_out = rows_at(out, step, i)
        for pair in range(step // PAIR):
            both = two_sided(
                jnp.where(mask, spread(scales, 2 * pair), 0.0),
                jnp.where(mask, spread(scales, 2 * pair + 1), 0.0),
            )
            high = both.astype(jnp.bfloat16).astype(jnp.float32)
            both = jnp.concatenate([high, both - high], axis=0).astype(jnp.bfloat16)
            table = both_powers(own_rates, hops, pair, window, False)
            up[pair] = table
            down[pair] = both_powers(own_rates, hops, pair, window, True)
            found = dot_turned(both, table)
            out_rows = pl.ds(pair * PAIR, PAIR)
            own_out[out_rows, :] = found[:PAIR] + found[PAIR:]

    for copy in copies:
        copy.wait()


def response_call(place, rates, residues, gates, inputs, taps, tables, window, share):
    tokens = inputs.shape[1]
    step = min(STEP, share)
    modes = rates.shape[0]
    lanes = ROWS * modes
    small = (step // ROWS, lanes)
    shape = lambda dims, kind=jnp.float32: jax.ShapeDtypeStruct(dims, kind)
    power_shape = shape((share // PAIR, window, 2 * lanes), jnp.bfloat16)
    outs = [shape((share, window))] + [shape((share // ROWS, lanes))] * 2
    outs += [power_shape] * 2
    outs += [
        shape((2, share, tokens), gates.dtype),
        shape((share, tokens), inputs.dtype),
        shape((share, window), taps.dtype),
    ]
    outs += [shape(t.shape, t.dtype) for t in tables]
    staged = 3 + len(tables)
    found = pl.pallas_call(
        functools.partial(response_kernel, len(tables), window),
        out_shape=tuple(outs),
        in_specs=[SMEM_SPEC] * 2 + [VMEM_SPEC] * 2 + [ANY_SPEC] * staged,
        out_specs=(VMEM_SPEC,) * len(outs),
        scratch_shapes=[
            pltpu.VMEM((step, modes), jnp.float32),
            pltpu.VMEM(small, jnp.float32),
            pltpu.VMEM(small, jnp.float32),
            pltpu.SemaphoreType.DMA((staged,)),
        ],
        name="response",
        cost_estimate=cost(share, 4 * window, 900),
        compiler_params=COMPILER,
    )(*place, rates, residues, *parked(gates, inputs, taps, *tables))
    return found[:5], found[5:8], found[8:]


def products(members, tap_spec):
    window = tap_spec.shape[1] // 2
    real, packed = tap_spec[:, :window], tap_spec[:, window:]
    lane = lax.broadcasted_iota(jnp.int32, real.shape, 1)
    real_b = jnp.where(lane == 0, packed, real)
    imag = jnp.where(lane == 0, 0.0, packed)
    found = []
    for mixed in members:
        a, b = mixed[:, :window], mixed[:, window:]
        found.append(
            jnp.concatenate([a * real - b * imag, a * imag + b * real_b], axis=1).astype(
                jnp.bfloat16
            )
        )
    return found


def doubled_spectrum(members, table):
    rows = jnp.concatenate(members, axis=0)
    found = dot_f32(jnp.concatenate([rows, rows], axis=1), table[...])
    size = members[0].shape[0]
    return [found[k * size : (k + 1) * size] for k in range(len(members))]


def finish_medium(members, table, gates_out, gates_in, streams, targets):
    found = dot_f32(jnp.concatenate(members, axis=0), table[...])
    size, window = streams[0].shape
    signals = []
    for k in range(len(members)):
        rows = slice(k * size, (k + 1) * size)
        medium = found[rows, :window] + found[rows, window:]
        gated = (gates_out[k].astype(jnp.float32) * medium).astype(jnp.bfloat16)
        targets[k][...] = gated
        stream = streams[k].astype(jnp.float32) + gated.astype(jnp.float32)
        signals.append((gates_in[k].astype(jnp.float32) * stream).astype(jnp.bfloat16))
    return signals


def end_states(signals, powers_of_pair, pair, modes, mask):
    rows = slice(pair * PAIR, (pair + 1) * PAIR)
    lanes = ROWS * modes
    left = jnp.concatenate([signal[rows] for signal in signals], axis=0)
    found = dot_f32(left, powers_of_pair)
    sides = []
    for side in range(2):
        tops = [k * PAIR + side * ROWS for k in range(len(signals))]
        sides.append(
            [
                jnp.where(mask, found[top : top + ROWS, side * lanes : (side + 1) * lanes], 0.0)
                for top in tops
            ]
        )
    return sides


def later_kernel(
    step,
    sec,
    tok,
    local_all,
    swapped,
    inputs_all,
    taps_all,
    fwd_even,
    fwd_odd,
    inv_even,
    inv_odd,
    medium_all,
    signals_all,
    tap_spec_all,
    edge_spec_all,
    remote_all,
    arrival,
):
    share, tokens = inputs_all.shape
    window = taps_all.shape[1]
    blocks = tokens // window
    parts = [slice(b * window, (b + 1) * window) for b in range(blocks)]

    def fetch(kind, i):
        source = pl.ds(pl.multiple_of(sec[0] * share + i * step, step), step)
        return pltpu.make_async_copy(
            swapped.at[kind, source, :],
            rows_at(remote_all.at[kind], step, i),
            arrival.at[kind, i],
        )

    def chunk(section, i):
        if section == 1:
            fetch(1, i).wait()
        first, second = both_gates(local_all, remote_all, section, step, i)
        inputs = rows_at(inputs_all, step, i)
        medium_out, signals = rows_at(medium_all, step, i), rows_at(signals_all, step, i)
        sources = [first[1, :, part] * inputs[:, part] for part in parts]
        tap_rows = rows_at(taps_all, step, i)[...]
        tap_spec, *even = doubled_spectrum([tap_rows] + sources[0::2], fwd_even)
        odd = doubled_spectrum(sources[1::2], fwd_odd)
        in_order = [None] * blocks
        in_order[0::2] = even
        in_order[1::2] = odd
        rows_at(tap_spec_all, step, i)[...] = tap_spec
        rows_at(edge_spec_all, step, i)[...] = in_order[0]
        mixed = products([in_order[b - 1] + in_order[b] for b in range(1, blocks)], tap_spec)
        if section == 0:
            fetch(1, i).wait()
            fetch(0, i).start()
        else:
            fetch(0, i).wait()
        for parity, table in enumerate((inv_even, inv_odd)):
            chosen = [b for b in range(1, blocks) if b % 2 == parity]
            if not chosen:
                continue
            found = finish_medium(
                [mixed[b - 1] for b in chosen],
                table,
                [first[0, :, parts[b]] for b in chosen],
                [second[1, :, parts[b]] for b in chosen],
                [inputs[:, parts[b]] for b in chosen],
                [medium_out.at[:, parts[b]] for b in chosen],
            )
            for b, signal in zip(chosen, found):
                signals[:, parts[b]] = signal

    def body(section):
        for i in range(share // step):
            fetch(1, i).start()
            if section == 1:
                fetch(0, i).start()
        pl.loop(0, share // step)(functools.partial(chunk, section))
        if section == 0:
            for i in range(share // step):
                fetch(0, i).wait()

    by_section(sec, body)


def later_call(place, gates, swapped, inputs, taps, tables):
    share, tokens = inputs.shape
    window = taps.shape[1]
    operands = [gates, *parked(swapped), inputs, taps, *tables]
    spec = jax.ShapeDtypeStruct((share, 2 * window), jnp.float32)
    wide = jax.ShapeDtypeStruct((share, tokens), jnp.bfloat16)
    return pl.pallas_call(
        functools.partial(later_kernel, min(STEP, share)),
        out_shape=(wide, wide, spec, spec, jax.ShapeDtypeStruct(gates.shape, gates.dtype)),
        in_specs=[SMEM_SPEC] * 2 + [VMEM_SPEC, ANY_SPEC] + [VMEM_SPEC] * (len(operands) - 2),
        out_specs=(VMEM_SPEC,) * 5,
        scratch_shapes=[pltpu.SemaphoreType.DMA((2, share // min(STEP, share)))],
        name="later",
        cost_estimate=cost(share, tokens, 1500),
        compiler_params=COMPILER,
    )(*place, *operands)


def first_kernel(
    modes,
    step,
    sec,
    tok,
    local_all,
    remote_all,
    inputs_all,
    halo_low,
    halo_high,
    rates,
    falling_all,
    tap_spec_all,
    edge_spec_all,
    fwd_odd,
    inv_even,
    medium_before,
    signals_before,
    medium_all,
    signals_all,
    ends_all,
    total_all,
    leaps_all,
):
    share = inputs_all.shape[0]
    window = tap_spec_all.shape[1] // 2
    part = slice(0, window)
    mask = lane_mask(modes)
    leaps_all[...] = jnp.exp(-rates[...] * window)

    def chunk(section, i):
        first, second = both_gates(local_all, remote_all, section, step, i)
        halo = rows_at(halo_low if section == 0 else halo_high, step, i)
        leaps = rows_at(leaps_all, step // ROWS, i)
        falling = rows_at(falling_all, step // PAIR, i)
        ends = rows_at(ends_all, step, i, 1)
        started = jnp.where(tok[0] > 0, 1.0, 0.0).astype(jnp.bfloat16)
        (before,) = doubled_spectrum([halo[...] * started], fwd_odd)
        mixed = products(
            [before + rows_at(edge_spec_all, step, i)[...]],
            rows_at(tap_spec_all, step, i)[...],
        )
        (signal,) = finish_medium(
            mixed,
            inv_even,
            [first[0, :, part]],
            [second[1, :, part]],
            [rows_at(inputs_all, step, i)[:, part]],
            [rows_at(medium_all, step, i).at[:, part]],
        )
        signals = rows_at(signals_all, step, i)
        signals[:, part] = signal
        members = [signal] + [
            signals[:, b * window : (b + 1) * window] for b in range(1, ends.shape[0])
        ]
        sums = []
        for pair in range(step // PAIR):
            sides = end_states(members, falling[pair], pair, modes, mask)
            for side, found in enumerate(sides):
                at = pair * PAIR + side * ROWS
                leap = spread(leaps, 2 * pair + side)
                state = None
                for b, end in enumerate(found):
                    ends[b, at : at + ROWS, :] = end
                    state = end if state is None else state * leap + end
                sums.append(jnp.sum(state, axis=0, keepdims=True))
        total = rows_at(total_all, step // ROWS, i)
        total[...] = jnp.concatenate(sums, axis=0).astype(total.dtype)

    def body(section):
        pl.loop(0, share // step)(functools.partial(chunk, section))

    by_section(sec, body)


def first_call(
    place, gates, swapped, inputs, halos, rates, falling, specs, tables, medium, signals, modes
):
    share, tokens = inputs.shape
    window = halos[0].shape[1]
    lanes = ROWS * modes
    small = (share // ROWS, lanes)
    operands = [gates, swapped, inputs, *halos, rates, falling, *specs, *tables, medium, signals]
    return pl.pallas_call(
        functools.partial(first_kernel, modes, min(2 * STEP, share)),
        out_shape=(
            jax.ShapeDtypeStruct(medium.shape, medium.dtype),
            jax.ShapeDtypeStruct(signals.shape, signals.dtype),
            jax.ShapeDtypeStruct((tokens // window, share, lanes), jnp.float32),
            jax.ShapeDtypeStruct(small, jnp.bfloat16),
        ),
        in_specs=[SMEM_SPEC] * 2 + [VMEM_SPEC] * len(operands),
        out_specs=(VMEM_SPEC,) * 4,
        scratch_shapes=[pltpu.VMEM(small, jnp.float32)],
        input_output_aliases={len(operands): 0, len(operands) + 1: 1},
        name="first",
        cost_estimate=cost(share, tokens, 500),
        compiler_params=COMPILER,
    )(*place, *operands)


def within_kernel(
    step,
    signals_all,
    response_all,
    fwd_h,
    fwd_l,
    inverse,
    table_h,
    table_l,
    out_all,
):
    share, tokens = signals_all.shape
    size = fwd_h.shape[0]
    half = size // 2

    def chunk(i):
        signals = rows_at(signals_all, step, i)
        taps, out = rows_at(response_all, step, i)[...], rows_at(out_all, step, i)
        high = taps.astype(jnp.bfloat16)
        low = (taps - high.astype(jnp.float32)).astype(jnp.bfloat16)
        response = dot_f32(jnp.concatenate([high, low], axis=1), table_h[...]) + dot_f32(
            high, table_l[...]
        )
        channels = step
        real, imag = response[:, :half], response[:, half:]
        parts = [slice(k * size, (k + 1) * size) for k in range(tokens // size)]
        signal = jnp.concatenate([signals[:, part] for part in parts], axis=0)
        spec = dot_f32(signal, fwd_h[...]) + dot_f32(signal, fwd_l[...])
        filtered = []
        for k in range(len(parts)):
            rows = slice(k * channels, (k + 1) * channels)
            a, b = spec[rows, :half], spec[rows, half:]
            filtered.append(
                jnp.concatenate([a * real - b * imag, a * imag + b * real], axis=1).astype(
                    jnp.bfloat16
                )
            )
        found = dot_f32(jnp.concatenate(filtered, axis=0), inverse[...])
        for k, part in enumerate(parts):
            out[:, part] = found[k * channels : (k + 1) * channels]

    pl.loop(0, share // step)(chunk)


def within_call(signals, response, tables):
    share, tokens = signals.shape
    operands = [signals, response, *tables]
    return pl.pallas_call(
        functools.partial(within_kernel, min(2 * STEP, share)),
        out_shape=jax.ShapeDtypeStruct((share, tokens), jnp.float32),
        in_specs=[VMEM_SPEC] * len(operands),
        out_specs=VMEM_SPEC,
        name="within",
        cost_estimate=cost(share, tokens, 1500),
        compiler_params=COMPILER,
    )(*operands)


def output_kernel(
    count,
    modes,
    window,
    step,
    first,
    share,
    sec,
    tok,
    local_all,
    remote_all,
    within_all,
    inputs_all,
    medium_all,
    rates,
    scale_rows,
    rising_all,
    ends_all,
    *rest,
):
    arrived = rest[:count]
    (result, send, keep, leaps_all, scales_all, shares_all, starts_all, done) = rest[-8:]
    part_rows, tokens = send.shape
    base = first // step
    groups = pl.ds(first // ROWS, part_rows // ROWS)
    blocks = tokens // window
    mask = lane_mask(modes)
    slow = rates[groups, :]
    leap_all = jnp.exp(-slow * window)
    scale_all = scale_rows[groups, :] * jnp.exp(-slow)
    leaps_all[...] = leap_all
    scales_all[...] = scale_all
    shares_all[...] = scale_all / (1.0 + leap_all)
    entering = jnp.zeros_like(slow)
    for k in range(count):
        gap = tok[0] - (tok[0] ^ (k + 1))
        known = jnp.where(gap > 0, 1.0, 0.0)
        distance = (tokens * jnp.maximum(gap - 1, 0)).astype(jnp.float32)
        entering = entering + arrived[k][groups, :].astype(jnp.float32) * (
            jnp.exp(-slow * distance) * known
        )
    starts_all[...] = entering

    def chunk(section, out_all, i):
        out = rows_at(out_all, step, i)
        at_all = base + i
        gate_out = both_gates(local_all, remote_all, section, step, at_all)[1].at[0]
        inputs = rows_at(inputs_all, step, at_all)
        gated_medium = rows_at(medium_all, step, at_all)
        within = rows_at(within_all, step, at_all)
        ends = rows_at(ends_all, step, at_all, 1)
        rising = rows_at(rising_all, step // PAIR, at_all)
        small = step // ROWS
        leaps, scales = rows_at(leaps_all, small, i), rows_at(scales_all, small, i)
        shares, starts = rows_at(shares_all, small, i), rows_at(starts_all, small, i)
        channels = step
        for pair in range(channels // PAIR):
            rows = slice(pair * PAIR, (pair + 1) * PAIR)
            sides = []
            for side in range(2):
                group = 2 * pair + side
                leap, scale = spread(leaps, group), spread(scales, group)
                portion = spread(shares, group)
                state = jnp.where(mask, spread(starts, group), 0.0)
                at = pair * PAIR + side * ROWS
                lefts = []
                for b in range(blocks):
                    end = ends[b, at : at + ROWS, :]
                    lefts.append(state * scale + end * portion)
                    state = state * leap + end
                sides.append(lefts)
            left = jnp.concatenate(
                [two_sided(upper, lower) for upper, lower in zip(*sides)], axis=0
            ).astype(jnp.bfloat16)
            across = dot_turned(left, rising[pair])
            for b in range(blocks):
                part = slice(b * window, (b + 1) * window)
                stream = inputs[rows, part].astype(jnp.float32) + gated_medium[
                    rows, part
                ].astype(jnp.float32)
                long_out = within[rows, part] + across[b * PAIR : (b + 1) * PAIR]
                gate = gate_out[rows, part].astype(jnp.float32)
                out[rows, part] = (stream + gate * long_out).astype(jnp.bfloat16)

    def body(section):
        target = result.at[0, pl.ds(section * share + first, part_rows), :]
        source = medium_all.at[pl.ds(first, part_rows), :]
        copy = pltpu.make_async_copy(source, send if section else target, done)
        copy.start()
        pl.loop(0, part_rows // step)(
            functools.partial(chunk, section, keep if section else send)
        )
        copy.wait()

    by_section(sec, body)


def output_call(
    place, half, gates, swapped, within, inputs, medium, rates, scales, rising, ends, arrived, before
):
    share, tokens = medium.shape
    lanes = rates.shape[1]
    window = rising.shape[1]
    part_rows = share // HALVES
    step = min(STEP, part_rows)
    small = (part_rows // ROWS, lanes)
    operands = [gates, swapped, within, inputs, medium, rates, scales, rising, ends, *arrived]
    result = jax.ShapeDtypeStruct((1, 2 * share, tokens), jnp.bfloat16)
    chained = [] if before is None else [before]
    return pl.pallas_call(
        functools.partial(
            output_kernel,
            len(arrived),
            lanes // ROWS,
            window,
            step,
            half * part_rows,
            share,
        ),
        out_shape=(result,) + (jax.ShapeDtypeStruct((part_rows, tokens), jnp.bfloat16),) * 2,
        in_specs=[SMEM_SPEC] * 2 + [VMEM_SPEC] * len(operands) + [ANY_SPEC] * len(chained),
        out_specs=(ANY_SPEC, VMEM_SPEC, VMEM_SPEC),
        scratch_shapes=[pltpu.VMEM(small, jnp.float32)] * 4
        + [pltpu.SemaphoreType.DMA],
        input_output_aliases={2 + len(operands): 0} if chained else {},
        name="output",
        cost_estimate=cost(part_rows, tokens, 1500),
        compiler_params=COMPILER,
    )(*place, *operands, *chained)


def place_kernel(first, share, sec, before, received, *rest):
    kept, (out, done) = rest[:-2], rest[-2:]
    rows = received.shape[0]

    def target(section, start):
        return out.at[0, pl.ds(pl.multiple_of(section * share + start, rows), rows), :]

    foreign = pltpu.make_async_copy(received, target(1 - sec[0], first), done.at[0])
    foreign.start()

    @pl.when(sec[0] == 1)
    def _():
        copies = [
            pltpu.make_async_copy(keep, target(1, k * rows), done.at[k + 1])
            for k, keep in enumerate(kept)
        ]
        for copy in copies:
            copy.start()
        for copy in copies:
            copy.wait()

    foreign.wait()


def place_call(place, half, before, received, kept):
    rows, tokens = received.shape
    return pl.pallas_call(
        functools.partial(place_kernel, half * rows, before.shape[1] // 2),
        out_shape=jax.ShapeDtypeStruct(before.shape, before.dtype),
        in_specs=[SMEM_SPEC, ANY_SPEC] + [VMEM_SPEC] * (1 + len(kept)),
        out_specs=ANY_SPEC,
        scratch_shapes=[pltpu.SemaphoreType.DMA((1 + len(kept),))],
        input_output_aliases={1: 0},
        name="placing",
        cost_estimate=cost(rows, tokens, 2),
        compiler_params=COMPILER,
    )(place[0], before, received, *kept)


def edge_kernel(gates, inputs, low, high, gate_tail, input_tail, arrival):
    share, window = low.shape
    tail = pl.ds(inputs.shape[1] - window, window)
    pairs = [(gates.at[0, 1, :, tail], gate_tail), (inputs.at[:, tail], input_tail)]
    copies = [
        pltpu.make_async_copy(source, target, arrival.at[k])
        for k, (source, target) in enumerate(pairs)
    ]
    for copy in copies:
        copy.start()
    for copy in copies:
        copy.wait()
    low[...] = gate_tail[:share, :] * input_tail[:share, :]
    high[...] = gate_tail[share:, :] * input_tail[share:, :]


def edge_call(gate_streams, inputs, window, share):
    channels, tokens = inputs.shape
    edge = jax.ShapeDtypeStruct((share, window), jnp.bfloat16)
    return pl.pallas_call(
        edge_kernel,
        out_shape=(edge, edge),
        in_specs=[ANY_SPEC] * 2,
        out_specs=(VMEM_SPEC,) * 2,
        scratch_shapes=[pltpu.VMEM((channels, window), jnp.bfloat16)] * 2
        + [pltpu.SemaphoreType.DMA((2,))],
        name="edge",
        cost_estimate=cost(share, tokens, 2),
        compiler_params=COMPILER,
    )(*parked(gate_streams, inputs))


def ring(value, axis, by):
    peers = lax.axis_size(axis)
    return lax.ppermute(value, axis, [(i, (i + by) % peers) for i in range(peers)])


def met(value, by):
    peers = lax.axis_size("tok")
    return lax.ppermute(value, "tok", [(i, i ^ by) for i in range(peers)])


def edge_to(value, section):
    peers = lax.axis_size("tok")
    pairs = [(i, section * peers + (i + 1) % peers) for i in range(peers)]
    pairs += [(peers + i, (1 - section) * peers + i) for i in range(peers)]
    return lax.ppermute(value, ("section", "tok"), pairs)


def on_device(gate_streams, inputs, medium_taps, residues, decay_rates):
    channels, _ = inputs.shape
    share = channels // 2
    window = medium_taps.shape[1]
    modes = decay_rates.shape[1]
    place = tuple(
        lax.axis_index(axis).astype(jnp.int32).reshape(1) for axis in ("section", "tok")
    )
    edges = edge_call(gate_streams, inputs, window, share)
    halos = [edge_to(edges[s], s) for s in range(2)]
    swapped = ring(gate_streams[0], "section", 1)
    forward, inverse = fourier_tables(window)
    turned, back, doubled = turned_tables(window)
    tables = [*forward, *inverse, *split_pair(turned), split_pair(back)[0]]
    high, low = split_pair(doubled)
    tables += [jnp.concatenate([high, high], axis=0), low]
    built, own, tables = response_call(
        place,
        decay_rates.T,
        residues.T,
        gate_streams,
        inputs,
        medium_taps,
        tables,
        window,
        share,
    )
    response, rates, scales, rising, falling = built
    gates, inputs, taps = own
    medium, signals, *specs, remote = later_call(
        place, gates, swapped, inputs, taps, tables[:4]
    )
    medium, signals, ends, total = first_call(
        place,
        gates,
        remote,
        inputs,
        halos,
        rates,
        falling,
        specs,
        tables[1:3],
        medium,
        signals,
        modes,
    )
    arrived = []
    for by in range(1, lax.axis_size("tok")):
        arrived.append(met(total, by))
    within = within_call(signals, response, tables[4:])
    result, waiting = None, []
    for half in range(HALVES):
        result, send, keep = output_call(
            place,
            half,
            gates,
            remote,
            within,
            inputs,
            medium,
            rates,
            scales,
            rising,
            ends,
            arrived,
            result,
        )
        waiting.append((ring(send, "section", 1), keep))
    kept = [keep for _, keep in waiting]
    for half, (received, _) in enumerate(waiting):
        result = place_call(place, half, result, received, [] if half else kept)
    return result


def solution(mesh):
    placed = (
        P("section", None, "chan", "tok"),
        P("chan", "tok"),
        P("chan", None),
        P("chan", None),
        P("chan", None),
    )
    return jax.shard_map(
        on_device,
        mesh=mesh,
        in_specs=placed,
        out_specs=P("section", "chan", "tok"),
        check_vma=False,
    )
```

```python
import functools

import jax
import jax.numpy as jnp
import numpy as np
from jax import lax
from jax.experimental import pallas as pl
from jax.experimental.pallas import tpu as pltpu
from jax.sharding import PartitionSpec as P


ROWS = 8


def split_pair(matrix):
    high = jnp.asarray(matrix, jnp.float32).astype(jnp.bfloat16)
    low = (jnp.asarray(matrix, jnp.float32) - high.astype(jnp.float32)).astype(jnp.bfloat16)
    return high, low


def stacked(matrix, axis):
    return jnp.concatenate(split_pair(matrix), axis=axis)


def fourier_tables(window):
    size = 2 * window
    time = np.arange(window)[:, None]
    freq = np.arange(window)[None, :]
    angle = 2.0 * np.pi * ((time * freq) % size) / size
    sign = np.where(freq % 2 == 0, 1.0, -1.0)
    nyquist = np.where(time % 2 == 0, 1.0, -1.0)
    weight = np.where(freq == 0, 1.0, 2.0) / size
    forward, inverse = [], []
    for odd in range(2):
        flip = sign if odd else np.ones_like(sign)
        real = np.cos(angle) * flip
        imag = -np.sin(angle) * flip
        imag[:, :1] = nyquist
        forward.append(stacked(np.concatenate([real, imag], axis=1), 0))
        back_real = np.cos(angle) * weight * flip
        back_imag = -np.sin(angle) * weight * flip
        back_imag[:, :1] = nyquist / size
        inverse.append(stacked(np.concatenate([back_real.T, back_imag.T], axis=0), 1))
    return forward, inverse


def turned_tables(window):
    half = window // 2
    time = np.arange(window)[:, None]
    freq = 2 * np.arange(half)[None, :] + 1
    angle = np.pi * ((time * freq) % (2 * window)) / window
    real, imag = np.cos(angle), -np.sin(angle)
    zero = np.zeros_like(real)
    forward = np.concatenate(
        [
            np.concatenate([real, zero, imag, zero], axis=1),
            np.concatenate([zero, real, zero, imag], axis=1),
        ],
        axis=0,
    )
    inverse = forward.T * (2.0 / window)
    doubled = np.concatenate([real, real, imag, imag], axis=1)
    return forward, inverse, doubled


PAIR = 16
STEP = 512
HALVES = 2
COMPILER = pltpu.CompilerParams(vmem_limit_bytes=16 << 20)


def parked(*arrays):
    return [pltpu.with_memory_space_constraint(a, pltpu.HBM) for a in arrays]


def cost(share, tokens, work):
    size = share * tokens
    return pl.CostEstimate(
        flops=size * work, bytes_accessed=size * 12, transcendentals=size // 64
    )


def dot_f32(left, right):
    return jnp.dot(left, right, preferred_element_type=jnp.float32)


def dot_turned(left, right):
    return lax.dot_general(
        left, right, (((1,), (1,)), ((), ())), preferred_element_type=jnp.float32
    )


VMEM_SPEC = pl.BlockSpec(memory_space=pltpu.VMEM)
SMEM_SPEC = pl.BlockSpec(memory_space=pltpu.SMEM)
ANY_SPEC = pl.BlockSpec(memory_space=pl.ANY)


def rows_at(ref, step, i, axis=0):
    start = i * step
    if not isinstance(i, int):
        start = pl.multiple_of(start, step)
    return ref.at[(slice(None),) * axis + (pl.ds(start, step),)]


def both_gates(local, remote, section, step, i):
    mine, other = rows_at(local, step, i, 1), rows_at(remote, step, i, 1)
    return (mine, other) if section == 0 else (other, mine)


def by_section(sec, body):
    for section in range(2):
        pl.when(sec[0] == section)(functools.partial(body, section))


def lane_mask(modes):
    shape = (ROWS, ROWS * modes)
    lane = lax.broadcasted_iota(jnp.int32, shape, 1)
    return lane // modes == lax.broadcasted_iota(jnp.int32, shape, 0)


def spread(ref, group):
    return jnp.broadcast_to(ref[group : group + 1, :], (ROWS, ref.shape[1]))


def powers(slow, hop, window, first, falling):
    row = lax.broadcasted_iota(jnp.int32, slow.shape, 0).astype(jnp.float32)
    tiles = [jnp.exp(-slow * (first + (ROWS - 1 - row if falling else row)))]
    while len(tiles) < window // ROWS:
        tiles = tiles + [tile * hop for tile in tiles]
        hop = hop * hop
    if falling:
        tiles = tiles[::-1]
    return jnp.concatenate(tiles, axis=0).astype(jnp.bfloat16)


def both_powers(rates, hops, pair, window, falling):
    sides = [
        powers(spread(rates, g), spread(hops, g), window, 0.0, falling)
        for g in (2 * pair, 2 * pair + 1)
    ]
    return jnp.concatenate(sides, axis=1)


def two_sided(upper, lower):
    zero = jnp.zeros_like(upper)
    return jnp.concatenate(
        [
            jnp.concatenate([upper, zero], axis=1),
            jnp.concatenate([zero, lower], axis=1),
        ],
        axis=0,
    )


def scale_of(residues, slow):
    return residues * jnp.sqrt(1.0 - jnp.exp(-2.0 * slow))


def in_rows(ref, tall):
    _, channels = ref.shape
    tall[...] = ref[...].T
    count = channels // ROWS
    return jnp.concatenate(
        [tall[pl.ds(c, count, stride=ROWS), :] for c in range(ROWS)], axis=1
    )


def response_kernel(count, window, sec, tok, rates, residues, *rest):
    gates, inputs, taps = rest[:3]
    tables = rest[3 : 3 + count]
    out, rate_rows, scale_rows, rising, falling = rest[3 + count : 8 + count]
    own_gates, own_inputs, own_taps = rest[8 + count : 11 + count]
    own_tables = rest[11 + count : 11 + 2 * count]
    tall, hops, scales, arrival = rest[11 + 2 * count :]
    share = out.shape[0]
    step = tall.shape[0]
    modes = rates.shape[0]
    first = pl.multiple_of(sec[0] * share, share)
    mine = pl.ds(first, share)
    pairs = [(gates.at[0, :, mine, :], own_gates)]
    pairs += [(inputs.at[mine, :], own_inputs), (taps.at[mine, :], own_taps)]
    pairs += list(zip(tables, own_tables))
    copies = [
        pltpu.make_async_copy(source, target, arrival.at[k])
        for k, (source, target) in enumerate(pairs)
    ]
    for copy in copies:
        copy.start()
    mask = lane_mask(modes)

    @pl.loop(0, share // step)
    def _(i):
        lanes = pl.ds(pl.multiple_of(first + i * step, step), step)
        slow = in_rows(rates.at[:, lanes], tall)
        scale = scale_of(in_rows(residues.at[:, lanes], tall), slow)
        small = step // ROWS
        own_rates = rows_at(rate_rows, small, i)
        own_rates[...] = slow
        rows_at(scale_rows, small, i)[...] = scale
        hops[...] = jnp.exp(-slow * ROWS)
        scales[...] = scale / (1.0 + jnp.exp(-slow * window))
        up, down = rows_at(rising, step // PAIR, i), rows_at(falling, step // PAIR, i)
        own_out = rows_at(out, step, i)
        for pair in range(step // PAIR):
            both = two_sided(
                jnp.where(mask, spread(scales, 2 * pair), 0.0),
                jnp.where(mask, spread(scales, 2 * pair + 1), 0.0),
            )
            high = both.astype(jnp.bfloat16).astype(jnp.float32)
            both = jnp.concatenate([high, both - high], axis=0).astype(jnp.bfloat16)
            table = both_powers(own_rates, hops, pair, window, False)
            up[pair] = table
            down[pair] = both_powers(own_rates, hops, pair, window, True)
            found = dot_turned(both, table)
            out_rows = pl.ds(pair * PAIR, PAIR)
            own_out[out_rows, :] = found[:PAIR] + found[PAIR:]

    for copy in copies:
        copy.wait()


def response_call(place, rates, residues, gates, inputs, taps, tables, window, share):
    tokens = inputs.shape[1]
    step = min(STEP, share)
    modes = rates.shape[0]
    lanes = ROWS * modes
    small = (step // ROWS, lanes)
    shape = lambda dims, kind=jnp.float32: jax.ShapeDtypeStruct(dims, kind)
    power_shape = shape((share // PAIR, window, 2 * lanes), jnp.bfloat16)
    outs = [shape((share, window))] + [shape((share // ROWS, lanes))] * 2
    outs += [power_shape] * 2
    outs += [
        shape((2, share, tokens), gates.dtype),
        shape((share, tokens), inputs.dtype),
        shape((share, window), taps.dtype),
    ]
    outs += [shape(t.shape, t.dtype) for t in tables]
    staged = 3 + len(tables)
    found = pl.pallas_call(
        functools.partial(response_kernel, len(tables), window),
        out_shape=tuple(outs),
        in_specs=[SMEM_SPEC] * 2 + [VMEM_SPEC] * 2 + [ANY_SPEC] * staged,
        out_specs=(VMEM_SPEC,) * len(outs),
        scratch_shapes=[
            pltpu.VMEM((step, modes), jnp.float32),
            pltpu.VMEM(small, jnp.float32),
            pltpu.VMEM(small, jnp.float32),
            pltpu.SemaphoreType.DMA((staged,)),
        ],
        name="response",
        cost_estimate=cost(share, 4 * window, 900),
        compiler_params=COMPILER,
    )(*place, rates, residues, *parked(gates, inputs, taps, *tables))
    return found[:5], found[5:8], found[8:]


def products(members, tap_spec):
    window = tap_spec.shape[1] // 2
    real, packed = tap_spec[:, :window], tap_spec[:, window:]
    lane = lax.broadcasted_iota(jnp.int32, real.shape, 1)
    real_b = jnp.where(lane == 0, packed, real)
    imag = jnp.where(lane == 0, 0.0, packed)
    found = []
    for mixed in members:
        a, b = mixed[:, :window], mixed[:, window:]
        found.append(
            jnp.concatenate([a * real - b * imag, a * imag + b * real_b], axis=1).astype(
                jnp.bfloat16
            )
        )
    return found


def doubled_spectrum(members, table):
    rows = jnp.concatenate(members, axis=0)
    found = dot_f32(jnp.concatenate([rows, rows], axis=1), table[...])
    size = members[0].shape[0]
    return [found[k * size : (k + 1) * size] for k in range(len(members))]


def finish_medium(members, table, gates_out, gates_in, streams, targets):
    found = dot_f32(jnp.concatenate(members, axis=0), table[...])
    size, window = streams[0].shape
    signals = []
    for k in range(len(members)):
        rows = slice(k * size, (k + 1) * size)
        medium = found[rows, :window] + found[rows, window:]
        gated = (gates_out[k].astype(jnp.float32) * medium).astype(jnp.bfloat16)
        targets[k][...] = gated
        stream = streams[k].astype(jnp.float32) + gated.astype(jnp.float32)
        signals.append((gates_in[k].astype(jnp.float32) * stream).astype(jnp.bfloat16))
    return signals


def end_states(signals, powers_of_pair, pair, modes, mask):
    rows = slice(pair * PAIR, (pair + 1) * PAIR)
    lanes = ROWS * modes
    left = jnp.concatenate([signal[rows] for signal in signals], axis=0)
    found = dot_f32(left, powers_of_pair)
    sides = []
    for side in range(2):
        tops = [k * PAIR + side * ROWS for k in range(len(signals))]
        sides.append(
            [
                jnp.where(mask, found[top : top + ROWS, side * lanes : (side + 1) * lanes], 0.0)
                for top in tops
            ]
        )
    return sides


def later_kernel(
    step,
    sec,
    tok,
    local_all,
    swapped,
    inputs_all,
    taps_all,
    fwd_even,
    fwd_odd,
    inv_even,
    inv_odd,
    medium_all,
    signals_all,
    tap_spec_all,
    edge_spec_all,
    remote_all,
    arrival,
):
    share, tokens = inputs_all.shape
    window = taps_all.shape[1]
    blocks = tokens // window
    parts = [slice(b * window, (b + 1) * window) for b in range(blocks)]

    def fetch(i):
        source = pl.ds(pl.multiple_of(sec[0] * share + i * step, step), step)
        return pltpu.make_async_copy(
            swapped.at[:, source, :], rows_at(remote_all, step, i, 1), arrival.at[i]
        )

    for i in range(share // step):
        fetch(i).start()

    def chunk(section, i):
        fetch(i).wait()
        first, second = both_gates(local_all, remote_all, section, step, i)
        inputs = rows_at(inputs_all, step, i)
        medium_out, signals = rows_at(medium_all, step, i), rows_at(signals_all, step, i)
        sources = [first[1, :, part] * inputs[:, part] for part in parts]
        tap_rows = rows_at(taps_all, step, i)[...]
        tap_spec, *even = doubled_spectrum([tap_rows] + sources[0::2], fwd_even)
        odd = doubled_spectrum(sources[1::2], fwd_odd)
        in_order = [None] * blocks
        in_order[0::2] = even
        in_order[1::2] = odd
        rows_at(tap_spec_all, step, i)[...] = tap_spec
        rows_at(edge_spec_all, step, i)[...] = in_order[0]
        mixed = products([in_order[b - 1] + in_order[b] for b in range(1, blocks)], tap_spec)
        for parity, table in enumerate((inv_even, inv_odd)):
            chosen = [b for b in range(1, blocks) if b % 2 == parity]
            if not chosen:
                continue
            found = finish_medium(
                [mixed[b - 1] for b in chosen],
                table,
                [first[0, :, parts[b]] for b in chosen],
                [second[1, :, parts[b]] for b in chosen],
                [inputs[:, parts[b]] for b in chosen],
                [medium_out.at[:, parts[b]] for b in chosen],
            )
            for b, signal in zip(chosen, found):
                signals[:, parts[b]] = signal

    def body(section):
        pl.loop(0, share // step)(functools.partial(chunk, section))

    by_section(sec, body)


def later_call(place, gates, swapped, inputs, taps, tables):
    share, tokens = inputs.shape
    window = taps.shape[1]
    operands = [gates, *parked(swapped), inputs, taps, *tables]
    spec = jax.ShapeDtypeStruct((share, 2 * window), jnp.float32)
    wide = jax.ShapeDtypeStruct((share, tokens), jnp.bfloat16)
    return pl.pallas_call(
        functools.partial(later_kernel, min(STEP, share)),
        out_shape=(wide, wide, spec, spec, jax.ShapeDtypeStruct(gates.shape, gates.dtype)),
        in_specs=[SMEM_SPEC] * 2 + [VMEM_SPEC, ANY_SPEC] + [VMEM_SPEC] * (len(operands) - 2),
        out_specs=(VMEM_SPEC,) * 5,
        scratch_shapes=[pltpu.SemaphoreType.DMA((share // min(STEP, share),))],
        name="later",
        cost_estimate=cost(share, tokens, 1500),
        compiler_params=COMPILER,
    )(*place, *operands)


def first_kernel(
    modes,
    step,
    sec,
    tok,
    local_all,
    remote_all,
    inputs_all,
    halo_low,
    halo_high,
    rates,
    falling_all,
    tap_spec_all,
    edge_spec_all,
    fwd_odd,
    inv_even,
    medium_before,
    signals_before,
    medium_all,
    signals_all,
    ends_all,
    total_all,
    leaps_all,
):
    share = inputs_all.shape[0]
    window = tap_spec_all.shape[1] // 2
    part = slice(0, window)
    mask = lane_mask(modes)
    leaps_all[...] = jnp.exp(-rates[...] * window)

    def chunk(section, i):
        first, second = both_gates(local_all, remote_all, section, step, i)
        halo = rows_at(halo_low if section == 0 else halo_high, step, i)
        leaps = rows_at(leaps_all, step // ROWS, i)
        falling = rows_at(falling_all, step // PAIR, i)
        ends = rows_at(ends_all, step, i, 1)
        started = jnp.where(tok[0] > 0, 1.0, 0.0).astype(jnp.bfloat16)
        (before,) = doubled_spectrum([halo[...] * started], fwd_odd)
        mixed = products(
            [before + rows_at(edge_spec_all, step, i)[...]],
            rows_at(tap_spec_all, step, i)[...],
        )
        (signal,) = finish_medium(
            mixed,
            inv_even,
            [first[0, :, part]],
            [second[1, :, part]],
            [rows_at(inputs_all, step, i)[:, part]],
            [rows_at(medium_all, step, i).at[:, part]],
        )
        signals = rows_at(signals_all, step, i)
        signals[:, part] = signal
        members = [signal] + [
            signals[:, b * window : (b + 1) * window] for b in range(1, ends.shape[0])
        ]
        sums = []
        for pair in range(step // PAIR):
            sides = end_states(members, falling[pair], pair, modes, mask)
            for side, found in enumerate(sides):
                at = pair * PAIR + side * ROWS
                leap = spread(leaps, 2 * pair + side)
                state = None
                for b, end in enumerate(found):
                    ends[b, at : at + ROWS, :] = end
                    state = end if state is None else state * leap + end
                sums.append(jnp.sum(state, axis=0, keepdims=True))
        total = rows_at(total_all, step // ROWS, i)
        total[...] = jnp.concatenate(sums, axis=0).astype(total.dtype)

    def body(section):
        pl.loop(0, share // step)(functools.partial(chunk, section))

    by_section(sec, body)


def first_call(
    place, gates, swapped, inputs, halos, rates, falling, specs, tables, medium, signals, modes
):
    share, tokens = inputs.shape
    window = halos[0].shape[1]
    lanes = ROWS * modes
    small = (share // ROWS, lanes)
    operands = [gates, swapped, inputs, *halos, rates, falling, *specs, *tables, medium, signals]
    return pl.pallas_call(
        functools.partial(first_kernel, modes, min(2 * STEP, share)),
        out_shape=(
            jax.ShapeDtypeStruct(medium.shape, medium.dtype),
            jax.ShapeDtypeStruct(signals.shape, signals.dtype),
            jax.ShapeDtypeStruct((tokens // window, share, lanes), jnp.float32),
            jax.ShapeDtypeStruct(small, jnp.bfloat16),
        ),
        in_specs=[SMEM_SPEC] * 2 + [VMEM_SPEC] * len(operands),
        out_specs=(VMEM_SPEC,) * 4,
        scratch_shapes=[pltpu.VMEM(small, jnp.float32)],
        input_output_aliases={len(operands): 0, len(operands) + 1: 1},
        name="first",
        cost_estimate=cost(share, tokens, 500),
        compiler_params=COMPILER,
    )(*place, *operands)


def within_kernel(
    step,
    signals_all,
    response_all,
    fwd_h,
    fwd_l,
    inverse,
    table_h,
    table_l,
    out_all,
):
    share, tokens = signals_all.shape
    size = fwd_h.shape[0]
    half = size // 2

    def chunk(i):
        signals = rows_at(signals_all, step, i)
        taps, out = rows_at(response_all, step, i)[...], rows_at(out_all, step, i)
        high = taps.astype(jnp.bfloat16)
        low = (taps - high.astype(jnp.float32)).astype(jnp.bfloat16)
        response = dot_f32(jnp.concatenate([high, low], axis=1), table_h[...]) + dot_f32(
            high, table_l[...]
        )
        channels = step
        real, imag = response[:, :half], response[:, half:]
        parts = [slice(k * size, (k + 1) * size) for k in range(tokens // size)]
        signal = jnp.concatenate([signals[:, part] for part in parts], axis=0)
        spec = dot_f32(signal, fwd_h[...]) + dot_f32(signal, fwd_l[...])
        filtered = []
        for k in range(len(parts)):
            rows = slice(k * channels, (k + 1) * channels)
            a, b = spec[rows, :half], spec[rows, half:]
            filtered.append(
                jnp.concatenate([a * real - b * imag, a * imag + b * real], axis=1).astype(
                    jnp.bfloat16
                )
            )
        found = dot_f32(jnp.concatenate(filtered, axis=0), inverse[...])
        for k, part in enumerate(parts):
            out[:, part] = found[k * channels : (k + 1) * channels]

    pl.loop(0, share // step)(chunk)


def within_call(signals, response, tables):
    share, tokens = signals.shape
    operands = [signals, response, *tables]
    return pl.pallas_call(
        functools.partial(within_kernel, min(2 * STEP, share)),
        out_shape=jax.ShapeDtypeStruct((share, tokens), jnp.float32),
        in_specs=[VMEM_SPEC] * len(operands),
        out_specs=VMEM_SPEC,
        name="within",
        cost_estimate=cost(share, tokens, 1500),
        compiler_params=COMPILER,
    )(*operands)


def output_kernel(
    count,
    modes,
    window,
    step,
    first,
    share,
    sec,
    tok,
    local_all,
    remote_all,
    within_all,
    inputs_all,
    medium_all,
    rates,
    scale_rows,
    rising_all,
    ends_all,
    *rest,
):
    arrived = rest[:count]
    (result, send, keep, leaps_all, scales_all, shares_all, starts_all, done) = rest[-8:]
    part_rows, tokens = send.shape
    base = first // step
    groups = pl.ds(first // ROWS, part_rows // ROWS)
    blocks = tokens // window
    mask = lane_mask(modes)
    slow = rates[groups, :]
    leap_all = jnp.exp(-slow * window)
    scale_all = scale_rows[groups, :] * jnp.exp(-slow)
    leaps_all[...] = leap_all
    scales_all[...] = scale_all
    shares_all[...] = scale_all / (1.0 + leap_all)
    entering = jnp.zeros_like(slow)
    for k in range(count):
        gap = tok[0] - (tok[0] ^ (k + 1))
        known = jnp.where(gap > 0, 1.0, 0.0)
        distance = (tokens * jnp.maximum(gap - 1, 0)).astype(jnp.float32)
        entering = entering + arrived[k][groups, :].astype(jnp.float32) * (
            jnp.exp(-slow * distance) * known
        )
    starts_all[...] = entering

    def chunk(section, out_all, i):
        out = rows_at(out_all, step, i)
        at_all = base + i
        gate_out = both_gates(local_all, remote_all, section, step, at_all)[1].at[0]
        inputs = rows_at(inputs_all, step, at_all)
        gated_medium = rows_at(medium_all, step, at_all)
        within = rows_at(within_all, step, at_all)
        ends = rows_at(ends_all, step, at_all, 1)
        rising = rows_at(rising_all, step // PAIR, at_all)
        small = step // ROWS
        leaps, scales = rows_at(leaps_all, small, i), rows_at(scales_all, small, i)
        shares, starts = rows_at(shares_all, small, i), rows_at(starts_all, small, i)
        channels = step
        for pair in range(channels // PAIR):
            rows = slice(pair * PAIR, (pair + 1) * PAIR)
            sides = []
            for side in range(2):
                group = 2 * pair + side
                leap, scale = spread(leaps, group), spread(scales, group)
                portion = spread(shares, group)
                state = jnp.where(mask, spread(starts, group), 0.0)
                at = pair * PAIR + side * ROWS
                lefts = []
                for b in range(blocks):
                    end = ends[b, at : at + ROWS, :]
                    lefts.append(state * scale + end * portion)
                    state = state * leap + end
                sides.append(lefts)
            left = jnp.concatenate(
                [two_sided(upper, lower) for upper, lower in zip(*sides)], axis=0
            ).astype(jnp.bfloat16)
            across = dot_turned(left, rising[pair])
            for b in range(blocks):
                part = slice(b * window, (b + 1) * window)
                stream = inputs[rows, part].astype(jnp.float32) + gated_medium[
                    rows, part
                ].astype(jnp.float32)
                long_out = within[rows, part] + across[b * PAIR : (b + 1) * PAIR]
                gate = gate_out[rows, part].astype(jnp.float32)
                out[rows, part] = (stream + gate * long_out).astype(jnp.bfloat16)

    def body(section):
        target = result.at[0, pl.ds(section * share + first, part_rows), :]
        source = medium_all.at[pl.ds(first, part_rows), :]
        copy = pltpu.make_async_copy(source, send if section else target, done)
        copy.start()
        pl.loop(0, part_rows // step)(
            functools.partial(chunk, section, keep if section else send)
        )
        copy.wait()

    by_section(sec, body)


def output_call(
    place, half, gates, swapped, within, inputs, medium, rates, scales, rising, ends, arrived, before
):
    share, tokens = medium.shape
    lanes = rates.shape[1]
    window = rising.shape[1]
    part_rows = share // HALVES
    step = min(STEP, part_rows)
    small = (part_rows // ROWS, lanes)
    operands = [gates, swapped, within, inputs, medium, rates, scales, rising, ends, *arrived]
    result = jax.ShapeDtypeStruct((1, 2 * share, tokens), jnp.bfloat16)
    chained = [] if before is None else [before]
    return pl.pallas_call(
        functools.partial(
            output_kernel,
            len(arrived),
            lanes // ROWS,
            window,
            step,
            half * part_rows,
            share,
        ),
        out_shape=(result,) + (jax.ShapeDtypeStruct((part_rows, tokens), jnp.bfloat16),) * 2,
        in_specs=[SMEM_SPEC] * 2 + [VMEM_SPEC] * len(operands) + [ANY_SPEC] * len(chained),
        out_specs=(ANY_SPEC, VMEM_SPEC, VMEM_SPEC),
        scratch_shapes=[pltpu.VMEM(small, jnp.float32)] * 4
        + [pltpu.SemaphoreType.DMA],
        input_output_aliases={2 + len(operands): 0} if chained else {},
        name="output",
        cost_estimate=cost(part_rows, tokens, 1500),
        compiler_params=COMPILER,
    )(*place, *operands, *chained)


def place_kernel(first, share, sec, before, received, *rest):
    kept, (out, done) = rest[:-2], rest[-2:]
    rows = received.shape[0]

    def target(section, start):
        return out.at[0, pl.ds(pl.multiple_of(section * share + start, rows), rows), :]

    foreign = pltpu.make_async_copy(received, target(1 - sec[0], first), done.at[0])
    foreign.start()

    @pl.when(sec[0] == 1)
    def _():
        copies = [
            pltpu.make_async_copy(keep, target(1, k * rows), done.at[k + 1])
            for k, keep in enumerate(kept)
        ]
        for copy in copies:
            copy.start()
        for copy in copies:
            copy.wait()

    foreign.wait()


def place_call(place, half, before, received, kept):
    rows, tokens = received.shape
    return pl.pallas_call(
        functools.partial(place_kernel, half * rows, before.shape[1] // 2),
        out_shape=jax.ShapeDtypeStruct(before.shape, before.dtype),
        in_specs=[SMEM_SPEC, ANY_SPEC] + [VMEM_SPEC] * (1 + len(kept)),
        out_specs=ANY_SPEC,
        scratch_shapes=[pltpu.SemaphoreType.DMA((1 + len(kept),))],
        input_output_aliases={1: 0},
        name="placing",
        cost_estimate=cost(rows, tokens, 2),
        compiler_params=COMPILER,
    )(place[0], before, received, *kept)


def edge_kernel(gates, inputs, low, high, gate_tail, input_tail, arrival):
    share, window = low.shape
    tail = pl.ds(inputs.shape[1] - window, window)
    pairs = [(gates.at[0, 1, :, tail], gate_tail), (inputs.at[:, tail], input_tail)]
    copies = [
        pltpu.make_async_copy(source, target, arrival.at[k])
        for k, (source, target) in enumerate(pairs)
    ]
    for copy in copies:
        copy.start()
    for copy in copies:
        copy.wait()
    low[...] = gate_tail[:share, :] * input_tail[:share, :]
    high[...] = gate_tail[share:, :] * input_tail[share:, :]


def edge_call(gate_streams, inputs, window, share):
    channels, tokens = inputs.shape
    edge = jax.ShapeDtypeStruct((share, window), jnp.bfloat16)
    return pl.pallas_call(
        edge_kernel,
        out_shape=(edge, edge),
        in_specs=[ANY_SPEC] * 2,
        out_specs=(VMEM_SPEC,) * 2,
        scratch_shapes=[pltpu.VMEM((channels, window), jnp.bfloat16)] * 2
        + [pltpu.SemaphoreType.DMA((2,))],
        name="edge",
        cost_estimate=cost(share, tokens, 2),
        compiler_params=COMPILER,
    )(*parked(gate_streams, inputs))


def ring(value, axis, by):
    peers = lax.axis_size(axis)
    return lax.ppermute(value, axis, [(i, (i + by) % peers) for i in range(peers)])


def met(value, by):
    peers = lax.axis_size("tok")
    return lax.ppermute(value, "tok", [(i, i ^ by) for i in range(peers)])


def edge_to(value, section):
    peers = lax.axis_size("tok")
    pairs = [(i, section * peers + (i + 1) % peers) for i in range(peers)]
    pairs += [(peers + i, (1 - section) * peers + i) for i in range(peers)]
    return lax.ppermute(value, ("section", "tok"), pairs)


def on_device(gate_streams, inputs, medium_taps, residues, decay_rates):
    channels, _ = inputs.shape
    share = channels // 2
    window = medium_taps.shape[1]
    modes = decay_rates.shape[1]
    place = tuple(
        lax.axis_index(axis).astype(jnp.int32).reshape(1) for axis in ("section", "tok")
    )
    edges = edge_call(gate_streams, inputs, window, share)
    halos = [edge_to(edges[s], s) for s in range(2)]
    swapped = ring(gate_streams[0], "section", 1)
    forward, inverse = fourier_tables(window)
    turned, back, doubled = turned_tables(window)
    tables = [*forward, *inverse, *split_pair(turned), split_pair(back)[0]]
    high, low = split_pair(doubled)
    tables += [jnp.concatenate([high, high], axis=0), low]
    built, own, tables = response_call(
        place,
        decay_rates.T,
        residues.T,
        gate_streams,
        inputs,
        medium_taps,
        tables,
        window,
        share,
    )
    response, rates, scales, rising, falling = built
    gates, inputs, taps = own
    medium, signals, *specs, remote = later_call(
        place, gates, swapped, inputs, taps, tables[:4]
    )
    medium, signals, ends, total = first_call(
        place,
        gates,
        remote,
        inputs,
        halos,
        rates,
        falling,
        specs,
        tables[1:3],
        medium,
        signals,
        modes,
    )
    arrived = []
    for by in range(1, lax.axis_size("tok")):
        arrived.append(met(total, by))
    within = within_call(signals, response, tables[4:])
    result, waiting = None, []
    for half in range(HALVES):
        result, send, keep = output_call(
            place,
            half,
            gates,
            remote,
            within,
            inputs,
            medium,
            rates,
            scales,
            rising,
            ends,
            arrived,
            result,
        )
        waiting.append((ring(send, "section", 1), keep))
    kept = [keep for _, keep in waiting]
    for half, (received, _) in enumerate(waiting):
        result = place_call(place, half, result, received, [] if half else kept)
    return result


def solution(mesh):
    placed = (
        P("section", None, "chan", "tok"),
        P("chan", "tok"),
        P("chan", None),
        P("chan", None),
        P("chan", None),
    )
    return jax.shard_map(
        on_device,
        mesh=mesh,
        in_specs=placed,
        out_specs=P("section", "chan", "tok"),
        check_vma=False,
    )
```

```python
import functools

import jax
import jax.numpy as jnp
import numpy as np
from jax import lax
from jax.experimental import pallas as pl
from jax.experimental.pallas import tpu as pltpu
from jax.sharding import PartitionSpec as P


ROWS = 8


def split_pair(matrix):
    high = jnp.asarray(matrix, jnp.float32).astype(jnp.bfloat16)
    low = (jnp.asarray(matrix, jnp.float32) - high.astype(jnp.float32)).astype(jnp.bfloat16)
    return high, low


def stacked(matrix, axis):
    return jnp.concatenate(split_pair(matrix), axis=axis)


def fourier_tables(window):
    size = 2 * window
    time = np.arange(window)[:, None]
    freq = np.arange(window)[None, :]
    angle = 2.0 * np.pi * ((time * freq) % size) / size
    sign = np.where(freq % 2 == 0, 1.0, -1.0)
    nyquist = np.where(time % 2 == 0, 1.0, -1.0)
    weight = np.where(freq == 0, 1.0, 2.0) / size
    forward, inverse = [], []
    for odd in range(2):
        flip = sign if odd else np.ones_like(sign)
        real = np.cos(angle) * flip
        imag = -np.sin(angle) * flip
        imag[:, :1] = nyquist
        forward.append(stacked(np.concatenate([real, imag], axis=1), 0))
        back_real = np.cos(angle) * weight * flip
        back_imag = -np.sin(angle) * weight * flip
        back_imag[:, :1] = nyquist / size
        inverse.append(stacked(np.concatenate([back_real.T, back_imag.T], axis=0), 1))
    return forward, inverse


def turned_tables(window):
    half = window // 2
    time = np.arange(window)[:, None]
    freq = 2 * np.arange(half)[None, :] + 1
    angle = np.pi * ((time * freq) % (2 * window)) / window
    real, imag = np.cos(angle), -np.sin(angle)
    zero = np.zeros_like(real)
    forward = np.concatenate(
        [
            np.concatenate([real, zero, imag, zero], axis=1),
            np.concatenate([zero, real, zero, imag], axis=1),
        ],
        axis=0,
    )
    inverse = forward.T * (2.0 / window)
    doubled = np.concatenate([real, real, imag, imag], axis=1)
    return forward, inverse, doubled


PAIR = 16
STEP = 512
HALVES = 2
COMPILER = pltpu.CompilerParams(vmem_limit_bytes=16 << 20)


def parked(*arrays):
    return [pltpu.with_memory_space_constraint(a, pltpu.HBM) for a in arrays]


def cost(share, tokens, work):
    size = share * tokens
    return pl.CostEstimate(
        flops=size * work, bytes_accessed=size * 12, transcendentals=size // 64
    )


def dot_f32(left, right):
    return jnp.dot(left, right, preferred_element_type=jnp.float32)


def dot_turned(left, right):
    return lax.dot_general(
        left, right, (((1,), (1,)), ((), ())), preferred_element_type=jnp.float32
    )


VMEM_SPEC = pl.BlockSpec(memory_space=pltpu.VMEM)
SMEM_SPEC = pl.BlockSpec(memory_space=pltpu.SMEM)
ANY_SPEC = pl.BlockSpec(memory_space=pl.ANY)


def rows_at(ref, step, i, axis=0):
    start = i * step
    if not isinstance(i, int):
        start = pl.multiple_of(start, step)
    return ref.at[(slice(None),) * axis + (pl.ds(start, step),)]


def both_gates(local, remote, section, step, i):
    mine, other = rows_at(local, step, i, 1), rows_at(remote, step, i, 1)
    return (mine, other) if section == 0 else (other, mine)


def by_section(sec, body):
    for section in range(2):
        pl.when(sec[0] == section)(functools.partial(body, section))


def lane_mask(modes):
    shape = (ROWS, ROWS * modes)
    lane = lax.broadcasted_iota(jnp.int32, shape, 1)
    return lane // modes == lax.broadcasted_iota(jnp.int32, shape, 0)


def spread(ref, group):
    return jnp.broadcast_to(ref[group : group + 1, :], (ROWS, ref.shape[1]))


def powers(slow, hop, window, first, falling):
    row = lax.broadcasted_iota(jnp.int32, slow.shape, 0).astype(jnp.float32)
    tiles = [jnp.exp(-slow * (first + (ROWS - 1 - row if falling else row)))]
    while len(tiles) < window // ROWS:
        tiles = tiles + [tile * hop for tile in tiles]
        hop = hop * hop
    if falling:
        tiles = tiles[::-1]
    return jnp.concatenate(tiles, axis=0).astype(jnp.bfloat16)


def both_powers(rates, hops, pair, window, falling):
    sides = [
        powers(spread(rates, g), spread(hops, g), window, 0.0, falling)
        for g in (2 * pair, 2 * pair + 1)
    ]
    return jnp.concatenate(sides, axis=1)


def two_sided(upper, lower):
    zero = jnp.zeros_like(upper)
    return jnp.concatenate(
        [
            jnp.concatenate([upper, zero], axis=1),
            jnp.concatenate([zero, lower], axis=1),
        ],
        axis=0,
    )


def scale_of(residues, slow):
    return residues * jnp.sqrt(1.0 - jnp.exp(-2.0 * slow))


def in_rows(ref, tall):
    _, channels = ref.shape
    tall[...] = ref[...].T
    count = channels // ROWS
    return jnp.concatenate(
        [tall[pl.ds(c, count, stride=ROWS), :] for c in range(ROWS)], axis=1
    )


def response_kernel(count, window, sec, tok, rates, residues, *rest):
    gates, inputs, taps = rest[:3]
    tables = rest[3 : 3 + count]
    out, rate_rows, scale_rows, rising, falling = rest[3 + count : 8 + count]
    own_gates, own_inputs, own_taps = rest[8 + count : 11 + count]
    own_tables = rest[11 + count : 11 + 2 * count]
    tall, hops, scales, arrival = rest[11 + 2 * count :]
    share = out.shape[0]
    step = tall.shape[0]
    modes = rates.shape[0]
    first = pl.multiple_of(sec[0] * share, share)
    mine = pl.ds(first, share)
    pairs = [(gates.at[0, :, mine, :], own_gates)]
    pairs += [(inputs.at[mine, :], own_inputs), (taps.at[mine, :], own_taps)]
    pairs += list(zip(tables, own_tables))
    copies = [
        pltpu.make_async_copy(source, target, arrival.at[k])
        for k, (source, target) in enumerate(pairs)
    ]
    for copy in copies:
        copy.start()
    mask = lane_mask(modes)

    @pl.loop(0, share // step)
    def _(i):
        lanes = pl.ds(pl.multiple_of(first + i * step, step), step)
        slow = in_rows(rates.at[:, lanes], tall)
        scale = scale_of(in_rows(residues.at[:, lanes], tall), slow)
        small = step // ROWS
        own_rates = rows_at(rate_rows, small, i)
        own_rates[...] = slow
        rows_at(scale_rows, small, i)[...] = scale
        hops[...] = jnp.exp(-slow * ROWS)
        scales[...] = scale / (1.0 + jnp.exp(-slow * window))
        up, down = rows_at(rising, step // PAIR, i), rows_at(falling, step // PAIR, i)
        own_out = rows_at(out, step, i)
        for pair in range(step // PAIR):
            both = two_sided(
                jnp.where(mask, spread(scales, 2 * pair), 0.0),
                jnp.where(mask, spread(scales, 2 * pair + 1), 0.0),
            )
            high = both.astype(jnp.bfloat16).astype(jnp.float32)
            both = jnp.concatenate([high, both - high], axis=0).astype(jnp.bfloat16)
            table = both_powers(own_rates, hops, pair, window, False)
            up[pair] = table
            down[pair] = both_powers(own_rates, hops, pair, window, True)
            found = dot_turned(both, table)
            out_rows = pl.ds(pair * PAIR, PAIR)
            own_out[out_rows, :] = found[:PAIR] + found[PAIR:]

    for copy in copies:
        copy.wait()


def response_call(place, rates, residues, gates, inputs, taps, tables, window, share):
    tokens = inputs.shape[1]
    step = min(STEP, share)
    modes = rates.shape[0]
    lanes = ROWS * modes
    small = (step // ROWS, lanes)
    shape = lambda dims, kind=jnp.float32: jax.ShapeDtypeStruct(dims, kind)
    power_shape = shape((share // PAIR, window, 2 * lanes), jnp.bfloat16)
    outs = [shape((share, window))] + [shape((share // ROWS, lanes))] * 2
    outs += [power_shape] * 2
    outs += [
        shape((2, share, tokens), gates.dtype),
        shape((share, tokens), inputs.dtype),
        shape((share, window), taps.dtype),
    ]
    outs += [shape(t.shape, t.dtype) for t in tables]
    staged = 3 + len(tables)
    found = pl.pallas_call(
        functools.partial(response_kernel, len(tables), window),
        out_shape=tuple(outs),
        in_specs=[SMEM_SPEC] * 2 + [VMEM_SPEC] * 2 + [ANY_SPEC] * staged,
        out_specs=(VMEM_SPEC,) * len(outs),
        scratch_shapes=[
            pltpu.VMEM((step, modes), jnp.float32),
            pltpu.VMEM(small, jnp.float32),
            pltpu.VMEM(small, jnp.float32),
            pltpu.SemaphoreType.DMA((staged,)),
        ],
        name="response",
        cost_estimate=cost(share, 4 * window, 900),
        compiler_params=COMPILER,
    )(*place, rates, residues, *parked(gates, inputs, taps, *tables))
    return found[:5], found[5:8], found[8:]


def products(members, tap_spec):
    window = tap_spec.shape[1] // 2
    real, packed = tap_spec[:, :window], tap_spec[:, window:]
    lane = lax.broadcasted_iota(jnp.int32, real.shape, 1)
    real_b = jnp.where(lane == 0, packed, real)
    imag = jnp.where(lane == 0, 0.0, packed)
    found = []
    for mixed in members:
        a, b = mixed[:, :window], mixed[:, window:]
        found.append(
            jnp.concatenate([a * real - b * imag, a * imag + b * real_b], axis=1).astype(
                jnp.bfloat16
            )
        )
    return found


def doubled_spectrum(members, table):
    rows = jnp.concatenate(members, axis=0)
    found = dot_f32(jnp.concatenate([rows, rows], axis=1), table[...])
    size = members[0].shape[0]
    return [found[k * size : (k + 1) * size] for k in range(len(members))]


def finish_medium(members, table, gates_out, gates_in, streams, targets):
    found = dot_f32(jnp.concatenate(members, axis=0), table[...])
    size, window = streams[0].shape
    signals = []
    for k in range(len(members)):
        rows = slice(k * size, (k + 1) * size)
        medium = found[rows, :window] + found[rows, window:]
        gated = (gates_out[k].astype(jnp.float32) * medium).astype(jnp.bfloat16)
        targets[k][...] = gated
        stream = streams[k].astype(jnp.float32) + gated.astype(jnp.float32)
        signals.append((gates_in[k].astype(jnp.float32) * stream).astype(jnp.bfloat16))
    return signals


def end_states(signals, powers_of_pair, pair, modes, mask):
    rows = slice(pair * PAIR, (pair + 1) * PAIR)
    lanes = ROWS * modes
    left = jnp.concatenate([signal[rows] for signal in signals], axis=0)
    found = dot_f32(left, powers_of_pair)
    sides = []
    for side in range(2):
        tops = [k * PAIR + side * ROWS for k in range(len(signals))]
        sides.append(
            [
                jnp.where(mask, found[top : top + ROWS, side * lanes : (side + 1) * lanes], 0.0)
                for top in tops
            ]
        )
    return sides


def later_kernel(
    step,
    sec,
    tok,
    local_all,
    swapped,
    inputs_all,
    taps_all,
    fwd_even,
    fwd_odd,
    inv_even,
    inv_odd,
    medium_all,
    signals_all,
    tap_spec_all,
    edge_spec_all,
    remote_all,
    arrival,
):
    share, tokens = inputs_all.shape
    window = taps_all.shape[1]
    blocks = tokens // window
    parts = [slice(b * window, (b + 1) * window) for b in range(blocks)]

    def fetch(i):
        source = pl.ds(pl.multiple_of(sec[0] * share + i * step, step), step)
        return pltpu.make_async_copy(
            swapped.at[:, source, :], rows_at(remote_all, step, i, 1), arrival.at[i]
        )

    for i in range(share // step):
        fetch(i).start()

    def chunk(section, i):
        fetch(i).wait()
        first, second = both_gates(local_all, remote_all, section, step, i)
        inputs = rows_at(inputs_all, step, i)
        medium_out, signals = rows_at(medium_all, step, i), rows_at(signals_all, step, i)
        sources = [first[1, :, part] * inputs[:, part] for part in parts]
        tap_rows = rows_at(taps_all, step, i)[...]
        tap_spec, *even = doubled_spectrum([tap_rows] + sources[0::2], fwd_even)
        odd = doubled_spectrum(sources[1::2], fwd_odd)
        in_order = [None] * blocks
        in_order[0::2] = even
        in_order[1::2] = odd
        rows_at(tap_spec_all, step, i)[...] = tap_spec
        rows_at(edge_spec_all, step, i)[...] = in_order[0]
        mixed = products([in_order[b - 1] + in_order[b] for b in range(1, blocks)], tap_spec)
        for parity, table in enumerate((inv_even, inv_odd)):
            chosen = [b for b in range(1, blocks) if b % 2 == parity]
            if not chosen:
                continue
            found = finish_medium(
                [mixed[b - 1] for b in chosen],
                table,
                [first[0, :, parts[b]] for b in chosen],
                [second[1, :, parts[b]] for b in chosen],
                [inputs[:, parts[b]] for b in chosen],
                [medium_out.at[:, parts[b]] for b in chosen],
            )
            for b, signal in zip(chosen, found):
                signals[:, parts[b]] = signal

    def body(section):
        pl.loop(0, share // step)(functools.partial(chunk, section))

    by_section(sec, body)


def later_call(place, gates, swapped, inputs, taps, tables):
    share, tokens = inputs.shape
    window = taps.shape[1]
    operands = [gates, *parked(swapped), inputs, taps, *tables]
    spec = jax.ShapeDtypeStruct((share, 2 * window), jnp.float32)
    wide = jax.ShapeDtypeStruct((share, tokens), jnp.bfloat16)
    return pl.pallas_call(
        functools.partial(later_kernel, min(STEP, share)),
        out_shape=(wide, wide, spec, spec, jax.ShapeDtypeStruct(gates.shape, gates.dtype)),
        in_specs=[SMEM_SPEC] * 2 + [VMEM_SPEC, ANY_SPEC] + [VMEM_SPEC] * (len(operands) - 2),
        out_specs=(VMEM_SPEC,) * 5,
        scratch_shapes=[pltpu.SemaphoreType.DMA((share // min(STEP, share),))],
        name="later",
        cost_estimate=cost(share, tokens, 1500),
        compiler_params=COMPILER,
    )(*place, *operands)


def first_kernel(
    modes,
    step,
    sec,
    tok,
    local_all,
    remote_all,
    inputs_all,
    halo_low,
    halo_high,
    rates,
    falling_all,
    tap_spec_all,
    edge_spec_all,
    fwd_odd,
    inv_even,
    medium_before,
    signals_before,
    medium_all,
    signals_all,
    ends_all,
    total_all,
    leaps_all,
):
    share = inputs_all.shape[0]
    window = tap_spec_all.shape[1] // 2
    part = slice(0, window)
    mask = lane_mask(modes)
    leaps_all[...] = jnp.exp(-rates[...] * window)

    def chunk(section, i):
        first, second = both_gates(local_all, remote_all, section, step, i)
        halo = rows_at(halo_low if section == 0 else halo_high, step, i)
        leaps = rows_at(leaps_all, step // ROWS, i)
        falling = rows_at(falling_all, step // PAIR, i)
        ends = rows_at(ends_all, step, i, 1)
        started = jnp.where(tok[0] > 0, 1.0, 0.0).astype(jnp.bfloat16)
        (before,) = doubled_spectrum([halo[...] * started], fwd_odd)
        mixed = products(
            [before + rows_at(edge_spec_all, step, i)[...]],
            rows_at(tap_spec_all, step, i)[...],
        )
        (signal,) = finish_medium(
            mixed,
            inv_even,
            [first[0, :, part]],
            [second[1, :, part]],
            [rows_at(inputs_all, step, i)[:, part]],
            [rows_at(medium_all, step, i).at[:, part]],
        )
        signals = rows_at(signals_all, step, i)
        signals[:, part] = signal
        members = [signal] + [
            signals[:, b * window : (b + 1) * window] for b in range(1, ends.shape[0])
        ]
        sums = []
        for pair in range(step // PAIR):
            sides = end_states(members, falling[pair], pair, modes, mask)
            for side, found in enumerate(sides):
                at = pair * PAIR + side * ROWS
                leap = spread(leaps, 2 * pair + side)
                state = None
                for b, end in enumerate(found):
                    ends[b, at : at + ROWS, :] = end
                    state = end if state is None else state * leap + end
                sums.append(jnp.sum(state, axis=0, keepdims=True))
        total = rows_at(total_all, step // ROWS, i)
        total[...] = jnp.concatenate(sums, axis=0).astype(total.dtype)

    def body(section):
        pl.loop(0, share // step)(functools.partial(chunk, section))

    by_section(sec, body)


def first_call(
    place, gates, swapped, inputs, halos, rates, falling, specs, tables, medium, signals, modes
):
    share, tokens = inputs.shape
    window = halos[0].shape[1]
    lanes = ROWS * modes
    small = (share // ROWS, lanes)
    operands = [gates, swapped, inputs, *halos, rates, falling, *specs, *tables, medium, signals]
    return pl.pallas_call(
        functools.partial(first_kernel, modes, min(2 * STEP, share)),
        out_shape=(
            jax.ShapeDtypeStruct(medium.shape, medium.dtype),
            jax.ShapeDtypeStruct(signals.shape, signals.dtype),
            jax.ShapeDtypeStruct((tokens // window, share, lanes), jnp.float32),
            jax.ShapeDtypeStruct(small, jnp.bfloat16),
        ),
        in_specs=[SMEM_SPEC] * 2 + [VMEM_SPEC] * len(operands),
        out_specs=(VMEM_SPEC,) * 4,
        scratch_shapes=[pltpu.VMEM(small, jnp.float32)],
        input_output_aliases={len(operands): 0, len(operands) + 1: 1},
        name="first",
        cost_estimate=cost(share, tokens, 500),
        compiler_params=COMPILER,
    )(*place, *operands)


def within_kernel(
    step,
    signals_all,
    response_all,
    fwd_h,
    fwd_l,
    inverse,
    table_h,
    table_l,
    out_all,
):
    share, tokens = signals_all.shape
    size = fwd_h.shape[0]
    half = size // 2

    def chunk(i):
        signals = rows_at(signals_all, step, i)
        taps, out = rows_at(response_all, step, i)[...], rows_at(out_all, step, i)
        high = taps.astype(jnp.bfloat16)
        low = (taps - high.astype(jnp.float32)).astype(jnp.bfloat16)
        response = dot_f32(jnp.concatenate([high, low], axis=1), table_h[...]) + dot_f32(
            high, table_l[...]
        )
        channels = step
        real, imag = response[:, :half], response[:, half:]
        parts = [slice(k * size, (k + 1) * size) for k in range(tokens // size)]
        signal = jnp.concatenate([signals[:, part] for part in parts], axis=0)
        spec = dot_f32(signal, fwd_h[...]) + dot_f32(signal, fwd_l[...])
        filtered = []
        for k in range(len(parts)):
            rows = slice(k * channels, (k + 1) * channels)
            a, b = spec[rows, :half], spec[rows, half:]
            filtered.append(
                jnp.concatenate([a * real - b * imag, a * imag + b * real], axis=1).astype(
                    jnp.bfloat16
                )
            )
        found = dot_f32(jnp.concatenate(filtered, axis=0), inverse[...])
        for k, part in enumerate(parts):
            out[:, part] = found[k * channels : (k + 1) * channels]

    pl.loop(0, share // step)(chunk)


def within_call(signals, response, tables):
    share, tokens = signals.shape
    operands = [signals, response, *tables]
    return pl.pallas_call(
        functools.partial(within_kernel, min(2 * STEP, share)),
        out_shape=jax.ShapeDtypeStruct((share, tokens), jnp.float32),
        in_specs=[VMEM_SPEC] * len(operands),
        out_specs=VMEM_SPEC,
        name="within",
        cost_estimate=cost(share, tokens, 1500),
        compiler_params=COMPILER,
    )(*operands)


def output_kernel(
    count,
    modes,
    window,
    step,
    first,
    share,
    sec,
    tok,
    local_all,
    remote_all,
    within_all,
    inputs_all,
    medium_all,
    rates,
    scale_rows,
    rising_all,
    ends_all,
    *rest,
):
    arrived = rest[:count]
    (result, send, keep, leaps_all, scales_all, shares_all, starts_all, done) = rest[-8:]
    part_rows, tokens = send.shape
    base = first // step
    groups = pl.ds(first // ROWS, part_rows // ROWS)
    blocks = tokens // window
    mask = lane_mask(modes)
    slow = rates[groups, :]
    leap_all = jnp.exp(-slow * window)
    scale_all = scale_rows[groups, :] * jnp.exp(-slow)
    leaps_all[...] = leap_all
    scales_all[...] = scale_all
    shares_all[...] = scale_all / (1.0 + leap_all)
    entering = jnp.zeros_like(slow)
    for k in range(count):
        gap = tok[0] - (tok[0] ^ (k + 1))
        known = jnp.where(gap > 0, 1.0, 0.0)
        distance = (tokens * jnp.maximum(gap - 1, 0)).astype(jnp.float32)
        entering = entering + arrived[k][groups, :].astype(jnp.float32) * (
            jnp.exp(-slow * distance) * known
        )
    starts_all[...] = entering

    def chunk(section, out_all, i):
        out = rows_at(out_all, step, i)
        at_all = base + i
        gate_out = both_gates(local_all, remote_all, section, step, at_all)[1].at[0]
        inputs = rows_at(inputs_all, step, at_all)
        gated_medium = rows_at(medium_all, step, at_all)
        within = rows_at(within_all, step, at_all)
        ends = rows_at(ends_all, step, at_all, 1)
        rising = rows_at(rising_all, step // PAIR, at_all)
        small = step // ROWS
        leaps, scales = rows_at(leaps_all, small, i), rows_at(scales_all, small, i)
        shares, starts = rows_at(shares_all, small, i), rows_at(starts_all, small, i)
        channels = step
        for pair in range(channels // PAIR):
            rows = slice(pair * PAIR, (pair + 1) * PAIR)
            sides = []
            for side in range(2):
                group = 2 * pair + side
                leap, scale = spread(leaps, group), spread(scales, group)
                portion = spread(shares, group)
                state = jnp.where(mask, spread(starts, group), 0.0)
                at = pair * PAIR + side * ROWS
                lefts = []
                for b in range(blocks):
                    end = ends[b, at : at + ROWS, :]
                    lefts.append(state * scale + end * portion)
                    state = state * leap + end
                sides.append(lefts)
            left = jnp.concatenate(
                [two_sided(upper, lower) for upper, lower in zip(*sides)], axis=0
            ).astype(jnp.bfloat16)
            across = dot_turned(left, rising[pair])
            for b in range(blocks):
                part = slice(b * window, (b + 1) * window)
                stream = inputs[rows, part].astype(jnp.float32) + gated_medium[
                    rows, part
                ].astype(jnp.float32)
                long_out = within[rows, part] + across[b * PAIR : (b + 1) * PAIR]
                gate = gate_out[rows, part].astype(jnp.float32)
                out[rows, part] = (stream + gate * long_out).astype(jnp.bfloat16)

    def body(section):
        target = result.at[0, pl.ds(section * share + first, part_rows), :]
        source = medium_all.at[pl.ds(first, part_rows), :]
        copy = pltpu.make_async_copy(source, send if section else target, done)
        copy.start()
        pl.loop(0, part_rows // step)(
            functools.partial(chunk, section, keep if section else send)
        )
        copy.wait()

    by_section(sec, body)


def output_call(
    place, half, gates, swapped, within, inputs, medium, rates, scales, rising, ends, arrived, before
):
    share, tokens = medium.shape
    lanes = rates.shape[1]
    window = rising.shape[1]
    part_rows = share // HALVES
    step = min(STEP, part_rows)
    small = (part_rows // ROWS, lanes)
    operands = [gates, swapped, within, inputs, medium, rates, scales, rising, ends, *arrived]
    result = jax.ShapeDtypeStruct((1, 2 * share, tokens), jnp.bfloat16)
    chained = [] if before is None else [before]
    return pl.pallas_call(
        functools.partial(
            output_kernel,
            len(arrived),
            lanes // ROWS,
            window,
            step,
            half * part_rows,
            share,
        ),
        out_shape=(result,) + (jax.ShapeDtypeStruct((part_rows, tokens), jnp.bfloat16),) * 2,
        in_specs=[SMEM_SPEC] * 2 + [VMEM_SPEC] * len(operands) + [ANY_SPEC] * len(chained),
        out_specs=(ANY_SPEC, VMEM_SPEC, VMEM_SPEC),
        scratch_shapes=[pltpu.VMEM(small, jnp.float32)] * 4
        + [pltpu.SemaphoreType.DMA],
        input_output_aliases={2 + len(operands): 0} if chained else {},
        name="output",
        cost_estimate=cost(part_rows, tokens, 1500),
        compiler_params=COMPILER,
    )(*place, *operands, *chained)


def place_kernel(first, share, sec, tok, before, received, keep, out, done):
    rows = received.shape[0]

    def target(section):
        return out.at[0, pl.ds(pl.multiple_of(section * share + first, rows), rows), :]

    foreign = pltpu.make_async_copy(received, target(1 - sec[0]), done.at[0])
    foreign.start()

    @pl.when(sec[0] == 1)
    def _():
        own = pltpu.make_async_copy(keep, target(1), done.at[1])
        own.start()
        own.wait()

    foreign.wait()


def place_call(place, half, before, received, keep):
    rows, tokens = received.shape
    return pl.pallas_call(
        functools.partial(place_kernel, half * rows, before.shape[1] // 2),
        out_shape=jax.ShapeDtypeStruct(before.shape, before.dtype),
        in_specs=[SMEM_SPEC] * 2 + [ANY_SPEC, VMEM_SPEC, VMEM_SPEC],
        out_specs=ANY_SPEC,
        scratch_shapes=[pltpu.SemaphoreType.DMA((2,))],
        input_output_aliases={2: 0},
        name="placing",
        cost_estimate=cost(rows, tokens, 2),
        compiler_params=COMPILER,
    )(*place, before, received, keep)


def edge_kernel(gates, inputs, low, high, gate_tail, input_tail, arrival):
    share, window = low.shape
    tail = pl.ds(inputs.shape[1] - window, window)
    halves = [pl.ds(k * share, share) for k in range(2)]
    copies = []
    for k, rows in enumerate(halves):
        pairs = [(gates.at[0, 1, rows, tail], gate_tail), (inputs.at[rows, tail], input_tail)]
        for m, (source, target) in enumerate(pairs):
            copies.append(
                pltpu.make_async_copy(source, target.at[rows, :], arrival.at[2 * k + m])
            )
    for copy in copies:
        copy.start()
    for k, (rows, edge) in enumerate(zip(halves, (low, high))):
        copies[2 * k].wait()
        copies[2 * k + 1].wait()
        edge[...] = gate_tail[rows, :] * input_tail[rows, :]


def edge_call(gate_streams, inputs, window, share):
    channels, tokens = inputs.shape
    edge = jax.ShapeDtypeStruct((share, window), jnp.bfloat16)
    return pl.pallas_call(
        edge_kernel,
        out_shape=(edge, edge),
        in_specs=[ANY_SPEC] * 2,
        out_specs=(VMEM_SPEC,) * 2,
        scratch_shapes=[pltpu.VMEM((channels, window), jnp.bfloat16)] * 2
        + [pltpu.SemaphoreType.DMA((4,))],
        name="edge",
        cost_estimate=cost(share, tokens, 2),
        compiler_params=COMPILER,
    )(*parked(gate_streams, inputs))


def ring(value, axis, by):
    peers = lax.axis_size(axis)
    return lax.ppermute(value, axis, [(i, (i + by) % peers) for i in range(peers)])


def met(value, by):
    peers = lax.axis_size("tok")
    return lax.ppermute(value, "tok", [(i, i ^ by) for i in range(peers)])


def edge_to(value, section):
    peers = lax.axis_size("tok")
    pairs = [(i, section * peers + (i + 1) % peers) for i in range(peers)]
    pairs += [(peers + i, (1 - section) * peers + i) for i in range(peers)]
    return lax.ppermute(value, ("section", "tok"), pairs)


def on_device(gate_streams, inputs, medium_taps, residues, decay_rates):
    channels, _ = inputs.shape
    share = channels // 2
    window = medium_taps.shape[1]
    modes = decay_rates.shape[1]
    place = tuple(
        lax.axis_index(axis).astype(jnp.int32).reshape(1) for axis in ("section", "tok")
    )
    edges = edge_call(gate_streams, inputs, window, share)
    halos = [edge_to(edges[s], s) for s in range(2)]
    swapped = ring(gate_streams[0], "section", 1)
    forward, inverse = fourier_tables(window)
    turned, back, doubled = turned_tables(window)
    tables = [*forward, *inverse, *split_pair(turned), split_pair(back)[0]]
    high, low = split_pair(doubled)
    tables += [jnp.concatenate([high, high], axis=0), low]
    built, own, tables = response_call(
        place,
        decay_rates.T,
        residues.T,
        gate_streams,
        inputs,
        medium_taps,
        tables,
        window,
        share,
    )
    response, rates, scales, rising, falling = built
    gates, inputs, taps = own
    medium, signals, *specs, remote = later_call(
        place, gates, swapped, inputs, taps, tables[:4]
    )
    medium, signals, ends, total = first_call(
        place,
        gates,
        remote,
        inputs,
        halos,
        rates,
        falling,
        specs,
        tables[1:3],
        medium,
        signals,
        modes,
    )
    arrived = []
    for by in range(1, lax.axis_size("tok")):
        arrived.append(met(total, by))
    within = within_call(signals, response, tables[4:])
    result, waiting = None, []
    for half in range(HALVES):
        result, send, keep = output_call(
            place,
            half,
            gates,
            remote,
            within,
            inputs,
            medium,
            rates,
            scales,
            rising,
            ends,
            arrived,
            result,
        )
        waiting.append((ring(send, "section", 1), keep))
    for half, (received, keep) in enumerate(waiting):
        result = place_call(place, half, result, received, keep)
    return result


def solution(mesh):
    placed = (
        P("section", None, "chan", "tok"),
        P("chan", "tok"),
        P("chan", None),
        P("chan", None),
        P("chan", None),
    )
    return jax.shard_map(
        on_device,
        mesh=mesh,
        in_specs=placed,
        out_specs=P("section", "chan", "tok"),
        check_vma=False,
    )
```
